32 devices in a mesh: rep: 4 (over y, x), ctx: 8 (over z, core).
Axes of the slice: x: 2, y: 2, z: 4, core: 2. Of those that a mesh axis runs over, the one named last changes fastest.
Arguments:
- inputs: bfloat16 [4, 1024, 1536], P('rep', 'ctx'), may hold values from -6 to 6
- segments: int32 [4, 1024], P('rep', 'ctx'), may hold values from 0 to 8, as said below
- positions: int32 [4, 1024], P('rep', 'ctx'), may hold values from 0 to 3070, as said below
- expert_ids: int32 [4, 1024, 8], P('rep', 'ctx'), may hold values from 0 to 15, all different within a row; in each aligned block of 128 rows (0 to 127, 128 to 255, ..., all dimensions but the last counted through in order) at most 96 rows name the same one
- attn_gain: bfloat16 [1536], P('ctx'), may hold values from 0.099609375 to 1.8984375
- w_query: bfloat16 [1536, 1536], P('ctx'), may hold values from -0.15625 to 0.15625
- key_weight: bfloat16 [1536, 512], P('ctx'), may hold values from -0.15625 to 0.15625
- value_weight: bfloat16 [1536, 512], P('ctx'), may hold values from -0.15625 to 0.15625
- w_out: bfloat16 [1536, 1536], P('ctx'), may hold values from -1.25 to 1.25
- ffn_gain: bfloat16 [1536], P('ctx'), may hold values from 0.099609375 to 1.8984375
- router: bfloat16 [1536, 16], P('ctx'), may hold values from -0.078125 to 0.078125
- w_gate: bfloat16 [16, 1536, 512], P('ctx'), may hold values from -0.15625 to 0.15625
- w_up: bfloat16 [16, 1536, 512], P('ctx'), may hold values from -0.15625 to 0.15625
- w_down: bfloat16 [16, 512, 1536], P('ctx'), may hold values from -1 to 1
- grad_out: bfloat16 [4, 1024, 1536], P('rep', 'ctx'), may hold values from -6 to 6
Outputs:
- outputs: bfloat16 [4, 1024, 1536], P('rep', 'ctx')
- grad_in: float32 [4, 1024, 1536], P('rep', 'ctx')
- grad_attn_gain: float32 [1536], P('ctx')
- grad_query: float32 [1536, 1536], P('ctx')
- grad_key: float32 [1536, 512], P('ctx')
- grad_value: float32 [1536, 512], P('ctx')
- grad_proj_out: float32 [1536, 1536], P('ctx')
- grad_ffn_gain: float32 [1536], P('ctx')
- grad_router: float32 [1536, 16], P('ctx')
- grad_gate: float32 [16, 1536, 512], P('ctx')
- grad_up: float32 [16, 1536, 512], P('ctx')
- grad_down: float32 [16, 512, 1536], P('ctx')
The draws below stay inside these ranges and needn't reach their ends.
Inputs may be any that keep to these rules, and one draw needn't show every extreme that they name: `segments`: per sequence, segment numbers rise from 1 to 8, each document one run of positions of heavy-tailed length, followed by a padding tail of segment 0 with at least 1 and fewer than 51 positions. Within a document the positions rise by one from a starting offset; offsets of all documents but the last are under 2048, and the last document ends at position 3070; in the padding they rise by one from 0. `expert_ids`: each token names 8 different experts; among the 128 tokens of one device (aligned blocks) no expert is named more than 96 times.
All inputs are finite; a program needn't handle non-finite values.
Results may differ from the reference program's by a relative error of at most 0.024.
Values may be sent and summed in bfloat16 or wider, within the bound.
No kernel may reach another device: no remote copies, remote signals or barrier semaphores. Data moves between devices by JAX's collectives and lax.ppermute only.
A program may use at most 192 MiB of HBM per device.

```python
import math
import jax
import jax.numpy as jnp
import numpy as np
from jax import lax

MODEL_WIDTH = 1536
QUERY_HEADS = 24
KEY_VALUE_HEADS = 8
HEAD_SIZE = 64
F = 512
TOPK = 8
DOCS = 8
TOK_DEV = 128
EXPERTS = 16
SEQ = 1024
SEQS = 4
CAP = 96


def document_layout(key):
    pad_key = jax.random.fold_in(key, 101)
    weight_key = jax.random.fold_in(key, 202)
    offset_key = jax.random.fold_in(key, 303)
    padding = jax.random.randint(pad_key, (SEQS, 1), 1, SEQ // 20).astype(jnp.int32)
    weights = (64 // jax.random.randint(weight_key, (SEQS, DOCS), 1, 65)).astype(jnp.int32)
    running = jnp.cumsum(weights, axis=1).astype(jnp.int32)
    live_length = SEQ - padding
    spread = running * (live_length - DOCS) // running[:, -1:]
    ends = spread + jnp.arange(1, DOCS + 1, dtype=jnp.int32)[None, :]
    starts = jnp.concatenate([jnp.zeros((SEQS, 1), jnp.int32), ends[:, :-1]], 1)
    places = jnp.arange(SEQ, dtype=jnp.int32)[None, :, None]
    inside = ((places >= starts[:, None, :]) & (places < ends[:, None, :])).astype(jnp.int32)
    numbers = jnp.sum(inside * jnp.arange(1, DOCS + 1, dtype=jnp.int32)[None, None, :], -1)
    offsets = jax.random.randint(offset_key, (SEQS, DOCS), 0, 2048).astype(jnp.int32)
    last_length = ends[:, -1:] - starts[:, -1:]
    last_offset = (SEQ + 2046 - (last_length - 1)).astype(jnp.int32)
    offsets = jnp.concatenate([offsets[:, :-1], last_offset], 1)
    within = jnp.sum(inside * (places - starts[:, None, :] + offsets[:, None, :]), -1)
    padded_place = jnp.arange(SEQ, dtype=jnp.int32)[None, :] - live_length
    placed = jnp.where(numbers > 0, within, padded_place)
    return (numbers.astype(jnp.int32), placed.astype(jnp.int32))


def draw_segments(key, part):
    return document_layout(key)[0]


def draw_positions(key, part):
    return document_layout(key)[1]


def shard_levels(rng, dims, cuts, least, largest):
    level = 1.0
    for dim, shards_of in cuts:
        heights = jax.random.uniform(jax.random.fold_in(jax.random.fold_in(rng, 6), dim), (shards_of,), jnp.float32, least / len(cuts), largest / len(cuts))
        level = level * jnp.repeat(jnp.exp(heights), dims[dim] // shards_of).reshape((-1,) + (1,) * (len(dims) - 1 - dim))
    return level


def deal_out(stream_key, own, number, rows, amount, top, reach, slope):
    sequence = jax.random.permutation(stream_key, amount)
    heavy_load, common = portions_of(amount, rows * top, reach, slope, True), portions_of(amount, rows * top, reach, slope, False)
    places = jnp.arange(amount)

    def named(tallies, rotation):
        used = int((tallies > 0).sum())
        fixed = max(1, used // 4)
        moved = fixed + (places - fixed + rotation * (used - fixed)) % max(1, amount - fixed)
        return jnp.zeros((amount,), jnp.int32).at[sequence[jnp.where(places < fixed, places, moved)]].set(jnp.asarray(tallies, jnp.int32))

    tallies = jnp.where(number % 4 == 0, named(heavy_load, number // 4), named(common, number - number // 4 - 1))
    mixed = jax.random.permutation(jax.random.fold_in(own, 3), amount)
    donor, receiver = mixed[0:amount // 2 * 2:2], mixed[1:amount // 2 * 2:2]
    room = jnp.minimum(tallies[donor] - 1, reach - tallies[receiver]) // 2
    room = jnp.where((donor == sequence[0]) | (receiver == sequence[0]) | (tallies[receiver] == 0), 0, jnp.maximum(room, 0))
    moved = jax.random.randint(jax.random.fold_in(own, 4), (amount // 2,), 0, 1 << 20) % (room + 1)
    tallies = tallies.at[donor].add(-moved).at[receiver].add(moved)
    items = jnp.searchsorted(jnp.cumsum(tallies), jnp.arange(rows * top), side="right").astype(jnp.int32)
    grid = items.reshape(top, rows).T
    grid = grid[jax.random.permutation(jax.random.fold_in(own, 1), rows)]
    rotation = jax.random.randint(jax.random.fold_in(own, 2), (rows, 1), 0, top)
    return jnp.take_along_axis(grid, (jnp.arange(top)[None, :] + rotation) % top, axis=1)


def portions_of(amount, total, bound, skew, full):
    weights = [(1 << 20) // math.isqrt(rank ** skew) + 1 for rank in range(1, amount + 1)]
    largest = bound if full else min(bound, max(-(-total // amount), total * weights[0] // sum(weights)))
    least = 1 if total - largest >= amount - 1 else 0
    given, surplus = [largest] + [least] * (amount - 1), total - largest - least * (amount - 1)
    while surplus > 0:
        free = [i for i in range(1, amount) if given[i] < largest] or [i for i in range(1, amount) if given[i] < bound]
        mass, left = sum([weights[i] for i in free]), surplus
        for i in free:
            addition = min(bound - given[i], max(1, left * weights[i] // mass), surplus)
            given[i] = given[i] + addition
            surplus = surplus - addition
    return np.array(given)


def normal_values(rng, extent, deviation, bound, cuts=(), held_as=jnp.bfloat16):
    gain = shard_levels(rng, extent, cuts, -0.22, 0.18) if cuts else 1.0
    drawn = jax.random.normal(rng, extent, jnp.float32) * deviation * gain
    return jnp.minimum(jnp.maximum(drawn, -bound), bound).astype(held_as)


def setup_inputs(seed: int = 0) -> dict:
    keys = jax.random.split(jax.random.key(seed), 16)
    inputs = normal_values(keys[0], (SEQS, SEQ, MODEL_WIDTH), 1.0, 6.0, ((0, 4), (1, 8)))
    segments = draw_segments(jax.random.fold_in(keys[15], 71), 0)
    positions = draw_positions(jax.random.fold_in(keys[15], 71), 0)
    expert_ids_keys = jax.random.split(jax.random.fold_in(keys[3], 1), SEQS * SEQ // TOK_DEV)
    expert_ids_turns = jax.random.permutation(jax.random.fold_in(keys[3], 3), SEQS * SEQ // TOK_DEV)
    expert_ids = jax.vmap(lambda own, number: deal_out(jax.random.fold_in(keys[3], 2), own, number, TOK_DEV, EXPERTS, TOPK, CAP, 1))(expert_ids_keys, expert_ids_turns).reshape((SEQS, SEQ, TOPK))
    attn_gain = jnp.clip(1.0 + 0.18 * jax.random.normal(keys[4], (MODEL_WIDTH,), jnp.float32), 0.099609375, 1.8984375).astype(jnp.bfloat16)
    w_query = normal_values(keys[5], (MODEL_WIDTH, QUERY_HEADS * HEAD_SIZE), MODEL_WIDTH ** -0.5, 0.15625, ((0, 8),))
    key_weight = normal_values(keys[6], (MODEL_WIDTH, KEY_VALUE_HEADS * HEAD_SIZE), MODEL_WIDTH ** -0.5, 0.15625, ((0, 8),))
    value_weight = normal_values(keys[7], (MODEL_WIDTH, KEY_VALUE_HEADS * HEAD_SIZE), MODEL_WIDTH ** -0.5, 0.15625, ((0, 8),))
    w_out = normal_values(keys[8], (QUERY_HEADS * HEAD_SIZE, MODEL_WIDTH), (max(QUERY_HEADS * HEAD_SIZE // 64, 1)) ** -0.5, 1.25, ((0, 8),))
    ffn_gain = jnp.clip(1.0 + 0.18 * jax.random.normal(keys[9], (MODEL_WIDTH,), jnp.float32), 0.099609375, 1.8984375).astype(jnp.bfloat16)
    router = normal_values(keys[10], (MODEL_WIDTH, EXPERTS), (4 * MODEL_WIDTH) ** -0.5, 0.078125, ((0, 8),))
    w_gate = normal_values(keys[11], (EXPERTS, MODEL_WIDTH, F), MODEL_WIDTH ** -0.5, 0.15625, ((0, 8),))
    w_up = normal_values(keys[12], (EXPERTS, MODEL_WIDTH, F), MODEL_WIDTH ** -0.5, 0.15625, ((0, 8),))
    w_down = normal_values(keys[13], (EXPERTS, F, MODEL_WIDTH), (max(F // 16, 1)) ** -0.5, 1.0, ((0, 8),))
    grad_out = normal_values(keys[14], (SEQS, SEQ, MODEL_WIDTH), 1.0, 6.0, ((0, 4), (1, 8)))
    return {"inputs": inputs, "segments": segments, "positions": positions, "expert_ids": expert_ids, "attn_gain": attn_gain, "w_query": w_query, "key_weight": key_weight, "value_weight": value_weight, "w_out": w_out, "ffn_gain": ffn_gain, "router": router, "w_gate": w_gate, "w_up": w_up, "w_down": w_down, "grad_out": grad_out}


EPS = 1e-06
THETA = 10000.0
MASK_FLOOR = -1e+30
TOP_PRECISION = lax.Precision.HIGHEST

@jax.custom_vjp
def lower_precision(v):
    return lax.optimization_barrier(v.astype(jnp.bfloat16)).astype(jnp.float32)

@jax.custom_vjp
def lower_backward(v):
    return v

def low_keep(v):
    return (lower_precision(v), None)

def low_pass(kept, grad):
    return (grad,)

def back_keep(v):
    return (v, None)

def back_low(kept, grad):
    return (lower_precision(grad),)
lower_precision.defvjp(low_keep, low_pass)
lower_backward.defvjp(back_keep, back_low)

def rope_tables(position_row):
    steps = jnp.arange(HEAD_SIZE // 2, dtype=jnp.float32)
    inverse = THETA ** (-(2.0 * steps) / HEAD_SIZE)
    angles = position_row.astype(jnp.float32)[:, None] * inverse[None, :]
    cosine_table = jnp.cos(angles)
    sine_table = jnp.sin(angles)
    return (jnp.concatenate([cosine_table, cosine_table], -1), jnp.concatenate([sine_table, sine_table], -1))

def apply_rotary(value_block, cosine_table, sine_table):
    half = value_block.shape[-1] // 2
    turned = jnp.concatenate([-value_block[..., half:], value_block[..., :half]], -1)
    return value_block * cosine_table[:, None, :] + turned * sine_table[:, None, :]

def attend(rotated_query, key_rot, value_matrix, segment_row):
    segment_length = rotated_query.shape[0]
    head_group = QUERY_HEADS // KEY_VALUE_HEADS
    score_scale = HEAD_SIZE ** (-0.5)
    grouped_rows = rotated_query.reshape(segment_length, KEY_VALUE_HEADS, head_group, HEAD_SIZE)
    block = min(512, segment_length)
    key_place = jnp.arange(segment_length, dtype=jnp.int32)

    def one_block(start):
        rows = lax.dynamic_slice_in_dim(grouped_rows, start, block, 0)
        row_segments = lax.dynamic_slice_in_dim(segment_row, start, block, 0)
        row_place = start + jnp.arange(block, dtype=jnp.int32)
        scores = lower_backward(jnp.einsum('tvgd,kvd->vgtk', rows, key_rot, precision=TOP_PRECISION) * score_scale)
        allowed = (row_segments[:, None] == segment_row[None, :]) & (key_place[None, :] <= row_place[:, None])
        masked = jnp.where(allowed, scores, MASK_FLOOR)
        weights = jnp.exp(masked - lax.optimization_barrier(jnp.max(masked, -1, keepdims=True)))
        probs = weights / lax.optimization_barrier(jnp.sum(weights, -1, keepdims=True))
        mixed = jnp.einsum('vgtk,kvd->tvgd', lower_precision(probs), value_matrix, precision=TOP_PRECISION)
        return mixed.reshape(block, QUERY_HEADS * HEAD_SIZE)
    starts = jnp.arange(segment_length // block, dtype=jnp.int32) * block
    return lax.map(jax.checkpoint(one_block), starts).reshape(segment_length, QUERY_HEADS * HEAD_SIZE)

def experts(normed_two, combine, w_gate, w_up, w_down):
    segment_length = normed_two.shape[0]
    block = min(512, segment_length)
    number = w_gate.shape[0]

    def one_block(start):
        rows = lax.dynamic_slice_in_dim(normed_two, start, block, 0)
        weights = lax.dynamic_slice_in_dim(combine, start, block, 0)
        copies = lower_backward(jnp.broadcast_to(rows[None], (number, block, rows.shape[1])))
        gate_pre = lower_backward(jnp.einsum('etd,edf->etf', copies, w_gate, precision=TOP_PRECISION))
        up_pre = lower_backward(jnp.einsum('etd,edf->etf', copies, w_up, precision=TOP_PRECISION))
        acted = lower_precision(gate_pre * jax.nn.sigmoid(gate_pre) * up_pre)
        result = lower_precision(lower_backward(jnp.einsum('etf,efd->etd', acted, w_down, precision=TOP_PRECISION)))
        return jnp.einsum('te,etd->td', weights, result, precision=TOP_PRECISION)
    starts = jnp.arange(segment_length // block, dtype=jnp.int32) * block
    return lax.map(jax.checkpoint(one_block), starts).reshape(segment_length, normed_two.shape[1])

def layer(hidden, attn_gain, w_query, key_weight, value_weight, w_out, ffn_gain, router, w_gate, w_up, w_down, segment_row, position_row, id_rows):
    segment_length = hidden.shape[0]
    live = (segment_row != 0).astype(hidden.dtype)[:, None]
    cosine_table, sine_table = rope_tables(position_row)
    base_one = hidden * lax.rsqrt(lax.optimization_barrier(jnp.mean(hidden * hidden, -1, keepdims=True)) + EPS)
    first_normed = lower_precision(base_one * attn_gain)
    query = lower_backward(jnp.dot(first_normed, w_query, precision=TOP_PRECISION)).reshape(segment_length, QUERY_HEADS, HEAD_SIZE)
    key = lower_backward(jnp.dot(first_normed, key_weight, precision=TOP_PRECISION)).reshape(segment_length, KEY_VALUE_HEADS, HEAD_SIZE)
    value_matrix = lower_precision(lower_backward(jnp.dot(first_normed, value_weight, precision=TOP_PRECISION))).reshape(segment_length, KEY_VALUE_HEADS, HEAD_SIZE)
    rotated_query = lower_precision(apply_rotary(query, cosine_table, sine_table))
    key_rot = lower_precision(apply_rotary(key, cosine_table, sine_table))
    mixed = attend(rotated_query, key_rot, value_matrix, segment_row)
    branch = lower_backward(jnp.dot(lower_precision(lower_backward(mixed)), w_out, precision=TOP_PRECISION))
    middle = hidden + branch
    base_two = middle * lax.rsqrt(lax.optimization_barrier(jnp.mean(middle * middle, -1, keepdims=True)) + EPS)
    normed_two = lower_precision(base_two * ffn_gain)
    logits = lower_backward(jnp.dot(normed_two, router, precision=TOP_PRECISION))
    choose = (id_rows[:, :, None] == jnp.arange(router.shape[1], dtype=jnp.int32)[None, None, :]).astype(hidden.dtype)
    chosen = jnp.einsum('tke,te->tk', choose, logits, precision=TOP_PRECISION)
    shifted = jnp.exp(chosen - lax.optimization_barrier(jnp.max(chosen, -1, keepdims=True)))
    gates = shifted / lax.optimization_barrier(jnp.sum(shifted, -1, keepdims=True))
    combine = jnp.einsum('tk,tke->te', gates, choose, precision=TOP_PRECISION)
    return live * (middle + experts(normed_two, combine, w_gate, w_up, w_down))

def reference(inputs, segments, positions, expert_ids, attn_gain, w_query, key_weight, value_weight, w_out, ffn_gain, router, w_gate, w_up, w_down, grad_out):
    params = tuple((array.astype(jnp.float32) for array in (attn_gain, w_query, key_weight, value_weight, w_out, ffn_gain, router, w_gate, w_up, w_down)))
    zero_filled = tuple((jnp.zeros_like(array) for array in params))

    def one_sequence(totals, items):
        hidden, segment_row, position_row, id_rows, cotangent = items

        def forward(hidden_values, *weights):
            return layer(hidden_values, *weights, segment_row, position_row, id_rows)
        result, pullback = jax.vjp(forward, hidden.astype(jnp.float32), *params)
        grads = pullback(cotangent.astype(jnp.float32))
        totals = tuple((running + grad for running, grad in zip(totals, grads[1:])))
        return (totals, (result.astype(jnp.bfloat16), grads[0]))
    totals, (outputs, grad_in) = lax.scan(one_sequence, zero_filled, (inputs, segments, positions, expert_ids, grad_out))
    return (outputs, grad_in, totals[0], totals[1], totals[2], totals[3], totals[4], totals[5], totals[6], totals[7], totals[8], totals[9])
```

```python
import jax
import jax.numpy as jnp
from jax import lax
from jax.experimental import pallas as pl
from jax.experimental.pallas import tpu as pltpu
from jax.sharding import PartitionSpec as P

MODEL_WIDTH = 1536
QUERY_HEADS = 24
KEY_VALUE_HEADS = 8
HEAD_GROUP = QUERY_HEADS // KEY_VALUE_HEADS
HEAD_SIZE = 64

EPS = 1e-06
THETA = 10000.0
MASK_FLOOR = -1e30

ROWS = (((0,), (0,)), ((), ()))
COLUMNS = (((1,), (1,)), ((), ()))


def dot(left, right, contract=(((1,), (0,)), ((), ()))):
    return lax.dot_general(left, right, contract, preferred_element_type=jnp.float32)


def rope_tables(position_row):
    steps = jnp.arange(HEAD_SIZE // 2, dtype=jnp.float32)
    inverse = THETA ** (-(2.0 * steps) / HEAD_SIZE)
    angles = position_row.astype(jnp.float32)[:, None] * inverse[None, :]
    cosine_table = jnp.cos(angles)
    sine_table = jnp.sin(angles)
    return (
        jnp.concatenate([cosine_table, cosine_table], -1),
        jnp.concatenate([sine_table, sine_table], -1),
    )


def norm_back(grad_base, base, scale):
    return scale * (grad_base - base * jnp.mean(grad_base * base, -1, keepdims=True))


def turn(rows):
    half = HEAD_SIZE // 2
    return jnp.concatenate([-rows[:, half:], rows[:, :half]], 1)


def turn_back(rows):
    half = HEAD_SIZE // 2
    return jnp.concatenate([rows[:, half:], -rows[:, :half]], 1)


def stack_heads(rows):
    return jnp.concatenate(
        [rows[:, h * HEAD_SIZE : (h + 1) * HEAD_SIZE] for h in range(HEAD_GROUP)], 0
    )


def side_heads(rows):
    block = rows.shape[0] // HEAD_GROUP
    return jnp.concatenate([rows[h * block : (h + 1) * block] for h in range(HEAD_GROUP)], 1)


def lanes(values, combine):
    total = values[:, :128]
    for start in range(128, values.shape[1], 128):
        total = combine(total, values[:, start : start + 128])
    return total


def masked_scores(stacked, keys, row_segments, key_segments, row_start, key_start):
    block = row_segments.shape[0]
    scores = dot(stacked, keys, COLUMNS) * HEAD_SIZE ** (-0.5)
    row_place = row_start + lax.broadcasted_iota(jnp.int32, (block, block), 0)
    key_place = key_start + lax.broadcasted_iota(jnp.int32, (block, block), 1)
    allowed = (row_segments == key_segments) & (key_place <= row_place)
    scores = scores.reshape(HEAD_GROUP, block, block)
    return jnp.where(allowed[None], scores, MASK_FLOOR).reshape(HEAD_GROUP * block, block)


def attend_kernel(
    first_ref,
    hidden_ref,
    gain_ref,
    weight_ref,
    cosine_ref,
    sine_ref,
    row_segment_ref,
    key_segment_ref,
    normed_ref,
    query_ref,
    key_ref,
    value_ref,
    mixed_ref,
    log_ref,
    score_ref,
):
    step = pl.program_id(0)
    block = hidden_ref.shape[0]
    query_width = query_ref.shape[1]
    here = pl.ds(pl.multiple_of(step * block, block), block)
    hidden = hidden_ref[...].astype(jnp.float32)
    scale = lax.rsqrt(jnp.mean(hidden * hidden, -1, keepdims=True) + EPS)
    normed = (hidden * scale * gain_ref[...]).astype(jnp.bfloat16)
    normed_ref[...] = normed
    raw = dot(normed, weight_ref[...])
    cosine = cosine_ref[...]
    sine = sine_ref[...]
    key_raw = raw[:, query_width : query_width + HEAD_SIZE]
    key_ref[here, :] = (key_raw * cosine + turn(key_raw) * sine).astype(jnp.bfloat16)
    value_ref[here, :] = raw[:, query_width + HEAD_SIZE :].astype(jnp.bfloat16)
    query_raw = stack_heads(raw[:, :query_width])
    cosine = jnp.concatenate([cosine] * HEAD_GROUP, 0)
    sine = jnp.concatenate([sine] * HEAD_GROUP, 0)
    query = (query_raw * cosine + turn(query_raw) * sine).astype(jnp.bfloat16)
    query_ref[...] = side_heads(query)
    rows = HEAD_GROUP * block
    row_segments = row_segment_ref[...]

    def first_pass(index, top):
        there = pl.ds(pl.multiple_of(index * block, block), block)
        scores = masked_scores(
            query,
            key_ref[there, :],
            row_segments,
            key_segment_ref[:, there],
            step * block,
            index * block,
        )
        score_ref[index] = scores
        return jnp.maximum(top, lanes(scores, jnp.maximum))

    top = lax.fori_loop(
        first_ref[step], step + 1, first_pass, jnp.full((rows, 128), MASK_FLOOR, jnp.float32)
    )
    top = jnp.max(top, -1, keepdims=True)

    def second_pass(index, carry):
        total, mixed = carry
        there = pl.ds(pl.multiple_of(index * block, block), block)
        weights = jnp.exp(score_ref[index] - top)
        mixed = mixed + dot(weights.astype(jnp.bfloat16), value_ref[there, :])
        return total + lanes(weights, jnp.add), mixed

    total, mixed = lax.fori_loop(
        first_ref[step],
        step + 1,
        second_pass,
        (
            jnp.zeros((rows, 128), jnp.float32),
            jnp.zeros((rows, HEAD_SIZE), jnp.float32),
        ),
    )
    total = jnp.sum(total, -1, keepdims=True)
    mixed_ref[...] = side_heads((mixed / total).astype(jnp.bfloat16))
    log_ref[...] = (top + jnp.log(total)).reshape(HEAD_GROUP, block, 1)


def attend(hidden, gain, weight, cosine, sine, segment_row, block, first):
    tokens, features = hidden.shape
    query_width = HEAD_GROUP * HEAD_SIZE
    steps = tokens // block
    rows = lambda width: pl.BlockSpec((block, width), lambda i, f: (i, 0))
    whole = lambda height, width: pl.BlockSpec((height, width), lambda i, f: (0, 0))
    return pl.pallas_call(
        attend_kernel,
        out_shape=(
            jax.ShapeDtypeStruct((tokens, features), jnp.bfloat16),
            jax.ShapeDtypeStruct((tokens, query_width), jnp.bfloat16),
            jax.ShapeDtypeStruct((tokens, HEAD_SIZE), jnp.bfloat16),
            jax.ShapeDtypeStruct((tokens, HEAD_SIZE), jnp.bfloat16),
            jax.ShapeDtypeStruct((tokens, query_width), jnp.bfloat16),
            jax.ShapeDtypeStruct((HEAD_GROUP, tokens, 1), jnp.float32),
        ),
        grid_spec=pltpu.PrefetchScalarGridSpec(
            num_scalar_prefetch=1,
            grid=(steps,),
            in_specs=[
                rows(features),
                whole(1, features),
                whole(*weight.shape),
                rows(HEAD_SIZE),
                rows(HEAD_SIZE),
                rows(1),
                whole(1, tokens),
            ],
            out_specs=[
                rows(features),
                rows(query_width),
                whole(tokens, HEAD_SIZE),
                whole(tokens, HEAD_SIZE),
                rows(query_width),
                pl.BlockSpec((HEAD_GROUP, block, 1), lambda i, f: (0, i, 0)),
            ],
            scratch_shapes=[pltpu.VMEM((steps, HEAD_GROUP * block, block), jnp.float32)],
        ),
        compiler_params=pltpu.CompilerParams(vmem_limit_bytes=48 << 20),
        cost_estimate=pl.CostEstimate(
            flops=2 * tokens * features * weight.shape[1] + 4 * tokens * tokens * query_width,
            bytes_accessed=4 * tokens * features + 2 * weight.size,
            transcendentals=tokens * tokens * HEAD_GROUP // 2,
        ),
    )(
        first,
        hidden,
        gain[None, :],
        weight,
        cosine,
        sine,
        segment_row[:, None],
        segment_row[None, :],
    )


def attend_back_kernel(
    first_ref,
    query_ref,
    grad_ref,
    log_ref,
    cosine_ref,
    sine_ref,
    row_segment_ref,
    key_segment_ref,
    key_ref,
    value_ref,
    key_cosine_ref,
    key_sine_ref,
    grad_query_ref,
    grad_pair_ref,
    probs_ref,
    grad_probs_ref,
    grad_key_ref,
    grad_value_ref,
):
    step = pl.program_id(0)
    block = query_ref.shape[0]
    rows = HEAD_GROUP * block

    @pl.when(step == 0)
    def _():
        grad_key_ref[...] = jnp.zeros_like(grad_key_ref)
        grad_value_ref[...] = jnp.zeros_like(grad_value_ref)

    query = stack_heads(query_ref[...])
    grad = stack_heads(grad_ref[...])
    log_total = log_ref[...].reshape(rows, 1)
    row_segments = row_segment_ref[...]

    def first_pass(index, delta):
        there = pl.ds(pl.multiple_of(index * block, block), block)
        scores = masked_scores(
            query,
            key_ref[there, :],
            row_segments,
            key_segment_ref[:, there],
            step * block,
            index * block,
        )
        probs = jnp.exp(scores - log_total)
        grad_probs = dot(grad, value_ref[there, :], COLUMNS)
        probs_ref[index] = probs
        grad_probs_ref[index] = grad_probs
        grad_value_ref[there, :] += dot(probs.astype(jnp.bfloat16), grad, ROWS)
        return delta + lanes(probs * grad_probs, jnp.add)

    delta = lax.fori_loop(
        first_ref[step], step + 1, first_pass, jnp.zeros((rows, 128), jnp.float32)
    )
    delta = jnp.sum(delta, -1, keepdims=True)

    def second_pass(index, grad_query):
        there = pl.ds(pl.multiple_of(index * block, block), block)
        grad_scores = (probs_ref[index] * (grad_probs_ref[index] - delta)).astype(jnp.bfloat16)
        grad_key_ref[there, :] += dot(grad_scores, query, ROWS)
        return grad_query + dot(grad_scores, key_ref[there, :])

    grad_query = lax.fori_loop(
        first_ref[step], step + 1, second_pass, jnp.zeros((rows, HEAD_SIZE), jnp.float32)
    )
    score_scale = HEAD_SIZE ** (-0.5)
    cosine = jnp.concatenate([cosine_ref[...]] * HEAD_GROUP, 0)
    sine = jnp.concatenate([sine_ref[...]] * HEAD_GROUP, 0)
    grad_query = grad_query * score_scale
    grad_query = grad_query * cosine + turn_back(grad_query * sine)
    grad_query_ref[...] = side_heads(grad_query.astype(jnp.bfloat16))

    @pl.when(step == pl.num_programs(0) - 1)
    def _():
        grad_key = grad_key_ref[...] * score_scale
        grad_key = grad_key * key_cosine_ref[...] + turn_back(grad_key * key_sine_ref[...])
        grad_pair_ref[...] = jnp.concatenate([grad_key, grad_value_ref[...]], 1).astype(
            jnp.bfloat16
        )


def attend_back(query, grad, log_total, cosine, sine, segment_row, key, value, block, first):
    tokens, query_width = query.shape
    steps = tokens // block
    rows = lambda width: pl.BlockSpec((block, width), lambda i, f: (i, 0))
    whole = lambda height, width: pl.BlockSpec((height, width), lambda i, f: (0, 0))
    return pl.pallas_call(
        attend_back_kernel,
        out_shape=(
            jax.ShapeDtypeStruct((tokens, query_width), jnp.bfloat16),
            jax.ShapeDtypeStruct((tokens, 2 * HEAD_SIZE), jnp.bfloat16),
        ),
        grid_spec=pltpu.PrefetchScalarGridSpec(
            num_scalar_prefetch=1,
            grid=(steps,),
            in_specs=[
                rows(query_width),
                rows(query_width),
                pl.BlockSpec((HEAD_GROUP, block, 1), lambda i, f: (0, i, 0)),
                rows(HEAD_SIZE),
                rows(HEAD_SIZE),
                rows(1),
                whole(1, tokens),
                whole(tokens, HEAD_SIZE),
                whole(tokens, HEAD_SIZE),
                whole(tokens, HEAD_SIZE),
                whole(tokens, HEAD_SIZE),
            ],
            out_specs=[rows(query_width), whole(tokens, 2 * HEAD_SIZE)],
            scratch_shapes=[
                pltpu.VMEM((steps, HEAD_GROUP * block, block), jnp.float32),
                pltpu.VMEM((steps, HEAD_GROUP * block, block), jnp.float32),
                pltpu.VMEM((tokens, HEAD_SIZE), jnp.float32),
                pltpu.VMEM((tokens, HEAD_SIZE), jnp.float32),
            ],
        ),
        compiler_params=pltpu.CompilerParams(vmem_limit_bytes=48 << 20),
        cost_estimate=pl.CostEstimate(
            flops=10 * tokens * tokens * query_width,
            bytes_accessed=20 * tokens * query_width,
            transcendentals=tokens * tokens * HEAD_GROUP // 2,
        ),
    )(
        first,
        query,
        grad,
        log_total,
        cosine,
        sine,
        segment_row[:, None],
        segment_row[None, :],
        key,
        value,
        cosine,
        sine,
    )


def after(value, *others):
    return lax.optimization_barrier((value, *others))[0]


def swap(value, bit):
    size = lax.axis_size("rep")
    return lax.ppermute(value, "rep", [(i, i ^ bit) for i in range(size)])


def has(bit):
    return (lax.axis_index("rep") & bit) != 0


def halve(value, bit):
    half = value.shape[0] // 2
    kept = lax.dynamic_slice_in_dim(value, jnp.where(has(bit), half, 0), half, 0)
    sent = lax.dynamic_slice_in_dim(value, jnp.where(has(bit), 0, half), half, 0)
    return kept, sent.astype(jnp.bfloat16)


def join(value, came, bit, axis):
    upper = has(bit)
    return jnp.concatenate(
        [jnp.where(upper, came, value), jnp.where(upper, value, came)], axis
    )


def rep_sum(value, bits):
    for bit in bits:
        value, sent = halve(value, bit)
        value = value.astype(jnp.float32) + swap(sent, bit).astype(jnp.float32)
    value = value.astype(jnp.bfloat16)
    for bit in reversed(bits):
        value = join(value, swap(value, bit), bit, 0)
    return value


def gather_rows(block, bits):
    reps = lax.axis_size("rep")
    share = block.shape[0] // reps
    own = lax.dynamic_slice_in_dim(block, lax.axis_index("rep") * share, share, 0)
    fetched = lax.all_gather(own, "ctx", axis=0)
    size = fetched.shape[0]
    fetched = fetched.reshape((size,) + (1,) * len(bits) + fetched.shape[1:])
    width = fetched.shape[-1] // 2
    halves = []
    for start, order in ((0, bits), (width, bits[::-1])):
        value = fetched[..., start : start + width]
        for bit in order:
            value = join(value, swap(value, bit), bit, len(bits) - (bit.bit_length() - 1))
        halves.append(value.reshape(-1, width))
    return jnp.concatenate(halves, 1)


def per_device(
    inputs,
    segments,
    positions,
    expert_ids,
    attn_gain,
    w_query,
    key_weight,
    value_weight,
    w_out,
    ffn_gain,
    router,
    w_gate,
    w_up,
    w_down,
    grad_out,
):
    size = lax.axis_size("ctx")
    me = lax.axis_index("ctx")
    reps = lax.axis_size("rep")
    bits = [1 << i for i in range(reps.bit_length() - 1)]
    own = inputs.shape[1]
    tokens = size * own
    groups = KEY_VALUE_HEADS
    copies = size // groups
    query_width = HEAD_GROUP * HEAD_SIZE
    width = query_width + 2 * HEAD_SIZE
    copy_index = me % copies
    rows_own = w_out.shape[0]
    experts_own = w_gate.shape[0]
    experts_all = size * experts_own
    slots = expert_ids.shape[2]
    block = min(256, tokens)

    columns = jnp.concatenate(
        [segments[0][:, None], positions[0][:, None] // 64, positions[0][:, None] % 64, expert_ids[0]],
        1,
    ).astype(jnp.bfloat16)
    columns = jnp.pad(columns, ((0, 0), (0, 128 - columns.shape[1])))
    gathered = lax.all_gather(
        jnp.concatenate([inputs[0], columns], 1), "ctx", axis=0, tiled=True
    )
    hidden_low = gathered[:, :MODEL_WIDTH]
    numbers = gathered[:, MODEL_WIDTH:].astype(jnp.int32)
    segment_row = numbers[:, 0]
    position_row = numbers[:, 1] * 64 + numbers[:, 2]
    ids = numbers[:, 3 : 3 + slots]

    head_columns = jnp.concatenate(
        [
            w_query.reshape(rows_own, groups, query_width),
            key_weight.reshape(rows_own, groups, HEAD_SIZE),
            value_weight.reshape(rows_own, groups, HEAD_SIZE),
            jnp.broadcast_to(attn_gain[:, None, None], (rows_own, groups, 1)),
            jnp.broadcast_to(ffn_gain[:, None, None], (rows_own, groups, 1)),
            jnp.broadcast_to(router[:, None, :], (rows_own, groups, router.shape[1])),
        ],
        -1,
    )
    head_columns = jnp.repeat(jnp.transpose(head_columns, (1, 0, 2)), copies, 0)
    head_columns = lax.all_to_all(head_columns, "ctx", split_axis=0, concat_axis=0, tiled=True)
    head_columns = head_columns.reshape(size * rows_own, -1)
    w_heads = head_columns[:, :width]
    gain_one = head_columns[:, width].astype(jnp.float32)
    gain_two = head_columns[:, width + 1].astype(jnp.float32)
    router_all = head_columns[:, width + 2 :]

    live = segment_row != 0
    cosine_table, sine_table = rope_tables(position_row)
    places = jnp.arange(tokens, dtype=jnp.int32)
    starts = segment_row[:: block]
    first = jnp.min(
        jnp.where(segment_row[None, :] == starts[:, None], places[None, :], tokens), 1
    ) // block
    normed_one, query, key, value, mixed, log_total = attend(
        hidden_low, gain_one, w_heads, cosine_table, sine_table, segment_row, block, first
    )
    w_out_all = gather_rows(after(w_out, hidden_low), bits)

    share = tokens // copies
    mixed_all = lax.all_gather(
        lax.dynamic_slice_in_dim(mixed, copy_index * share, share, 0), "ctx", axis=0
    )
    cotangent = lax.all_gather(after(grad_out[0], mixed), "ctx", axis=0, tiled=True)
    mixed_all = jnp.transpose(mixed_all.reshape(groups, tokens, query_width), (1, 0, 2))
    mixed_all = mixed_all.reshape(tokens, QUERY_HEADS * HEAD_SIZE)
    hidden = hidden_low.astype(jnp.float32)
    middle = hidden + dot(mixed_all, w_out_all)
    scale_two = lax.rsqrt(jnp.mean(middle * middle, -1, keepdims=True) + EPS)
    base_two = middle * scale_two
    normed_two = (base_two * gain_two).astype(jnp.bfloat16)

    logits = dot(normed_two, router_all)
    named = jnp.any(ids[:, :, None] == jnp.arange(experts_all, dtype=jnp.int32)[None, None, :], 1)
    top = jnp.max(jnp.where(named, logits, MASK_FLOOR), -1, keepdims=True)
    shifted = jnp.where(named, jnp.exp(jnp.where(named, logits, top) - top), 0.0)
    gates = shifted / jnp.sum(shifted, -1, keepdims=True)
    gates_own = lax.dynamic_slice_in_dim(gates, me * experts_own, experts_own, 1)

    grad_live = jnp.where(live[:, None], cotangent, jnp.zeros((), jnp.bfloat16))
    gate_list = [gates_own[:, e : e + 1] for e in range(experts_own)]
    gate_pre = [dot(normed_two, w_gate[e]) for e in range(experts_own)]
    up_pre = [dot(normed_two, w_up[e]) for e in range(experts_own)]
    sigma = [jax.nn.sigmoid(v) for v in gate_pre]
    acted = [gate_pre[e] * sigma[e] * up_pre[e] for e in range(experts_own)]
    scaled = [(gate_list[e] * acted[e]).astype(jnp.bfloat16) for e in range(experts_own)]
    grad_plain = [dot(grad_live, w_down[e], COLUMNS) for e in range(experts_own)]
    grad_acted = [gate_list[e] * grad_plain[e] for e in range(experts_own)]
    grad_gate_pre = [
        (
            grad_acted[e] * up_pre[e] * (sigma[e] * (1.0 + gate_pre[e] * (1.0 - sigma[e])))
        ).astype(jnp.bfloat16)
        for e in range(experts_own)
    ]
    grad_up_pre = [
        (grad_acted[e] * gate_pre[e] * sigma[e]).astype(jnp.bfloat16) for e in range(experts_own)
    ]

    half = MODEL_WIDTH // 2
    chains = [
        (lambda e: scaled[e], lambda e: grad_live[:, :half], bits),
        (lambda e: scaled[e], lambda e: grad_live[:, half:], bits[::-1]),
        (lambda e: normed_two, lambda e: grad_gate_pre[e], bits),
        (lambda e: normed_two, lambda e: grad_up_pre[e], bits[::-1]),
    ]
    pick = experts_own // 2

    def product(left, right, upper):
        terms = [
            dot(
                jnp.where(upper, left(e + pick), left(e)),
                jnp.where(upper, right(e + pick), right(e)),
                ROWS,
            )
            for e in range(pick)
        ]
        return jnp.concatenate(terms, 0)

    kept, flying = [], []
    for left, right, order in chains:
        sent = product(left, right, jnp.logical_not(has(order[0]))).astype(jnp.bfloat16)
        flying.append(swap(sent, order[0]))

    grad_two_part = 0.0
    for e in range(experts_own):
        grad_two_part = (
            grad_two_part
            + dot(grad_gate_pre[e], w_gate[e], COLUMNS)
            + dot(grad_up_pre[e], w_up[e], COLUMNS)
        )
    expert_index = jnp.arange(experts_all, dtype=jnp.int32)[None, :]
    grad_gates = 0.0
    for e in range(experts_own):
        grad_gates = grad_gates + jnp.where(
            expert_index == me * experts_own + e,
            jnp.sum(acted[e] * grad_plain[e], -1, keepdims=True),
            0.0,
        )
    rough = lax.reduce_precision(grad_gates, 8, 7)
    extra = jnp.concatenate([rough, grad_gates - rough], 1).astype(jnp.bfloat16)
    extra = jnp.pad(extra, ((0, 0), (0, 128 - 2 * experts_all)))
    grad_two_sum = lax.psum_scatter(
        jnp.concatenate([grad_two_part.astype(jnp.bfloat16), extra], 1),
        "ctx",
        scatter_dimension=0,
        tiled=True,
    ).astype(jnp.float32)
    for left, right, order in chains:
        kept.append(product(left, right, has(order[0])))
    moe_part = 0.0
    for e in range(experts_own):
        moe_part = moe_part + dot(scaled[e], w_down[e])

    def mine(array):
        return lax.dynamic_slice_in_dim(array, me * own, own, 0)

    gates_mine = mine(gates)
    grad_gates = (
        grad_two_sum[:, MODEL_WIDTH : MODEL_WIDTH + experts_all]
        + grad_two_sum[:, MODEL_WIDTH + experts_all : MODEL_WIDTH + 2 * experts_all]
    )
    grad_logits = (
        gates_mine * (grad_gates - jnp.sum(gates_mine * grad_gates, -1, keepdims=True))
    ).astype(jnp.bfloat16)
    grad_normed_two = grad_two_sum[:, :MODEL_WIDTH] + dot(grad_logits, router_all, COLUMNS)
    base_two_own = mine(base_two)
    grad_middle = mine(grad_live).astype(jnp.float32) + norm_back(
        grad_normed_two * gain_two, base_two_own, mine(scale_two)
    )
    grad_branch = grad_middle.astype(jnp.bfloat16)
    grad_mixed = dot(grad_branch, w_out_all, COLUMNS).astype(jnp.bfloat16)
    grad_mixed = jnp.transpose(grad_mixed.reshape(own, groups, query_width), (1, 0, 2))
    grad_mixed = jnp.repeat(grad_mixed, copies, 0)
    grad_mixed_all = lax.all_to_all(
        grad_mixed, "ctx", split_axis=0, concat_axis=0, tiled=True
    ).reshape(tokens, query_width)
    grad_branch_all = lax.all_gather(grad_branch, "ctx", axis=0, tiled=True)

    stage = 1
    sent_list = []
    for c, (_, _, order) in enumerate(chains):
        came = after(flying[c], grad_mixed)
        kept[c] = kept[c] + came.astype(jnp.float32)
    while stage < len(bits):
        for c, (_, _, order) in enumerate(chains):
            kept[c], sent = halve(kept[c], order[stage])
            sent_list.append(sent)
            flying[c] = swap(sent, order[stage])
        stage += 1
        if stage < len(bits):
            for c in range(len(chains)):
                kept[c] = kept[c] + flying[c].astype(jnp.float32)

    grad_query, grad_pair = attend_back(
        query,
        after(grad_mixed_all, *sent_list),
        log_total,
        cosine_table,
        sine_table,
        segment_row,
        key,
        value,
        block,
        first,
    )
    if copies > 1:
        counted = (places // share == copy_index)[:, None]
        grad_query = jnp.where(counted, grad_query, jnp.zeros((), jnp.bfloat16))
        grad_pair = jnp.where(counted, grad_pair, jnp.zeros((), jnp.bfloat16))
    grad_one_part = dot(grad_query, w_heads[:, :query_width], COLUMNS) + dot(
        grad_pair, w_heads[:, query_width:], COLUMNS
    )
    grad_one_low = grad_one_part.astype(jnp.bfloat16)
    grad_one = lax.psum_scatter(
        grad_one_low, "ctx", scatter_dimension=0, tiled=True
    ).astype(jnp.float32)
    scale_one = lax.rsqrt(jnp.mean(hidden * hidden, -1, keepdims=True) + EPS)
    gain_one_term = jnp.sum(grad_one_part * (hidden * scale_one), 0)
    gain_two_term = jnp.sum(grad_normed_two * base_two_own, 0)
    head_grads = jnp.concatenate(
        [
            dot(normed_one, grad_query, ROWS),
            dot(normed_one, grad_pair, ROWS),
            gain_one_term[:, None],
            gain_two_term[:, None],
            dot(mine(normed_two), grad_logits, ROWS),
        ],
        1,
    ).astype(jnp.bfloat16)
    head_grads = head_grads.reshape(size, rows_own, -1)
    head_grads_all = lax.all_to_all(
        head_grads, "ctx", split_axis=0, concat_axis=0, tiled=True
    )

    shared = []
    flying_back = []
    for c, (_, _, order) in enumerate(chains):
        came = after(flying[c], grad_one_low, head_grads)
        shared.append((kept[c] + came.astype(jnp.float32)).astype(jnp.bfloat16))
        flying_back.append(swap(shared[c], order[-1]))

    grad_proj_out = dot(
        lax.dynamic_slice_in_dim(mixed, copy_index * rows_own, rows_own, 1), grad_branch_all, ROWS
    )
    small = jnp.sum(head_grads_all[:, :, width:].astype(jnp.float32), 0)
    projections = head_grads_all[:, :, :width]
    if copies > 1:
        projections = jnp.sum(
            projections.reshape(groups, copies, rows_own, width).astype(jnp.float32), 1
        )
    projections = jnp.transpose(projections.astype(jnp.bfloat16), (1, 0, 2))
    query_end = query_width + HEAD_SIZE
    last_one = jnp.concatenate(
        [
            projections[:, :, :query_width].reshape(rows_own, -1),
            projections[:, :, query_width:query_end].reshape(rows_own, -1),
        ],
        1,
    )
    last_two = jnp.concatenate(
        [
            projections[:, :, query_end:].reshape(rows_own, -1),
            grad_proj_out.astype(jnp.bfloat16),
            small.astype(jnp.bfloat16),
        ],
        1,
    )
    for stage in reversed(range(1, len(bits))):
        for c, (_, _, order) in enumerate(chains):
            shared[c] = join(shared[c], after(flying_back[c], last_one), order[stage], 0)
            flying_back[c] = swap(shared[c], order[stage - 1])
    last_one = rep_sum(last_one, bits).astype(jnp.float32)
    last_two = rep_sum(last_two, bits[::-1]).astype(jnp.float32)

    moe_sum = lax.psum_scatter(
        after(moe_part.astype(jnp.bfloat16), grad_branch),
        "ctx",
        scatter_dimension=0,
        tiled=True,
    ).astype(jnp.float32)
    output = jnp.where(mine(live)[:, None], mine(middle) + moe_sum, 0.0).astype(jnp.bfloat16)
    own_hidden = inputs[0].astype(jnp.float32)
    own_scale = lax.rsqrt(jnp.mean(own_hidden * own_hidden, -1, keepdims=True) + EPS)
    grad_in = grad_middle + norm_back(grad_one * gain_one, own_hidden * own_scale, own_scale)

    def whole(c):
        value = join(shared[c], flying_back[c], chains[c][2][0], 0)
        return value.astype(jnp.float32).reshape(experts_own, -1, value.shape[-1])

    grad_down = jnp.concatenate([whole(0), whole(1)], 2)
    kv_all = KEY_VALUE_HEADS * HEAD_SIZE
    query_all = QUERY_HEADS * HEAD_SIZE
    out_end = kv_all + MODEL_WIDTH
    return (
        output[None],
        grad_in[None],
        last_two[:, out_end],
        last_one[:, :query_all],
        last_one[:, query_all:],
        last_two[:, :kv_all],
        last_two[:, kv_all:out_end],
        last_two[:, out_end + 1],
        last_two[:, out_end + 2 :],
        whole(2),
        whole(3),
        grad_down,
    )


def solution(mesh):
    return jax.shard_map(
        per_device,
        mesh=mesh,
        in_specs=(
            P("rep", "ctx", None),
            P("rep", "ctx"),
            P("rep", "ctx"),
            P("rep", "ctx", None),
            P("ctx"),
            P("ctx", None),
            P("ctx", None),
            P("ctx", None),
            P("ctx", None),
            P("ctx"),
            P("ctx", None),
            P("ctx", None, None),
            P("ctx", None, None),
            P("ctx", None, None),
            P("rep", "ctx", None),
        ),
        out_specs=(
            P("rep", "ctx", None),
            P("rep", "ctx", None),
            P("ctx"),
            P("ctx", None),
            P("ctx", None),
            P("ctx", None),
            P("ctx", None),
            P("ctx"),
            P("ctx", None),
            P("ctx", None, None),
            P("ctx", None, None),
            P("ctx", None, None),
        ),
        check_vma=False,
    )
```

```python
import jax
import jax.numpy as jnp
from jax import lax
from jax.experimental import pallas as pl
from jax.experimental.pallas import tpu as pltpu
from jax.sharding import PartitionSpec as P

MODEL_WIDTH = 1536
QUERY_HEADS = 24
KEY_VALUE_HEADS = 8
HEAD_GROUP = QUERY_HEADS // KEY_VALUE_HEADS
HEAD_SIZE = 64

EPS = 1e-06
THETA = 10000.0
MASK_FLOOR = -1e30

ROWS = (((0,), (0,)), ((), ()))
COLUMNS = (((1,), (1,)), ((), ()))


def dot(left, right, contract=(((1,), (0,)), ((), ()))):
    return lax.dot_general(left, right, contract, preferred_element_type=jnp.float32)


def rope_tables(position_row):
    steps = jnp.arange(HEAD_SIZE // 2, dtype=jnp.float32)
    inverse = THETA ** (-(2.0 * steps) / HEAD_SIZE)
    angles = position_row.astype(jnp.float32)[:, None] * inverse[None, :]
    cosine_table = jnp.cos(angles)
    sine_table = jnp.sin(angles)
    return (
        jnp.concatenate([cosine_table, cosine_table], -1),
        jnp.concatenate([sine_table, sine_table], -1),
    )


def norm_back(grad_base, base, scale):
    return scale * (grad_base - base * jnp.mean(grad_base * base, -1, keepdims=True))


def turn(rows):
    half = HEAD_SIZE // 2
    return jnp.concatenate([-rows[:, half:], rows[:, :half]], 1)


def turn_back(rows):
    half = HEAD_SIZE // 2
    return jnp.concatenate([rows[:, half:], -rows[:, :half]], 1)


def stack_heads(rows):
    return jnp.concatenate(
        [rows[:, h * HEAD_SIZE : (h + 1) * HEAD_SIZE] for h in range(HEAD_GROUP)], 0
    )


def side_heads(rows):
    block = rows.shape[0] // HEAD_GROUP
    return jnp.concatenate([rows[h * block : (h + 1) * block] for h in range(HEAD_GROUP)], 1)


def lanes(values, combine):
    total = values[:, :128]
    for start in range(128, values.shape[1], 128):
        total = combine(total, values[:, start : start + 128])
    return total


def masked_scores(stacked, keys, row_segments, key_segments, row_start, key_start):
    block = row_segments.shape[0]
    scores = dot(stacked, keys, COLUMNS) * HEAD_SIZE ** (-0.5)
    row_place = row_start + lax.broadcasted_iota(jnp.int32, (block, block), 0)
    key_place = key_start + lax.broadcasted_iota(jnp.int32, (block, block), 1)
    allowed = (row_segments == key_segments) & (key_place <= row_place)
    scores = scores.reshape(HEAD_GROUP, block, block)
    return jnp.where(allowed[None], scores, MASK_FLOOR).reshape(HEAD_GROUP * block, block)


def attend_kernel(
    first_ref,
    hidden_ref,
    gain_ref,
    low_ref,
    high_ref,
    cosine_ref,
    sine_ref,
    row_segment_ref,
    key_segment_ref,
    normed_ref,
    query_ref,
    key_ref,
    value_ref,
    mixed_ref,
    log_ref,
    score_ref,
):
    step = pl.program_id(0)
    block = hidden_ref.shape[0]
    query_width = query_ref.shape[1]
    here = pl.ds(pl.multiple_of(step * block, block), block)
    hidden = hidden_ref[...].astype(jnp.float32)
    scale = lax.rsqrt(jnp.mean(hidden * hidden, -1, keepdims=True) + EPS)
    normed = (hidden * scale * gain_ref[...]).astype(jnp.bfloat16)
    normed_ref[...] = normed
    middle = low_ref.shape[0]
    raw = dot(normed[:, :middle], low_ref[...]) + dot(normed[:, middle:], high_ref[...])
    cosine = cosine_ref[...]
    sine = sine_ref[...]
    key_raw = raw[:, query_width : query_width + HEAD_SIZE]
    key_ref[here, :] = (key_raw * cosine + turn(key_raw) * sine).astype(jnp.bfloat16)
    value_ref[here, :] = raw[:, query_width + HEAD_SIZE :].astype(jnp.bfloat16)
    query_raw = stack_heads(raw[:, :query_width])
    cosine = jnp.concatenate([cosine] * HEAD_GROUP, 0)
    sine = jnp.concatenate([sine] * HEAD_GROUP, 0)
    query = (query_raw * cosine + turn(query_raw) * sine).astype(jnp.bfloat16)
    query_ref[...] = side_heads(query)
    rows = HEAD_GROUP * block
    row_segments = row_segment_ref[...]

    def first_pass(index, top):
        there = pl.ds(pl.multiple_of(index * block, block), block)
        scores = masked_scores(
            query,
            key_ref[there, :],
            row_segments,
            key_segment_ref[:, there],
            step * block,
            index * block,
        )
        score_ref[index] = scores
        return jnp.maximum(top, lanes(scores, jnp.maximum))

    top = lax.fori_loop(
        first_ref[step], step + 1, first_pass, jnp.full((rows, 128), MASK_FLOOR, jnp.float32)
    )
    top = jnp.max(top, -1, keepdims=True)

    def second_pass(index, carry):
        total, mixed = carry
        there = pl.ds(pl.multiple_of(index * block, block), block)
        weights = jnp.exp(score_ref[index] - top)
        mixed = mixed + dot(weights.astype(jnp.bfloat16), value_ref[there, :])
        return total + lanes(weights, jnp.add), mixed

    total, mixed = lax.fori_loop(
        first_ref[step],
        step + 1,
        second_pass,
        (
            jnp.zeros((rows, 128), jnp.float32),
            jnp.zeros((rows, HEAD_SIZE), jnp.float32),
        ),
    )
    total = jnp.sum(total, -1, keepdims=True)
    mixed_ref[...] = side_heads((mixed / total).astype(jnp.bfloat16))
    log_ref[...] = (top + jnp.log(total)).reshape(HEAD_GROUP, block, 1)


def attend(hidden, gain, weights, cosine, sine, segment_row, block, first):
    tokens, features = hidden.shape[0], gain.shape[0]
    width = weights[0].shape[1]
    query_width = HEAD_GROUP * HEAD_SIZE
    steps = tokens // block
    rows = lambda width: pl.BlockSpec((block, width), lambda i, f: (i, 0))
    whole = lambda height, width: pl.BlockSpec((height, width), lambda i, f: (0, 0))
    return pl.pallas_call(
        attend_kernel,
        out_shape=(
            jax.ShapeDtypeStruct((tokens, features), jnp.bfloat16),
            jax.ShapeDtypeStruct((tokens, query_width), jnp.bfloat16),
            jax.ShapeDtypeStruct((tokens, HEAD_SIZE), jnp.bfloat16),
            jax.ShapeDtypeStruct((tokens, HEAD_SIZE), jnp.bfloat16),
            jax.ShapeDtypeStruct((tokens, query_width), jnp.bfloat16),
            jax.ShapeDtypeStruct((HEAD_GROUP, tokens, 1), jnp.float32),
        ),
        grid_spec=pltpu.PrefetchScalarGridSpec(
            num_scalar_prefetch=1,
            grid=(steps,),
            in_specs=[
                rows(features),
                whole(1, features),
                whole(*weights[0].shape),
                whole(*weights[1].shape),
                rows(HEAD_SIZE),
                rows(HEAD_SIZE),
                rows(1),
                whole(1, tokens),
            ],
            out_specs=[
                rows(features),
                rows(query_width),
                whole(tokens, HEAD_SIZE),
                whole(tokens, HEAD_SIZE),
                rows(query_width),
                pl.BlockSpec((HEAD_GROUP, block, 1), lambda i, f: (0, i, 0)),
            ],
            scratch_shapes=[pltpu.VMEM((steps, HEAD_GROUP * block, block), jnp.float32)],
        ),
        compiler_params=pltpu.CompilerParams(vmem_limit_bytes=48 << 20),
        cost_estimate=pl.CostEstimate(
            flops=2 * tokens * features * width + 4 * tokens * tokens * query_width,
            bytes_accessed=4 * tokens * features + 2 * features * width,
            transcendentals=tokens * tokens * HEAD_GROUP // 2,
        ),
    )(
        first,
        hidden,
        gain[None, :],
        *weights,
        cosine,
        sine,
        segment_row[:, None],
        segment_row[None, :],
    )


def attend_back_kernel(
    first_ref,
    query_ref,
    grad_ref,
    log_ref,
    cosine_ref,
    sine_ref,
    row_segment_ref,
    key_segment_ref,
    key_ref,
    value_ref,
    key_cosine_ref,
    key_sine_ref,
    grad_query_ref,
    grad_pair_ref,
    probs_ref,
    grad_probs_ref,
    grad_key_ref,
    grad_value_ref,
):
    step = pl.program_id(0)
    block = query_ref.shape[0]
    rows = HEAD_GROUP * block

    @pl.when(step == 0)
    def _():
        grad_key_ref[...] = jnp.zeros_like(grad_key_ref)
        grad_value_ref[...] = jnp.zeros_like(grad_value_ref)

    query = stack_heads(query_ref[...])
    grad = stack_heads(grad_ref[...])
    log_total = log_ref[...].reshape(rows, 1)
    row_segments = row_segment_ref[...]

    def first_pass(index, delta):
        there = pl.ds(pl.multiple_of(index * block, block), block)
        scores = masked_scores(
            query,
            key_ref[there, :],
            row_segments,
            key_segment_ref[:, there],
            step * block,
            index * block,
        )
        probs = jnp.exp(scores - log_total)
        grad_probs = dot(grad, value_ref[there, :], COLUMNS)
        probs_ref[index] = probs
        grad_probs_ref[index] = grad_probs
        grad_value_ref[there, :] += dot(probs.astype(jnp.bfloat16), grad, ROWS)
        return delta + lanes(probs * grad_probs, jnp.add)

    delta = lax.fori_loop(
        first_ref[step], step + 1, first_pass, jnp.zeros((rows, 128), jnp.float32)
    )
    delta = jnp.sum(delta, -1, keepdims=True)

    def second_pass(index, grad_query):
        there = pl.ds(pl.multiple_of(index * block, block), block)
        grad_scores = (probs_ref[index] * (grad_probs_ref[index] - delta)).astype(jnp.bfloat16)
        grad_key_ref[there, :] += dot(grad_scores, query, ROWS)
        return grad_query + dot(grad_scores, key_ref[there, :])

    grad_query = lax.fori_loop(
        first_ref[step], step + 1, second_pass, jnp.zeros((rows, HEAD_SIZE), jnp.float32)
    )
    score_scale = HEAD_SIZE ** (-0.5)
    cosine = jnp.concatenate([cosine_ref[...]] * HEAD_GROUP, 0)
    sine = jnp.concatenate([sine_ref[...]] * HEAD_GROUP, 0)
    grad_query = grad_query * score_scale
    grad_query = grad_query * cosine + turn_back(grad_query * sine)
    grad_query_ref[...] = side_heads(grad_query.astype(jnp.bfloat16))

    @pl.when(step == pl.num_programs(0) - 1)
    def _():
        grad_key = grad_key_ref[...] * score_scale
        grad_key = grad_key * key_cosine_ref[...] + turn_back(grad_key * key_sine_ref[...])
        grad_pair_ref[...] = jnp.concatenate([grad_key, grad_value_ref[...]], 1).astype(
            jnp.bfloat16
        )


def attend_back(query, grad, log_total, cosine, sine, segment_row, key, value, block, first):
    tokens, query_width = query.shape
    steps = tokens // block
    rows = lambda width: pl.BlockSpec((block, width), lambda i, f: (i, 0))
    whole = lambda height, width: pl.BlockSpec((height, width), lambda i, f: (0, 0))
    return pl.pallas_call(
        attend_back_kernel,
        out_shape=(
            jax.ShapeDtypeStruct((tokens, query_width), jnp.bfloat16),
            jax.ShapeDtypeStruct((tokens, 2 * HEAD_SIZE), jnp.bfloat16),
        ),
        grid_spec=pltpu.PrefetchScalarGridSpec(
            num_scalar_prefetch=1,
            grid=(steps,),
            in_specs=[
                rows(query_width),
                rows(query_width),
                pl.BlockSpec((HEAD_GROUP, block, 1), lambda i, f: (0, i, 0)),
                rows(HEAD_SIZE),
                rows(HEAD_SIZE),
                rows(1),
                whole(1, tokens),
                whole(tokens, HEAD_SIZE),
                whole(tokens, HEAD_SIZE),
                whole(tokens, HEAD_SIZE),
                whole(tokens, HEAD_SIZE),
            ],
            out_specs=[rows(query_width), whole(tokens, 2 * HEAD_SIZE)],
            scratch_shapes=[
                pltpu.VMEM((steps, HEAD_GROUP * block, block), jnp.float32),
                pltpu.VMEM((steps, HEAD_GROUP * block, block), jnp.float32),
                pltpu.VMEM((tokens, HEAD_SIZE), jnp.float32),
                pltpu.VMEM((tokens, HEAD_SIZE), jnp.float32),
            ],
        ),
        compiler_params=pltpu.CompilerParams(vmem_limit_bytes=48 << 20),
        cost_estimate=pl.CostEstimate(
            flops=10 * tokens * tokens * query_width,
            bytes_accessed=20 * tokens * query_width,
            transcendentals=tokens * tokens * HEAD_GROUP // 2,
        ),
    )(
        first,
        query,
        grad,
        log_total,
        cosine,
        sine,
        segment_row[:, None],
        segment_row[None, :],
        key,
        value,
        cosine,
        sine,
    )


def middle_kernel(
    mixed_ref,
    low_ref,
    high_ref,
    hidden_ref,
    gain_ref,
    router_ref,
    named_ref,
    middle_ref,
    normed_ref,
    gates_ref,
):
    groups, _, width = mixed_ref.shape
    middle = hidden_ref[...].astype(jnp.float32)
    for g in range(groups):
        weight_ref = low_ref if g < groups // 2 else high_ref
        start = (g % (groups // 2)) * width
        middle = middle + dot(mixed_ref[g], weight_ref[start : start + width, :])
    middle_ref[...] = middle
    scale = lax.rsqrt(jnp.mean(middle * middle, -1, keepdims=True) + EPS)
    normed = (middle * scale * gain_ref[...]).astype(jnp.bfloat16)
    normed_ref[...] = normed
    logits = dot(normed, router_ref[...])
    named = named_ref[...] > 0
    logits = jnp.where(named, logits, MASK_FLOOR)
    shifted = jnp.exp(logits - jnp.max(logits, -1, keepdims=True))
    shifted = jnp.where(named, shifted, 0.0)
    gates_ref[...] = shifted / jnp.sum(shifted, -1, keepdims=True)


def middle_rows(mixed, weights, hidden, gain, router, named, block):
    groups, tokens, width = mixed.shape
    features = gain.shape[0]
    experts = router.shape[1]
    rows = lambda columns: pl.BlockSpec((block, columns), lambda i: (i, 0))
    whole = lambda height, columns: pl.BlockSpec(
        (height, columns), lambda i: (0, 0), pipeline_mode=pl.Buffered(1)
    )
    return pl.pallas_call(
        middle_kernel,
        out_shape=(
            jax.ShapeDtypeStruct((tokens, features), jnp.float32),
            jax.ShapeDtypeStruct((tokens, features), jnp.bfloat16),
            jax.ShapeDtypeStruct((tokens, experts), jnp.float32),
        ),
        grid=(tokens // block,),
        in_specs=[
            pl.BlockSpec((groups, block, width), lambda i: (0, i, 0)),
            whole(*weights[0].shape),
            whole(*weights[1].shape),
            rows(features),
            whole(1, features),
            whole(features, experts),
            rows(experts),
        ],
        out_specs=[rows(features), rows(features), rows(experts)],
        compiler_params=pltpu.CompilerParams(vmem_limit_bytes=48 << 20),
        cost_estimate=pl.CostEstimate(
            flops=2 * tokens * features * groups * width,
            bytes_accessed=12 * tokens * features,
            transcendentals=0,
        ),
    )(mixed, *weights, hidden, gain[None, :], router, named)


def expert_kernel(
    place_ref,
    normed_ref,
    cotangent_ref,
    live_ref,
    gates_ref,
    gate_weight_ref,
    up_weight_ref,
    down_weight_ref,
    scaled_ref,
    grad_gate_ref,
    grad_up_ref,
    grad_live_ref,
    extra_ref,
):
    experts_own = gate_weight_ref.shape[0]
    experts_all = gates_ref.shape[1]
    first = place_ref[1] * experts_own
    normed = normed_ref[...]
    grad_live = jnp.where(live_ref[...] > 0, cotangent_ref[...], jnp.zeros((), jnp.bfloat16))
    grad_live_ref[...] = grad_live
    gates = gates_ref[...]
    number = lax.broadcasted_iota(jnp.int32, gates.shape, 1)
    grad_gates = jnp.zeros(gates.shape, jnp.float32)
    for e in range(experts_own):
        gate = jnp.sum(jnp.where(number == first + e, gates, 0.0), -1, keepdims=True)
        gate_pre = dot(normed, gate_weight_ref[e])
        up_pre = dot(normed, up_weight_ref[e])
        grad_plain = dot(grad_live, down_weight_ref[e], COLUMNS)
        sigma = jax.nn.sigmoid(gate_pre)
        silu = gate_pre * sigma
        acted = silu * up_pre
        grad_gates = grad_gates + jnp.where(
            number == first + e, jnp.sum(acted * grad_plain, -1, keepdims=True), 0.0
        )
        grad_acted = gate * grad_plain
        scaled_ref[e] = (gate * acted).astype(jnp.bfloat16)
        grad_gate_ref[e] = (
            grad_acted * up_pre * (sigma * (1.0 + gate_pre * (1.0 - sigma)))
        ).astype(jnp.bfloat16)
        grad_up_ref[e] = (grad_acted * silu).astype(jnp.bfloat16)
    rough = grad_gates.astype(jnp.bfloat16)
    fine = (grad_gates - rough.astype(jnp.float32)).astype(jnp.bfloat16)
    rest = jnp.zeros((gates.shape[0], extra_ref.shape[1] - 2 * experts_all), jnp.bfloat16)
    extra_ref[...] = jnp.concatenate([rough, fine, rest], 1)


def expert_rows(place, normed, cotangent, live, gates, w_gate, w_up, w_down):
    tokens, features = normed.shape
    experts_own, _, hidden = w_gate.shape
    experts_all = gates.shape[1]
    chips, block, _ = cotangent.shape
    rows = lambda columns: pl.BlockSpec((block, columns), lambda i, p: (i, 0))
    whole = lambda *shape: pl.BlockSpec(
        shape, lambda i, p: (0,) * len(shape), pipeline_mode=pl.Buffered(1)
    )
    spread = pl.BlockSpec((experts_own, block, hidden), lambda i, p: (0, i, 0))
    wide = jax.ShapeDtypeStruct((experts_own, tokens, hidden), jnp.bfloat16)
    return pl.pallas_call(
        expert_kernel,
        out_shape=(
            wide,
            wide,
            wide,
            jax.ShapeDtypeStruct((tokens, features), jnp.bfloat16),
            jax.ShapeDtypeStruct((tokens, 128), jnp.bfloat16),
        ),
        grid_spec=pltpu.PrefetchScalarGridSpec(
            num_scalar_prefetch=1,
            grid=(chips,),
            in_specs=[
                rows(features),
                pl.BlockSpec(
                    (None, block, features), lambda i, p: (lax.rem(p[0] - i + chips, chips), 0, 0)
                ),
                rows(1),
                rows(experts_all),
                whole(*w_gate.shape),
                whole(*w_up.shape),
                whole(*w_down.shape),
            ],
            out_specs=[spread, spread, spread, rows(features), rows(128)],
        ),
        compiler_params=pltpu.CompilerParams(vmem_limit_bytes=52 << 20),
        cost_estimate=pl.CostEstimate(
            flops=6 * tokens * features * hidden * experts_own,
            bytes_accessed=6 * features * hidden * experts_own + 10 * tokens * features,
            transcendentals=tokens * hidden * experts_own,
        ),
    )(place, normed, cotangent, live, gates, w_gate, w_up, w_down)


def rows_kernel(
    scaled_ref,
    grad_gate_ref,
    grad_up_ref,
    extra_ref,
    gate_weight_ref,
    up_weight_ref,
    down_weight_ref,
    grad_ref,
    out_ref,
):
    features = out_ref.shape[1]
    grad = 0.0
    out = 0.0
    for e in range(scaled_ref.shape[0]):
        grad = grad + dot(grad_gate_ref[e], gate_weight_ref[e], COLUMNS)
        grad = grad + dot(grad_up_ref[e], up_weight_ref[e], COLUMNS)
        out = out + dot(scaled_ref[e], down_weight_ref[e])
    grad_ref[:, :features] = grad.astype(jnp.bfloat16)
    grad_ref[:, features:] = extra_ref[...]
    out_ref[...] = out.astype(jnp.bfloat16)


def expert_sums(scaled, grad_gate_pre, grad_up_pre, extra, w_gate, w_up, w_down, block):
    experts_own, tokens, hidden = scaled.shape
    features = w_gate.shape[1]
    rows = lambda columns: pl.BlockSpec((block, columns), lambda i: (i, 0))
    whole = lambda *shape: pl.BlockSpec(
        shape, lambda i: (0,) * len(shape), pipeline_mode=pl.Buffered(1)
    )
    spread = pl.BlockSpec((experts_own, block, hidden), lambda i: (0, i, 0))
    return pl.pallas_call(
        rows_kernel,
        out_shape=(
            jax.ShapeDtypeStruct((tokens, features + extra.shape[1]), jnp.bfloat16),
            jax.ShapeDtypeStruct((tokens, features), jnp.bfloat16),
        ),
        grid=(tokens // block,),
        in_specs=[
            spread,
            spread,
            spread,
            rows(extra.shape[1]),
            whole(*w_gate.shape),
            whole(*w_up.shape),
            whole(*w_down.shape),
        ],
        out_specs=[rows(features + extra.shape[1]), rows(features)],
        compiler_params=pltpu.CompilerParams(vmem_limit_bytes=52 << 20),
        cost_estimate=pl.CostEstimate(
            flops=6 * tokens * features * hidden * experts_own,
            bytes_accessed=6 * features * hidden * experts_own + 10 * tokens * features,
            transcendentals=0,
        ),
    )(scaled, grad_gate_pre, grad_up_pre, extra, w_gate, w_up, w_down)


def after(values, *others):
    values, _ = lax.optimization_barrier((values, others))
    return values


def swap(value, bit):
    size = lax.axis_size("rep")
    return lax.ppermute(value, "rep", [(i, i ^ bit) for i in range(size)])


def has(bit):
    return (lax.axis_index("rep") & bit) != 0


def halve(value, came, bit):
    half = value.shape[0] // 2
    keep = jnp.where(has(bit), half, 0)
    part = lambda array, start: lax.dynamic_slice_in_dim(array, start, half, 0).astype(jnp.float32)
    kept = part(value, keep)
    sent = part(value, half - keep)
    if came is not None:
        kept = kept + part(came, keep)
        sent = sent + part(came, half - keep)
    return kept, sent.astype(jnp.bfloat16)


def join(value, came, bit, axis):
    upper = has(bit)
    return jnp.concatenate(
        [jnp.where(upper, came, value), jnp.where(upper, value, came)], axis
    )


class Chain:
    def __init__(self, order):
        self.order = order
        self.stage = 0
        self.steps = 2 * len(order)

    def send(self, sent):
        bit = self.order[min(self.stage, self.steps - 1 - self.stage)]
        self.sent = sent
        self.flying = swap(sent, bit)
        self.stage += 1

    def start(self, value):
        self.kept, sent = halve(value, None, self.order[0])
        self.send(sent)

    def step(self, *others):
        came = after(self.flying, *others)
        bits = len(self.order)
        if self.stage < bits:
            self.kept, sent = halve(self.kept, came, self.order[self.stage])
            self.send(sent)
        elif self.stage == bits:
            self.send((self.kept + came.astype(jnp.float32)).astype(jnp.bfloat16))
        else:
            bit = self.order[self.steps - self.stage]
            self.send(join(self.sent, came, bit, 0))
        return self.sent

    def finish(self, *others):
        came = after(self.flying, *others)
        return join(self.sent, came, self.order[0], 0)


def exchange(fetched, bits):
    size = fetched.shape[0]
    fetched = fetched.reshape((size,) + (1,) * len(bits) + fetched.shape[1:])
    values = [fetched[: size // 2], fetched[size // 2 :]]
    for stage in range(len(bits)):
        for h, order in enumerate((bits, bits[::-1])):
            bit = order[stage]
            values[h] = join(
                values[h], swap(values[h], bit), bit, len(bits) - (bit.bit_length() - 1)
            )
    return [value.reshape(-1, value.shape[-1]) for value in values]


def per_device(
    inputs,
    segments,
    positions,
    expert_ids,
    attn_gain,
    w_query,
    key_weight,
    value_weight,
    w_out,
    ffn_gain,
    router,
    w_gate,
    w_up,
    w_down,
    grad_out,
):
    size = lax.axis_size("ctx")
    me = lax.axis_index("ctx")
    reps = lax.axis_size("rep")
    bits = [1 << i for i in range(reps.bit_length() - 1)]
    own = inputs.shape[1]
    tokens = size * own
    groups = KEY_VALUE_HEADS
    copies = size // groups
    query_width = HEAD_GROUP * HEAD_SIZE
    width = query_width + 2 * HEAD_SIZE
    copy_index = me % copies
    rows_own = w_out.shape[0]
    experts_own = w_gate.shape[0]
    experts_all = size * experts_own
    slots = expert_ids.shape[2]
    block = 2 * own
    chips = size // 2
    share = rows_own // reps
    share_start = lax.axis_index("rep") * share

    columns = jnp.concatenate(
        [
            segments[0][:, None],
            positions[0][:, None] // 64,
            positions[0][:, None] % 64,
            expert_ids[0],
        ],
        1,
    ).astype(jnp.bfloat16)
    columns = jnp.pad(columns, ((0, 0), (0, 128 - columns.shape[1])))
    gathered = lax.all_gather(
        jnp.concatenate([inputs[0], columns], 1), "ctx", axis=0, tiled=True
    )

    shared = lambda array: lax.dynamic_slice_in_dim(array, share_start, share, 0)
    head_columns = jnp.concatenate(
        [
            shared(w_query).reshape(share, groups, query_width),
            shared(key_weight).reshape(share, groups, HEAD_SIZE),
            shared(value_weight).reshape(share, groups, HEAD_SIZE),
            jnp.broadcast_to(shared(attn_gain)[:, None, None], (share, groups, 1)),
            jnp.broadcast_to(shared(ffn_gain)[:, None, None], (share, groups, 1)),
            jnp.broadcast_to(shared(router)[:, None, :], (share, groups, router.shape[1])),
        ],
        -1,
    )
    head_columns = jnp.repeat(jnp.transpose(head_columns, (1, 0, 2)), copies, 0)
    head_columns = lax.all_to_all(head_columns, "ctx", split_axis=0, concat_axis=0, tiled=True)
    head_halves = exchange(head_columns, bits)
    head_columns = jnp.concatenate(head_halves, 0)
    w_heads = head_columns[:, :width]
    gain_one = head_columns[:, width].astype(jnp.float32)
    gain_two = head_columns[:, width + 1].astype(jnp.float32)
    router_all = head_columns[:, width + 2 :]

    numbers = gathered[:, MODEL_WIDTH : MODEL_WIDTH + 3 + slots].astype(jnp.int32)
    segment_row = numbers[:, 0]
    position_row = numbers[:, 1] * 64 + numbers[:, 2]
    ids = numbers[:, 3:]
    cosine_table, sine_table = rope_tables(position_row)
    places = jnp.arange(tokens, dtype=jnp.int32)
    starts = segment_row[::block]
    first = (
        jnp.min(jnp.where(segment_row[None, :] == starts[:, None], places[None, :], tokens), 1)
        // block
    )
    normed_one, query, key, value, mixed, log_total = attend(
        gathered,
        gain_one,
        [half[:, :width] for half in head_halves],
        cosine_table,
        sine_table,
        segment_row,
        block,
        first,
    )
    w_out_halves = exchange(
        lax.all_gather(shared(after(w_out, gathered)), "ctx", axis=0), bits
    )

    turned = [after(grad_out[0], gathered)]
    for k in range(1, chips):
        turned.append(
            lax.ppermute(turned[0], "ctx", [(i, (i + 2 * k) % size) for i in range(size)])
        )
    turned = jnp.stack(turned)
    other = lax.ppermute(turned, "ctx", [(i, i ^ 1) for i in range(size)])
    odd = me % 2 == 1
    cotangent = jnp.concatenate(
        [jnp.where(odd, other, turned), jnp.where(odd, turned, other)], 1
    )

    part = tokens // copies
    mixed_all = lax.all_gather(
        lax.dynamic_slice_in_dim(mixed, copy_index * part, part, 0), "ctx", axis=0
    ).reshape(groups, tokens, query_width)
    named = jnp.any(
        ids[:, :, None] == jnp.arange(experts_all, dtype=jnp.int32)[None, None, :], 1
    ).astype(jnp.float32)
    middle, normed_two, gates = middle_rows(
        mixed_all, w_out_halves, gathered, gain_two, router_all, named, block
    )
    place = jnp.stack([me // 2, me]).astype(jnp.int32)
    scaled, grad_gate_pre, grad_up_pre, grad_live, extra = expert_rows(
        place,
        normed_two,
        cotangent,
        (segment_row != 0).astype(jnp.float32)[:, None],
        gates,
        w_gate,
        w_up,
        w_down,
    )

    pick = experts_own // 2
    half = MODEL_WIDTH // 2

    def product(left, right, upper):
        terms = [
            dot(
                jnp.where(upper, left(e + pick), left(e)),
                jnp.where(upper, right(e + pick), right(e)),
                ROWS,
            )
            for e in range(pick)
        ]
        return jnp.concatenate(terms, 0)

    down_sides = [
        (lambda e: scaled[e], lambda e: grad_live[:, :half]),
        (lambda e: scaled[e], lambda e: grad_live[:, half:]),
    ]
    input_sides = [
        (lambda e: normed_two, lambda e: grad_gate_pre[e]),
        (lambda e: normed_two, lambda e: grad_up_pre[e]),
    ]
    down = [Chain(bits), Chain(bits[::-1])]
    into = [Chain(bits), Chain(bits[::-1])]
    for chain, sides in zip(down + into, down_sides + input_sides):
        chain.send(product(*sides, jnp.logical_not(has(chain.order[0]))).astype(jnp.bfloat16))
    sent = [chain.sent for chain in down + into]
    grad_rows, out_rows = expert_sums(
        *after((scaled, grad_gate_pre, grad_up_pre), *sent),
        extra,
        w_gate,
        w_up,
        w_down,
        block,
    )
    grad_two_sum = lax.psum_scatter(grad_rows, "ctx", scatter_dimension=0, tiled=True)
    scaled, grad_gate_pre, grad_up_pre = after((scaled, grad_gate_pre, grad_up_pre), grad_rows)
    for chain, sides in zip(down + into, down_sides + input_sides):
        chain.kept = product(*sides, has(chain.order[0]))
    sent = [chain.step(*[c.kept for c in down + into]) for chain in down]
    grad_two_sum = after(grad_two_sum, *sent).astype(jnp.float32)

    def mine(array):
        return lax.dynamic_slice_in_dim(array, me * own, own, 0)

    gates_own = mine(gates)
    grad_gates = (
        grad_two_sum[:, MODEL_WIDTH : MODEL_WIDTH + experts_all]
        + grad_two_sum[:, MODEL_WIDTH + experts_all : MODEL_WIDTH + 2 * experts_all]
    )
    grad_logits = (
        gates_own * (grad_gates - jnp.sum(gates_own * grad_gates, -1, keepdims=True))
    ).astype(jnp.bfloat16)
    grad_normed_two = grad_two_sum[:, :MODEL_WIDTH] + dot(grad_logits, router_all, COLUMNS)
    middle_own = mine(middle)
    scale_two = lax.rsqrt(jnp.mean(middle_own * middle_own, -1, keepdims=True) + EPS)
    base_two = middle_own * scale_two
    grad_middle = mine(grad_live).astype(jnp.float32) + norm_back(
        grad_normed_two * gain_two, base_two, scale_two
    )
    grad_branch = grad_middle.astype(jnp.bfloat16)
    grad_mixed = jnp.concatenate(
        [dot(grad_branch, weight, COLUMNS) for weight in w_out_halves], 1
    ).astype(jnp.bfloat16)
    grad_mixed = jnp.transpose(grad_mixed.reshape(own, groups, query_width), (1, 0, 2))
    grad_mixed = jnp.repeat(grad_mixed, copies, 0)
    grad_mixed_all = lax.all_to_all(
        grad_mixed, "ctx", split_axis=0, concat_axis=0, tiled=True
    ).reshape(tokens, query_width)
    grad_branch_all = lax.all_gather(grad_branch, "ctx", axis=0, tiled=True)

    sent = [chain.step(grad_mixed) for chain in into]
    sent = sent + [chain.step(*sent) for chain in down]

    grad_query, grad_pair = attend_back(
        query,
        after(grad_mixed_all, *sent),
        log_total,
        cosine_table,
        sine_table,
        segment_row,
        key,
        value,
        block,
        first,
    )
    if copies > 1:
        counted = (places // part == copy_index)[:, None]
        grad_query = jnp.where(counted, grad_query, jnp.zeros((), jnp.bfloat16))
        grad_pair = jnp.where(counted, grad_pair, jnp.zeros((), jnp.bfloat16))
    grad_one_part = dot(grad_query, w_heads[:, :query_width], COLUMNS) + dot(
        grad_pair, w_heads[:, query_width:], COLUMNS
    )
    grad_one_low = grad_one_part.astype(jnp.bfloat16)
    grad_one = lax.psum_scatter(
        grad_one_low, "ctx", scatter_dimension=0, tiled=True
    ).astype(jnp.float32)
    hidden = gathered[:, :MODEL_WIDTH].astype(jnp.float32)
    scale_one = lax.rsqrt(jnp.mean(hidden * hidden, -1, keepdims=True) + EPS)
    gain_one_term = jnp.sum(grad_one_part * (hidden * scale_one), 0)
    gain_two_term = jnp.sum(grad_normed_two * base_two, 0)
    head_grads = jnp.concatenate(
        [
            dot(normed_one, grad_query, ROWS),
            dot(normed_one, grad_pair, ROWS),
            gain_one_term[:, None],
            gain_two_term[:, None],
            dot(mine(normed_two), grad_logits, ROWS),
        ],
        1,
    ).astype(jnp.bfloat16)
    head_grads = head_grads.reshape(size, rows_own, -1)
    head_grads_all = lax.all_to_all(
        head_grads, "ctx", split_axis=0, concat_axis=0, tiled=True
    )

    sent = [chain.step(grad_one_low, head_grads) for chain in into]
    sent = sent + [chain.step(*sent) for chain in down]
    grad_proj_out = dot(
        lax.dynamic_slice_in_dim(mixed, copy_index * rows_own, rows_own, 1),
        after(grad_branch_all, *sent),
        ROWS,
    )
    out_chain = Chain(bits[::-1])
    out_chain.start(grad_proj_out)
    if copies > 1:
        head_grads_all = jnp.sum(
            head_grads_all.reshape(groups, copies, rows_own, -1).astype(jnp.float32), 1
        )
    heads = [Chain(bits), Chain(bits[::-1])]
    head_grads_all = after(head_grads_all, out_chain.sent)
    heads[0].start(head_grads_all[: groups // 2].reshape(groups // 2 * rows_own, -1))
    heads[1].start(head_grads_all[groups // 2 :].reshape(groups // 2 * rows_own, -1))
    sent = [chain.sent for chain in heads]
    while into[0].stage < into[0].steps:
        sent = [chain.step(*sent) for chain in into]
        sent = sent + [chain.step(*sent) for chain in [out_chain] + heads]
        if down[0].stage < down[0].steps:
            sent = sent + [chain.step(*sent) for chain in down]
    whole = lambda value: value.astype(jnp.float32).reshape(experts_own, -1, value.shape[-1])
    grad_down = jnp.concatenate([whole(chain.finish(*sent)) for chain in down], 2)
    sent = sent + [grad_down]
    while heads[0].stage < heads[0].steps:
        sent = [chain.step(*sent) for chain in [out_chain] + heads]
    grad_gate, grad_up = [whole(chain.finish(*sent)) for chain in into]
    last = [chain.finish(grad_gate, grad_up) for chain in [out_chain] + heads]
    grad_out_rows = last[0].astype(jnp.float32)
    head_rows = jnp.concatenate(last[1:], 0).reshape(groups, rows_own, -1).astype(jnp.float32)
    side = lambda begin, end: jnp.transpose(head_rows[:, :, begin:end], (1, 0, 2)).reshape(
        rows_own, -1
    )
    small = jnp.sum(head_rows[:, :, width:], 0)

    moe_sum = lax.psum_scatter(
        after(out_rows, grad_branch), "ctx", scatter_dimension=0, tiled=True
    ).astype(jnp.float32)
    live_own = (segments[0] != 0)[:, None]
    output = jnp.where(live_own, middle_own + moe_sum, 0.0).astype(jnp.bfloat16)
    own_hidden = inputs[0].astype(jnp.float32)
    own_scale = lax.rsqrt(jnp.mean(own_hidden * own_hidden, -1, keepdims=True) + EPS)
    grad_in = grad_middle + norm_back(grad_one * gain_one, own_hidden * own_scale, own_scale)

    return (
        output[None],
        grad_in[None],
        small[:, 0],
        side(0, query_width),
        side(query_width, query_width + HEAD_SIZE),
        side(query_width + HEAD_SIZE, width),
        grad_out_rows,
        small[:, 1],
        small[:, 2:],
        grad_gate,
        grad_up,
        grad_down,
    )


def solution(mesh):
    return jax.shard_map(
        per_device,
        mesh=mesh,
        in_specs=(
            P("rep", "ctx", None),
            P("rep", "ctx"),
            P("rep", "ctx"),
            P("rep", "ctx", None),
            P("ctx"),
            P("ctx", None),
            P("ctx", None),
            P("ctx", None),
            P("ctx", None),
            P("ctx"),
            P("ctx", None),
            P("ctx", None, None),
            P("ctx", None, None),
            P("ctx", None, None),
            P("rep", "ctx", None),
        ),
        out_specs=(
            P("rep", "ctx", None),
            P("rep", "ctx", None),
            P("ctx"),
            P("ctx", None),
            P("ctx", None),
            P("ctx", None),
            P("ctx", None),
            P("ctx"),
            P("ctx", None),
            P("ctx", None, None),
            P("ctx", None, None),
            P("ctx", None, None),
        ),
        check_vma=False,
    )
```

```python
import jax
import jax.numpy as jnp
from jax import lax
from jax.experimental import pallas as pl
from jax.experimental.pallas import tpu as pltpu
from jax.sharding import PartitionSpec as P

MODEL_WIDTH = 1536
QUERY_HEADS = 24
KEY_VALUE_HEADS = 8
HEAD_GROUP = QUERY_HEADS // KEY_VALUE_HEADS
HEAD_SIZE = 64
TOPK = 8

EPS = 1e-06
THETA = 10000.0
MASK_FLOOR = -1e30

ROWS = (((0,), (0,)), ((), ()))
COLUMNS = (((1,), (1,)), ((), ()))


def dot(left, right, contract=(((1,), (0,)), ((), ()))):
    return lax.dot_general(left, right, contract, preferred_element_type=jnp.float32)


def norm_back(grad_base, base, scale):
    return scale * (grad_base - base * jnp.mean(grad_base * base, -1, keepdims=True))


def turn(rows):
    half = HEAD_SIZE // 2
    return jnp.concatenate([-rows[:, half:], rows[:, :half]], 1)


def turn_back(rows):
    half = HEAD_SIZE // 2
    return jnp.concatenate([rows[:, half:], -rows[:, :half]], 1)


def stack_heads(rows):
    return jnp.concatenate(
        [rows[:, h * HEAD_SIZE : (h + 1) * HEAD_SIZE] for h in range(HEAD_GROUP)], 0
    )


def side_heads(rows):
    block = rows.shape[0] // HEAD_GROUP
    return jnp.concatenate([rows[h * block : (h + 1) * block] for h in range(HEAD_GROUP)], 1)


def lanes(values, combine):
    total = values[:, :128]
    for start in range(128, values.shape[1], 128):
        total = combine(total, values[:, start : start + 128])
    return total


def masked_scores(stacked, keys, row_segments, key_segments, row_start, key_start):
    block = row_segments.shape[0]
    scores = dot(stacked, keys, COLUMNS) * HEAD_SIZE ** (-0.5)
    row_place = row_start + lax.broadcasted_iota(jnp.int32, (block, block), 0)
    key_place = key_start + lax.broadcasted_iota(jnp.int32, (block, block), 1)
    allowed = (row_segments == key_segments) & (key_place <= row_place)
    scores = scores.reshape(HEAD_GROUP, block, block)
    return jnp.where(allowed[None], scores, MASK_FLOOR).reshape(HEAD_GROUP * block, block)


def first_block(row_segments, segment_ref, step):
    here = jnp.max(row_segments[:1, :1])
    segments = segment_ref[...]
    number = lax.broadcasted_iota(jnp.int32, segments.shape, 0)
    return jnp.min(jnp.where((segments == here) & (number <= step), number, step))


def whole_block(*shape, grid=1, prefetch=0):
    return pl.BlockSpec(shape, lambda *i: (0,) * len(shape), pipeline_mode=pl.Buffered(1))


def attend_kernel(
    hidden_ref,
    column_ref,
    gain_ref,
    low_ref,
    high_ref,
    rate_ref,
    normed_ref,
    query_ref,
    key_ref,
    value_ref,
    mixed_ref,
    log_ref,
    cosine_ref,
    sine_ref,
    segment_ref,
    score_ref,
):
    step = pl.program_id(0)
    block = hidden_ref.shape[0]
    query_width = query_ref.shape[1]
    width = query_width + 2 * HEAD_SIZE
    here = pl.ds(pl.multiple_of(step * block, block), block)
    columns = column_ref[...].astype(jnp.float32)
    row_segments = columns[:, :1]
    segment_ref[step] = jnp.transpose(columns)[:1, :]
    angles = (columns[:, 1:2] * 64.0 + columns[:, 2:3]) * rate_ref[...]
    cosine = jnp.cos(angles)
    sine = jnp.sin(angles)
    cosine_ref[...] = cosine
    sine_ref[...] = sine
    hidden = hidden_ref[...].astype(jnp.float32)
    scale = lax.rsqrt(jnp.mean(hidden * hidden, -1, keepdims=True) + EPS)
    normed = (hidden * scale * gain_ref[...]).astype(jnp.bfloat16)
    normed_ref[...] = normed
    middle = low_ref.shape[0]
    raw = dot(normed[:, :middle], low_ref[:, :width]) + dot(
        normed[:, middle:], high_ref[:, :width]
    )
    key_raw = raw[:, query_width : query_width + HEAD_SIZE]
    key_ref[here, :] = (key_raw * cosine + turn(key_raw) * sine).astype(jnp.bfloat16)
    value_ref[here, :] = raw[:, query_width + HEAD_SIZE :].astype(jnp.bfloat16)
    query_raw = stack_heads(raw[:, :query_width])
    cosine = jnp.concatenate([cosine] * HEAD_GROUP, 0)
    sine = jnp.concatenate([sine] * HEAD_GROUP, 0)
    query = (query_raw * cosine + turn(query_raw) * sine).astype(jnp.bfloat16)
    query_ref[...] = side_heads(query)
    rows = HEAD_GROUP * block
    first = first_block(row_segments, segment_ref, step)

    def first_pass(index, top):
        there = pl.ds(pl.multiple_of(index * block, block), block)
        scores = masked_scores(
            query,
            key_ref[there, :],
            row_segments,
            segment_ref[index],
            step * block,
            index * block,
        )
        score_ref[index] = scores
        return jnp.maximum(top, lanes(scores, jnp.maximum))

    top = lax.fori_loop(
        first, step + 1, first_pass, jnp.full((rows, 128), MASK_FLOOR, jnp.float32)
    )
    top = jnp.max(top, -1, keepdims=True)

    def second_pass(index, carry):
        total, mixed = carry
        there = pl.ds(pl.multiple_of(index * block, block), block)
        weights = jnp.exp(score_ref[index] - top)
        mixed = mixed + dot(weights.astype(jnp.bfloat16), value_ref[there, :])
        return total + lanes(weights, jnp.add), mixed

    total, mixed = lax.fori_loop(
        first,
        step + 1,
        second_pass,
        (
            jnp.zeros((rows, 128), jnp.float32),
            jnp.zeros((rows, HEAD_SIZE), jnp.float32),
        ),
    )
    total = jnp.sum(total, -1, keepdims=True)
    mixed_ref[...] = side_heads((mixed / total).astype(jnp.bfloat16))
    log_ref[...] = (top + jnp.log(total)).reshape(HEAD_GROUP, block, 1)


def attend(gathered, gain, weights, block):
    tokens, features = gathered.shape[0], gain.shape[0]
    query_width = HEAD_GROUP * HEAD_SIZE
    steps = tokens // block
    half = jnp.arange(HEAD_SIZE // 2, dtype=jnp.float32)
    rate = THETA ** (-(2.0 * half) / HEAD_SIZE)
    rate = jnp.concatenate([rate, rate])[None, :]
    rows = lambda width: pl.BlockSpec((block, width), lambda i: (i, 0))
    resident = lambda *shape: pl.BlockSpec(shape, lambda i: (0,) * len(shape))
    shaped = jax.ShapeDtypeStruct
    return pl.pallas_call(
        attend_kernel,
        out_shape=(
            shaped((tokens, features), jnp.bfloat16),
            shaped((tokens, query_width), jnp.bfloat16),
            shaped((tokens, HEAD_SIZE), jnp.bfloat16),
            shaped((tokens, HEAD_SIZE), jnp.bfloat16),
            shaped((tokens, query_width), jnp.bfloat16),
            shaped((HEAD_GROUP, tokens, 1), jnp.float32),
            shaped((tokens, HEAD_SIZE), jnp.float32),
            shaped((tokens, HEAD_SIZE), jnp.float32),
            shaped((steps, 1, block), jnp.float32),
        ),
        grid=(steps,),
        in_specs=[
            rows(features),
            pl.BlockSpec((block, 128), lambda i: (i, features // 128)),
            whole_block(1, features),
            whole_block(*weights[0].shape),
            whole_block(*weights[1].shape),
            whole_block(1, HEAD_SIZE),
        ],
        out_specs=[
            rows(features),
            rows(query_width),
            resident(tokens, HEAD_SIZE),
            resident(tokens, HEAD_SIZE),
            rows(query_width),
            pl.BlockSpec((HEAD_GROUP, block, 1), lambda i: (0, i, 0)),
            rows(HEAD_SIZE),
            rows(HEAD_SIZE),
            resident(steps, 1, block),
        ],
        scratch_shapes=[pltpu.VMEM((steps, HEAD_GROUP * block, block), jnp.float32)],
        compiler_params=pltpu.CompilerParams(vmem_limit_bytes=48 << 20),
        cost_estimate=pl.CostEstimate(
            flops=6 * tokens * features * query_width,
            bytes_accessed=4 * tokens * features,
            transcendentals=tokens * tokens * HEAD_GROUP // 2,
        ),
    )(gathered, gathered, gain[None, :], *weights, rate)


def attend_back_kernel(
    query_ref,
    grad_ref,
    log_ref,
    cosine_ref,
    sine_ref,
    column_ref,
    segment_ref,
    key_ref,
    value_ref,
    key_cosine_ref,
    key_sine_ref,
    grad_query_ref,
    grad_pair_ref,
    probs_ref,
    grad_probs_ref,
    grad_key_ref,
    grad_value_ref,
):
    step = pl.program_id(0)
    block = query_ref.shape[0]
    rows = HEAD_GROUP * block

    @pl.when(step == 0)
    def _():
        grad_key_ref[...] = jnp.zeros_like(grad_key_ref)
        grad_value_ref[...] = jnp.zeros_like(grad_value_ref)

    query = stack_heads(query_ref[...])
    grad = stack_heads(grad_ref[...])
    log_total = log_ref[...].reshape(rows, 1)
    row_segments = column_ref[...].astype(jnp.float32)[:, :1]
    first = first_block(row_segments, segment_ref, step)

    def first_pass(index, delta):
        there = pl.ds(pl.multiple_of(index * block, block), block)
        scores = masked_scores(
            query,
            key_ref[there, :],
            row_segments,
            segment_ref[index],
            step * block,
            index * block,
        )
        probs = jnp.exp(scores - log_total)
        grad_probs = dot(grad, value_ref[there, :], COLUMNS)
        probs_ref[index] = probs
        grad_probs_ref[index] = grad_probs
        grad_value_ref[there, :] += dot(probs.astype(jnp.bfloat16), grad, ROWS)
        return delta + lanes(probs * grad_probs, jnp.add)

    delta = lax.fori_loop(first, step + 1, first_pass, jnp.zeros((rows, 128), jnp.float32))
    delta = jnp.sum(delta, -1, keepdims=True)

    def second_pass(index, grad_query):
        there = pl.ds(pl.multiple_of(index * block, block), block)
        grad_scores = (probs_ref[index] * (grad_probs_ref[index] - delta)).astype(jnp.bfloat16)
        grad_key_ref[there, :] += dot(grad_scores, query, ROWS)
        return grad_query + dot(grad_scores, key_ref[there, :])

    grad_query = lax.fori_loop(
        first, step + 1, second_pass, jnp.zeros((rows, HEAD_SIZE), jnp.float32)
    )
    score_scale = HEAD_SIZE ** (-0.5)
    cosine = jnp.concatenate([cosine_ref[...]] * HEAD_GROUP, 0)
    sine = jnp.concatenate([sine_ref[...]] * HEAD_GROUP, 0)
    grad_query = grad_query * score_scale
    grad_query = grad_query * cosine + turn_back(grad_query * sine)
    grad_query_ref[...] = side_heads(grad_query.astype(jnp.bfloat16))

    @pl.when(step == pl.num_programs(0) - 1)
    def _():
        grad_key = grad_key_ref[...] * score_scale
        grad_key = grad_key * key_cosine_ref[...] + turn_back(grad_key * key_sine_ref[...])
        grad_pair_ref[...] = jnp.concatenate([grad_key, grad_value_ref[...]], 1).astype(
            jnp.bfloat16
        )


def attend_back(query, grad, log_total, cosine, sine, gathered, segments, key, value):
    tokens, query_width = query.shape
    steps, _, block = segments.shape
    features = gathered.shape[1] - 128
    rows = lambda width: pl.BlockSpec((block, width), lambda i: (i, 0))
    resident = lambda *shape: pl.BlockSpec(shape, lambda i: (0,) * len(shape))
    return pl.pallas_call(
        attend_back_kernel,
        out_shape=(
            jax.ShapeDtypeStruct((tokens, query_width), jnp.bfloat16),
            jax.ShapeDtypeStruct((tokens, 2 * HEAD_SIZE), jnp.bfloat16),
        ),
        grid=(steps,),
        in_specs=[
            rows(query_width),
            rows(query_width),
            pl.BlockSpec((HEAD_GROUP, block, 1), lambda i: (0, i, 0)),
            rows(HEAD_SIZE),
            rows(HEAD_SIZE),
            pl.BlockSpec((block, 128), lambda i: (i, features // 128)),
            whole_block(steps, 1, block),
            whole_block(tokens, HEAD_SIZE),
            whole_block(tokens, HEAD_SIZE),
            whole_block(tokens, HEAD_SIZE),
            whole_block(tokens, HEAD_SIZE),
        ],
        out_specs=[rows(query_width), resident(tokens, 2 * HEAD_SIZE)],
        scratch_shapes=[
            pltpu.VMEM((steps, HEAD_GROUP * block, block), jnp.float32),
            pltpu.VMEM((steps, HEAD_GROUP * block, block), jnp.float32),
            pltpu.VMEM((tokens, HEAD_SIZE), jnp.float32),
            pltpu.VMEM((tokens, HEAD_SIZE), jnp.float32),
        ],
        compiler_params=pltpu.CompilerParams(vmem_limit_bytes=48 << 20),
        cost_estimate=pl.CostEstimate(flops=0, bytes_accessed=tokens, transcendentals=0),
    )(query, grad, log_total, cosine, sine, gathered, segments, key, value, cosine, sine)


def middle_kernel(
    mixed_ref,
    low_ref,
    high_ref,
    hidden_ref,
    column_ref,
    gain_ref,
    router_ref,
    middle_ref,
    normed_ref,
    gates_ref,
):
    groups = mixed_ref.shape[0]
    mixed = jnp.concatenate([mixed_ref[g] for g in range(groups)], 1)
    half = low_ref.shape[0]
    middle = dot(mixed[:, :half], low_ref[...]) + dot(mixed[:, half:], high_ref[...])
    middle = hidden_ref[...].astype(jnp.float32) + middle
    middle_ref[...] = middle
    scale = lax.rsqrt(jnp.mean(middle * middle, -1, keepdims=True) + EPS)
    normed = (middle * scale * gain_ref[...]).astype(jnp.bfloat16)
    normed_ref[...] = normed
    logits = dot(normed, router_ref[...])
    columns = column_ref[...].astype(jnp.float32)
    number = lax.broadcasted_iota(jnp.int32, logits.shape, 1).astype(jnp.float32)
    named = columns[:, 3:4] == number
    for slot in range(1, TOPK):
        named = named | (columns[:, 3 + slot : 4 + slot] == number)
    logits = jnp.where(named, logits, MASK_FLOOR)
    shifted = jnp.exp(logits - jnp.max(logits, -1, keepdims=True))
    shifted = jnp.where(named, shifted, 0.0)
    gates_ref[...] = shifted / jnp.sum(shifted, -1, keepdims=True)


def middle_rows(mixed, weights, gathered, gain, router, block):
    groups, tokens, width = mixed.shape
    features = gain.shape[0]
    experts = router.shape[1]
    rows = lambda columns: pl.BlockSpec((block, columns), lambda i: (i, 0))
    return pl.pallas_call(
        middle_kernel,
        out_shape=(
            jax.ShapeDtypeStruct((tokens, features), jnp.float32),
            jax.ShapeDtypeStruct((tokens, features), jnp.bfloat16),
            jax.ShapeDtypeStruct((tokens, experts), jnp.float32),
        ),
        grid=(tokens // block,),
        in_specs=[
            pl.BlockSpec((groups, block, width), lambda i: (0, i, 0)),
            whole_block(*weights[0].shape),
            whole_block(*weights[1].shape),
            rows(features),
            pl.BlockSpec((block, 128), lambda i: (i, features // 128)),
            whole_block(1, features),
            whole_block(features, experts),
        ],
        out_specs=[rows(features), rows(features), rows(experts)],
        compiler_params=pltpu.CompilerParams(vmem_limit_bytes=48 << 20),
        cost_estimate=pl.CostEstimate(
            flops=2 * tokens * features * groups * width,
            bytes_accessed=12 * tokens * features,
            transcendentals=0,
        ),
    )(mixed, *weights, gathered, gathered, gain[None, :], router)


def slot_of(e, keeps, experts_own):
    pick = experts_own // 2
    high, low = e // pick, e % pick
    return (1 - (high ^ keeps)) * pick + low


def expert_kernel(
    place_ref,
    normed_ref,
    cotangent_ref,
    column_ref,
    gates_ref,
    gate_weight_ref,
    up_weight_ref,
    down_weight_ref,
    scaled_one_ref,
    scaled_two_ref,
    grad_gate_ref,
    grad_up_ref,
    grad_live_ref,
    extra_ref,
):
    experts_own = gate_weight_ref.shape[0]
    experts_all = gates_ref.shape[1]
    first = place_ref[1] * experts_own
    normed = normed_ref[...]
    live = column_ref[...].astype(jnp.float32)[:, :1] > 0
    grad_live = jnp.where(live, cotangent_ref[...], jnp.zeros((), jnp.bfloat16))
    grad_live_ref[...] = grad_live
    gates = gates_ref[...]
    number = lax.broadcasted_iota(jnp.int32, gates.shape, 1)
    grad_gates = jnp.zeros(gates.shape, jnp.float32)
    for e in range(experts_own):
        one = slot_of(e, place_ref[2], experts_own)
        two = slot_of(e, place_ref[3], experts_own)
        gate = jnp.sum(jnp.where(number == first + e, gates, 0.0), -1, keepdims=True)
        gate_pre = dot(normed, gate_weight_ref[e])
        up_pre = dot(normed, up_weight_ref[e])
        grad_plain = dot(grad_live, down_weight_ref[e], COLUMNS)
        sigma = jax.nn.sigmoid(gate_pre)
        silu = gate_pre * sigma
        acted = silu * up_pre
        grad_gates = grad_gates + jnp.where(
            number == first + e, jnp.sum(acted * grad_plain, -1, keepdims=True), 0.0
        )
        grad_acted = gate * grad_plain
        scaled = (gate * acted).astype(jnp.bfloat16)
        scaled_one_ref[one] = scaled
        scaled_two_ref[two] = scaled
        grad_gate_ref[one] = (
            grad_acted * up_pre * (sigma * (1.0 + gate_pre * (1.0 - sigma)))
        ).astype(jnp.bfloat16)
        grad_up_ref[two] = (grad_acted * silu).astype(jnp.bfloat16)
    rough = grad_gates.astype(jnp.bfloat16)
    fine = (grad_gates - rough.astype(jnp.float32)).astype(jnp.bfloat16)
    rest = jnp.zeros((gates.shape[0], extra_ref.shape[1] - 2 * experts_all), jnp.bfloat16)
    extra_ref[...] = jnp.concatenate([rough, fine, rest], 1)


def expert_rows(place, normed, cotangent, gathered, gates, w_gate, w_up, w_down):
    tokens, features = normed.shape
    experts_own, _, hidden = w_gate.shape
    experts_all = gates.shape[1]
    chips, block, _ = cotangent.shape
    rows = lambda columns: pl.BlockSpec((block, columns), lambda i, p: (i, 0))
    spread = pl.BlockSpec((experts_own, block, hidden), lambda i, p: (0, i, 0))
    wide = jax.ShapeDtypeStruct((experts_own, tokens, hidden), jnp.bfloat16)
    return pl.pallas_call(
        expert_kernel,
        out_shape=(
            wide,
            wide,
            wide,
            wide,
            jax.ShapeDtypeStruct((tokens, features), jnp.bfloat16),
            jax.ShapeDtypeStruct((tokens, 128), jnp.bfloat16),
        ),
        grid_spec=pltpu.PrefetchScalarGridSpec(
            num_scalar_prefetch=1,
            grid=(chips,),
            in_specs=[
                rows(features),
                pl.BlockSpec(
                    (None, block, features), lambda i, p: (lax.rem(i - p[0] + chips, chips), 0, 0)
                ),
                pl.BlockSpec((block, 128), lambda i, p: (i, features // 128)),
                rows(experts_all),
                whole_block(*w_gate.shape),
                whole_block(*w_up.shape),
                whole_block(*w_down.shape),
            ],
            out_specs=[spread, spread, spread, spread, rows(features), rows(128)],
        ),
        compiler_params=pltpu.CompilerParams(vmem_limit_bytes=52 << 20),
        cost_estimate=pl.CostEstimate(
            flops=6 * tokens * features * hidden * experts_own,
            bytes_accessed=6 * features * hidden * experts_own + 10 * tokens * features,
            transcendentals=tokens * hidden * experts_own,
        ),
    )(place, normed, cotangent, gathered, gates, w_gate, w_up, w_down)


def product_kernel(left_ref, right_ref, scaled_ref, live_ref, out_ref):
    step = pl.program_id(0)
    tile, hidden = left_ref.shape[1], right_ref.shape[1]
    tops = pl.num_programs(0) - 3
    top = tops * tile

    @pl.when(step < tops)
    def _():
        out_ref[pl.ds(pl.multiple_of(step * tile, tile), tile), :] = dot(
            left_ref[...], right_ref[...], ROWS
        ).astype(out_ref.dtype)

    for part in range(3):

        @pl.when(step == tops + part)
        def _():
            product = dot(scaled_ref[...], live_ref[...], ROWS).astype(out_ref.dtype)
            if part < 2:
                out_ref[top : top + hidden, part * tile : (part + 1) * tile] = product
            else:
                out_ref[top + hidden :, :tile] = product[:tile]
                out_ref[top + hidden :, tile:] = product[tile:]


def expert_product(left, right, scaled, live, side, dtype):
    tokens, features = left.shape
    hidden = right.shape[1]
    tile = hidden // 2
    tops = features // tile
    return pl.pallas_call(
        product_kernel,
        out_shape=jax.ShapeDtypeStruct((features + features // 2, hidden), dtype),
        grid=(tops + 3,),
        in_specs=[
            pl.BlockSpec((tokens, tile), lambda i: (0, jnp.minimum(i, tops - 1))),
            whole_block(tokens, hidden),
            whole_block(tokens, hidden),
            pl.BlockSpec((tokens, tile), lambda i: (0, 3 * side + jnp.maximum(i - tops, 0))),
        ],
        out_specs=pl.BlockSpec((features + features // 2, hidden), lambda i: (0, 0)),
        compiler_params=pltpu.CompilerParams(vmem_limit_bytes=40 << 20),
        cost_estimate=pl.CostEstimate(
            flops=3 * tokens * features * hidden,
            bytes_accessed=4 * tokens * features,
            transcendentals=0,
        ),
    )(left, right, scaled, live)


def split_product(value):
    features = value.shape[1] * 2 // 3
    hidden = value.shape[2]
    tile = hidden // 2
    low = value[:, features:]
    down = jnp.concatenate(
        [
            low[:, :hidden],
            jnp.concatenate([low[:, hidden:, :tile], low[:, hidden:, tile:]], 1),
        ],
        2,
    )
    return value[:, :features], down


def rows_kernel(
    place_ref,
    scaled_ref,
    grad_gate_ref,
    grad_up_ref,
    extra_ref,
    gate_weight_ref,
    up_weight_ref,
    down_weight_ref,
    grad_ref,
    out_ref,
):
    experts_own = scaled_ref.shape[0]
    features = out_ref.shape[1]
    one = [slot_of(e, place_ref[2], experts_own) for e in range(experts_own)]
    two = [slot_of(e, place_ref[3], experts_own) for e in range(experts_own)]
    for start in range(0, features, 256):
        part = slice(start, start + 256)
        grad = 0.0
        out = 0.0
        for e in range(experts_own):
            grad = grad + dot(grad_gate_ref[one[e]], gate_weight_ref[e, part, :], COLUMNS)
            grad = grad + dot(grad_up_ref[two[e]], up_weight_ref[e, part, :], COLUMNS)
            out = out + dot(scaled_ref[one[e]], down_weight_ref[e, :, part])
        grad_ref[:, part] = grad.astype(jnp.bfloat16)
        out_ref[:, part] = out.astype(jnp.bfloat16)
    grad_ref[:, features:] = extra_ref[...]


def expert_sums(place, scaled, grad_gate_pre, grad_up_pre, extra, w_gate, w_up, w_down, block):
    experts_own, tokens, hidden = scaled.shape
    features = w_gate.shape[1]
    rows = lambda columns: pl.BlockSpec((block, columns), lambda i, p: (i, 0))
    spread = pl.BlockSpec((experts_own, block, hidden), lambda i, p: (0, i, 0))
    return pl.pallas_call(
        rows_kernel,
        out_shape=(
            jax.ShapeDtypeStruct((tokens, features + extra.shape[1]), jnp.bfloat16),
            jax.ShapeDtypeStruct((tokens, features), jnp.bfloat16),
        ),
        grid_spec=pltpu.PrefetchScalarGridSpec(
            num_scalar_prefetch=1,
            grid=(tokens // block,),
            in_specs=[
                spread,
                spread,
                spread,
                rows(extra.shape[1]),
                whole_block(*w_gate.shape),
                whole_block(*w_up.shape),
                whole_block(*w_down.shape),
            ],
            out_specs=[rows(features + extra.shape[1]), rows(features)],
        ),
        compiler_params=pltpu.CompilerParams(vmem_limit_bytes=52 << 20),
        cost_estimate=pl.CostEstimate(flops=0, bytes_accessed=tokens, transcendentals=0),
    )(place, scaled, grad_gate_pre, grad_up_pre, extra, w_gate, w_up, w_down)


def turn_kernel(
    sum_ref,
    gates_ref,
    router_ref,
    gain_ref,
    middle_ref,
    live_ref,
    low_ref,
    high_ref,
    grad_middle_ref,
    branch_ref,
    mixed_ref,
    logits_ref,
    gain_grad_ref,
):
    features = middle_ref.shape[1]
    experts = gates_ref.shape[1]
    groups, _, width = mixed_ref.shape
    extra = sum_ref[:, features:].astype(jnp.float32)
    grad_gates = extra[:, :experts] + extra[:, experts : 2 * experts]
    gates = gates_ref[...]
    grad_logits = gates * (grad_gates - jnp.sum(gates * grad_gates, -1, keepdims=True))
    grad_logits = grad_logits.astype(jnp.bfloat16)
    logits_ref[...] = grad_logits
    grad = sum_ref[:, :features].astype(jnp.float32) + dot(grad_logits, router_ref[...], COLUMNS)
    middle = middle_ref[...]
    scale = lax.rsqrt(jnp.mean(middle * middle, -1, keepdims=True) + EPS)
    base = middle * scale
    gain_grad_ref[...] = jnp.sum(grad * base, 0, keepdims=True)
    grad_middle = live_ref[...].astype(jnp.float32) + norm_back(grad * gain_ref[...], base, scale)
    grad_middle_ref[...] = grad_middle
    branch = grad_middle.astype(jnp.bfloat16)
    branch_ref[...] = branch
    for half, weight_ref in enumerate((low_ref, high_ref)):
        mixed = dot(branch, weight_ref[...], COLUMNS).astype(jnp.bfloat16)
        for g in range(groups // 2):
            mixed_ref[half * (groups // 2) + g] = mixed[:, g * width : (g + 1) * width]


def turn_rows(sums, gates, router, gain, middle, live, weights):
    own, features = middle.shape
    experts = gates.shape[1]
    groups = KEY_VALUE_HEADS
    shaped = jax.ShapeDtypeStruct
    return pl.pallas_call(
        turn_kernel,
        out_shape=(
            shaped((own, features), jnp.float32),
            shaped((own, features), jnp.bfloat16),
            shaped((groups, own, features // groups), jnp.bfloat16),
            shaped((own, experts), jnp.bfloat16),
            shaped((1, features), jnp.float32),
        ),
        compiler_params=pltpu.CompilerParams(vmem_limit_bytes=32 << 20),
        cost_estimate=pl.CostEstimate(flops=0, bytes_accessed=own, transcendentals=0),
    )(sums, gates, router, gain[None, :], middle, live, *weights)


def close_kernel(
    query_ref, pair_ref, weight_ref, hidden_ref, normed_ref, grad_ref, product_ref, gain_grad_ref
):
    step = pl.program_id(0)
    width = query_ref.shape[1]
    both = width + pair_ref.shape[1]
    query = query_ref[...]
    pair = pair_ref[...]
    grad = dot(query, weight_ref[:, :width], COLUMNS) + dot(
        pair, weight_ref[:, width:both], COLUMNS
    )
    grad_ref[...] = grad.astype(jnp.bfloat16)
    hidden = hidden_ref[...].astype(jnp.float32)
    scale = lax.rsqrt(jnp.mean(hidden * hidden, -1, keepdims=True) + EPS)
    gain_grad = jnp.sum(grad * (hidden * scale), 0, keepdims=True)
    normed = normed_ref[...]

    @pl.when(step == 0)
    def _():
        gain_grad_ref[...] = jnp.zeros_like(gain_grad_ref)
        product_ref[...] = jnp.zeros_like(product_ref)

    gain_grad_ref[...] += gain_grad
    product_ref[:, :width] += dot(normed, query, ROWS)
    product_ref[:, width:] += dot(normed, pair, ROWS)


def close_rows(query, pair, weight, gathered, normed, block):
    tokens, features = normed.shape
    both = query.shape[1] + pair.shape[1]
    rows = lambda width: pl.BlockSpec((block, width), lambda i: (i, 0))
    resident = lambda *shape: pl.BlockSpec(shape, lambda i: (0,) * len(shape))
    shaped = jax.ShapeDtypeStruct
    return pl.pallas_call(
        close_kernel,
        out_shape=(
            shaped((tokens, features), jnp.bfloat16),
            shaped((features, both), jnp.float32),
            shaped((1, features), jnp.float32),
        ),
        grid=(tokens // block,),
        in_specs=[
            rows(query.shape[1]),
            rows(pair.shape[1]),
            whole_block(*weight.shape),
            rows(features),
            rows(features),
        ],
        out_specs=[rows(features), resident(features, both), resident(1, features)],
        compiler_params=pltpu.CompilerParams(vmem_limit_bytes=40 << 20),
        cost_estimate=pl.CostEstimate(flops=0, bytes_accessed=tokens, transcendentals=0),
    )(query, pair, weight, gathered, normed)


def after(values, *others):
    values, _ = lax.optimization_barrier((values, others))
    return values


def swap(value, bit):
    size = lax.axis_size("rep")
    return lax.ppermute(value, "rep", [(i, i ^ bit) for i in range(size)])


def has(bit):
    return (lax.axis_index("rep") & bit) != 0


def halve(value, came, bit):
    half = value.shape[0] // 2
    keep = jnp.where(has(bit), half, 0)
    part = lambda array, start: lax.dynamic_slice_in_dim(array, start, half, 0).astype(jnp.float32)
    kept = part(value, keep)
    sent = part(value, half - keep)
    if came is not None:
        kept = kept + part(came, keep)
        sent = sent + part(came, half - keep)
    return kept, sent.astype(jnp.bfloat16)


def join(value, came, bit, axis):
    upper = has(bit)
    return jnp.concatenate(
        [jnp.where(upper, came, value), jnp.where(upper, value, came)], axis
    )


class Chain:
    def __init__(self, order):
        self.order = order
        self.stage = 0
        self.steps = 2 * len(order)

    def send(self, sent):
        bit = self.order[min(self.stage, self.steps - 1 - self.stage)]
        self.sent = sent
        self.flying = swap(sent, bit)
        self.stage += 1

    def start(self, value):
        self.kept, sent = halve(value, None, self.order[0])
        self.send(sent)
        return self.sent

    def total(self, *others):
        return self.kept + after(self.flying, *others).astype(jnp.float32)

    def step(self, *others):
        bits = len(self.order)
        if self.stage < bits:
            came = after(self.flying, *others)
            self.kept, sent = halve(self.kept, came, self.order[self.stage])
            self.send(sent)
        elif self.stage == bits:
            self.send(self.total(*others).astype(jnp.bfloat16))
        else:
            came = after(self.flying, *others)
            self.send(join(self.sent, came, self.order[self.steps - self.stage], 0))
        return self.sent

    def finish(self, *others):
        return join(self.sent, after(self.flying, *others), self.order[0], 0)


class Exchange:
    def __init__(self, fetched, bits):
        size = fetched.shape[0]
        fetched = fetched.reshape((size,) + (1,) * len(bits) + fetched.shape[1:])
        self.values = [fetched[: size // 2], fetched[size // 2 :]]
        self.orders = (bits, bits[::-1])
        self.stage = 0
        self.fly()

    def fly(self):
        self.flying = [
            swap(value, order[self.stage]) for value, order in zip(self.values, self.orders)
        ]

    def step(self, *others):
        bits = len(self.orders[0])
        for h, order in enumerate(self.orders):
            bit = order[self.stage]
            came = after(self.flying[h], *others)
            self.values[h] = join(self.values[h], came, bit, bits - (bit.bit_length() - 1))
        self.stage += 1
        if self.stage < bits:
            self.fly()
        return list(self.values)

    def finish(self, *others):
        while self.stage < len(self.orders[0]):
            self.step(*others)
        return [value.reshape(-1, value.shape[-1]) for value in self.values]


def per_device(
    inputs,
    segments,
    positions,
    expert_ids,
    attn_gain,
    w_query,
    key_weight,
    value_weight,
    w_out,
    ffn_gain,
    router,
    w_gate,
    w_up,
    w_down,
    grad_out,
):
    size = lax.axis_size("ctx")
    me = lax.axis_index("ctx")
    reps = lax.axis_size("rep")
    bits = [1 << i for i in range(reps.bit_length() - 1)]
    own = inputs.shape[1]
    tokens = size * own
    groups = KEY_VALUE_HEADS
    copies = size // groups
    query_width = HEAD_GROUP * HEAD_SIZE
    width = query_width + 2 * HEAD_SIZE
    copy_index = me % copies
    rows_own = w_out.shape[0]
    experts_own = w_gate.shape[0]
    experts_all = size * experts_own
    block = 2 * own
    chips = size // 2
    chip = me // 2
    odd = me % 2 == 1
    share = rows_own // reps
    share_start = lax.axis_index("rep") * share

    columns = jnp.concatenate(
        [
            segments[0][:, None],
            positions[0][:, None] // 64,
            positions[0][:, None] % 64,
            expert_ids[0],
        ],
        1,
    ).astype(jnp.bfloat16)
    columns = jnp.pad(columns, ((0, 0), (0, 128 - columns.shape[1])))
    gathered = lax.all_gather(
        jnp.concatenate([inputs[0], columns], 1), "ctx", axis=0, tiled=True
    )

    def from_chip(value, k):
        return lax.ppermute(value, "ctx", [(i, (i - 2 * k) % size) for i in range(size)])

    def from_core(value):
        return lax.ppermute(value, "ctx", [(i, i ^ 1) for i in range(size)])

    def cores(mine, others, axis):
        return jnp.concatenate(
            [jnp.where(odd, others, mine), jnp.where(odd, mine, others)], axis
        )

    shared = lambda array: lax.dynamic_slice_in_dim(array, share_start, share, 0)
    side_width = -(-(width + 2 + router.shape[1]) // 128) * 128
    head_columns = jnp.concatenate(
        [
            shared(w_query).reshape(share, groups, query_width),
            shared(key_weight).reshape(share, groups, HEAD_SIZE),
            shared(value_weight).reshape(share, groups, HEAD_SIZE),
            jnp.broadcast_to(shared(attn_gain)[:, None, None], (share, groups, 1)),
            jnp.broadcast_to(shared(ffn_gain)[:, None, None], (share, groups, 1)),
            jnp.broadcast_to(shared(router)[:, None, :], (share, groups, router.shape[1])),
        ],
        -1,
    )
    used = head_columns.shape[-1]
    head_columns = jnp.pad(head_columns, ((0, 0), (0, 0), (0, side_width - used)))
    head_columns = jnp.repeat(jnp.transpose(head_columns, (1, 0, 2)), copies, 0)
    head_columns = head_columns.reshape(chips, 2, share, side_width)
    out_share = shared(w_out)
    parcels = []
    for k in range(chips):
        to = head_columns[(chip - k) % chips]
        parcel = jnp.concatenate([out_share, to[0], to[1]], 1)
        parcels.append(from_chip(parcel, k) if k else parcel)
    parcels = jnp.stack(parcels)
    out_part = parcels[:, :, :MODEL_WIDTH]
    heads = [
        parcels[:, :, MODEL_WIDTH : MODEL_WIDTH + side_width],
        parcels[:, :, MODEL_WIDTH + side_width :],
    ]
    for_core = jnp.where(odd, heads[0], heads[1])
    mine_part = jnp.concatenate([out_part, jnp.where(odd, heads[1], heads[0])], 2)
    core_part = from_core(jnp.concatenate([out_part, for_core], 2))
    fetched = cores(mine_part[:, None], core_part[:, None], 1)
    fetched = lax.dynamic_slice_in_dim(
        jnp.concatenate([fetched, fetched], 0), (chips - chip) % chips, chips, 0
    ).reshape(size, share, MODEL_WIDTH + side_width)
    head_exchange = Exchange(fetched[:, :, MODEL_WIDTH:], bits)
    out_exchange = Exchange(fetched[:, :, :MODEL_WIDTH], bits)
    head_halves = head_exchange.finish()
    ready = out_exchange.step(*head_halves)
    head_all = jnp.concatenate(head_halves, 0)
    gain_one = head_all[:, width].astype(jnp.float32)
    gain_two = head_all[:, width + 1].astype(jnp.float32)
    router_all = head_all[:, width + 2 : used]

    (
        normed_one,
        query,
        key,
        value,
        mixed,
        log_total,
        cosine_table,
        sine_table,
        segment_rows,
    ) = attend(after(gathered, *ready), gain_one, head_halves, block)

    turned = after(grad_out[0], gathered, *ready)
    turned = jnp.stack([turned] + [from_chip(turned, k) for k in range(1, chips)])
    part = tokens // copies
    mixed_all = lax.all_gather(
        lax.dynamic_slice_in_dim(mixed, copy_index * part, part, 0), "ctx", axis=0
    ).reshape(groups, tokens, query_width)
    w_out_halves = out_exchange.finish(mixed)
    cotangent = cores(turned, from_core(turned), 1)

    middle, normed_two, gates = middle_rows(
        mixed_all, after(w_out_halves, cotangent), gathered, gain_two, router_all, block
    )
    flag = lambda bit: has(bit).astype(jnp.int32)
    place = jnp.stack([chip, me, flag(bits[0]), flag(bits[-1])]).astype(jnp.int32)
    scaled_one, scaled_two, grad_gate_pre, grad_up_pre, grad_live, extra = expert_rows(
        place, normed_two, cotangent, gathered, gates, w_gate, w_up, w_down
    )

    pick = experts_own // 2

    def product(side, start, dtype):
        right, scaled = ((grad_gate_pre, scaled_one), (grad_up_pre, scaled_two))[side]
        parts = [
            expert_product(normed_two, right[e], scaled[e], grad_live, side, dtype)
            for e in range(start, start + pick)
        ]
        return parts[0] if pick == 1 else jnp.concatenate(parts, 0)

    chains = [Chain(bits), Chain(bits[::-1])]
    for side, chain in enumerate(chains):
        chain.send(product(side, 0, jnp.bfloat16))
    grad_rows, out_rows = expert_sums(
        place,
        *after((scaled_one, grad_gate_pre, grad_up_pre), *[chain.sent for chain in chains]),
        extra,
        w_gate,
        w_up,
        w_down,
        block,
    )
    grad_two_sum = lax.psum_scatter(grad_rows, "ctx", scatter_dimension=0, tiled=True)
    scaled_one, scaled_two, grad_gate_pre, grad_up_pre = after(
        (scaled_one, scaled_two, grad_gate_pre, grad_up_pre), grad_rows
    )
    for side, chain in enumerate(chains):
        chain.kept = product(side, pick, jnp.float32)

    def mine(array):
        return lax.dynamic_slice_in_dim(array, me * own, own, 0)

    sent = [c.kept for c in chains]
    while chains[0].stage < len(bits):
        sent = [chain.step(*sent) for chain in chains]
    middle_own, gates_own, live_own = mine(middle), mine(gates), mine(grad_live)
    grad_middle, grad_branch, grad_mixed, grad_logits, gain_two_grad = turn_rows(
        after(grad_two_sum, *sent),
        gates_own,
        router_all,
        gain_two,
        middle_own,
        live_own,
        w_out_halves,
    )
    grad_mixed_all = lax.all_to_all(
        jnp.repeat(grad_mixed, copies, 0), "ctx", split_axis=0, concat_axis=0, tiled=True
    ).reshape(tokens, query_width)
    grad_branch_all = lax.all_gather(grad_branch, "ctx", axis=0, tiled=True)

    sent = [chain.step(grad_mixed) for chain in chains]
    grad_query, grad_pair = attend_back(
        query,
        after(grad_mixed_all, *sent),
        log_total,
        cosine_table,
        sine_table,
        gathered,
        segment_rows,
        key,
        value,
    )
    if copies > 1:
        places = jnp.arange(tokens, dtype=jnp.int32)
        counted = (places // part == copy_index)[:, None]
        grad_query = jnp.where(counted, grad_query, jnp.zeros((), jnp.bfloat16))
        grad_pair = jnp.where(counted, grad_pair, jnp.zeros((), jnp.bfloat16))
    grad_one_low, head_product, gain_one_grad = close_rows(
        grad_query, grad_pair, head_all, gathered, normed_one, block
    )
    grad_one = lax.psum_scatter(
        grad_one_low, "ctx", scatter_dimension=0, tiled=True
    ).astype(jnp.float32)
    head_grads = jnp.concatenate(
        [
            head_product,
            gain_one_grad.reshape(-1, 1),
            gain_two_grad.reshape(-1, 1),
            dot(mine(normed_two), grad_logits, ROWS),
        ],
        1,
    )

    spread = head_grads.reshape((size,) + (2,) * len(bits) + (share, used))
    axes = list(range(1, len(bits) + 1))
    head_chains = [Chain(bits), Chain(bits[::-1])]
    sent = []
    for h, chain in enumerate(head_chains):
        part_grads = spread[h * (size // 2) : (h + 1) * (size // 2)]
        lead = axes[::-1] if h == 0 else axes
        part_grads = jnp.transpose(part_grads, lead + [0, len(bits) + 1, len(bits) + 2])
        sent.append(chain.start(part_grads.reshape(-1, used)))

    sent = [chain.step(*sent) for chain in chains]
    grad_proj_out = dot(
        lax.dynamic_slice_in_dim(mixed, copy_index * rows_own, rows_own, 1),
        after(grad_branch_all, *sent),
        ROWS,
    )
    while head_chains[0].stage < len(bits):
        sent = [chain.step(*sent) for chain in head_chains]
    totals = [chain.total(*sent) for chain in head_chains]
    totals = jnp.concatenate(
        [total.reshape(size // 2, share, used) for total in totals], 0
    ).astype(jnp.bfloat16)
    head_sums = lax.all_to_all(totals, "ctx", split_axis=0, concat_axis=0, tiled=True)
    out_chain = Chain(bits[::-1])
    out_sent = out_chain.start(after(grad_proj_out, totals))
    while out_chain.stage < len(bits):
        out_sent = out_chain.step(out_sent)
    back = Exchange(after(head_sums, out_sent), bits)
    out_chain.step(*back.values)
    while out_chain.stage < out_chain.steps:
        ready = back.step(out_chain.sent) if back.stage < len(bits) - 1 else []
        out_chain.step(*ready)
    halves = back.finish(out_chain.sent)
    head_rows = jnp.concatenate(halves, 0).reshape(size, rows_own, used).astype(jnp.float32)
    if copies > 1:
        head_rows = jnp.sum(head_rows.reshape(groups, copies, rows_own, used), 1)
    side = lambda begin, end: jnp.transpose(head_rows[:, :, begin:end], (1, 0, 2)).reshape(
        rows_own, -1
    )
    small = jnp.sum(head_rows[:, :, width:], 0)
    head_outs = (
        side(0, query_width),
        side(query_width, query_width + HEAD_SIZE),
        side(query_width + HEAD_SIZE, width),
    )
    grad_out_rows = out_chain.finish(*head_outs).astype(jnp.float32)
    while chains[0].stage < chains[0].steps:
        sent = [chain.step(grad_out_rows) for chain in chains]
    expert_parts = []
    for chain in chains:
        value = chain.finish(grad_out_rows, *head_outs)
        expert_parts.append(split_product(value.reshape(experts_own, -1, value.shape[1])))
    grad_gate, grad_up = [parts[0].astype(jnp.float32) for parts in expert_parts]
    grad_down = jnp.concatenate([parts[1] for parts in expert_parts], 2).astype(jnp.float32)

    moe_sum = lax.psum_scatter(
        after(out_rows, grad_branch), "ctx", scatter_dimension=0, tiled=True
    ).astype(jnp.float32)
    output = jnp.where((segments[0] != 0)[:, None], middle_own + moe_sum, 0.0)
    own_hidden = inputs[0].astype(jnp.float32)
    own_scale = lax.rsqrt(jnp.mean(own_hidden * own_hidden, -1, keepdims=True) + EPS)
    grad_in = grad_middle + norm_back(grad_one * gain_one, own_hidden * own_scale, own_scale)

    return (
        output.astype(jnp.bfloat16)[None],
        grad_in[None],
        small[:, 0],
        *head_outs,
        grad_out_rows,
        small[:, 1],
        small[:, 2:],
        grad_gate,
        grad_up,
        grad_down,
    )


def solution(mesh):
    return jax.shard_map(
        per_device,
        mesh=mesh,
        in_specs=(
            P("rep", "ctx", None),
            P("rep", "ctx"),
            P("rep", "ctx"),
            P("rep", "ctx", None),
            P("ctx"),
            P("ctx", None),
            P("ctx", None),
            P("ctx", None),
            P("ctx", None),
            P("ctx"),
            P("ctx", None),
            P("ctx", None, None),
            P("ctx", None, None),
            P("ctx", None, None),
            P("rep", "ctx", None),
        ),
        out_specs=(
            P("rep", "ctx", None),
            P("rep", "ctx", None),
            P("ctx"),
            P("ctx", None),
            P("ctx", None),
            P("ctx", None),
            P("ctx", None),
            P("ctx"),
            P("ctx", None),
            P("ctx", None, None),
            P("ctx", None, None),
            P("ctx", None, None),
        ),
        check_vma=False,
    )
```

```python
import jax
import jax.numpy as jnp
from jax import lax
from jax.experimental import pallas as pl
from jax.experimental.pallas import tpu as pltpu
from jax.sharding import PartitionSpec as P

MODEL_WIDTH = 1536
QUERY_HEADS = 24
KEY_VALUE_HEADS = 8
HEAD_GROUP = QUERY_HEADS // KEY_VALUE_HEADS
HEAD_SIZE = 64
TOPK = 8

EPS = 1e-06
THETA = 10000.0
MASK_FLOOR = -1e30

ROWS = (((0,), (0,)), ((), ()))
COLUMNS = (((1,), (1,)), ((), ()))


def dot(left, right, contract=(((1,), (0,)), ((), ()))):
    return lax.dot_general(left, right, contract, preferred_element_type=jnp.float32)


def norm_back(grad_base, base, scale):
    return scale * (grad_base - base * jnp.mean(grad_base * base, -1, keepdims=True))


def turn(rows):
    half = HEAD_SIZE // 2
    return jnp.concatenate([-rows[:, half:], rows[:, :half]], 1)


def turn_back(rows):
    half = HEAD_SIZE // 2
    return jnp.concatenate([rows[:, half:], -rows[:, :half]], 1)


def stack_heads(rows):
    return jnp.concatenate(
        [rows[:, h * HEAD_SIZE : (h + 1) * HEAD_SIZE] for h in range(HEAD_GROUP)], 0
    )


def side_heads(rows):
    block = rows.shape[0] // HEAD_GROUP
    return jnp.concatenate([rows[h * block : (h + 1) * block] for h in range(HEAD_GROUP)], 1)


def lanes(values, combine):
    total = values[:, :128]
    for start in range(128, values.shape[1], 128):
        total = combine(total, values[:, start : start + 128])
    return total


def masked_scores(stacked, keys, row_segments, key_segments, row_start, key_start):
    block = row_segments.shape[0]
    scores = dot(stacked, keys, COLUMNS) * HEAD_SIZE ** (-0.5)
    row_place = row_start + lax.broadcasted_iota(jnp.int32, (block, block), 0)
    key_place = key_start + lax.broadcasted_iota(jnp.int32, (block, block), 1)
    allowed = (row_segments == key_segments) & (key_place <= row_place)
    scores = scores.reshape(HEAD_GROUP, block, block)
    return jnp.where(allowed[None], scores, MASK_FLOOR).reshape(HEAD_GROUP * block, block)


def first_block(row_segments, segment_ref, step):
    here = jnp.max(row_segments[:1, :1])
    segments = segment_ref[...]
    number = lax.broadcasted_iota(jnp.int32, segments.shape, 0)
    return jnp.min(jnp.where((segments == here) & (number <= step), number, step))


def whole_block(*shape, grid=1, prefetch=0):
    return pl.BlockSpec(shape, lambda *i: (0,) * len(shape), pipeline_mode=pl.Buffered(1))


def attend_kernel(
    hidden_ref,
    column_ref,
    gain_ref,
    low_ref,
    high_ref,
    rate_ref,
    normed_ref,
    query_ref,
    key_ref,
    value_ref,
    mixed_ref,
    log_ref,
    cosine_ref,
    sine_ref,
    segment_ref,
    score_ref,
):
    step = pl.program_id(0)
    block = hidden_ref.shape[0]
    query_width = query_ref.shape[1]
    width = query_width + 2 * HEAD_SIZE
    here = pl.ds(pl.multiple_of(step * block, block), block)
    columns = column_ref[...].astype(jnp.float32)
    row_segments = columns[:, :1]
    segment_ref[step] = jnp.transpose(columns)[:1, :]
    angles = (columns[:, 1:2] * 64.0 + columns[:, 2:3]) * rate_ref[...]
    cosine = jnp.cos(angles)
    sine = jnp.sin(angles)
    cosine_ref[...] = cosine
    sine_ref[...] = sine
    hidden = hidden_ref[...].astype(jnp.float32)
    scale = lax.rsqrt(jnp.mean(hidden * hidden, -1, keepdims=True) + EPS)
    normed = (hidden * scale * gain_ref[...]).astype(jnp.bfloat16)
    normed_ref[...] = normed
    middle = low_ref.shape[0]
    raw = dot(normed[:, :middle], low_ref[:, :width]) + dot(
        normed[:, middle:], high_ref[:, :width]
    )
    key_raw = raw[:, query_width : query_width + HEAD_SIZE]
    key_ref[here, :] = (key_raw * cosine + turn(key_raw) * sine).astype(jnp.bfloat16)
    value_ref[here, :] = raw[:, query_width + HEAD_SIZE :].astype(jnp.bfloat16)
    query_raw = stack_heads(raw[:, :query_width])
    cosine = jnp.concatenate([cosine] * HEAD_GROUP, 0)
    sine = jnp.concatenate([sine] * HEAD_GROUP, 0)
    query = (query_raw * cosine + turn(query_raw) * sine).astype(jnp.bfloat16)
    query_ref[...] = side_heads(query)
    rows = HEAD_GROUP * block
    first = first_block(row_segments, segment_ref, step)

    def first_pass(index, top):
        there = pl.ds(pl.multiple_of(index * block, block), block)
        scores = masked_scores(
            query,
            key_ref[there, :],
            row_segments,
            segment_ref[index],
            step * block,
            index * block,
        )
        score_ref[index] = scores
        return jnp.maximum(top, lanes(scores, jnp.maximum))

    top = lax.fori_loop(
        first, step + 1, first_pass, jnp.full((rows, 128), MASK_FLOOR, jnp.float32)
    )
    top = jnp.max(top, -1, keepdims=True)

    def second_pass(index, carry):
        total, mixed = carry
        there = pl.ds(pl.multiple_of(index * block, block), block)
        weights = jnp.exp(score_ref[index] - top)
        mixed = mixed + dot(weights.astype(jnp.bfloat16), value_ref[there, :])
        return total + lanes(weights, jnp.add), mixed

    total, mixed = lax.fori_loop(
        first,
        step + 1,
        second_pass,
        (
            jnp.zeros((rows, 128), jnp.float32),
            jnp.zeros((rows, HEAD_SIZE), jnp.float32),
        ),
    )
    total = jnp.sum(total, -1, keepdims=True)
    mixed_ref[...] = side_heads((mixed / total).astype(jnp.bfloat16))
    log_ref[...] = (top + jnp.log(total)).reshape(HEAD_GROUP, block, 1)


def attend(gathered, gain, weights, block):
    tokens, features = gathered.shape[0], gain.shape[0]
    query_width = HEAD_GROUP * HEAD_SIZE
    steps = tokens // block
    half = jnp.arange(HEAD_SIZE // 2, dtype=jnp.float32)
    rate = THETA ** (-(2.0 * half) / HEAD_SIZE)
    rate = jnp.concatenate([rate, rate])[None, :]
    rows = lambda width: pl.BlockSpec((block, width), lambda i: (i, 0))
    resident = lambda *shape: pl.BlockSpec(shape, lambda i: (0,) * len(shape))
    shaped = jax.ShapeDtypeStruct
    return pl.pallas_call(
        attend_kernel,
        out_shape=(
            shaped((tokens, features), jnp.bfloat16),
            shaped((tokens, query_width), jnp.bfloat16),
            shaped((tokens, HEAD_SIZE), jnp.bfloat16),
            shaped((tokens, HEAD_SIZE), jnp.bfloat16),
            shaped((tokens, query_width), jnp.bfloat16),
            shaped((HEAD_GROUP, tokens, 1), jnp.float32),
            shaped((tokens, HEAD_SIZE), jnp.float32),
            shaped((tokens, HEAD_SIZE), jnp.float32),
            shaped((steps, 1, block), jnp.float32),
        ),
        grid=(steps,),
        in_specs=[
            rows(features),
            pl.BlockSpec((block, 128), lambda i: (i, features // 128)),
            whole_block(1, features),
            whole_block(*weights[0].shape),
            whole_block(*weights[1].shape),
            whole_block(1, HEAD_SIZE),
        ],
        out_specs=[
            rows(features),
            rows(query_width),
            resident(tokens, HEAD_SIZE),
            resident(tokens, HEAD_SIZE),
            rows(query_width),
            pl.BlockSpec((HEAD_GROUP, block, 1), lambda i: (0, i, 0)),
            rows(HEAD_SIZE),
            rows(HEAD_SIZE),
            resident(steps, 1, block),
        ],
        scratch_shapes=[pltpu.VMEM((steps, HEAD_GROUP * block, block), jnp.float32)],
        compiler_params=pltpu.CompilerParams(vmem_limit_bytes=48 << 20),
        cost_estimate=pl.CostEstimate(flops=0, bytes_accessed=tokens, transcendentals=0),
    )(gathered, gathered, gain[None, :], *weights, rate)


def attend_back_kernel(
    query_ref,
    grad_ref,
    log_ref,
    cosine_ref,
    sine_ref,
    column_ref,
    segment_ref,
    key_ref,
    value_ref,
    key_cosine_ref,
    key_sine_ref,
    grad_query_ref,
    grad_pair_ref,
    probs_ref,
    grad_probs_ref,
    grad_key_ref,
    grad_value_ref,
):
    step = pl.program_id(0)
    block = query_ref.shape[0]
    rows = HEAD_GROUP * block

    @pl.when(step == 0)
    def _():
        grad_key_ref[...] = jnp.zeros_like(grad_key_ref)
        grad_value_ref[...] = jnp.zeros_like(grad_value_ref)

    query = stack_heads(query_ref[...])
    grad = stack_heads(grad_ref[...])
    log_total = log_ref[...].reshape(rows, 1)
    row_segments = column_ref[...].astype(jnp.float32)[:, :1]
    first = first_block(row_segments, segment_ref, step)

    def first_pass(index, delta):
        there = pl.ds(pl.multiple_of(index * block, block), block)
        scores = masked_scores(
            query,
            key_ref[there, :],
            row_segments,
            segment_ref[index],
            step * block,
            index * block,
        )
        probs = jnp.exp(scores - log_total)
        grad_probs = dot(grad, value_ref[there, :], COLUMNS)
        probs_ref[index] = probs
        grad_probs_ref[index] = grad_probs
        grad_value_ref[there, :] += dot(probs.astype(jnp.bfloat16), grad, ROWS)
        return delta + lanes(probs * grad_probs, jnp.add)

    delta = lax.fori_loop(first, step + 1, first_pass, jnp.zeros((rows, 128), jnp.float32))
    delta = jnp.sum(delta, -1, keepdims=True)

    def second_pass(index, grad_query):
        there = pl.ds(pl.multiple_of(index * block, block), block)
        grad_scores = (probs_ref[index] * (grad_probs_ref[index] - delta)).astype(jnp.bfloat16)
        grad_key_ref[there, :] += dot(grad_scores, query, ROWS)
        return grad_query + dot(grad_scores, key_ref[there, :])

    grad_query = lax.fori_loop(
        first, step + 1, second_pass, jnp.zeros((rows, HEAD_SIZE), jnp.float32)
    )
    score_scale = HEAD_SIZE ** (-0.5)
    cosine = jnp.concatenate([cosine_ref[...]] * HEAD_GROUP, 0)
    sine = jnp.concatenate([sine_ref[...]] * HEAD_GROUP, 0)
    grad_query = grad_query * score_scale
    grad_query = grad_query * cosine + turn_back(grad_query * sine)
    grad_query_ref[...] = side_heads(grad_query.astype(jnp.bfloat16))

    @pl.when(step == pl.num_programs(0) - 1)
    def _():
        grad_key = grad_key_ref[...] * score_scale
        grad_key = grad_key * key_cosine_ref[...] + turn_back(grad_key * key_sine_ref[...])
        grad_pair_ref[...] = jnp.concatenate([grad_key, grad_value_ref[...]], 1).astype(
            jnp.bfloat16
        )


def attend_back(query, grad, log_total, cosine, sine, gathered, segments, key, value):
    tokens, query_width = query.shape
    steps, _, block = segments.shape
    features = gathered.shape[1] - 128
    rows = lambda width: pl.BlockSpec((block, width), lambda i: (i, 0))
    resident = lambda *shape: pl.BlockSpec(shape, lambda i: (0,) * len(shape))
    return pl.pallas_call(
        attend_back_kernel,
        out_shape=(
            jax.ShapeDtypeStruct((tokens, query_width), jnp.bfloat16),
            jax.ShapeDtypeStruct((tokens, 2 * HEAD_SIZE), jnp.bfloat16),
        ),
        grid=(steps,),
        in_specs=[
            rows(query_width),
            rows(query_width),
            pl.BlockSpec((HEAD_GROUP, block, 1), lambda i: (0, i, 0)),
            rows(HEAD_SIZE),
            rows(HEAD_SIZE),
            pl.BlockSpec((block, 128), lambda i: (i, features // 128)),
            whole_block(steps, 1, block),
            whole_block(tokens, HEAD_SIZE),
            whole_block(tokens, HEAD_SIZE),
            whole_block(tokens, HEAD_SIZE),
            whole_block(tokens, HEAD_SIZE),
        ],
        out_specs=[rows(query_width), resident(tokens, 2 * HEAD_SIZE)],
        scratch_shapes=[
            pltpu.VMEM((steps, HEAD_GROUP * block, block), jnp.float32),
            pltpu.VMEM((steps, HEAD_GROUP * block, block), jnp.float32),
            pltpu.VMEM((tokens, HEAD_SIZE), jnp.float32),
            pltpu.VMEM((tokens, HEAD_SIZE), jnp.float32),
        ],
        compiler_params=pltpu.CompilerParams(vmem_limit_bytes=48 << 20),
        cost_estimate=pl.CostEstimate(flops=0, bytes_accessed=tokens, transcendentals=0),
    )(query, grad, log_total, cosine, sine, gathered, segments, key, value, cosine, sine)


def middle_kernel(
    mixed_ref,
    low_ref,
    high_ref,
    hidden_ref,
    column_ref,
    gain_ref,
    router_ref,
    middle_ref,
    normed_ref,
    gates_ref,
):
    groups = mixed_ref.shape[0]
    mixed = jnp.concatenate([mixed_ref[g] for g in range(groups)], 1)
    half = low_ref.shape[0]
    middle = dot(mixed[:, :half], low_ref[...]) + dot(mixed[:, half:], high_ref[...])
    middle = hidden_ref[...].astype(jnp.float32) + middle
    middle_ref[...] = middle
    scale = lax.rsqrt(jnp.mean(middle * middle, -1, keepdims=True) + EPS)
    normed = (middle * scale * gain_ref[...]).astype(jnp.bfloat16)
    normed_ref[...] = normed
    logits = dot(normed, router_ref[...])
    columns = column_ref[...].astype(jnp.float32)
    number = lax.broadcasted_iota(jnp.int32, logits.shape, 1).astype(jnp.float32)
    named = columns[:, 3:4] == number
    for slot in range(1, TOPK):
        named = named | (columns[:, 3 + slot : 4 + slot] == number)
    logits = jnp.where(named, logits, MASK_FLOOR)
    shifted = jnp.exp(logits - jnp.max(logits, -1, keepdims=True))
    shifted = jnp.where(named, shifted, 0.0)
    gates_ref[...] = shifted / jnp.sum(shifted, -1, keepdims=True)


def middle_rows(mixed, weights, gathered, gain, router, block):
    groups, tokens, width = mixed.shape
    features = gain.shape[0]
    experts = router.shape[1]
    rows = lambda columns: pl.BlockSpec((block, columns), lambda i: (i, 0))
    return pl.pallas_call(
        middle_kernel,
        out_shape=(
            jax.ShapeDtypeStruct((tokens, features), jnp.float32),
            jax.ShapeDtypeStruct((tokens, features), jnp.bfloat16),
            jax.ShapeDtypeStruct((tokens, experts), jnp.float32),
        ),
        grid=(tokens // block,),
        in_specs=[
            pl.BlockSpec((groups, block, width), lambda i: (0, i, 0)),
            whole_block(*weights[0].shape),
            whole_block(*weights[1].shape),
            rows(features),
            pl.BlockSpec((block, 128), lambda i: (i, features // 128)),
            whole_block(1, features),
            whole_block(features, experts),
        ],
        out_specs=[rows(features), rows(features), rows(experts)],
        compiler_params=pltpu.CompilerParams(vmem_limit_bytes=48 << 20),
        cost_estimate=pl.CostEstimate(
            flops=2 * tokens * features * groups * width,
            bytes_accessed=12 * tokens * features,
            transcendentals=0,
        ),
    )(mixed, *weights, gathered, gathered, gain[None, :], router)


def slot_of(e, keeps, experts_own):
    pick = experts_own // 2
    high, low = e // pick, e % pick
    return (1 - (high ^ keeps)) * pick + low


def expert_kernel(
    place_ref,
    normed_ref,
    cotangent_ref,
    column_ref,
    gates_ref,
    gate_weight_ref,
    up_weight_ref,
    down_weight_ref,
    scaled_one_ref,
    scaled_two_ref,
    grad_gate_ref,
    grad_up_ref,
    grad_live_ref,
    extra_ref,
):
    experts_own = gate_weight_ref.shape[0]
    experts_all = gates_ref.shape[1]
    first = place_ref[1] * experts_own
    normed = normed_ref[...]
    live = column_ref[...].astype(jnp.float32)[:, :1] > 0
    grad_live = jnp.where(live, cotangent_ref[...], jnp.zeros((), jnp.bfloat16))
    grad_live_ref[...] = grad_live
    gates = gates_ref[...]
    number = lax.broadcasted_iota(jnp.int32, gates.shape, 1)
    grad_gates = jnp.zeros(gates.shape, jnp.float32)
    for e in range(experts_own):
        one = slot_of(e, place_ref[2], experts_own)
        two = slot_of(e, place_ref[3], experts_own)
        gate = jnp.sum(jnp.where(number == first + e, gates, 0.0), -1, keepdims=True)
        gate_pre = dot(normed, gate_weight_ref[e])
        up_pre = dot(normed, up_weight_ref[e])
        grad_plain = dot(grad_live, down_weight_ref[e], COLUMNS)
        sigma = jax.nn.sigmoid(gate_pre)
        silu = gate_pre * sigma
        acted = silu * up_pre
        grad_gates = grad_gates + jnp.where(
            number == first + e, jnp.sum(acted * grad_plain, -1, keepdims=True), 0.0
        )
        grad_acted = gate * grad_plain
        scaled = (gate * acted).astype(jnp.bfloat16)
        scaled_one_ref[one] = scaled
        scaled_two_ref[two] = scaled
        grad_gate_ref[one] = (
            grad_acted * up_pre * (sigma * (1.0 + gate_pre * (1.0 - sigma)))
        ).astype(jnp.bfloat16)
        grad_up_ref[two] = (grad_acted * silu).astype(jnp.bfloat16)
    rough = grad_gates.astype(jnp.bfloat16)
    fine = (grad_gates - rough.astype(jnp.float32)).astype(jnp.bfloat16)
    rest = jnp.zeros((gates.shape[0], extra_ref.shape[1] - 2 * experts_all), jnp.bfloat16)
    extra_ref[...] = jnp.concatenate([rough, fine, rest], 1)


def expert_rows(place, normed, cotangent, gathered, gates, w_gate, w_up, w_down, block):
    tokens, features = normed.shape
    experts_own, _, hidden = w_gate.shape
    experts_all = gates.shape[1]
    rows = lambda columns: pl.BlockSpec((block, columns), lambda i, p: (i, 0))
    spread = pl.BlockSpec((experts_own, block, hidden), lambda i, p: (0, i, 0))
    wide = jax.ShapeDtypeStruct((experts_own, tokens, hidden), jnp.bfloat16)
    return pl.pallas_call(
        expert_kernel,
        out_shape=(
            wide,
            wide,
            wide,
            wide,
            jax.ShapeDtypeStruct((tokens, features), jnp.bfloat16),
            jax.ShapeDtypeStruct((tokens, 128), jnp.bfloat16),
        ),
        grid_spec=pltpu.PrefetchScalarGridSpec(
            num_scalar_prefetch=1,
            grid=(tokens // block,),
            in_specs=[
                rows(features),
                rows(features),
                pl.BlockSpec((block, 128), lambda i, p: (i, features // 128)),
                rows(experts_all),
                whole_block(*w_gate.shape),
                whole_block(*w_up.shape),
                whole_block(*w_down.shape),
            ],
            out_specs=[spread, spread, spread, spread, rows(features), rows(128)],
        ),
        compiler_params=pltpu.CompilerParams(vmem_limit_bytes=52 << 20),
        cost_estimate=pl.CostEstimate(
            flops=6 * tokens * features * hidden * experts_own,
            bytes_accessed=6 * features * hidden * experts_own + 10 * tokens * features,
            transcendentals=tokens * hidden * experts_own,
        ),
    )(place, normed, cotangent, gathered, gates, w_gate, w_up, w_down)


def product_kernel(left_ref, right_ref, scaled_ref, live_ref, out_ref):
    step = pl.program_id(0)
    tile, hidden = left_ref.shape[1], right_ref.shape[1]
    narrow = live_ref.shape[1]
    tops = pl.num_programs(0) - 3
    top = tops * tile

    @pl.when(step < tops)
    def _():
        out_ref[pl.ds(pl.multiple_of(step * tile, tile), tile), :] = dot(
            left_ref[...], right_ref[...], ROWS
        ).astype(out_ref.dtype)

    for part in range(3):

        @pl.when(step == tops + part)
        def _():
            product = dot(scaled_ref[...], live_ref[...], ROWS).astype(out_ref.dtype)
            if part < 2:
                out_ref[top : top + hidden, part * narrow : (part + 1) * narrow] = product
            else:
                out_ref[top + hidden :, :narrow] = product[:narrow]
                out_ref[top + hidden :, narrow:] = product[narrow:]


def expert_product(left, right, scaled, live, e, side, dtype):
    tokens, features = left.shape
    hidden = right.shape[2]
    narrow = hidden // 2
    tile = 512
    tops = features // tile
    return pl.pallas_call(
        product_kernel,
        out_shape=jax.ShapeDtypeStruct((features + features // 2, hidden), dtype),
        grid=(tops + 3,),
        in_specs=[
            pl.BlockSpec((tokens, tile), lambda i: (0, jnp.minimum(i, tops - 1))),
            pl.BlockSpec((None, tokens, hidden), lambda i: (e, 0, 0), pipeline_mode=pl.Buffered(1)),
            pl.BlockSpec((None, tokens, hidden), lambda i: (e, 0, 0), pipeline_mode=pl.Buffered(1)),
            pl.BlockSpec((tokens, narrow), lambda i: (0, 3 * side + jnp.maximum(i - tops, 0))),
        ],
        out_specs=pl.BlockSpec((features + features // 2, hidden), lambda i: (0, 0)),
        compiler_params=pltpu.CompilerParams(vmem_limit_bytes=40 << 20),
        cost_estimate=pl.CostEstimate(flops=0, bytes_accessed=tokens, transcendentals=0),
    )(left, right, scaled, live)


def rows_kernel(
    place_ref,
    scaled_ref,
    grad_gate_ref,
    grad_up_ref,
    extra_ref,
    gate_weight_ref,
    up_weight_ref,
    down_weight_ref,
    grad_ref,
    out_ref,
):
    experts_own = scaled_ref.shape[0]
    features = out_ref.shape[1]
    one = [slot_of(e, place_ref[2], experts_own) for e in range(experts_own)]
    two = [slot_of(e, place_ref[3], experts_own) for e in range(experts_own)]
    for start in range(0, features, 512):
        part = slice(start, start + 512)
        grad = 0.0
        out = 0.0
        for e in range(experts_own):
            grad = grad + dot(grad_gate_ref[one[e]], gate_weight_ref[e, part, :], COLUMNS)
            grad = grad + dot(grad_up_ref[two[e]], up_weight_ref[e, part, :], COLUMNS)
            out = out + dot(scaled_ref[one[e]], down_weight_ref[e, :, part])
        grad_ref[:, part] = grad.astype(jnp.bfloat16)
        out_ref[:, part] = out.astype(jnp.bfloat16)
    grad_ref[:, features:] = extra_ref[...]


def expert_sums(place, scaled, grad_gate_pre, grad_up_pre, extra, w_gate, w_up, w_down, block):
    experts_own, tokens, hidden = scaled.shape
    features = w_gate.shape[1]
    rows = lambda columns: pl.BlockSpec((block, columns), lambda i, p: (i, 0))
    spread = pl.BlockSpec((experts_own, block, hidden), lambda i, p: (0, i, 0))
    return pl.pallas_call(
        rows_kernel,
        out_shape=(
            jax.ShapeDtypeStruct((tokens, features + extra.shape[1]), jnp.bfloat16),
            jax.ShapeDtypeStruct((tokens, features), jnp.bfloat16),
        ),
        grid_spec=pltpu.PrefetchScalarGridSpec(
            num_scalar_prefetch=1,
            grid=(tokens // block,),
            in_specs=[
                spread,
                spread,
                spread,
                rows(extra.shape[1]),
                whole_block(*w_gate.shape),
                whole_block(*w_up.shape),
                whole_block(*w_down.shape),
            ],
            out_specs=[rows(features + extra.shape[1]), rows(features)],
        ),
        compiler_params=pltpu.CompilerParams(vmem_limit_bytes=52 << 20),
        cost_estimate=pl.CostEstimate(flops=0, bytes_accessed=tokens, transcendentals=0),
    )(place, scaled, grad_gate_pre, grad_up_pre, extra, w_gate, w_up, w_down)


def turn_kernel(
    sum_ref,
    gates_ref,
    router_ref,
    gain_ref,
    middle_ref,
    live_ref,
    low_ref,
    high_ref,
    grad_middle_ref,
    branch_ref,
    mixed_ref,
    logits_ref,
    gain_grad_ref,
):
    features = middle_ref.shape[1]
    experts = gates_ref.shape[1]
    groups, _, width = mixed_ref.shape
    extra = sum_ref[:, features:].astype(jnp.float32)
    grad_gates = extra[:, :experts] + extra[:, experts : 2 * experts]
    gates = gates_ref[...]
    grad_logits = gates * (grad_gates - jnp.sum(gates * grad_gates, -1, keepdims=True))
    grad_logits = grad_logits.astype(jnp.bfloat16)
    logits_ref[...] = grad_logits
    grad = sum_ref[:, :features].astype(jnp.float32) + dot(grad_logits, router_ref[...], COLUMNS)
    middle = middle_ref[...]
    scale = lax.rsqrt(jnp.mean(middle * middle, -1, keepdims=True) + EPS)
    base = middle * scale
    gain_grad_ref[...] = jnp.sum(grad * base, 0, keepdims=True)
    grad_middle = live_ref[...].astype(jnp.float32) + norm_back(grad * gain_ref[...], base, scale)
    grad_middle_ref[...] = grad_middle
    branch = grad_middle.astype(jnp.bfloat16)
    branch_ref[...] = branch
    for half, weight_ref in enumerate((low_ref, high_ref)):
        mixed = dot(branch, weight_ref[...], COLUMNS).astype(jnp.bfloat16)
        for g in range(groups // 2):
            mixed_ref[half * (groups // 2) + g] = mixed[:, g * width : (g + 1) * width]


def turn_rows(sums, gates, router, gain, middle, live, weights):
    own, features = middle.shape
    experts = gates.shape[1]
    groups = KEY_VALUE_HEADS
    shaped = jax.ShapeDtypeStruct
    return pl.pallas_call(
        turn_kernel,
        out_shape=(
            shaped((own, features), jnp.float32),
            shaped((own, features), jnp.bfloat16),
            shaped((groups, own, features // groups), jnp.bfloat16),
            shaped((own, experts), jnp.bfloat16),
            shaped((1, features), jnp.float32),
        ),
        compiler_params=pltpu.CompilerParams(vmem_limit_bytes=32 << 20),
        cost_estimate=pl.CostEstimate(flops=0, bytes_accessed=own, transcendentals=0),
    )(sums, gates, router, gain[None, :], middle, live, *weights)


def close_kernel(
    query_ref,
    pair_ref,
    weight_ref,
    hidden_ref,
    normed_ref,
    gain_two_ref,
    normed_own_ref,
    logits_ref,
    grad_ref,
    head_ref,
    product_ref,
    gain_ref,
):
    step = pl.program_id(0)
    width = query_ref.shape[1]
    both = width + pair_ref.shape[1]
    query = query_ref[...]
    pair = pair_ref[...]
    grad = dot(query, weight_ref[:, :width], COLUMNS) + dot(
        pair, weight_ref[:, width:both], COLUMNS
    )
    grad_ref[...] = grad.astype(jnp.bfloat16)
    hidden = hidden_ref[...].astype(jnp.float32)
    scale = lax.rsqrt(jnp.mean(hidden * hidden, -1, keepdims=True) + EPS)
    normed = normed_ref[...]

    @pl.when(step == 0)
    def _():
        gain_ref[...] = jnp.zeros_like(gain_ref)
        product_ref[...] = jnp.zeros_like(product_ref)

    gain_ref[...] += jnp.sum(grad * (hidden * scale), 0, keepdims=True)
    product_ref[:, :width] += dot(normed, query, ROWS)
    product_ref[:, width:] += dot(normed, pair, ROWS)

    @pl.when(step == pl.num_programs(0) - 1)
    def _():
        features = product_ref.shape[0]
        rows = head_ref.shape[0]
        experts = logits_ref.shape[1]
        side = head_ref.shape[1] // (features // rows)
        gains = jnp.concatenate(
            [gain_ref[...], gain_two_ref[...], jnp.zeros((6, features), jnp.float32)], 0
        )
        gains = jnp.transpose(gains)
        router = dot(normed_own_ref[...], logits_ref[...], ROWS)
        for c in range(features // rows):
            part = slice(c * rows, (c + 1) * rows)
            rest = jnp.zeros((rows, side - both - 8 - experts), jnp.float32)
            head_ref[:, c * side : (c + 1) * side] = jnp.concatenate(
                [product_ref[part, :], gains[part], router[part], rest], 1
            )


def close_rows(
    query, pair, weight, gathered, normed, gain_two_grad, normed_own, logits, rows_own, side, block
):
    tokens, features = normed.shape
    both = query.shape[1] + pair.shape[1]
    rows = lambda width: pl.BlockSpec((block, width), lambda i: (i, 0))
    resident = lambda *shape: pl.BlockSpec(shape, lambda i: (0,) * len(shape))
    shaped = jax.ShapeDtypeStruct
    head = (rows_own, features // rows_own * side)
    return pl.pallas_call(
        close_kernel,
        out_shape=(shaped((tokens, features), jnp.bfloat16), shaped(head, jnp.float32)),
        grid=(tokens // block,),
        in_specs=[
            rows(query.shape[1]),
            rows(pair.shape[1]),
            whole_block(*weight.shape),
            rows(features),
            rows(features),
            whole_block(1, features),
            whole_block(*normed_own.shape),
            whole_block(*logits.shape),
        ],
        out_specs=[rows(features), resident(*head)],
        scratch_shapes=[
            pltpu.VMEM((features, both), jnp.float32),
            pltpu.VMEM((1, features), jnp.float32),
        ],
        compiler_params=pltpu.CompilerParams(vmem_limit_bytes=48 << 20),
        cost_estimate=pl.CostEstimate(flops=0, bytes_accessed=tokens, transcendentals=0),
    )(query, pair, weight, gathered, normed, gain_two_grad, normed_own, logits)


def head_kernel(copies, side, low_ref, high_ref, query_ref, key_ref, value_ref, out_ref, small_ref):
    groups = KEY_VALUE_HEADS
    count = groups * copies
    halves = [low_ref[...].astype(jnp.float32), high_ref[...].astype(jnp.float32)]
    width = query_ref.shape[1] // groups
    parts = []
    for c in range(count):
        place = c % (count // 2) * side
        parts.append(halves[c // (count // 2)][:, place : place + side])
    heads = []
    small = 0.0
    for g in range(groups):
        total = parts[g * copies]
        for p in range(1, copies):
            total = total + parts[g * copies + p]
        heads.append(total)
        small = small + total[:, width + 2 * HEAD_SIZE :]
    small_ref[...] = small
    query_ref[...] = jnp.concatenate([head[:, :width] for head in heads], 1)
    key_ref[...] = jnp.concatenate([head[:, width : width + HEAD_SIZE] for head in heads], 1)
    value_ref[...] = jnp.concatenate(
        [head[:, width + HEAD_SIZE : width + 2 * HEAD_SIZE] for head in heads], 1
    )
    out_ref[...] = jnp.concatenate([half[:, count // 2 * side :] for half in halves], 1)


def head_outputs(low, high, copies, side):
    rows = low.shape[0]
    groups = KEY_VALUE_HEADS
    query_width = QUERY_HEADS * HEAD_SIZE
    shaped = lambda width: jax.ShapeDtypeStruct((rows, width), jnp.float32)
    return pl.pallas_call(
        lambda *refs: head_kernel(copies, side, *refs),
        name="head_outputs",
        out_shape=(
            shaped(query_width),
            shaped(groups * HEAD_SIZE),
            shaped(groups * HEAD_SIZE),
            shaped(MODEL_WIDTH),
            shaped(side - (query_width // groups + 2 * HEAD_SIZE)),
        ),
        compiler_params=pltpu.CompilerParams(vmem_limit_bytes=40 << 20),
        cost_estimate=pl.CostEstimate(flops=0, bytes_accessed=rows, transcendentals=0),
    )(low, high)


def into_kernel(keeps_ref, side, sent_ref, first_ref, second_ref, out_ref):
    kept = pl.program_id(0) == keeps_ref[side]
    came = jnp.where(pl.program_id(1) == 0, first_ref[...], second_ref[...])
    out_ref[...] = jnp.where(kept, sent_ref[...], came).astype(jnp.float32)


def into_output(keeps, side, sent, first, second):
    rows, hidden = first.shape
    part = lambda index: pl.BlockSpec((rows, hidden), index)
    return pl.pallas_call(
        lambda k, *refs: into_kernel(k, side, *refs),
        name="into_output",
        out_shape=jax.ShapeDtypeStruct((2, 2 * rows, hidden), jnp.float32),
        grid_spec=pltpu.PrefetchScalarGridSpec(
            num_scalar_prefetch=1,
            grid=(2, 2),
            in_specs=[
                part(lambda e, h, k: (h, 0)),
                part(lambda e, h, k: (0, 0)),
                part(lambda e, h, k: (0, 0)),
            ],
            out_specs=pl.BlockSpec((None, rows, hidden), lambda e, h, k: (e, h, 0)),
        ),
        compiler_params=pltpu.CompilerParams(vmem_limit_bytes=32 << 20),
        cost_estimate=pl.CostEstimate(flops=0, bytes_accessed=rows, transcendentals=0),
    )(keeps, sent, first, second)


def down_kernel(keeps_ref, sent_low_ref, came_low_ref, sent_high_ref, came_high_ref, out_ref):
    rows, hidden = came_low_ref.shape
    narrow = hidden // 2
    pairs = ((sent_low_ref, came_low_ref), (sent_high_ref, came_high_ref))
    for side, (sent_ref, came_ref) in enumerate(pairs):
        kept = pl.program_id(0) == keeps_ref[side]
        value = jnp.where(kept, sent_ref[...], came_ref[...]).astype(jnp.float32)
        start = side * rows
        out_ref[:, start : start + hidden] = value[:hidden]
        out_ref[:narrow, start + hidden : start + rows] = value[hidden:, :narrow]
        out_ref[narrow:, start + hidden : start + rows] = value[hidden:, narrow:]


def down_output(keeps, sent_low, came_low, sent_high, came_high):
    rows, hidden = came_low.shape
    place = sent_low.shape[0] // rows - 1
    sent = pl.BlockSpec((rows, hidden), lambda e, k: (place, 0))
    came = pl.BlockSpec((rows, hidden), lambda e, k: (0, 0))
    return pl.pallas_call(
        down_kernel,
        out_shape=jax.ShapeDtypeStruct((2, hidden, 2 * rows), jnp.float32),
        grid_spec=pltpu.PrefetchScalarGridSpec(
            num_scalar_prefetch=1,
            grid=(2,),
            in_specs=[sent, came, sent, came],
            out_specs=pl.BlockSpec((None, hidden, 2 * rows), lambda e, k: (e, 0, 0)),
        ),
        compiler_params=pltpu.CompilerParams(vmem_limit_bytes=32 << 20),
        cost_estimate=pl.CostEstimate(flops=0, bytes_accessed=rows, transcendentals=0),
    )(keeps, sent_low, came_low, sent_high, came_high)


def after(values, *others):
    values, _ = lax.optimization_barrier((values, others))
    return values


def swap(value, bit):
    size = lax.axis_size("rep")
    return lax.ppermute(value, "rep", [(i, i ^ bit) for i in range(size)])


def has(bit):
    return (lax.axis_index("rep") & bit) != 0


def halve(value, came, bit):
    half = value.shape[0] // 2
    keep = jnp.where(has(bit), half, 0)
    part = lambda array, start: lax.dynamic_slice_in_dim(array, start, half, 0).astype(jnp.float32)
    kept = part(value, keep)
    sent = part(value, half - keep)
    if came is not None:
        kept = kept + part(came, keep)
        sent = sent + part(came, half - keep)
    return kept, sent.astype(jnp.bfloat16)


def join(value, came, bit, axis):
    upper = has(bit)
    return jnp.concatenate(
        [jnp.where(upper, came, value), jnp.where(upper, value, came)], axis
    )


class Chain:
    def __init__(self, order):
        self.order = order
        self.stage = 0
        self.steps = 2 * len(order)

    def send(self, sent):
        bit = self.order[min(self.stage, self.steps - 1 - self.stage)]
        self.sent = sent
        self.stage += 1
        if self.stage < self.steps:
            self.flying = swap(sent, bit)

    def step(self, *others):
        bits = len(self.order)
        came = after(self.flying, *others)
        if self.stage < bits:
            self.kept, sent = halve(self.kept, came, self.order[self.stage])
            self.send(sent)
        elif self.stage == bits:
            self.send((self.kept + came.astype(jnp.float32)).astype(jnp.bfloat16))
        else:
            self.send(join(self.sent, came, self.order[self.steps - self.stage], 0))
        return self.sent

    def piece(self, number, count, *others):
        rows = self.sent.shape[0] // count
        part = after(self.sent[number * rows : (number + 1) * rows], *others)
        return swap(part, self.order[0])


class Cube:
    def __init__(self, value, order):
        self.value = value
        self.order = order
        self.stage = 0

    def axis(self, bit):
        return len(self.order) - bit.bit_length()

    def halve(self, *others):
        bit = self.order[self.stage]
        keep = has(bit).astype(jnp.int32)
        part = lambda index: lax.dynamic_slice_in_dim(self.value, index, 1, self.axis(bit))
        self.value, sent = part(keep), part(1 - keep).astype(jnp.bfloat16)
        self.flying = swap(after(sent, *others), bit)
        self.stage += 1
        return sent

    def add(self, *others):
        self.value = self.value + after(self.flying, *others).astype(jnp.float32)

    def back(self, *others):
        self.stage -= 1
        self.flying = swap(after(self.value, *others), self.order[self.stage])
        return self.value

    def join(self, *others):
        bit = self.order[self.stage]
        self.value = join(self.value, after(self.flying, *others), bit, self.axis(bit))


class Exchange:
    def __init__(self, fetched, bits):
        size = fetched.shape[0]
        fetched = fetched.reshape((size,) + (1,) * len(bits) + fetched.shape[1:])
        self.values = [fetched[: size // 2], fetched[size // 2 :]]
        self.orders = (bits, bits[::-1])
        self.stage = 0
        self.fly()

    def fly(self):
        self.flying = [
            swap(value, order[self.stage]) for value, order in zip(self.values, self.orders)
        ]

    def step(self, *others):
        bits = len(self.orders[0])
        for h, order in enumerate(self.orders):
            bit = order[self.stage]
            came = after(self.flying[h], *others)
            self.values[h] = join(self.values[h], came, bit, bits - (bit.bit_length() - 1))
        self.stage += 1
        if self.stage < bits:
            self.fly()
        return list(self.values)

    def finish(self, *others):
        while self.stage < len(self.orders[0]):
            self.step(*others)
        return [value.reshape(-1, value.shape[-1]) for value in self.values]


def per_device(
    inputs,
    segments,
    positions,
    expert_ids,
    attn_gain,
    w_query,
    key_weight,
    value_weight,
    w_out,
    ffn_gain,
    router,
    w_gate,
    w_up,
    w_down,
    grad_out,
):
    size = lax.axis_size("ctx")
    me = lax.axis_index("ctx")
    reps = lax.axis_size("rep")
    bits = [1 << i for i in range(reps.bit_length() - 1)]
    own = inputs.shape[1]
    tokens = size * own
    groups = KEY_VALUE_HEADS
    copies = size // groups
    query_width = HEAD_GROUP * HEAD_SIZE
    width = query_width + 2 * HEAD_SIZE
    copy_index = me % copies
    rows_own = w_out.shape[0]
    experts_own = w_gate.shape[0]
    experts_all = size * experts_own
    block = 2 * own
    chips = size // 2
    chip = me // 2
    odd = me % 2 == 1
    share = rows_own // reps
    share_start = lax.axis_index("rep") * share

    columns = jnp.concatenate(
        [
            segments[0][:, None],
            positions[0][:, None] // 64,
            positions[0][:, None] % 64,
            expert_ids[0],
        ],
        1,
    ).astype(jnp.bfloat16)
    columns = jnp.pad(columns, ((0, 0), (0, 128 - columns.shape[1])))
    gathered = lax.all_gather(
        jnp.concatenate([inputs[0], columns], 1), "ctx", axis=0, tiled=True
    )

    def from_chip(value, k):
        return lax.ppermute(value, "ctx", [(i, (i - 2 * k) % size) for i in range(size)])

    def from_core(value):
        return lax.ppermute(value, "ctx", [(i, i ^ 1) for i in range(size)])

    def cores(mine, others, axis):
        return jnp.concatenate(
            [jnp.where(odd, others, mine), jnp.where(odd, mine, others)], axis
        )

    shared = lambda array: lax.dynamic_slice_in_dim(array, share_start, share, 0)
    side_width = -(-(width + 2 + router.shape[1]) // 128) * 128
    head_columns = jnp.concatenate(
        [
            shared(w_query).reshape(share, groups, query_width),
            shared(key_weight).reshape(share, groups, HEAD_SIZE),
            shared(value_weight).reshape(share, groups, HEAD_SIZE),
            jnp.broadcast_to(shared(attn_gain)[:, None, None], (share, groups, 1)),
            jnp.broadcast_to(shared(ffn_gain)[:, None, None], (share, groups, 1)),
            jnp.broadcast_to(shared(router)[:, None, :], (share, groups, router.shape[1])),
        ],
        -1,
    )
    used = head_columns.shape[-1]
    head_columns = jnp.pad(head_columns, ((0, 0), (0, 0), (0, side_width - used)))
    head_columns = jnp.repeat(jnp.transpose(head_columns, (1, 0, 2)), copies, 0)
    head_columns = head_columns.reshape(chips, 2, share, side_width)
    out_share = shared(w_out)
    parcels = []
    for k in range(chips):
        to = head_columns[(chip - k) % chips]
        parcel = jnp.concatenate([out_share, to[0], to[1]], 1)
        parcels.append(from_chip(parcel, k) if k else parcel)
    parcels = jnp.stack(parcels)
    out_part = parcels[:, :, :MODEL_WIDTH]
    heads = [
        parcels[:, :, MODEL_WIDTH : MODEL_WIDTH + side_width],
        parcels[:, :, MODEL_WIDTH + side_width :],
    ]
    for_core = jnp.where(odd, heads[0], heads[1])
    mine_part = jnp.concatenate([out_part, jnp.where(odd, heads[1], heads[0])], 2)
    core_part = from_core(jnp.concatenate([out_part, for_core], 2))
    fetched = cores(mine_part[:, None], core_part[:, None], 1)
    fetched = lax.dynamic_slice_in_dim(
        jnp.concatenate([fetched, fetched], 0), (chips - chip) % chips, chips, 0
    ).reshape(size, share, MODEL_WIDTH + side_width)
    head_exchange = Exchange(fetched[:, :, MODEL_WIDTH:], bits)
    out_exchange = Exchange(fetched[:, :, :MODEL_WIDTH], bits)
    head_halves = head_exchange.finish()
    ready = out_exchange.step(*head_halves)
    head_all = jnp.concatenate(head_halves, 0)
    gain_one = head_all[:, width].astype(jnp.float32)
    gain_two = head_all[:, width + 1].astype(jnp.float32)
    router_all = head_all[:, width + 2 : used]

    (
        normed_one,
        query,
        key,
        value,
        mixed,
        log_total,
        cosine_table,
        sine_table,
        segment_rows,
    ) = attend(after(gathered, *ready), gain_one, head_halves, block)

    part = tokens // copies
    cotangent = lax.all_gather(after(grad_out[0], *ready), "ctx", axis=0, tiled=True)
    mixed_all = lax.all_gather(
        after(lax.dynamic_slice_in_dim(mixed, copy_index * part, part, 0), cotangent),
        "ctx",
        axis=0,
    ).reshape(groups, tokens, query_width)
    w_out_halves = out_exchange.finish(mixed)

    wide = min(512, tokens)
    middle, normed_two, gates = middle_rows(
        mixed_all, w_out_halves, gathered, gain_two, router_all, wide
    )
    flag = lambda bit: has(bit).astype(jnp.int32)
    place = jnp.stack([chip, me, flag(bits[0]), flag(bits[-1])]).astype(jnp.int32)
    scaled_one, scaled_two, grad_gate_pre, grad_up_pre, grad_live, extra = expert_rows(
        place, normed_two, cotangent, gathered, gates, w_gate, w_up, w_down, wide
    )
    grad_rows, out_rows = expert_sums(
        place, scaled_one, grad_gate_pre, grad_up_pre, extra, w_gate, w_up, w_down, wide
    )
    grad_two_sum = lax.psum_scatter(grad_rows, "ctx", scatter_dimension=0, tiled=True)

    def mine(array):
        return lax.dynamic_slice_in_dim(array, me * own, own, 0)

    middle_own, gates_own, live_own, normed_own = [
        mine(array) for array in (middle, gates, grad_live, normed_two)
    ]

    def product(side, e, dtype):
        right, scaled = ((grad_gate_pre, scaled_one), (grad_up_pre, scaled_two))[side]
        return expert_product(normed_two, right, scaled, grad_live, e, side, dtype)

    normed_two, grad_live = after((normed_two, grad_live), grad_rows)
    chains = [Chain(bits), Chain(bits[::-1])]
    for side, chain in enumerate(chains):
        chain.send(product(side, 0, jnp.bfloat16))
    normed_two, grad_live = after((normed_two, grad_live), *[chain.sent for chain in chains])
    for side, chain in enumerate(chains):
        chain.kept = product(side, 1, jnp.float32)

    grad_middle, grad_branch, grad_mixed, grad_logits, gain_two_grad = turn_rows(
        after(grad_two_sum, *[(c.kept, c.flying) for c in chains]),
        gates_own,
        router_all,
        gain_two,
        middle_own,
        live_own,
        w_out_halves,
    )
    grad_branch_all = lax.all_gather(grad_branch, "ctx", axis=0, tiled=True)

    def deal(blocks, *others):
        blocks = blocks.reshape((chips, 2) + blocks.shape[1:])
        got = [blocks[(chip - k) % chips] for k in range(chips)]
        got = jnp.stack([got[0]] + [from_chip(got[k], k) for k in range(1, chips)])
        got = after(got, *others)
        stay = jnp.where(odd, got[:, 1], got[:, 0])
        go = from_core(jnp.where(odd, got[:, 0], got[:, 1]))
        both = cores(stay[:, None], go[:, None], 1)
        both = jnp.concatenate([both, both], 0)
        both = lax.dynamic_slice_in_dim(both, (chips - chip) % chips, chips, 0)
        return both.reshape((size,) + both.shape[2:])

    grad_mixed_all = deal(jnp.repeat(grad_mixed, copies, 0)).reshape(tokens, query_width)
    sent = [grad_mixed_all]
    while chains[0].stage < len(bits):
        sent = [chain.step(*sent) for chain in chains]
    grad_query, grad_pair = attend_back(
        query,
        after(grad_mixed_all, *sent),
        log_total,
        cosine_table,
        sine_table,
        gathered,
        segment_rows,
        key,
        value,
    )
    if copies > 1:
        places = jnp.arange(tokens, dtype=jnp.int32)
        counted = (places // part == copy_index)[:, None]
        grad_query = jnp.where(counted, grad_query, jnp.zeros((), jnp.bfloat16))
        grad_pair = jnp.where(counted, grad_pair, jnp.zeros((), jnp.bfloat16))
    sent = [chain.step(grad_pair) for chain in chains]
    grad_one_low, head_grads = close_rows(
        after(grad_query, *sent),
        grad_pair,
        head_all,
        gathered,
        normed_one,
        gain_two_grad,
        normed_own,
        grad_logits,
        rows_own,
        side_width,
        block,
    )
    grad_one = lax.psum_scatter(
        grad_one_low, "ctx", scatter_dimension=0, tiled=True
    ).astype(jnp.float32)
    grad_proj_out = dot(
        lax.dynamic_slice_in_dim(mixed, copy_index * rows_own, rows_own, 1),
        grad_branch_all,
        ROWS,
    )

    line = size // 2 * side_width
    half = MODEL_WIDTH // 2
    cubes = []
    for h, order in enumerate((bits, bits[::-1])):
        rows = jnp.concatenate(
            [
                head_grads[:, h * line : (h + 1) * line],
                grad_proj_out[:, h * half : (h + 1) * half],
            ],
            1,
        )
        cubes.append(Cube(rows.reshape((2,) * len(bits) + (share, line + half)), order))
    sent = [cube.halve() for cube in cubes]
    while chains[0].stage < chains[0].steps:
        sent = [chain.step(*sent) for chain in chains]
    while cubes[0].stage < len(bits):
        for cube in cubes:
            cube.add(*sent)
        sent = [cube.halve() for cube in cubes]
    first = [chain.piece(0, 3, *sent) for chain in chains]
    for cube in cubes:
        cube.add(*sent)
    totals = [cube.value.astype(jnp.bfloat16) for cube in cubes]
    blocks = jnp.concatenate(
        [
            jnp.transpose(
                total.reshape(share, -1)[:, :line].reshape(share, size // 2, side_width), (1, 0, 2)
            )
            for total in totals
        ],
        0,
    )
    head_sums = deal(blocks)
    for h, cube in enumerate(cubes):
        rows = jnp.transpose(head_sums[h * (size // 2) : (h + 1) * (size // 2)], (1, 0, 2))
        rows = jnp.concatenate(
            [rows.reshape(share, line), totals[h].reshape(share, -1)[:, line:]], 1
        )
        cube.value = rows.reshape(totals[h].shape)
    sent = [cube.back() for cube in cubes]
    second = [chain.piece(1, 3, *sent) for chain in chains]
    while cubes[0].stage > 0:
        for cube in cubes:
            cube.join(*sent)
        sent = [cube.back() for cube in cubes]
    third = [chain.piece(2, 3, *sent, *first) for chain in chains]
    keeps = place[2:]
    grad_gate, grad_up = [
        into_output(keeps, side, *after((chain.sent, first[side], second[side]), *sent))
        for side, chain in enumerate(chains)
    ]
    for cube in cubes:
        cube.join(grad_gate, grad_up)
    head_outs = head_outputs(*[cube.value.reshape(rows_own, -1) for cube in cubes], copies, side_width)
    small = head_outs[4]

    moe_sum = lax.psum_scatter(
        after(out_rows, grad_branch), "ctx", scatter_dimension=0, tiled=True
    ).astype(jnp.float32)
    output = jnp.where((segments[0] != 0)[:, None], middle_own + moe_sum, 0.0)
    own_hidden = inputs[0].astype(jnp.float32)
    own_scale = lax.rsqrt(jnp.mean(own_hidden * own_hidden, -1, keepdims=True) + EPS)
    grad_in = grad_middle + norm_back(grad_one * gain_one, own_hidden * own_scale, own_scale)
    grad_down = down_output(
        keeps,
        *after((chains[0].sent, third[0], chains[1].sent, third[1]), head_outs, grad_in, output),
    )

    return (
        output.astype(jnp.bfloat16)[None],
        grad_in[None],
        small[:, 0],
        *head_outs[:4],
        small[:, 1],
        small[:, 8 : 8 + experts_all],
        grad_gate,
        grad_up,
        grad_down,
    )


def solution(mesh):
    return jax.shard_map(
        per_device,
        mesh=mesh,
        in_specs=(
            P("rep", "ctx", None),
            P("rep", "ctx"),
            P("rep", "ctx"),
            P("rep", "ctx", None),
            P("ctx"),
            P("ctx", None),
            P("ctx", None),
            P("ctx", None),
            P("ctx", None),
            P("ctx"),
            P("ctx", None),
            P("ctx", None, None),
            P("ctx", None, None),
            P("ctx", None, None),
            P("rep", "ctx", None),
        ),
        out_specs=(
            P("rep", "ctx", None),
            P("rep", "ctx", None),
            P("ctx"),
            P("ctx", None),
            P("ctx", None),
            P("ctx", None),
            P("ctx", None),
            P("ctx"),
            P("ctx", None),
            P("ctx", None, None),
            P("ctx", None, None),
            P("ctx", None, None),
        ),
        check_vma=False,
    )
```

```python
import jax
import jax.numpy as jnp
from jax import lax
from jax.experimental import pallas as pl
from jax.experimental.pallas import tpu as pltpu
from jax.sharding import PartitionSpec as P

MODEL_WIDTH = 1536
QUERY_HEADS = 24
KEY_VALUE_HEADS = 8
HEAD_GROUP = QUERY_HEADS // KEY_VALUE_HEADS
HEAD_SIZE = 64
TOPK = 8

EPS = 1e-06
THETA = 10000.0
MASK_FLOOR = -1e30

ROWS = (((0,), (0,)), ((), ()))
COLUMNS = (((1,), (1,)), ((), ()))


def dot(left, right, contract=(((1,), (0,)), ((), ()))):
    return lax.dot_general(left, right, contract, preferred_element_type=jnp.float32)


def norm_back(grad_base, base, scale):
    return scale * (grad_base - base * jnp.mean(grad_base * base, -1, keepdims=True))


def turn(rows):
    half = HEAD_SIZE // 2
    return jnp.concatenate([-rows[:, half:], rows[:, :half]], 1)


def turn_back(rows):
    half = HEAD_SIZE // 2
    return jnp.concatenate([rows[:, half:], -rows[:, :half]], 1)


def stack_heads(rows):
    return jnp.concatenate(
        [rows[:, h * HEAD_SIZE : (h + 1) * HEAD_SIZE] for h in range(HEAD_GROUP)], 0
    )


def side_heads(rows):
    block = rows.shape[0] // HEAD_GROUP
    return jnp.concatenate([rows[h * block : (h + 1) * block] for h in range(HEAD_GROUP)], 1)


def lanes(values, combine):
    total = values[:, :128]
    for start in range(128, values.shape[1], 128):
        total = combine(total, values[:, start : start + 128])
    return total


def masked_scores(stacked, keys, row_segments, key_segments, row_start, key_start):
    block = row_segments.shape[0]
    scores = dot(stacked, keys, COLUMNS) * HEAD_SIZE ** (-0.5)
    row_place = row_start + lax.broadcasted_iota(jnp.int32, (block, block), 0)
    key_place = key_start + lax.broadcasted_iota(jnp.int32, (block, block), 1)
    allowed = (row_segments == key_segments) & (key_place <= row_place)
    scores = scores.reshape(HEAD_GROUP, block, block)
    return jnp.where(allowed[None], scores, MASK_FLOOR).reshape(HEAD_GROUP * block, block)


def first_block(row_segments, segment_ref, step):
    here = jnp.max(row_segments[:1, :1])
    segments = segment_ref[...]
    number = lax.broadcasted_iota(jnp.int32, segments.shape, 0)
    return jnp.min(jnp.where((segments == here) & (number <= step), number, step))


def token_rows(block, own, features):
    count = block // own
    return (
        pl.BlockSpec((count, own, features), lambda i, *_: (i, 0, 0)),
        pl.BlockSpec((count, own, 128), lambda i, *_: (i, 0, features // 128)),
    )


def flat(ref):
    return ref[...].reshape(-1, ref.shape[-1])


def whole_block(*shape):
    return pl.BlockSpec(shape, lambda *i: (0,) * len(shape), pipeline_mode=pl.Buffered(1))


def attend_kernel(
    hidden_ref,
    column_ref,
    gain_ref,
    low_ref,
    high_ref,
    rate_ref,
    normed_ref,
    query_ref,
    key_ref,
    value_ref,
    mixed_ref,
    log_ref,
    cosine_ref,
    sine_ref,
    segment_ref,
    score_ref,
):
    step = pl.program_id(0)
    block = query_ref.shape[0]
    query_width = query_ref.shape[1]
    width = query_width + 2 * HEAD_SIZE
    here = pl.ds(pl.multiple_of(step * block, block), block)
    columns = flat(column_ref).astype(jnp.float32)
    row_segments = columns[:, :1]
    segment_ref[step] = jnp.transpose(columns)[:1, :]
    angles = (columns[:, 1:2] * 64.0 + columns[:, 2:3]) * rate_ref[...]
    cosine = jnp.cos(angles)
    sine = jnp.sin(angles)
    cosine_ref[...] = cosine
    sine_ref[...] = sine
    hidden = flat(hidden_ref).astype(jnp.float32)
    scale = lax.rsqrt(jnp.mean(hidden * hidden, -1, keepdims=True) + EPS)
    normed = (hidden * scale * gain_ref[...]).astype(jnp.bfloat16)
    normed_ref[...] = normed
    middle = low_ref.shape[0]
    raw = dot(normed[:, :middle], low_ref[:, :width]) + dot(
        normed[:, middle:], high_ref[:, :width]
    )
    key_raw = raw[:, query_width : query_width + HEAD_SIZE]
    key_ref[here, :] = (key_raw * cosine + turn(key_raw) * sine).astype(jnp.bfloat16)
    value_ref[here, :] = raw[:, query_width + HEAD_SIZE :].astype(jnp.bfloat16)
    query_raw = stack_heads(raw[:, :query_width])
    cosine = jnp.concatenate([cosine] * HEAD_GROUP, 0)
    sine = jnp.concatenate([sine] * HEAD_GROUP, 0)
    query = (query_raw * cosine + turn(query_raw) * sine).astype(jnp.bfloat16)
    query_ref[...] = side_heads(query)
    rows = HEAD_GROUP * block
    first = first_block(row_segments, segment_ref, step)

    def first_pass(index, top):
        there = pl.ds(pl.multiple_of(index * block, block), block)
        scores = masked_scores(
            query,
            key_ref[there, :],
            row_segments,
            segment_ref[index],
            step * block,
            index * block,
        )
        score_ref[index] = scores
        return jnp.maximum(top, lanes(scores, jnp.maximum))

    top = lax.fori_loop(
        first, step + 1, first_pass, jnp.full((rows, 128), MASK_FLOOR, jnp.float32)
    )
    top = jnp.max(top, -1, keepdims=True)

    def second_pass(index, carry):
        total, mixed = carry
        there = pl.ds(pl.multiple_of(index * block, block), block)
        weights = jnp.exp(score_ref[index] - top)
        mixed = mixed + dot(weights.astype(jnp.bfloat16), value_ref[there, :])
        return total + lanes(weights, jnp.add), mixed

    total, mixed = lax.fori_loop(
        first,
        step + 1,
        second_pass,
        (
            jnp.zeros((rows, 128), jnp.float32),
            jnp.zeros((rows, HEAD_SIZE), jnp.float32),
        ),
    )
    total = jnp.sum(total, -1, keepdims=True)
    mixed_ref[...] = side_heads((mixed / total).astype(jnp.bfloat16))
    log_ref[...] = (top + jnp.log(total)).reshape(HEAD_GROUP, block, 1)


def attend(gathered, gain, weights, own, block):
    tokens, features = gathered.shape[0] * own, gain.shape[0]
    query_width = HEAD_GROUP * HEAD_SIZE
    steps = tokens // block
    half = jnp.arange(HEAD_SIZE // 2, dtype=jnp.float32)
    rate = THETA ** (-(2.0 * half) / HEAD_SIZE)
    rate = jnp.concatenate([rate, rate])[None, :]
    rows = lambda width: pl.BlockSpec((block, width), lambda i: (i, 0))
    resident = lambda *shape: pl.BlockSpec(shape, lambda i: (0,) * len(shape))
    shaped = jax.ShapeDtypeStruct
    return pl.pallas_call(
        attend_kernel,
        out_shape=(
            shaped((tokens, features), jnp.bfloat16),
            shaped((tokens, query_width), jnp.bfloat16),
            shaped((tokens, HEAD_SIZE), jnp.bfloat16),
            shaped((tokens, HEAD_SIZE), jnp.bfloat16),
            shaped((tokens, query_width), jnp.bfloat16),
            shaped((HEAD_GROUP, tokens, 1), jnp.float32),
            shaped((tokens, HEAD_SIZE), jnp.float32),
            shaped((tokens, HEAD_SIZE), jnp.float32),
            shaped((steps, 1, block), jnp.float32),
        ),
        grid=(steps,),
        in_specs=[
            *token_rows(block, own, features),
            whole_block(1, features),
            whole_block(*weights[0].shape),
            whole_block(*weights[1].shape),
            whole_block(1, HEAD_SIZE),
        ],
        out_specs=[
            rows(features),
            rows(query_width),
            resident(tokens, HEAD_SIZE),
            resident(tokens, HEAD_SIZE),
            rows(query_width),
            pl.BlockSpec((HEAD_GROUP, block, 1), lambda i: (0, i, 0)),
            rows(HEAD_SIZE),
            rows(HEAD_SIZE),
            resident(steps, 1, block),
        ],
        scratch_shapes=[pltpu.VMEM((steps, HEAD_GROUP * block, block), jnp.float32)],
        compiler_params=pltpu.CompilerParams(vmem_limit_bytes=48 << 20),
        cost_estimate=pl.CostEstimate(flops=0, bytes_accessed=tokens, transcendentals=0),
    )(gathered, gathered, gain[None, :], *weights, rate)


def attend_back_kernel(
    query_ref,
    grad_ref,
    log_ref,
    cosine_ref,
    sine_ref,
    column_ref,
    segment_ref,
    key_ref,
    value_ref,
    key_cosine_ref,
    key_sine_ref,
    grad_query_ref,
    grad_pair_ref,
    probs_ref,
    grad_probs_ref,
    grad_key_ref,
    grad_value_ref,
):
    step = pl.program_id(0)
    block = query_ref.shape[0]
    rows = HEAD_GROUP * block

    @pl.when(step == 0)
    def _():
        grad_key_ref[...] = jnp.zeros_like(grad_key_ref)
        grad_value_ref[...] = jnp.zeros_like(grad_value_ref)

    query = stack_heads(query_ref[...])
    grad = stack_heads(grad_ref[...])
    log_total = log_ref[...].reshape(rows, 1)
    row_segments = flat(column_ref).astype(jnp.float32)[:, :1]
    first = first_block(row_segments, segment_ref, step)

    def first_pass(index, delta):
        there = pl.ds(pl.multiple_of(index * block, block), block)
        scores = masked_scores(
            query,
            key_ref[there, :],
            row_segments,
            segment_ref[index],
            step * block,
            index * block,
        )
        probs = jnp.exp(scores - log_total)
        grad_probs = dot(grad, value_ref[there, :], COLUMNS)
        probs_ref[index] = probs
        grad_probs_ref[index] = grad_probs
        grad_value_ref[there, :] += dot(probs.astype(jnp.bfloat16), grad, ROWS)
        return delta + lanes(probs * grad_probs, jnp.add)

    delta = lax.fori_loop(first, step + 1, first_pass, jnp.zeros((rows, 128), jnp.float32))
    delta = jnp.sum(delta, -1, keepdims=True)

    def second_pass(index, grad_query):
        there = pl.ds(pl.multiple_of(index * block, block), block)
        grad_scores = (probs_ref[index] * (grad_probs_ref[index] - delta)).astype(jnp.bfloat16)
        grad_key_ref[there, :] += dot(grad_scores, query, ROWS)
        return grad_query + dot(grad_scores, key_ref[there, :])

    grad_query = lax.fori_loop(
        first, step + 1, second_pass, jnp.zeros((rows, HEAD_SIZE), jnp.float32)
    )
    score_scale = HEAD_SIZE ** (-0.5)
    cosine = jnp.concatenate([cosine_ref[...]] * HEAD_GROUP, 0)
    sine = jnp.concatenate([sine_ref[...]] * HEAD_GROUP, 0)
    grad_query = grad_query * score_scale
    grad_query = grad_query * cosine + turn_back(grad_query * sine)
    grad_query_ref[...] = side_heads(grad_query.astype(jnp.bfloat16))

    @pl.when(step == pl.num_programs(0) - 1)
    def _():
        grad_key = grad_key_ref[...] * score_scale
        grad_key = grad_key * key_cosine_ref[...] + turn_back(grad_key * key_sine_ref[...])
        grad_pair_ref[...] = jnp.concatenate([grad_key, grad_value_ref[...]], 1).astype(
            jnp.bfloat16
        )


def attend_back(query, grad, log_total, cosine, sine, gathered, segments, key, value, own):
    tokens, query_width = query.shape
    steps, _, block = segments.shape
    features = gathered.shape[2] - 128
    rows = lambda width: pl.BlockSpec((block, width), lambda i: (i, 0))
    resident = lambda *shape: pl.BlockSpec(shape, lambda i: (0,) * len(shape))
    return pl.pallas_call(
        attend_back_kernel,
        out_shape=(
            jax.ShapeDtypeStruct((tokens, query_width), jnp.bfloat16),
            jax.ShapeDtypeStruct((tokens, 2 * HEAD_SIZE), jnp.bfloat16),
        ),
        grid=(steps,),
        in_specs=[
            rows(query_width),
            rows(query_width),
            pl.BlockSpec((HEAD_GROUP, block, 1), lambda i: (0, i, 0)),
            rows(HEAD_SIZE),
            rows(HEAD_SIZE),
            token_rows(block, own, features)[1],
            whole_block(steps, 1, block),
            whole_block(tokens, HEAD_SIZE),
            whole_block(tokens, HEAD_SIZE),
            whole_block(tokens, HEAD_SIZE),
            whole_block(tokens, HEAD_SIZE),
        ],
        out_specs=[rows(query_width), resident(tokens, 2 * HEAD_SIZE)],
        scratch_shapes=[
            pltpu.VMEM((steps, HEAD_GROUP * block, block), jnp.float32),
            pltpu.VMEM((steps, HEAD_GROUP * block, block), jnp.float32),
            pltpu.VMEM((tokens, HEAD_SIZE), jnp.float32),
            pltpu.VMEM((tokens, HEAD_SIZE), jnp.float32),
        ],
        compiler_params=pltpu.CompilerParams(vmem_limit_bytes=48 << 20),
        cost_estimate=pl.CostEstimate(flops=0, bytes_accessed=tokens, transcendentals=0),
    )(query, grad, log_total, cosine, sine, gathered, segments, key, value, cosine, sine)


def middle_kernel(
    mixed_ref,
    low_ref,
    high_ref,
    hidden_ref,
    column_ref,
    gain_ref,
    router_ref,
    middle_ref,
    normed_ref,
    gates_ref,
):
    groups = mixed_ref.shape[0]
    mixed = jnp.concatenate([mixed_ref[g] for g in range(groups)], 1)
    half = low_ref.shape[0]
    middle = dot(mixed[:, :half], low_ref[...]) + dot(mixed[:, half:], high_ref[...])
    middle = flat(hidden_ref).astype(jnp.float32) + middle
    middle_ref[...] = middle
    scale = lax.rsqrt(jnp.mean(middle * middle, -1, keepdims=True) + EPS)
    normed = (middle * scale * gain_ref[...]).astype(jnp.bfloat16)
    normed_ref[...] = normed
    logits = dot(normed, router_ref[...])
    columns = flat(column_ref).astype(jnp.float32)
    number = lax.broadcasted_iota(jnp.int32, logits.shape, 1).astype(jnp.float32)
    named = columns[:, 3:4] == number
    for slot in range(1, TOPK):
        named = named | (columns[:, 3 + slot : 4 + slot] == number)
    logits = jnp.where(named, logits, MASK_FLOOR)
    shifted = jnp.exp(logits - jnp.max(logits, -1, keepdims=True))
    shifted = jnp.where(named, shifted, 0.0)
    gates_ref[...] = shifted / jnp.sum(shifted, -1, keepdims=True)


def middle_rows(mixed, weights, gathered, gain, router, own, block):
    groups, tokens, width = mixed.shape
    features = gain.shape[0]
    experts = router.shape[1]
    rows = lambda columns: pl.BlockSpec((block, columns), lambda i: (i, 0))
    return pl.pallas_call(
        middle_kernel,
        out_shape=(
            jax.ShapeDtypeStruct((tokens, features), jnp.float32),
            jax.ShapeDtypeStruct((tokens, features), jnp.bfloat16),
            jax.ShapeDtypeStruct((tokens, experts), jnp.float32),
        ),
        grid=(tokens // block,),
        in_specs=[
            pl.BlockSpec((groups, block, width), lambda i: (0, i, 0)),
            whole_block(*weights[0].shape),
            whole_block(*weights[1].shape),
            *token_rows(block, own, features),
            whole_block(1, features),
            whole_block(features, experts),
        ],
        out_specs=[rows(features), rows(features), rows(experts)],
        compiler_params=pltpu.CompilerParams(vmem_limit_bytes=48 << 20),
        cost_estimate=pl.CostEstimate(
            flops=2 * tokens * features * groups * width,
            bytes_accessed=12 * tokens * features,
            transcendentals=0,
        ),
    )(mixed, *weights, gathered, gathered, gain[None, :], router)


def slot_of(e, keeps, experts_own):
    pick = experts_own // 2
    high, low = e // pick, e % pick
    return (1 - (high ^ keeps)) * pick + low


def expert_kernel(
    place_ref,
    normed_ref,
    cotangent_ref,
    column_ref,
    gates_ref,
    gate_weight_ref,
    up_weight_ref,
    down_weight_ref,
    scaled_one_ref,
    scaled_two_ref,
    grad_gate_ref,
    grad_up_ref,
    grad_live_ref,
    extra_ref,
):
    experts_own = gate_weight_ref.shape[0]
    experts_all = gates_ref.shape[1]
    first = place_ref[1] * experts_own
    live = flat(column_ref).astype(jnp.float32)[:, :1] > 0
    grad_live_ref[...] = jnp.where(live, cotangent_ref[...], jnp.zeros((), jnp.bfloat16))
    gates = gates_ref[...]
    number = lax.broadcasted_iota(jnp.int32, gates.shape, 1)

    def one_expert(e, grad_gates):
        one = slot_of(e, place_ref[2], experts_own)
        two = slot_of(e, place_ref[3], experts_own)
        gate = jnp.sum(jnp.where(number == first + e, gates, 0.0), -1, keepdims=True)
        gate_pre = dot(normed_ref[...], gate_weight_ref[e])
        up_pre = dot(normed_ref[...], up_weight_ref[e])
        grad_plain = dot(grad_live_ref[...], down_weight_ref[e], COLUMNS)
        sigma = jax.nn.sigmoid(gate_pre)
        silu = gate_pre * sigma
        acted = silu * up_pre
        grad_acted = gate * grad_plain
        scaled = (gate * acted).astype(jnp.bfloat16)
        scaled_one_ref[one] = scaled
        scaled_two_ref[two] = scaled
        grad_gate_ref[one] = (
            grad_acted * up_pre * (sigma * (1.0 + gate_pre * (1.0 - sigma)))
        ).astype(jnp.bfloat16)
        grad_up_ref[two] = (grad_acted * silu).astype(jnp.bfloat16)
        return grad_gates + jnp.where(
            number == first + e, jnp.sum(acted * grad_plain, -1, keepdims=True), 0.0
        )

    grad_gates = lax.fori_loop(
        0, experts_own, one_expert, jnp.zeros(gates.shape, jnp.float32)
    )
    rough = grad_gates.astype(jnp.bfloat16)
    fine = (grad_gates - rough.astype(jnp.float32)).astype(jnp.bfloat16)
    rest = jnp.zeros((gates.shape[0], extra_ref.shape[1] - 2 * experts_all), jnp.bfloat16)
    extra_ref[...] = jnp.concatenate([rough, fine, rest], 1)


def expert_rows(place, normed, cotangent, gathered, gates, w_gate, w_up, w_down, own, block):
    tokens, features = normed.shape
    experts_own, _, hidden = w_gate.shape
    experts_all = gates.shape[1]
    rows = lambda columns: pl.BlockSpec((block, columns), lambda i, p: (i, 0))
    spread = pl.BlockSpec((experts_own, block, hidden), lambda i, p: (0, i, 0))
    wide = jax.ShapeDtypeStruct((experts_own, tokens, hidden), jnp.bfloat16)
    return pl.pallas_call(
        expert_kernel,
        out_shape=(
            wide,
            wide,
            wide,
            wide,
            jax.ShapeDtypeStruct((tokens, features), jnp.bfloat16),
            jax.ShapeDtypeStruct((tokens, 128), jnp.bfloat16),
        ),
        grid_spec=pltpu.PrefetchScalarGridSpec(
            num_scalar_prefetch=1,
            grid=(tokens // block,),
            in_specs=[
                rows(features),
                rows(features),
                token_rows(block, own, features)[1],
                rows(experts_all),
                whole_block(*w_gate.shape),
                whole_block(*w_up.shape),
                whole_block(*w_down.shape),
            ],
            out_specs=[spread, spread, spread, spread, rows(features), rows(128)],
        ),
        compiler_params=pltpu.CompilerParams(vmem_limit_bytes=52 << 20),
        cost_estimate=pl.CostEstimate(
            flops=6 * tokens * features * hidden * experts_own,
            bytes_accessed=6 * features * hidden * experts_own + 10 * tokens * features,
            transcendentals=tokens * hidden * experts_own,
        ),
    )(place, normed, cotangent, gathered, gates, w_gate, w_up, w_down)


def product_kernel(
    left_ref,
    gate_ref,
    up_ref,
    scaled_one_ref,
    scaled_two_ref,
    live_one_ref,
    live_two_ref,
    out_one_ref,
    out_two_ref,
):
    step = pl.program_id(0)
    tile, hidden = left_ref.shape[1], gate_ref.shape[1]
    narrow = live_one_ref.shape[1]
    tops = pl.num_programs(0) - 3
    top = tops * tile

    @pl.when(step < tops)
    def _():
        here = pl.ds(pl.multiple_of(step * tile, tile), tile)
        both = dot(left_ref[...], jnp.concatenate([gate_ref[...], up_ref[...]], 1), ROWS)
        out_one_ref[here, :] = both[:, :hidden].astype(out_one_ref.dtype)
        out_two_ref[here, :] = both[:, hidden:].astype(out_two_ref.dtype)

    @pl.when(step >= tops)
    def _():
        part = step - tops
        for scaled_ref, live_ref, out_ref in (
            (scaled_one_ref, live_one_ref, out_one_ref),
            (scaled_two_ref, live_two_ref, out_two_ref),
        ):
            product = dot(scaled_ref[...], live_ref[...], ROWS).astype(out_ref.dtype)

            @pl.when(part < 2)
            def _():
                there = pl.ds(pl.multiple_of(part * narrow, narrow), narrow)
                out_ref[top : top + hidden, there] = product

            @pl.when(part == 2)
            def _():
                out_ref[top + hidden :, :narrow] = product[:narrow]
                out_ref[top + hidden :, narrow:] = product[narrow:]


def expert_products(left, gate, up, scaled_one, scaled_two, live, e, dtype):
    tokens, features = left.shape
    hidden = gate.shape[2]
    narrow = hidden // 2
    tile = 512
    tops = features // tile
    rows = features + features // 2
    stack = pl.BlockSpec((None, tokens, hidden), lambda i: (e, 0, 0), pipeline_mode=pl.Buffered(1))
    lives = [
        pl.BlockSpec((tokens, narrow), lambda i, side=side: (0, 3 * side + jnp.maximum(i - tops, 0)))
        for side in range(2)
    ]
    out = pl.BlockSpec((rows, hidden), lambda i: (0, 0), pipeline_mode=pl.Buffered(1))
    return pl.pallas_call(
        product_kernel,
        out_shape=(jax.ShapeDtypeStruct((rows, hidden), dtype),) * 2,
        grid=(tops + 3,),
        in_specs=[
            pl.BlockSpec((tokens, tile), lambda i: (0, jnp.minimum(i, tops - 1))),
            stack,
            stack,
            stack,
            stack,
            *lives,
        ],
        out_specs=[out, out],
        compiler_params=pltpu.CompilerParams(vmem_limit_bytes=58 << 20),
        cost_estimate=pl.CostEstimate(flops=0, bytes_accessed=tokens, transcendentals=0),
    )(left, gate, up, scaled_one, scaled_two, live, live)


def rows_kernel(
    place_ref,
    scaled_ref,
    grad_gate_ref,
    grad_up_ref,
    extra_ref,
    gate_weight_ref,
    up_weight_ref,
    down_weight_ref,
    grad_ref,
    out_ref,
):
    experts_own = scaled_ref.shape[0]
    features = out_ref.shape[1]
    one = [slot_of(e, place_ref[2], experts_own) for e in range(experts_own)]
    two = [slot_of(e, place_ref[3], experts_own) for e in range(experts_own)]
    size = 512

    @pl.loop(0, features // size)
    def _(index):
        part = pl.ds(pl.multiple_of(index * size, size), size)
        grad = 0.0
        out = 0.0
        for e in range(experts_own):
            grad = grad + dot(grad_gate_ref[one[e]], gate_weight_ref[e, part, :], COLUMNS)
            grad = grad + dot(grad_up_ref[two[e]], up_weight_ref[e, part, :], COLUMNS)
            out = out + dot(scaled_ref[one[e]], down_weight_ref[e, :, part])
        grad_ref[:, part] = grad.astype(jnp.bfloat16)
        out_ref[:, part] = out.astype(jnp.bfloat16)

    grad_ref[:, features:] = extra_ref[...]


def expert_sums(place, scaled, grad_gate_pre, grad_up_pre, extra, w_gate, w_up, w_down, block):
    experts_own, tokens, hidden = scaled.shape
    features = w_gate.shape[1]
    rows = lambda columns: pl.BlockSpec((block, columns), lambda i, p: (i, 0))
    spread = pl.BlockSpec((experts_own, block, hidden), lambda i, p: (0, i, 0))
    return pl.pallas_call(
        rows_kernel,
        out_shape=(
            jax.ShapeDtypeStruct((tokens, features + extra.shape[1]), jnp.bfloat16),
            jax.ShapeDtypeStruct((tokens, features), jnp.bfloat16),
        ),
        grid_spec=pltpu.PrefetchScalarGridSpec(
            num_scalar_prefetch=1,
            grid=(tokens // block,),
            in_specs=[
                spread,
                spread,
                spread,
                rows(extra.shape[1]),
                whole_block(*w_gate.shape),
                whole_block(*w_up.shape),
                whole_block(*w_down.shape),
            ],
            out_specs=[rows(features + extra.shape[1]), rows(features)],
        ),
        compiler_params=pltpu.CompilerParams(vmem_limit_bytes=52 << 20),
        cost_estimate=pl.CostEstimate(flops=0, bytes_accessed=tokens, transcendentals=0),
    )(place, scaled, grad_gate_pre, grad_up_pre, extra, w_gate, w_up, w_down)


def turn_kernel(
    sum_ref,
    gates_ref,
    router_ref,
    gain_ref,
    middle_ref,
    live_ref,
    low_ref,
    high_ref,
    grad_middle_ref,
    branch_ref,
    mixed_ref,
    logits_ref,
    gain_grad_ref,
):
    features = middle_ref.shape[1]
    experts = gates_ref.shape[1]
    groups, _, width = mixed_ref.shape
    extra = sum_ref[:, features:].astype(jnp.float32)
    grad_gates = extra[:, :experts] + extra[:, experts : 2 * experts]
    gates = gates_ref[...]
    grad_logits = gates * (grad_gates - jnp.sum(gates * grad_gates, -1, keepdims=True))
    grad_logits = grad_logits.astype(jnp.bfloat16)
    logits_ref[...] = grad_logits
    grad = sum_ref[:, :features].astype(jnp.float32) + dot(grad_logits, router_ref[...], COLUMNS)
    middle = middle_ref[...]
    scale = lax.rsqrt(jnp.mean(middle * middle, -1, keepdims=True) + EPS)
    base = middle * scale
    gain_grad_ref[...] = jnp.sum(grad * base, 0, keepdims=True)
    grad_middle = live_ref[...].astype(jnp.float32) + norm_back(grad * gain_ref[...], base, scale)
    grad_middle_ref[...] = grad_middle
    branch = grad_middle.astype(jnp.bfloat16)
    branch_ref[...] = branch
    for half, weight_ref in enumerate((low_ref, high_ref)):
        mixed = dot(branch, weight_ref[...], COLUMNS).astype(jnp.bfloat16)
        for g in range(groups // 2):
            mixed_ref[half * (groups // 2) + g] = mixed[:, g * width : (g + 1) * width]


def turn_rows(sums, gates, router, gain, middle, live, weights):
    own, features = middle.shape
    experts = gates.shape[1]
    groups = KEY_VALUE_HEADS
    shaped = jax.ShapeDtypeStruct
    return pl.pallas_call(
        turn_kernel,
        out_shape=(
            shaped((own, features), jnp.float32),
            shaped((own, features), jnp.bfloat16),
            shaped((groups, own, features // groups), jnp.bfloat16),
            shaped((own, experts), jnp.bfloat16),
            shaped((1, features), jnp.float32),
        ),
        compiler_params=pltpu.CompilerParams(vmem_limit_bytes=58 << 20),
        cost_estimate=pl.CostEstimate(flops=0, bytes_accessed=own, transcendentals=0),
    )(sums, gates, router, gain[None, :], middle, live, *weights)


def close_kernel(
    query_ref,
    pair_ref,
    weight_ref,
    hidden_ref,
    normed_ref,
    gain_two_ref,
    normed_own_ref,
    logits_ref,
    rows_ref,
    grad_ref,
    head_ref,
    product_ref,
    gain_ref,
):
    step = pl.program_id(0)
    width = query_ref.shape[1]
    both = width + pair_ref.shape[1]
    query = query_ref[...]
    pair = pair_ref[...]
    grad = dot(query, weight_ref[:, :width], COLUMNS) + dot(
        pair, weight_ref[:, width:both], COLUMNS
    )
    grad_ref[:, : grad.shape[1]] = grad.astype(jnp.bfloat16)
    grad_ref[:, grad.shape[1] :] = rows_ref[...]
    hidden = flat(hidden_ref).astype(jnp.float32)
    scale = lax.rsqrt(jnp.mean(hidden * hidden, -1, keepdims=True) + EPS)
    normed = normed_ref[...]

    @pl.when(step == 0)
    def _():
        gain_ref[...] = jnp.zeros_like(gain_ref)
        product_ref[...] = jnp.zeros_like(product_ref)

    gain_ref[...] += jnp.sum(grad * (hidden * scale), 0, keepdims=True)
    product_ref[:, :width] += dot(normed, query, ROWS)
    product_ref[:, width:] += dot(normed, pair, ROWS)

    @pl.when(step == pl.num_programs(0) - 1)
    def _():
        features = product_ref.shape[0]
        rows = head_ref.shape[0]
        experts = logits_ref.shape[1]
        side = head_ref.shape[1] // (features // rows)
        gains = jnp.concatenate(
            [gain_ref[...], gain_two_ref[...], jnp.zeros((6, features), jnp.float32)], 0
        )
        gains = jnp.transpose(gains)
        router = dot(normed_own_ref[...], logits_ref[...], ROWS)
        for c in range(features // rows):
            part = slice(c * rows, (c + 1) * rows)
            rest = jnp.zeros((rows, side - both - 8 - experts), jnp.float32)
            head_ref[:, c * side : (c + 1) * side] = jnp.concatenate(
                [product_ref[part, :], gains[part], router[part], rest], 1
            )


def close_rows(
    query,
    pair,
    weight,
    gathered,
    normed,
    gain_two_grad,
    normed_own,
    logits,
    out_rows,
    rows_own,
    side,
    block,
):
    tokens, features = normed.shape
    both = query.shape[1] + pair.shape[1]
    rows = lambda width: pl.BlockSpec((block, width), lambda i: (i, 0))
    resident = lambda *shape: pl.BlockSpec(shape, lambda i: (0,) * len(shape))
    shaped = jax.ShapeDtypeStruct
    head = (rows_own, features // rows_own * side)
    return pl.pallas_call(
        close_kernel,
        out_shape=(shaped((tokens, 2 * features), jnp.bfloat16), shaped(head, jnp.float32)),
        grid=(tokens // block,),
        in_specs=[
            rows(query.shape[1]),
            rows(pair.shape[1]),
            whole_block(*weight.shape),
            token_rows(block, normed_own.shape[0], features)[0],
            rows(features),
            whole_block(1, features),
            whole_block(*normed_own.shape),
            whole_block(*logits.shape),
            rows(features),
        ],
        out_specs=[rows(2 * features), resident(*head)],
        scratch_shapes=[
            pltpu.VMEM((features, both), jnp.float32),
            pltpu.VMEM((1, features), jnp.float32),
        ],
        compiler_params=pltpu.CompilerParams(vmem_limit_bytes=48 << 20),
        cost_estimate=pl.CostEstimate(flops=0, bytes_accessed=tokens, transcendentals=0),
    )(query, pair, weight, gathered, normed, gain_two_grad, normed_own, logits, out_rows)


def head_kernel(copies, side, low_ref, high_ref, query_ref, key_ref, value_ref, out_ref, small_ref):
    groups = KEY_VALUE_HEADS
    count = groups * copies
    halves = [low_ref[...].astype(jnp.float32), high_ref[...].astype(jnp.float32)]
    width = query_ref.shape[1] // groups
    parts = []
    for c in range(count):
        place = c % (count // 2) * side
        parts.append(halves[c // (count // 2)][:, place : place + side])
    heads = []
    small = 0.0
    for g in range(groups):
        total = parts[g * copies]
        for p in range(1, copies):
            total = total + parts[g * copies + p]
        heads.append(total)
        small = small + total[:, width + 2 * HEAD_SIZE :]
    small_ref[...] = small
    query_ref[...] = jnp.concatenate([head[:, :width] for head in heads], 1)
    key_ref[...] = jnp.concatenate([head[:, width : width + HEAD_SIZE] for head in heads], 1)
    value_ref[...] = jnp.concatenate(
        [head[:, width + HEAD_SIZE : width + 2 * HEAD_SIZE] for head in heads], 1
    )
    out_ref[...] = jnp.concatenate([half[:, count // 2 * side :] for half in halves], 1)


def head_outputs(low, high, copies, side):
    rows = low.shape[0]
    groups = KEY_VALUE_HEADS
    query_width = QUERY_HEADS * HEAD_SIZE
    shaped = lambda width: jax.ShapeDtypeStruct((rows, width), jnp.float32)
    return pl.pallas_call(
        lambda *refs: head_kernel(copies, side, *refs),
        name="head_outputs",
        out_shape=(
            shaped(query_width),
            shaped(groups * HEAD_SIZE),
            shaped(groups * HEAD_SIZE),
            shaped(MODEL_WIDTH),
            shaped(side - (query_width // groups + 2 * HEAD_SIZE)),
        ),
        compiler_params=pltpu.CompilerParams(vmem_limit_bytes=40 << 20),
        cost_estimate=pl.CostEstimate(flops=0, bytes_accessed=rows, transcendentals=0),
    )(low, high)


def into_kernel(keeps_ref, side, sent_ref, first_ref, second_ref, out_ref):
    kept = pl.program_id(0) == keeps_ref[side]
    came = jnp.where(pl.program_id(1) == 0, first_ref[...], second_ref[...])
    out_ref[...] = jnp.where(kept, sent_ref[...], came).astype(jnp.float32)


def into_output(keeps, side, sent, first, second):
    rows, hidden = first.shape
    part = lambda index: pl.BlockSpec((rows, hidden), index)
    return pl.pallas_call(
        lambda k, *refs: into_kernel(k, side, *refs),
        name="into_output",
        out_shape=jax.ShapeDtypeStruct((2, 2 * rows, hidden), jnp.float32),
        grid_spec=pltpu.PrefetchScalarGridSpec(
            num_scalar_prefetch=1,
            grid=(2, 2),
            in_specs=[
                part(lambda e, h, k: (h, 0)),
                part(lambda e, h, k: (0, 0)),
                part(lambda e, h, k: (0, 0)),
            ],
            out_specs=pl.BlockSpec((None, rows, hidden), lambda e, h, k: (e, h, 0)),
        ),
        compiler_params=pltpu.CompilerParams(vmem_limit_bytes=32 << 20),
        cost_estimate=pl.CostEstimate(flops=0, bytes_accessed=rows, transcendentals=0),
    )(keeps, sent, first, second)


def down_kernel(keeps_ref, sent_low_ref, came_low_ref, sent_high_ref, came_high_ref, out_ref):
    rows, hidden = came_low_ref.shape
    narrow = hidden // 2
    pairs = ((sent_low_ref, came_low_ref), (sent_high_ref, came_high_ref))
    for side, (sent_ref, came_ref) in enumerate(pairs):
        kept = pl.program_id(0) == keeps_ref[side]
        value = jnp.where(kept, sent_ref[...], came_ref[...]).astype(jnp.float32)
        start = side * rows
        out_ref[:, start : start + hidden] = value[:hidden]
        out_ref[:narrow, start + hidden : start + rows] = value[hidden:, :narrow]
        out_ref[narrow:, start + hidden : start + rows] = value[hidden:, narrow:]


def down_output(keeps, sent_low, came_low, sent_high, came_high):
    rows, hidden = came_low.shape
    place = sent_low.shape[0] // rows - 1
    sent = pl.BlockSpec((rows, hidden), lambda e, k: (place, 0))
    came = pl.BlockSpec((rows, hidden), lambda e, k: (0, 0))
    return pl.pallas_call(
        down_kernel,
        out_shape=jax.ShapeDtypeStruct((2, hidden, 2 * rows), jnp.float32),
        grid_spec=pltpu.PrefetchScalarGridSpec(
            num_scalar_prefetch=1,
            grid=(2,),
            in_specs=[sent, came, sent, came],
            out_specs=pl.BlockSpec((None, hidden, 2 * rows), lambda e, k: (e, 0, 0)),
        ),
        compiler_params=pltpu.CompilerParams(vmem_limit_bytes=32 << 20),
        cost_estimate=pl.CostEstimate(flops=0, bytes_accessed=rows, transcendentals=0),
    )(keeps, sent_low, came_low, sent_high, came_high)


def after(values, *others):
    values, _ = lax.optimization_barrier((values, others))
    return values


def swap(value, bit):
    size = lax.axis_size("rep")
    return lax.ppermute(value, "rep", [(i, i ^ bit) for i in range(size)])


def has(bit):
    return (lax.axis_index("rep") & bit) != 0


def halve(value, came, bit):
    half = value.shape[0] // 2
    keep = jnp.where(has(bit), half, 0)
    part = lambda array, start: lax.dynamic_slice_in_dim(array, start, half, 0).astype(jnp.float32)
    kept = part(value, keep)
    sent = part(value, half - keep)
    if came is not None:
        kept = kept + part(came, keep)
        sent = sent + part(came, half - keep)
    return kept, sent.astype(jnp.bfloat16)


def join(value, came, bit, axis):
    upper = has(bit)
    return jnp.concatenate(
        [jnp.where(upper, came, value), jnp.where(upper, value, came)], axis
    )


class Chain:
    def __init__(self, order):
        self.order = order
        self.stage = 0
        self.steps = 2 * len(order)

    def send(self, sent):
        bit = self.order[min(self.stage, self.steps - 1 - self.stage)]
        self.sent = sent
        self.stage += 1
        if self.stage < self.steps:
            self.flying = swap(sent, bit)

    def step(self, *others):
        bits = len(self.order)
        came = after(self.flying, *others)
        if self.stage < bits:
            self.kept, sent = halve(self.kept, came, self.order[self.stage])
            self.send(sent)
        elif self.stage == bits:
            self.send((self.kept + came.astype(jnp.float32)).astype(jnp.bfloat16))
        else:
            self.send(join(self.sent, came, self.order[self.steps - self.stage], 0))
        return self.sent

    def piece(self, number, count, *others):
        rows = self.sent.shape[0] // count
        part = after(self.sent[number * rows : (number + 1) * rows], *others)
        return swap(part, self.order[0])


class Cube:
    def __init__(self, value, order):
        self.value = value
        self.order = order
        self.stage = 0

    def axis(self, bit):
        return len(self.order) - bit.bit_length()

    def halve(self, *others):
        bit = self.order[self.stage]
        keep = has(bit).astype(jnp.int32)
        part = lambda index: lax.dynamic_slice_in_dim(self.value, index, 1, self.axis(bit))
        self.value, sent = part(keep), part(1 - keep).astype(jnp.bfloat16)
        self.flying = swap(after(sent, *others), bit)
        self.stage += 1
        return sent

    def add(self, *others):
        self.value = self.value + after(self.flying, *others).astype(jnp.float32)

    def back(self, *others):
        self.stage -= 1
        self.flying = swap(after(self.value, *others), self.order[self.stage])
        return self.value

    def join(self, *others):
        bit = self.order[self.stage]
        self.value = join(self.value, after(self.flying, *others), bit, self.axis(bit))


class Exchange:
    def __init__(self, fetched, bits):
        size = fetched.shape[0]
        fetched = fetched.reshape((size,) + (1,) * len(bits) + fetched.shape[1:])
        self.values = [fetched[: size // 2], fetched[size // 2 :]]
        self.orders = (bits, bits[::-1])
        self.stage = 0
        self.fly()

    def fly(self):
        self.flying = [
            swap(value, order[self.stage]) for value, order in zip(self.values, self.orders)
        ]

    def step(self, *others):
        bits = len(self.orders[0])
        for h, order in enumerate(self.orders):
            bit = order[self.stage]
            came = after(self.flying[h], *others)
            self.values[h] = join(self.values[h], came, bit, bits - (bit.bit_length() - 1))
        self.stage += 1
        if self.stage < bits:
            self.fly()
        return list(self.values)

    def finish(self, *others):
        while self.stage < len(self.orders[0]):
            self.step(*others)
        return [value.reshape(-1, value.shape[-1]) for value in self.values]


def per_device(
    inputs,
    segments,
    positions,
    expert_ids,
    attn_gain,
    w_query,
    key_weight,
    value_weight,
    w_out,
    ffn_gain,
    router,
    w_gate,
    w_up,
    w_down,
    grad_out,
):
    size = lax.axis_size("ctx")
    me = lax.axis_index("ctx")
    reps = lax.axis_size("rep")
    bits = [1 << i for i in range(reps.bit_length() - 1)]
    own = inputs.shape[1]
    tokens = size * own
    groups = KEY_VALUE_HEADS
    copies = size // groups
    query_width = HEAD_GROUP * HEAD_SIZE
    width = query_width + 2 * HEAD_SIZE
    copy_index = me % copies
    rows_own = w_out.shape[0]
    experts_own = w_gate.shape[0]
    experts_all = size * experts_own
    block = 2 * own
    chips = size // 2
    chip = me // 2
    odd = me % 2 == 1
    share = rows_own // reps
    share_start = lax.axis_index("rep") * share

    columns = jnp.concatenate(
        [
            segments[0][:, None],
            positions[0][:, None] // 64,
            positions[0][:, None] % 64,
            expert_ids[0],
        ],
        1,
    ).astype(jnp.bfloat16)
    columns = jnp.pad(columns, ((0, 0), (0, 128 - columns.shape[1])))
    shared = lambda array: lax.dynamic_slice_in_dim(array, share_start, share, 0)

    rows = jnp.concatenate(
        [
            jnp.concatenate([inputs[0], columns], 1),
            jnp.pad(shared(w_out), ((0, 0), (0, 128))),
        ],
        0,
    )
    gathered = lax.all_gather(rows, "ctx", axis=0)
    cotangent = lax.all_gather(after(grad_out[0], rows), "ctx", axis=0, tiled=True)

    def from_chip(value, k):
        return lax.ppermute(value, "ctx", [(i, (i - 2 * k) % size) for i in range(size)])

    def from_core(value):
        return lax.ppermute(value, "ctx", [(i, i ^ 1) for i in range(size)])

    def cores(mine, others, axis):
        return jnp.concatenate(
            [jnp.where(odd, others, mine), jnp.where(odd, mine, others)], axis
        )

    side_width = -(-(width + 2 + router.shape[1]) // 128) * 128
    head_columns = jnp.concatenate(
        [
            shared(w_query).reshape(share, groups, query_width),
            shared(key_weight).reshape(share, groups, HEAD_SIZE),
            shared(value_weight).reshape(share, groups, HEAD_SIZE),
            jnp.broadcast_to(shared(attn_gain)[:, None, None], (share, groups, 1)),
            jnp.broadcast_to(shared(ffn_gain)[:, None, None], (share, groups, 1)),
            jnp.broadcast_to(shared(router)[:, None, :], (share, groups, router.shape[1])),
        ],
        -1,
    )
    used = head_columns.shape[-1]
    head_columns = jnp.pad(head_columns, ((0, 0), (0, 0), (0, side_width - used)))
    head_columns = jnp.repeat(jnp.transpose(head_columns, (1, 0, 2)), copies, 0)
    head_columns = lax.all_to_all(head_columns, "ctx", split_axis=0, concat_axis=0, tiled=True)
    head_halves = Exchange(head_columns, bits).finish()
    head_all = jnp.concatenate(head_halves, 0)
    gain_one = head_all[:, width].astype(jnp.float32)
    gain_two = head_all[:, width + 1].astype(jnp.float32)
    router_all = head_all[:, width + 2 : used]

    (
        normed_one,
        query,
        key,
        value,
        mixed,
        log_total,
        cosine_table,
        sine_table,
        segment_rows,
    ) = attend(gathered, gain_one, head_halves, own, block)
    out_exchange = Exchange(gathered[:, own:, :MODEL_WIDTH], bits)

    part = tokens // copies
    mixed_all = lax.all_gather(
        after(
            lax.dynamic_slice_in_dim(mixed, copy_index * part, part, 0), cotangent, out_exchange.step()
        ),
        "ctx",
        axis=0,
    ).reshape(groups, tokens, query_width)
    w_out_halves = out_exchange.finish()

    middle, normed_two, gates = middle_rows(
        mixed_all, w_out_halves, gathered, gain_two, router_all, own, block
    )
    flag = lambda bit: has(bit).astype(jnp.int32)
    place = jnp.stack([chip, me, flag(bits[0]), flag(bits[-1])]).astype(jnp.int32)
    scaled_one, scaled_two, grad_gate_pre, grad_up_pre, grad_live, extra = expert_rows(
        place, normed_two, cotangent, gathered, gates, w_gate, w_up, w_down, own, block
    )
    grad_rows, out_rows = expert_sums(
        place, scaled_one, grad_gate_pre, grad_up_pre, extra, w_gate, w_up, w_down, block
    )
    grad_two_sum = lax.psum_scatter(grad_rows, "ctx", scatter_dimension=0, tiled=True)

    def mine(array):
        return lax.dynamic_slice_in_dim(array, me * own, own, 0)

    middle_own, gates_own, live_own, normed_own = [
        mine(array) for array in (middle, gates, grad_live, normed_two)
    ]

    products = lambda e, dtype: expert_products(
        normed_two, grad_gate_pre, grad_up_pre, scaled_one, scaled_two, grad_live, e, dtype
    )
    normed_two, grad_live = after((normed_two, grad_live), grad_rows)
    chains = [Chain(bits), Chain(bits[::-1])]
    for chain, sent in zip(chains, products(0, jnp.bfloat16)):
        chain.send(sent)
    normed_two, grad_live = after((normed_two, grad_live), *[chain.sent for chain in chains])
    for chain, kept in zip(chains, products(1, jnp.float32)):
        chain.kept = kept

    grad_middle, grad_branch, grad_mixed, grad_logits, gain_two_grad = turn_rows(
        after(grad_two_sum, *[(c.kept, c.flying) for c in chains]),
        gates_own,
        router_all,
        gain_two,
        middle_own,
        live_own,
        w_out_halves,
    )

    def deal(blocks, *others):
        blocks = blocks.reshape((chips, 2) + blocks.shape[1:])
        got = [blocks[(chip - k) % chips] for k in range(chips)]
        got = jnp.stack([got[0]] + [from_chip(got[k], k) for k in range(1, chips)])
        got = after(got, *others)
        stay = jnp.where(odd, got[:, 1], got[:, 0])
        go = from_core(jnp.where(odd, got[:, 0], got[:, 1]))
        both = cores(stay[:, None], go[:, None], 1)
        both = jnp.concatenate([both, both], 0)
        both = lax.dynamic_slice_in_dim(both, (chips - chip) % chips, chips, 0)
        return both.reshape((size,) + both.shape[2:])

    sent = [grad_mixed]
    while chains[0].stage <= len(bits):
        sent = [chain.step(*sent) for chain in chains]
    grad_mixed_all = deal(jnp.repeat(grad_mixed, copies, 0), *sent).reshape(tokens, query_width)
    grad_branch_all = lax.all_gather(
        after(grad_branch, grad_mixed_all), "ctx", axis=0, tiled=True
    )
    grad_query, grad_pair = attend_back(
        query,
        grad_mixed_all,
        log_total,
        cosine_table,
        sine_table,
        gathered,
        segment_rows,
        key,
        value,
        own,
    )
    if copies > 1:
        places = jnp.arange(tokens, dtype=jnp.int32)
        counted = (places // part == copy_index)[:, None]
        grad_query = jnp.where(counted, grad_query, jnp.zeros((), jnp.bfloat16))
        grad_pair = jnp.where(counted, grad_pair, jnp.zeros((), jnp.bfloat16))
    both_rows, head_grads = close_rows(
        grad_query,
        grad_pair,
        head_all,
        gathered,
        normed_one,
        gain_two_grad,
        normed_own,
        grad_logits,
        out_rows,
        rows_own,
        side_width,
        block,
    )
    both_sums = lax.psum_scatter(
        both_rows, "ctx", scatter_dimension=0, tiled=True
    ).astype(jnp.float32)
    grad_one, out_sum = both_sums[:, :MODEL_WIDTH], both_sums[:, MODEL_WIDTH:]
    grad_proj_out = dot(
        lax.dynamic_slice_in_dim(mixed, copy_index * rows_own, rows_own, 1),
        grad_branch_all,
        ROWS,
    )

    line = size // 2 * side_width
    half = MODEL_WIDTH // 2
    cubes = []
    for h, order in enumerate((bits, bits[::-1])):
        rows = jnp.concatenate(
            [
                head_grads[:, h * line : (h + 1) * line],
                grad_proj_out[:, h * half : (h + 1) * half],
            ],
            1,
        )
        cubes.append(Cube(rows.reshape((2,) * len(bits) + (share, line + half)), order))
    sent = [cube.halve() for cube in cubes]
    while chains[0].stage < chains[0].steps:
        sent = [chain.step(*sent) for chain in chains]
    first = [chain.piece(0, 3) for chain in chains]
    while cubes[0].stage < len(bits):
        for cube in cubes:
            cube.add(*sent)
        sent = [cube.halve() for cube in cubes]
    second = [chain.piece(1, 3, *sent) for chain in chains]
    for cube in cubes:
        cube.add(*first)
    totals = [cube.value.astype(jnp.bfloat16) for cube in cubes]
    blocks = jnp.concatenate(
        [
            jnp.transpose(
                total.reshape(share, -1)[:, :line].reshape(share, size // 2, side_width), (1, 0, 2)
            )
            for total in totals
        ],
        0,
    )
    head_sums = deal(blocks)
    for h, cube in enumerate(cubes):
        rows = jnp.transpose(head_sums[h * (size // 2) : (h + 1) * (size // 2)], (1, 0, 2))
        rows = jnp.concatenate(
            [rows.reshape(share, line), totals[h].reshape(share, -1)[:, line:]], 1
        )
        cube.value = rows.reshape(totals[h].shape)
    sent = [cube.back(*second) for cube in cubes]
    third = [chain.piece(2, 3, *sent) for chain in chains]
    keeps = place[2:]
    grad_gate, grad_up = [
        into_output(keeps, side, *after((chain.sent, first[side], second[side]), *sent))
        for side, chain in enumerate(chains)
    ]
    while cubes[0].stage > 0:
        for cube in cubes:
            cube.join(*sent)
        sent = [cube.back() for cube in cubes]
    grad_down = down_output(
        keeps, *after((chains[0].sent, third[0], chains[1].sent, third[1]), grad_gate, grad_up)
    )
    for cube in cubes:
        cube.join(grad_down)
    head_outs = head_outputs(
        *[cube.value.reshape(rows_own, -1) for cube in cubes], copies, side_width
    )
    small = head_outs[4]
    output = jnp.where((segments[0] != 0)[:, None], middle_own + out_sum, 0.0)
    own_hidden = inputs[0].astype(jnp.float32)
    own_scale = lax.rsqrt(jnp.mean(own_hidden * own_hidden, -1, keepdims=True) + EPS)
    grad_in = grad_middle + norm_back(grad_one * gain_one, own_hidden * own_scale, own_scale)
    return (
        output.astype(jnp.bfloat16)[None],
        grad_in[None],
        small[:, 0],
        *head_outs[:4],
        small[:, 1],
        small[:, 8 : 8 + experts_all],
        grad_gate,
        grad_up,
        grad_down,
    )


def solution(mesh):
    return jax.shard_map(
        per_device,
        mesh=mesh,
        in_specs=(
            P("rep", "ctx", None),
            P("rep", "ctx"),
            P("rep", "ctx"),
            P("rep", "ctx", None),
            P("ctx"),
            P("ctx", None),
            P("ctx", None),
            P("ctx", None),
            P("ctx", None),
            P("ctx"),
            P("ctx", None),
            P("ctx", None, None),
            P("ctx", None, None),
            P("ctx", None, None),
            P("rep", "ctx", None),
        ),
        out_specs=(
            P("rep", "ctx", None),
            P("rep", "ctx", None),
            P("ctx"),
            P("ctx", None),
            P("ctx", None),
            P("ctx", None),
            P("ctx", None),
            P("ctx"),
            P("ctx", None),
            P("ctx", None, None),
            P("ctx", None, None),
            P("ctx", None, None),
        ),
        check_vma=False,
    )
```

```python
import jax
import jax.numpy as jnp
from jax import lax
from jax.experimental import pallas as pl
from jax.experimental.pallas import tpu as pltpu
from jax.sharding import PartitionSpec as P

MODEL_WIDTH = 1536
QUERY_HEADS = 24
KEY_VALUE_HEADS = 8
HEAD_GROUP = QUERY_HEADS // KEY_VALUE_HEADS
HEAD_SIZE = 64
TOPK = 8

EPS = 1e-06
THETA = 10000.0
MASK_FLOOR = -1e30

ROWS = (((0,), (0,)), ((), ()))
COLUMNS = (((1,), (1,)), ((), ()))


def dot(left, right, contract=(((1,), (0,)), ((), ()))):
    return lax.dot_general(left, right, contract, preferred_element_type=jnp.float32)


def norm_back(grad_base, base, scale):
    return scale * (grad_base - base * jnp.mean(grad_base * base, -1, keepdims=True))


def turn(rows):
    half = HEAD_SIZE // 2
    return jnp.concatenate([-rows[:, half:], rows[:, :half]], 1)


def turn_back(rows):
    half = HEAD_SIZE // 2
    return jnp.concatenate([rows[:, half:], -rows[:, :half]], 1)


def stack_heads(rows):
    return jnp.concatenate(
        [rows[:, h * HEAD_SIZE : (h + 1) * HEAD_SIZE] for h in range(HEAD_GROUP)], 0
    )


def side_heads(rows):
    block = rows.shape[0] // HEAD_GROUP
    return jnp.concatenate([rows[h * block : (h + 1) * block] for h in range(HEAD_GROUP)], 1)


def lanes(values, combine):
    total = values[:, :128]
    for start in range(128, values.shape[1], 128):
        total = combine(total, values[:, start : start + 128])
    return total


def masked_scores(stacked, keys, row_segments, key_segments, row_start, key_start):
    block = row_segments.shape[0]
    scores = dot(stacked, keys, COLUMNS) * HEAD_SIZE ** (-0.5)
    row_place = row_start + lax.broadcasted_iota(jnp.int32, (block, block), 0)
    key_place = key_start + lax.broadcasted_iota(jnp.int32, (block, block), 1)
    allowed = (row_segments == key_segments) & (key_place <= row_place)
    scores = scores.reshape(HEAD_GROUP, block, block)
    return jnp.where(allowed[None], scores, MASK_FLOOR).reshape(HEAD_GROUP * block, block)


def first_block(row_segments, segment_ref, step):
    here = jnp.max(row_segments[:1, :1])
    segments = segment_ref[...]
    number = lax.broadcasted_iota(jnp.int32, segments.shape, 0)
    return jnp.min(jnp.where((segments == here) & (number <= step), number, step))


def token_rows(block, own, features):
    count = block // own
    return (
        pl.BlockSpec((count, own, features), lambda i, *_: (i, 0, 0)),
        pl.BlockSpec((count, own, 128), lambda i, *_: (i, 0, features // 128)),
    )


def flat(ref):
    return ref[...].reshape(-1, ref.shape[-1])


def whole_block(*shape):
    return pl.BlockSpec(shape, lambda *i: (0,) * len(shape), pipeline_mode=pl.Buffered(1))


def attend_kernel(
    hidden_ref,
    column_ref,
    gain_ref,
    low_ref,
    high_ref,
    rate_ref,
    normed_ref,
    query_ref,
    key_ref,
    value_ref,
    mixed_ref,
    packed_ref,
    log_ref,
    cosine_ref,
    sine_ref,
    segment_ref,
    score_ref,
):
    step = pl.program_id(0)
    block = query_ref.shape[0]
    query_width = query_ref.shape[1]
    width = query_width + 2 * HEAD_SIZE
    here = pl.ds(pl.multiple_of(step * block, block), block)
    columns = flat(column_ref).astype(jnp.float32)
    row_segments = columns[:, :1]
    segment_ref[step] = jnp.transpose(columns)[:1, :]
    angles = (columns[:, 1:2] * 64.0 + columns[:, 2:3]) * rate_ref[...]
    cosine = jnp.cos(angles)
    sine = jnp.sin(angles)
    cosine_ref[...] = cosine
    sine_ref[...] = sine
    hidden = flat(hidden_ref).astype(jnp.float32)
    scale = lax.rsqrt(jnp.mean(hidden * hidden, -1, keepdims=True) + EPS)
    normed = (hidden * scale * gain_ref[...]).astype(jnp.bfloat16)
    normed_ref[...] = normed
    middle = low_ref.shape[0]
    raw = dot(normed[:, :middle], low_ref[:, :width]) + dot(
        normed[:, middle:], high_ref[:, :width]
    )
    key_raw = raw[:, query_width : query_width + HEAD_SIZE]
    key_ref[here, :] = (key_raw * cosine + turn(key_raw) * sine).astype(jnp.bfloat16)
    value_ref[here, :] = raw[:, query_width + HEAD_SIZE :].astype(jnp.bfloat16)
    query_raw = stack_heads(raw[:, :query_width])
    cosine = jnp.concatenate([cosine] * HEAD_GROUP, 0)
    sine = jnp.concatenate([sine] * HEAD_GROUP, 0)
    query = (query_raw * cosine + turn(query_raw) * sine).astype(jnp.bfloat16)
    query_ref[...] = side_heads(query)
    rows = HEAD_GROUP * block
    first = first_block(row_segments, segment_ref, step)

    def first_pass(index, top):
        there = pl.ds(pl.multiple_of(index * block, block), block)
        scores = masked_scores(
            query,
            key_ref[there, :],
            row_segments,
            segment_ref[index],
            step * block,
            index * block,
        )
        score_ref[index] = scores
        return jnp.maximum(top, lanes(scores, jnp.maximum))

    top = lax.fori_loop(
        first, step + 1, first_pass, jnp.full((rows, 128), MASK_FLOOR, jnp.float32)
    )
    top = jnp.max(top, -1, keepdims=True)

    def second_pass(index, carry):
        total, mixed = carry
        there = pl.ds(pl.multiple_of(index * block, block), block)
        weights = jnp.exp(score_ref[index] - top)
        mixed = mixed + dot(weights.astype(jnp.bfloat16), value_ref[there, :])
        return total + lanes(weights, jnp.add), mixed

    total, mixed = lax.fori_loop(
        first,
        step + 1,
        second_pass,
        (
            jnp.zeros((rows, 128), jnp.float32),
            jnp.zeros((rows, HEAD_SIZE), jnp.float32),
        ),
    )
    total = jnp.sum(total, -1, keepdims=True)
    mixed = side_heads((mixed / total).astype(jnp.bfloat16))
    mixed_ref[...] = mixed
    packed_ref[...] = jnp.concatenate([mixed[: block // 2], mixed[block // 2 :]], 1)
    log_ref[...] = (top + jnp.log(total)).reshape(HEAD_GROUP, block, 1)


def attend(gathered, gain, weights, own, block):
    tokens, features = gathered.shape[0] * own, gain.shape[0]
    query_width = HEAD_GROUP * HEAD_SIZE
    steps = tokens // block
    half = jnp.arange(HEAD_SIZE // 2, dtype=jnp.float32)
    rate = THETA ** (-(2.0 * half) / HEAD_SIZE)
    rate = jnp.concatenate([rate, rate])[None, :]
    rows = lambda width: pl.BlockSpec((block, width), lambda i: (i, 0))
    resident = lambda *shape: pl.BlockSpec(shape, lambda i: (0,) * len(shape))
    shaped = jax.ShapeDtypeStruct
    return pl.pallas_call(
        attend_kernel,
        out_shape=(
            shaped((tokens, features), jnp.bfloat16),
            shaped((tokens, query_width), jnp.bfloat16),
            shaped((tokens, HEAD_SIZE), jnp.bfloat16),
            shaped((tokens, HEAD_SIZE), jnp.bfloat16),
            shaped((tokens, query_width), jnp.bfloat16),
            shaped((tokens // 2, 2 * query_width), jnp.bfloat16),
            shaped((HEAD_GROUP, tokens, 1), jnp.float32),
            shaped((tokens, HEAD_SIZE), jnp.float32),
            shaped((tokens, HEAD_SIZE), jnp.float32),
            shaped((steps, 1, block), jnp.float32),
        ),
        grid=(steps,),
        in_specs=[
            *token_rows(block, own, features),
            whole_block(1, features),
            whole_block(*weights[0].shape),
            whole_block(*weights[1].shape),
            whole_block(1, HEAD_SIZE),
        ],
        out_specs=[
            rows(features),
            rows(query_width),
            resident(tokens, HEAD_SIZE),
            resident(tokens, HEAD_SIZE),
            rows(query_width),
            pl.BlockSpec((block // 2, 2 * query_width), lambda i: (i, 0)),
            pl.BlockSpec((HEAD_GROUP, block, 1), lambda i: (0, i, 0)),
            rows(HEAD_SIZE),
            rows(HEAD_SIZE),
            resident(steps, 1, block),
        ],
        scratch_shapes=[pltpu.VMEM((steps, HEAD_GROUP * block, block), jnp.float32)],
        compiler_params=pltpu.CompilerParams(vmem_limit_bytes=48 << 20),
        cost_estimate=pl.CostEstimate(flops=0, bytes_accessed=tokens, transcendentals=0),
    )(gathered, gathered, gain[None, :], *weights, rate)


def attend_back_kernel(
    query_ref,
    grad_ref,
    log_ref,
    cosine_ref,
    sine_ref,
    column_ref,
    segment_ref,
    key_ref,
    value_ref,
    key_cosine_ref,
    key_sine_ref,
    grad_query_ref,
    grad_pair_ref,
    probs_ref,
    grad_probs_ref,
    grad_key_ref,
    grad_value_ref,
):
    step = pl.program_id(0)
    block = query_ref.shape[0]
    rows = HEAD_GROUP * block

    @pl.when(step == 0)
    def _():
        grad_key_ref[...] = jnp.zeros_like(grad_key_ref)
        grad_value_ref[...] = jnp.zeros_like(grad_value_ref)

    query = stack_heads(query_ref[...])
    grad = stack_heads(grad_ref[...])
    log_total = log_ref[...].reshape(rows, 1)
    row_segments = flat(column_ref).astype(jnp.float32)[:, :1]
    first = first_block(row_segments, segment_ref, step)

    def first_pass(index, delta):
        there = pl.ds(pl.multiple_of(index * block, block), block)
        scores = masked_scores(
            query,
            key_ref[there, :],
            row_segments,
            segment_ref[index],
            step * block,
            index * block,
        )
        probs = jnp.exp(scores - log_total)
        grad_probs = dot(grad, value_ref[there, :], COLUMNS)
        probs_ref[index] = probs
        grad_probs_ref[index] = grad_probs
        grad_value_ref[there, :] += dot(probs.astype(jnp.bfloat16), grad, ROWS)
        return delta + lanes(probs * grad_probs, jnp.add)

    delta = lax.fori_loop(first, step + 1, first_pass, jnp.zeros((rows, 128), jnp.float32))
    delta = jnp.sum(delta, -1, keepdims=True)

    def second_pass(index, grad_query):
        there = pl.ds(pl.multiple_of(index * block, block), block)
        grad_scores = (probs_ref[index] * (grad_probs_ref[index] - delta)).astype(jnp.bfloat16)
        grad_key_ref[there, :] += dot(grad_scores, query, ROWS)
        return grad_query + dot(grad_scores, key_ref[there, :])

    grad_query = lax.fori_loop(
        first, step + 1, second_pass, jnp.zeros((rows, HEAD_SIZE), jnp.float32)
    )
    score_scale = HEAD_SIZE ** (-0.5)
    cosine = jnp.concatenate([cosine_ref[...]] * HEAD_GROUP, 0)
    sine = jnp.concatenate([sine_ref[...]] * HEAD_GROUP, 0)
    grad_query = grad_query * score_scale
    grad_query = grad_query * cosine + turn_back(grad_query * sine)
    grad_query_ref[...] = side_heads(grad_query.astype(jnp.bfloat16))

    @pl.when(step == pl.num_programs(0) - 1)
    def _():
        @pl.loop(0, pl.num_programs(0))
        def _(index):
            there = pl.ds(pl.multiple_of(index * block, block), block)
            grad_key = grad_key_ref[there, :] * score_scale
            turned = turn_back(grad_key * key_sine_ref[there, :])
            grad_key = grad_key * key_cosine_ref[there, :] + turned
            grad_pair_ref[there, :] = jnp.concatenate(
                [grad_key, grad_value_ref[there, :]], 1
            ).astype(jnp.bfloat16)


def attend_back(query, grad, log_total, cosine, sine, gathered, segments, key, value, own):
    tokens, query_width = query.shape
    steps, _, block = segments.shape
    features = gathered.shape[2] - 128
    rows = lambda width: pl.BlockSpec((block, width), lambda i: (i, 0))
    resident = lambda *shape: pl.BlockSpec(shape, lambda i: (0,) * len(shape))
    return pl.pallas_call(
        attend_back_kernel,
        out_shape=(
            jax.ShapeDtypeStruct((tokens, query_width), jnp.bfloat16),
            jax.ShapeDtypeStruct((tokens, 2 * HEAD_SIZE), jnp.bfloat16),
        ),
        grid=(steps,),
        in_specs=[
            rows(query_width),
            rows(query_width),
            pl.BlockSpec((HEAD_GROUP, block, 1), lambda i: (0, i, 0)),
            rows(HEAD_SIZE),
            rows(HEAD_SIZE),
            token_rows(block, own, features)[1],
            whole_block(steps, 1, block),
            whole_block(tokens, HEAD_SIZE),
            whole_block(tokens, HEAD_SIZE),
            whole_block(tokens, HEAD_SIZE),
            whole_block(tokens, HEAD_SIZE),
        ],
        out_specs=[rows(query_width), resident(tokens, 2 * HEAD_SIZE)],
        scratch_shapes=[
            pltpu.VMEM((steps, HEAD_GROUP * block, block), jnp.float32),
            pltpu.VMEM((steps, HEAD_GROUP * block, block), jnp.float32),
            pltpu.VMEM((tokens, HEAD_SIZE), jnp.float32),
            pltpu.VMEM((tokens, HEAD_SIZE), jnp.float32),
        ],
        compiler_params=pltpu.CompilerParams(vmem_limit_bytes=48 << 20),
        cost_estimate=pl.CostEstimate(flops=0, bytes_accessed=tokens, transcendentals=0),
    )(query, grad, log_total, cosine, sine, gathered, segments, key, value, cosine, sine)


def middle_kernel(
    mixed_ref,
    low_ref,
    high_ref,
    hidden_ref,
    column_ref,
    gain_ref,
    router_ref,
    middle_ref,
    normed_ref,
    gates_ref,
    mixed_low_ref,
    mixed_high_ref,
):
    groups = mixed_ref.shape[0]
    width = mixed_ref.shape[2] // 2
    mixed = jnp.concatenate(
        [
            jnp.concatenate([mixed_ref[g, :, side : side + width] for g in range(groups)], 1)
            for side in (0, width)
        ],
        0,
    )
    half = low_ref.shape[0]
    mixed_low_ref[...] = mixed[:, :half]
    mixed_high_ref[...] = mixed[:, half:]
    size = 512

    @pl.loop(0, middle_ref.shape[1] // size)
    def _(index):
        part = pl.ds(pl.multiple_of(index * size, size), size)
        hidden = hidden_ref[:, :, part].reshape(-1, size).astype(jnp.float32)
        middle_ref[:, part] = (
            hidden
            + dot(mixed_low_ref[...], low_ref[:, part])
            + dot(mixed_high_ref[...], high_ref[:, part])
        )

    middle = middle_ref[...]
    scale = lax.rsqrt(jnp.mean(middle * middle, -1, keepdims=True) + EPS)
    normed = (middle * scale * gain_ref[...]).astype(jnp.bfloat16)
    normed_ref[...] = normed
    logits = dot(normed, router_ref[...])
    columns = flat(column_ref).astype(jnp.float32)
    number = lax.broadcasted_iota(jnp.int32, logits.shape, 1).astype(jnp.float32)
    named = columns[:, 3:4] == number
    for slot in range(1, TOPK):
        named = named | (columns[:, 3 + slot : 4 + slot] == number)
    logits = jnp.where(named, logits, MASK_FLOOR)
    shifted = jnp.exp(logits - jnp.max(logits, -1, keepdims=True))
    shifted = jnp.where(named, shifted, 0.0)
    gates_ref[...] = shifted / jnp.sum(shifted, -1, keepdims=True)


def middle_rows(mixed, weights, gathered, gain, router, own, block):
    groups, _, width = mixed.shape
    tokens = gathered.shape[0] * own
    features = gain.shape[0]
    experts = router.shape[1]
    rows = lambda columns: pl.BlockSpec((block, columns), lambda i: (i, 0))
    return pl.pallas_call(
        middle_kernel,
        out_shape=(
            jax.ShapeDtypeStruct((tokens, features), jnp.float32),
            jax.ShapeDtypeStruct((tokens, features), jnp.bfloat16),
            jax.ShapeDtypeStruct((tokens, experts), jnp.float32),
        ),
        grid=(tokens // block,),
        in_specs=[
            pl.BlockSpec((groups, block // 2, width), lambda i: (0, i, 0)),
            whole_block(*weights[0].shape),
            whole_block(*weights[1].shape),
            *token_rows(block, own, features),
            whole_block(1, features),
            whole_block(features, experts),
        ],
        out_specs=[rows(features), rows(features), rows(experts)],
        scratch_shapes=[pltpu.VMEM((block, weights[0].shape[0]), jnp.bfloat16)] * 2,
        compiler_params=pltpu.CompilerParams(vmem_limit_bytes=48 << 20),
        cost_estimate=pl.CostEstimate(
            flops=tokens * features * groups * width,
            bytes_accessed=12 * tokens * features,
            transcendentals=0,
        ),
    )(mixed, *weights, gathered, gathered, gain[None, :], router)


def slot_of(e, keeps, experts_own):
    pick = experts_own // 2
    high, low = e // pick, e % pick
    return (1 - (high ^ keeps)) * pick + low


def expert_kernel(
    place_ref,
    normed_ref,
    cotangent_ref,
    column_ref,
    gates_ref,
    gate_weight_ref,
    up_weight_ref,
    down_weight_ref,
    scaled_one_ref,
    scaled_two_ref,
    grad_gate_ref,
    grad_up_ref,
    grad_live_ref,
    extra_ref,
):
    experts_own = gate_weight_ref.shape[0]
    experts_all = gates_ref.shape[1]
    first = place_ref[1] * experts_own
    live = flat(column_ref).astype(jnp.float32)[:, :1] > 0
    grad_live_ref[...] = jnp.where(live, cotangent_ref[...], jnp.zeros((), jnp.bfloat16))
    gates = gates_ref[...]
    number = lax.broadcasted_iota(jnp.int32, gates.shape, 1)

    def one_expert(e, grad_gates):
        one = slot_of(e, place_ref[2], experts_own)
        two = slot_of(e, place_ref[3], experts_own)
        gate = jnp.sum(jnp.where(number == first + e, gates, 0.0), -1, keepdims=True)
        gate_pre = dot(normed_ref[...], gate_weight_ref[e])
        up_pre = dot(normed_ref[...], up_weight_ref[e])
        grad_plain = dot(grad_live_ref[...], down_weight_ref[e], COLUMNS)
        sigma = jax.nn.sigmoid(gate_pre)
        silu = gate_pre * sigma
        acted = silu * up_pre
        grad_acted = gate * grad_plain
        scaled = (gate * acted).astype(jnp.bfloat16)
        scaled_one_ref[one] = scaled
        scaled_two_ref[two] = scaled
        grad_gate_ref[one] = (
            grad_acted * up_pre * (sigma * (1.0 + gate_pre * (1.0 - sigma)))
        ).astype(jnp.bfloat16)
        grad_up_ref[two] = (grad_acted * silu).astype(jnp.bfloat16)
        return grad_gates + jnp.where(
            number == first + e, jnp.sum(acted * grad_plain, -1, keepdims=True), 0.0
        )

    grad_gates = lax.fori_loop(
        0, experts_own, one_expert, jnp.zeros(gates.shape, jnp.float32)
    )
    rough = grad_gates.astype(jnp.bfloat16)
    fine = (grad_gates - rough.astype(jnp.float32)).astype(jnp.bfloat16)
    rest = jnp.zeros((gates.shape[0], extra_ref.shape[1] - 2 * experts_all), jnp.bfloat16)
    extra_ref[...] = jnp.concatenate([rough, fine, rest], 1)


def expert_rows(place, normed, cotangent, gathered, gates, w_gate, w_up, w_down, own, block):
    tokens, features = normed.shape
    experts_own, _, hidden = w_gate.shape
    experts_all = gates.shape[1]
    rows = lambda columns: pl.BlockSpec((block, columns), lambda i, p: (i, 0))
    spread = pl.BlockSpec((experts_own, block, hidden), lambda i, p: (0, i, 0))
    wide = jax.ShapeDtypeStruct((experts_own, tokens, hidden), jnp.bfloat16)
    return pl.pallas_call(
        expert_kernel,
        out_shape=(
            wide,
            wide,
            wide,
            wide,
            jax.ShapeDtypeStruct((tokens, features), jnp.bfloat16),
            jax.ShapeDtypeStruct((tokens, 128), jnp.bfloat16),
        ),
        grid_spec=pltpu.PrefetchScalarGridSpec(
            num_scalar_prefetch=1,
            grid=(tokens // block,),
            in_specs=[
                rows(features),
                rows(features),
                token_rows(block, own, features)[1],
                rows(experts_all),
                whole_block(*w_gate.shape),
                whole_block(*w_up.shape),
                whole_block(*w_down.shape),
            ],
            out_specs=[spread, spread, spread, spread, rows(features), rows(128)],
        ),
        compiler_params=pltpu.CompilerParams(vmem_limit_bytes=52 << 20),
        cost_estimate=pl.CostEstimate(
            flops=6 * tokens * features * hidden * experts_own,
            bytes_accessed=6 * features * hidden * experts_own + 10 * tokens * features,
            transcendentals=tokens * hidden * experts_own,
        ),
    )(place, normed, cotangent, gathered, gates, w_gate, w_up, w_down)


def product_kernel(
    left_ref,
    gate_ref,
    up_ref,
    scaled_one_ref,
    scaled_two_ref,
    live_one_ref,
    live_two_ref,
    out_one_ref,
    out_two_ref,
):
    step = pl.program_id(0)
    tile, hidden = left_ref.shape[1], gate_ref.shape[1]
    narrow = live_one_ref.shape[1]
    tops = pl.num_programs(0) - 3
    top = tops * tile

    @pl.when(step < tops)
    def _():
        here = pl.ds(pl.multiple_of(step * tile, tile), tile)
        both = dot(left_ref[...], jnp.concatenate([gate_ref[...], up_ref[...]], 1), ROWS)
        out_one_ref[here, :] = both[:, :hidden].astype(out_one_ref.dtype)
        out_two_ref[here, :] = both[:, hidden:].astype(out_two_ref.dtype)

    @pl.when(step >= tops)
    def _():
        part = step - tops
        for scaled_ref, live_ref, out_ref in (
            (scaled_one_ref, live_one_ref, out_one_ref),
            (scaled_two_ref, live_two_ref, out_two_ref),
        ):
            product = dot(scaled_ref[...], live_ref[...], ROWS).astype(out_ref.dtype)

            @pl.when(part < 2)
            def _():
                there = pl.ds(pl.multiple_of(part * narrow, narrow), narrow)
                out_ref[top : top + hidden, there] = product

            @pl.when(part == 2)
            def _():
                out_ref[top + hidden :, :narrow] = product[:narrow]
                out_ref[top + hidden :, narrow:] = product[narrow:]


def expert_products(left, gate, up, scaled_one, scaled_two, live, e, dtype):
    tokens, features = left.shape
    hidden = gate.shape[2]
    narrow = hidden // 2
    tile = 512
    tops = features // tile
    rows = features + features // 2
    stack = pl.BlockSpec((None, tokens, hidden), lambda i: (e, 0, 0), pipeline_mode=pl.Buffered(1))
    lives = [
        pl.BlockSpec((tokens, narrow), lambda i, side=side: (0, 3 * side + jnp.maximum(i - tops, 0)))
        for side in range(2)
    ]
    out = pl.BlockSpec((rows, hidden), lambda i: (0, 0), pipeline_mode=pl.Buffered(1))
    return pl.pallas_call(
        product_kernel,
        out_shape=(jax.ShapeDtypeStruct((rows, hidden), dtype),) * 2,
        grid=(tops + 3,),
        in_specs=[
            pl.BlockSpec((tokens, tile), lambda i: (0, jnp.minimum(i, tops - 1))),
            stack,
            stack,
            stack,
            stack,
            *lives,
        ],
        out_specs=[out, out],
        compiler_params=pltpu.CompilerParams(vmem_limit_bytes=58 << 20),
        cost_estimate=pl.CostEstimate(flops=0, bytes_accessed=tokens, transcendentals=0),
    )(left, gate, up, scaled_one, scaled_two, live, live)


def rows_kernel(
    place_ref,
    scaled_ref,
    grad_gate_ref,
    grad_up_ref,
    extra_ref,
    gate_weight_ref,
    up_weight_ref,
    down_weight_ref,
    grad_ref,
    out_ref,
):
    experts_own = scaled_ref.shape[0]
    features = out_ref.shape[1]
    one = [slot_of(e, place_ref[2], experts_own) for e in range(experts_own)]
    two = [slot_of(e, place_ref[3], experts_own) for e in range(experts_own)]
    size = 512

    @pl.loop(0, features // size)
    def _(index):
        part = pl.ds(pl.multiple_of(index * size, size), size)
        grad = 0.0
        out = 0.0
        for e in range(experts_own):
            grad = grad + dot(grad_gate_ref[one[e]], gate_weight_ref[e, part, :], COLUMNS)
            grad = grad + dot(grad_up_ref[two[e]], up_weight_ref[e, part, :], COLUMNS)
            out = out + dot(scaled_ref[one[e]], down_weight_ref[e, :, part])
        grad_ref[:, part] = grad.astype(jnp.bfloat16)
        out_ref[:, part] = out.astype(jnp.bfloat16)

    grad_ref[:, features:] = extra_ref[...]


def expert_sums(place, scaled, grad_gate_pre, grad_up_pre, extra, w_gate, w_up, w_down, block):
    experts_own, tokens, hidden = scaled.shape
    features = w_gate.shape[1]
    rows = lambda columns: pl.BlockSpec((block, columns), lambda i, p: (i, 0))
    spread = pl.BlockSpec((experts_own, block, hidden), lambda i, p: (0, i, 0))
    return pl.pallas_call(
        rows_kernel,
        out_shape=(
            jax.ShapeDtypeStruct((tokens, features + extra.shape[1]), jnp.bfloat16),
            jax.ShapeDtypeStruct((tokens, features), jnp.bfloat16),
        ),
        grid_spec=pltpu.PrefetchScalarGridSpec(
            num_scalar_prefetch=1,
            grid=(tokens // block,),
            in_specs=[
                spread,
                spread,
                spread,
                rows(extra.shape[1]),
                whole_block(*w_gate.shape),
                whole_block(*w_up.shape),
                whole_block(*w_down.shape),
            ],
            out_specs=[rows(features + extra.shape[1]), rows(features)],
        ),
        compiler_params=pltpu.CompilerParams(vmem_limit_bytes=52 << 20),
        cost_estimate=pl.CostEstimate(flops=0, bytes_accessed=tokens, transcendentals=0),
    )(place, scaled, grad_gate_pre, grad_up_pre, extra, w_gate, w_up, w_down)


def turn_kernel(
    place_ref,
    sum_ref,
    gates_ref,
    router_ref,
    gain_ref,
    middle_ref,
    live_ref,
    low_ref,
    high_ref,
    grad_middle_ref,
    branch_ref,
    mixed_ref,
    logits_ref,
    gain_grad_ref,
):
    features = middle_ref.shape[1]
    experts = gates_ref.shape[1]
    groups, _, width = mixed_ref.shape
    extra = sum_ref[:, features:].astype(jnp.float32)
    grad_gates = extra[:, :experts] + extra[:, experts : 2 * experts]
    gates = gates_ref[...]
    grad_logits = gates * (grad_gates - jnp.sum(gates * grad_gates, -1, keepdims=True))
    grad_logits = grad_logits.astype(jnp.bfloat16)
    logits_ref[...] = grad_logits
    grad = sum_ref[:, :features].astype(jnp.float32) + dot(grad_logits, router_ref[...], COLUMNS)
    middle = middle_ref[...]
    scale = lax.rsqrt(jnp.mean(middle * middle, -1, keepdims=True) + EPS)
    base = middle * scale
    gain_grad_ref[...] = jnp.sum(grad * base, 0, keepdims=True)
    grad_middle = live_ref[...].astype(jnp.float32) + norm_back(grad * gain_ref[...], base, scale)
    grad_middle_ref[...] = grad_middle
    branch = grad_middle.astype(jnp.bfloat16)
    branch_ref[...] = branch
    for half, weight_ref in enumerate((low_ref, high_ref)):

        @pl.loop(0, groups // 2)
        def _(g):
            part = weight_ref[pl.ds(pl.multiple_of(g * width, width), width), :]
            mixed_ref[half * (groups // 2) + g] = dot(branch_ref[...], part, COLUMNS).astype(
                jnp.bfloat16
            )


def turn_rows(place, sums, gates, router, gain, middle, live, weights):
    own, features = sums.shape[0], middle.shape[1]
    experts = gates.shape[1]
    groups = KEY_VALUE_HEADS
    shaped = jax.ShapeDtypeStruct
    rows = lambda width: pl.BlockSpec((own, width), lambda i, p: (p[1], 0))
    resident = lambda *shape: pl.BlockSpec(shape, lambda i, p: (0,) * len(shape))
    outs = (
        shaped((own, features), jnp.float32),
        shaped((own, features), jnp.bfloat16),
        shaped((groups, own, features // groups), jnp.bfloat16),
        shaped((own, experts), jnp.bfloat16),
        shaped((1, features), jnp.float32),
    )
    return pl.pallas_call(
        turn_kernel,
        out_shape=outs,
        grid_spec=pltpu.PrefetchScalarGridSpec(
            num_scalar_prefetch=1,
            grid=(1,),
            in_specs=[
                whole_block(*sums.shape),
                rows(experts),
                whole_block(*router.shape),
                whole_block(1, features),
                rows(features),
                rows(features),
                whole_block(*weights[0].shape),
                whole_block(*weights[1].shape),
            ],
            out_specs=[resident(*out.shape) for out in outs],
        ),
        compiler_params=pltpu.CompilerParams(vmem_limit_bytes=58 << 20),
        cost_estimate=pl.CostEstimate(flops=0, bytes_accessed=own, transcendentals=0),
    )(place, sums, gates, router, gain[None, :], middle, live, *weights)


def close_kernel(
    reps,
    place_ref,
    query_ref,
    pair_ref,
    weight_ref,
    hidden_ref,
    normed_ref,
    gain_two_ref,
    normed_own_ref,
    logits_ref,
    rows_ref,
    mixed_ref,
    branch_ref,
    grad_ref,
    kept_one_ref,
    kept_two_ref,
    sent_one_ref,
    sent_two_ref,
    product_ref,
    gain_ref,
    out_ref,
    head_ref,
):
    step = pl.program_id(0)
    both = query_ref.shape[1] + pair_ref.shape[1]
    heads = jnp.concatenate([query_ref[...], pair_ref[...]], 1)
    grad = dot(heads, weight_ref[:, :both], COLUMNS)
    grad_ref[:, : grad.shape[1]] = grad.astype(jnp.bfloat16)
    grad_ref[:, grad.shape[1] :] = rows_ref[...]
    hidden = flat(hidden_ref).astype(jnp.float32)
    scale = lax.rsqrt(jnp.mean(hidden * hidden, -1, keepdims=True) + EPS)
    normed = normed_ref[...]

    @pl.when(step == 0)
    def _():
        gain_ref[...] = jnp.zeros_like(gain_ref)
        product_ref[...] = jnp.zeros_like(product_ref)
        out_ref[...] = jnp.zeros_like(out_ref)

    gain_ref[...] += jnp.sum(grad * (hidden * scale), 0, keepdims=True)
    product_ref[...] += dot(normed, heads, ROWS)
    out_ref[...] += dot(mixed_ref[...], branch_ref[...], ROWS)

    @pl.when(step == pl.num_programs(0) - 1)
    def _():
        features = product_ref.shape[0]
        rows = out_ref.shape[0]
        share = rows // reps
        experts = logits_ref.shape[1]
        line = kept_one_ref.shape[1]
        count = features // rows
        side = (line - features // 2) // (count // 2)
        gains = jnp.concatenate(
            [gain_ref[...], gain_two_ref[...], jnp.zeros((6, features), jnp.float32)], 0
        )
        gains = jnp.transpose(gains)
        router = dot(normed_own_ref[...], logits_ref[...], ROWS)
        rest = jnp.zeros((rows, side - both - 8 - experts), jnp.float32)
        for h in range(2):
            for c in range(count // 2):
                place = h * (count // 2) + c
                part = slice(place * rows, (place + 1) * rows)
                head_ref[h, :, c * side : (c + 1) * side] = jnp.concatenate(
                    [product_ref[part, :], gains[part], router[part], rest], 1
                )
            half = features // 2
            head_ref[h, :, count // 2 * side :] = out_ref[:, h * half : (h + 1) * half]
        sides = ((0, kept_one_ref, sent_one_ref), (1, kept_two_ref, sent_two_ref))
        for h, kept_ref, sent_ref in sides:
            bit = 1 if h == 0 else reps // 2
            for index in range(reps // 2):
                base = index // bit * 2 * bit + index % bit
                here = slice(index * share, (index + 1) * share)
                lower = head_ref[h, base * share : (base + 1) * share, :]
                upper = head_ref[h, (base + bit) * share : (base + bit + 1) * share, :]
                kept_ref[here, :] = jnp.where(place_ref[2 + h] > 0, upper, lower)
                sent_ref[here, :] = jnp.where(place_ref[2 + h] > 0, lower, upper).astype(jnp.bfloat16)


def close_rows(
    place,
    query,
    pair,
    weight,
    gathered,
    normed,
    gain_two_grad,
    normed_two,
    logits,
    out_rows,
    mixed,
    branch,
    reps,
    side,
    block,
):
    tokens, features = normed.shape
    own = logits.shape[0]
    both = query.shape[1] + pair.shape[1]
    rows_own = mixed.shape[1]
    rows = lambda width: pl.BlockSpec((block, width), lambda i, k: (i, 0))
    resident = lambda *shape: pl.BlockSpec(shape, lambda i, k: (0,) * len(shape))
    shaped = jax.ShapeDtypeStruct
    line = features // rows_own // 2 * side + features // 2
    half = (rows_own // 2, line)
    return pl.pallas_call(
        lambda *refs: close_kernel(reps, *refs),
        name="close",
        out_shape=(
            shaped((tokens, 2 * features), jnp.bfloat16),
            shaped(half, jnp.float32),
            shaped(half, jnp.float32),
            shaped(half, jnp.bfloat16),
            shaped(half, jnp.bfloat16),
        ),
        grid_spec=pltpu.PrefetchScalarGridSpec(
            num_scalar_prefetch=1,
            grid=(tokens // block,),
            in_specs=[
                rows(query.shape[1]),
                rows(pair.shape[1]),
                whole_block(*weight.shape),
                token_rows(block, own, features)[0],
                rows(features),
                whole_block(1, features),
                pl.BlockSpec((own, features), lambda i, p: (p[1], 0)),
                whole_block(*logits.shape),
                rows(features),
                rows(rows_own),
                rows(features),
            ],
            out_specs=[rows(2 * features), *[resident(*half)] * 4],
            scratch_shapes=[
                pltpu.VMEM((features, both), jnp.float32),
                pltpu.VMEM((1, features), jnp.float32),
                pltpu.VMEM((rows_own, features), jnp.float32),
                pltpu.VMEM((2, rows_own, line), jnp.float32),
            ],
        ),
        compiler_params=pltpu.CompilerParams(vmem_limit_bytes=56 << 20),
        cost_estimate=pl.CostEstimate(flops=0, bytes_accessed=tokens, transcendentals=0),
    )(
        place,
        query,
        pair,
        weight,
        gathered,
        normed,
        gain_two_grad,
        normed_two,
        logits,
        out_rows,
        mixed,
        branch,
    )


def head_kernel(copies, side, low_ref, high_ref, query_ref, key_ref, value_ref, out_ref, small_ref):
    groups = KEY_VALUE_HEADS
    count = groups * copies
    halves = [low_ref[...].astype(jnp.float32), high_ref[...].astype(jnp.float32)]
    width = query_ref.shape[1] // groups
    parts = []
    for c in range(count):
        place = c % (count // 2) * side
        parts.append(halves[c // (count // 2)][:, place : place + side])
    heads = []
    small = 0.0
    for g in range(groups):
        total = parts[g * copies]
        for p in range(1, copies):
            total = total + parts[g * copies + p]
        heads.append(total)
        small = small + total[:, width + 2 * HEAD_SIZE :]
    small_ref[...] = small
    query_ref[...] = jnp.concatenate([head[:, :width] for head in heads], 1)
    key_ref[...] = jnp.concatenate([head[:, width : width + HEAD_SIZE] for head in heads], 1)
    value_ref[...] = jnp.concatenate(
        [head[:, width + HEAD_SIZE : width + 2 * HEAD_SIZE] for head in heads], 1
    )
    out_ref[...] = jnp.concatenate([half[:, count // 2 * side :] for half in halves], 1)


def head_outputs(low, high, copies, side):
    rows = low.shape[0]
    groups = KEY_VALUE_HEADS
    query_width = QUERY_HEADS * HEAD_SIZE
    shaped = lambda width: jax.ShapeDtypeStruct((rows, width), jnp.float32)
    return pl.pallas_call(
        lambda *refs: head_kernel(copies, side, *refs),
        name="head_outputs",
        out_shape=(
            shaped(query_width),
            shaped(groups * HEAD_SIZE),
            shaped(groups * HEAD_SIZE),
            shaped(MODEL_WIDTH),
            shaped(side - (query_width // groups + 2 * HEAD_SIZE)),
        ),
        compiler_params=pltpu.CompilerParams(vmem_limit_bytes=40 << 20),
        cost_estimate=pl.CostEstimate(flops=0, bytes_accessed=rows, transcendentals=0),
    )(low, high)


def into_kernel(keeps_ref, side, sent_ref, first_ref, second_ref, out_ref):
    kept = pl.program_id(0) == keeps_ref[side]
    came = jnp.where(pl.program_id(1) == 0, first_ref[...], second_ref[...])
    out_ref[...] = jnp.where(kept, sent_ref[...], came).astype(jnp.float32)


def into_output(keeps, side, sent, first, second):
    rows, hidden = first.shape
    part = lambda index: pl.BlockSpec((rows, hidden), index)
    return pl.pallas_call(
        lambda k, *refs: into_kernel(k, side, *refs),
        name="into_output",
        out_shape=jax.ShapeDtypeStruct((2, 2 * rows, hidden), jnp.float32),
        grid_spec=pltpu.PrefetchScalarGridSpec(
            num_scalar_prefetch=1,
            grid=(2, 2),
            in_specs=[
                part(lambda e, h, k: (h, 0)),
                part(lambda e, h, k: (0, 0)),
                part(lambda e, h, k: (0, 0)),
            ],
            out_specs=pl.BlockSpec((None, rows, hidden), lambda e, h, k: (e, h, 0)),
        ),
        compiler_params=pltpu.CompilerParams(vmem_limit_bytes=32 << 20),
        cost_estimate=pl.CostEstimate(flops=0, bytes_accessed=rows, transcendentals=0),
    )(keeps, sent, first, second)


def down_kernel(keeps_ref, sent_low_ref, came_low_ref, sent_high_ref, came_high_ref, out_ref):
    rows, hidden = came_low_ref.shape
    narrow = hidden // 2
    pairs = ((sent_low_ref, came_low_ref), (sent_high_ref, came_high_ref))
    for side, (sent_ref, came_ref) in enumerate(pairs):
        kept = pl.program_id(0) == keeps_ref[side]
        value = jnp.where(kept, sent_ref[...], came_ref[...]).astype(jnp.float32)
        start = side * rows
        out_ref[:, start : start + hidden] = value[:hidden]
        out_ref[:narrow, start + hidden : start + rows] = value[hidden:, :narrow]
        out_ref[narrow:, start + hidden : start + rows] = value[hidden:, narrow:]


def down_output(keeps, sent_low, came_low, sent_high, came_high):
    rows, hidden = came_low.shape
    place = sent_low.shape[0] // rows - 1
    sent = pl.BlockSpec((rows, hidden), lambda e, k: (place, 0))
    came = pl.BlockSpec((rows, hidden), lambda e, k: (0, 0))
    return pl.pallas_call(
        down_kernel,
        out_shape=jax.ShapeDtypeStruct((2, hidden, 2 * rows), jnp.float32),
        grid_spec=pltpu.PrefetchScalarGridSpec(
            num_scalar_prefetch=1,
            grid=(2,),
            in_specs=[sent, came, sent, came],
            out_specs=pl.BlockSpec((None, hidden, 2 * rows), lambda e, k: (e, 0, 0)),
        ),
        compiler_params=pltpu.CompilerParams(vmem_limit_bytes=32 << 20),
        cost_estimate=pl.CostEstimate(flops=0, bytes_accessed=rows, transcendentals=0),
    )(keeps, sent_low, came_low, sent_high, came_high)


def after(values, *others):
    values, _ = lax.optimization_barrier((values, others))
    return values


def swap(value, bit):
    size = lax.axis_size("rep")
    return lax.ppermute(value, "rep", [(i, i ^ bit) for i in range(size)])


def has(bit):
    return (lax.axis_index("rep") & bit) != 0


def halve(value, came, bit):
    half = value.shape[0] // 2
    keep = jnp.where(has(bit), half, 0)
    part = lambda array, start: lax.dynamic_slice_in_dim(array, start, half, 0).astype(jnp.float32)
    kept = part(value, keep)
    sent = part(value, half - keep)
    if came is not None:
        kept = kept + part(came, keep)
        sent = sent + part(came, half - keep)
    return kept, sent.astype(jnp.bfloat16)


def join(value, came, bit, axis):
    upper = has(bit)
    return jnp.concatenate(
        [jnp.where(upper, came, value), jnp.where(upper, value, came)], axis
    )


class Chain:
    def __init__(self, order):
        self.order = order
        self.stage = 0
        self.steps = 2 * len(order)

    def send(self, sent):
        bit = self.order[min(self.stage, self.steps - 1 - self.stage)]
        self.sent = sent
        self.stage += 1
        if self.stage < self.steps:
            self.flying = swap(sent, bit)

    def step(self, *others):
        bits = len(self.order)
        came = after(self.flying, *others)
        if self.stage < bits:
            self.kept, sent = halve(self.kept, came, self.order[self.stage])
            self.send(sent)
        elif self.stage == bits:
            self.send((self.kept + came.astype(jnp.float32)).astype(jnp.bfloat16))
        else:
            self.send(join(self.sent, came, self.order[self.steps - self.stage], 0))
        return self.sent

    def piece(self, number, count, *others):
        rows = self.sent.shape[0] // count
        part = after(self.sent[number * rows : (number + 1) * rows], *others)
        return swap(part, self.order[0])


class Cube:
    def __init__(self, kept, sent, order, share):
        shape = [2] * len(order)
        shape[len(order) - order[0].bit_length()] = 1
        self.value, sent = [array.reshape(*shape, share, -1) for array in (kept, sent)]
        self.order = order
        self.flying = swap(sent, order[0])
        self.stage = 1

    def axis(self, bit):
        return len(self.order) - bit.bit_length()

    def halve(self, *others):
        bit = self.order[self.stage]
        keep = has(bit).astype(jnp.int32)
        part = lambda index: lax.dynamic_slice_in_dim(self.value, index, 1, self.axis(bit))
        self.value, sent = part(keep), part(1 - keep).astype(jnp.bfloat16)
        self.flying = swap(after(sent, *others), bit)
        self.stage += 1
        return sent

    def add(self, *others):
        self.value = self.value + after(self.flying, *others).astype(jnp.float32)

    def back(self, *others):
        self.stage -= 1
        self.flying = swap(after(self.value, *others), self.order[self.stage])
        return self.value

    def join(self, *others):
        bit = self.order[self.stage]
        self.value = join(self.value, after(self.flying, *others), bit, self.axis(bit))


class Exchange:
    def __init__(self, fetched, bits):
        size = fetched.shape[0]
        fetched = fetched.reshape((size,) + (1,) * len(bits) + fetched.shape[1:])
        self.values = [fetched[: size // 2], fetched[size // 2 :]]
        self.orders = (bits, bits[::-1])
        self.stage = 0
        self.fly()

    def fly(self):
        self.flying = [
            swap(value, order[self.stage]) for value, order in zip(self.values, self.orders)
        ]

    def step(self, *others):
        bits = len(self.orders[0])
        for h, order in enumerate(self.orders):
            bit = order[self.stage]
            came = after(self.flying[h], *others)
            self.values[h] = join(self.values[h], came, bit, bits - (bit.bit_length() - 1))
        self.stage += 1
        if self.stage < bits:
            self.fly()
        return list(self.values)

    def finish(self, *others):
        while self.stage < len(self.orders[0]):
            self.step(*others)
        return [value.reshape(-1, value.shape[-1]) for value in self.values]


def per_device(
    inputs,
    segments,
    positions,
    expert_ids,
    attn_gain,
    w_query,
    key_weight,
    value_weight,
    w_out,
    ffn_gain,
    router,
    w_gate,
    w_up,
    w_down,
    grad_out,
):
    size = lax.axis_size("ctx")
    me = lax.axis_index("ctx")
    reps = lax.axis_size("rep")
    bits = [1 << i for i in range(reps.bit_length() - 1)]
    own = inputs.shape[1]
    tokens = size * own
    groups = KEY_VALUE_HEADS
    copies = size // groups
    query_width = HEAD_GROUP * HEAD_SIZE
    width = query_width + 2 * HEAD_SIZE
    copy_index = me % copies
    rows_own = w_out.shape[0]
    experts_own = w_gate.shape[0]
    experts_all = size * experts_own
    block = 2 * own
    chips = size // 2
    chip = me // 2
    odd = me % 2 == 1
    share = rows_own // reps
    share_start = lax.axis_index("rep") * share

    columns = jnp.concatenate(
        [
            segments[0][:, None],
            positions[0][:, None] // 64,
            positions[0][:, None] % 64,
            expert_ids[0],
        ],
        1,
    ).astype(jnp.bfloat16)
    columns = jnp.pad(columns, ((0, 0), (0, 128 - columns.shape[1])))
    shared = lambda array: lax.dynamic_slice_in_dim(array, share_start, share, 0)

    rows = jnp.concatenate(
        [
            jnp.concatenate([inputs[0], columns], 1),
            jnp.pad(shared(w_out), ((0, 0), (0, 128))),
        ],
        0,
    )
    gathered = lax.all_gather(rows, "ctx", axis=0)
    cotangent = lax.all_gather(after(grad_out[0], rows), "ctx", axis=0, tiled=True)

    def from_chip(value, k):
        return lax.ppermute(value, "ctx", [(i, (i - 2 * k) % size) for i in range(size)])

    def from_core(value):
        return lax.ppermute(value, "ctx", [(i, i ^ 1) for i in range(size)])

    def cores(mine, others, axis):
        return jnp.concatenate(
            [jnp.where(odd, others, mine), jnp.where(odd, mine, others)], axis
        )

    side_width = -(-(width + 2 + router.shape[1]) // 128) * 128
    head_columns = jnp.concatenate(
        [
            shared(w_query).reshape(share, groups, query_width),
            shared(key_weight).reshape(share, groups, HEAD_SIZE),
            shared(value_weight).reshape(share, groups, HEAD_SIZE),
            jnp.broadcast_to(shared(attn_gain)[:, None, None], (share, groups, 1)),
            jnp.broadcast_to(shared(ffn_gain)[:, None, None], (share, groups, 1)),
            jnp.broadcast_to(shared(router)[:, None, :], (share, groups, router.shape[1])),
        ],
        -1,
    )
    used = head_columns.shape[-1]
    head_columns = jnp.pad(head_columns, ((0, 0), (0, 0), (0, side_width - used)))
    head_columns = jnp.repeat(jnp.transpose(head_columns, (1, 0, 2)), copies, 0)
    head_columns = lax.all_to_all(head_columns, "ctx", split_axis=0, concat_axis=0, tiled=True)
    head_halves = Exchange(head_columns, bits).finish()
    head_all = jnp.concatenate(head_halves, 0)
    gain_one = head_all[:, width].astype(jnp.float32)
    gain_two = head_all[:, width + 1].astype(jnp.float32)
    router_all = head_all[:, width + 2 : used]

    (
        normed_one,
        query,
        key,
        value,
        mixed,
        packed,
        log_total,
        cosine_table,
        sine_table,
        segment_rows,
    ) = attend(gathered, gain_one, head_halves, own, block)
    out_exchange = Exchange(gathered[:, own:, :MODEL_WIDTH], bits)

    part = tokens // copies
    mixed_all = lax.all_gather(
        after(
            lax.dynamic_slice_in_dim(packed, copy_index * part // 2, part // 2, 0),
            cotangent,
            out_exchange.step(),
        ),
        "ctx",
        axis=0,
    ).reshape(groups, tokens // 2, 2 * query_width)
    w_out_halves = out_exchange.finish()

    middle, normed_two, gates = middle_rows(
        mixed_all, w_out_halves, gathered, gain_two, router_all, own, block
    )
    flag = lambda bit: has(bit).astype(jnp.int32)
    place = jnp.stack([chip, me, flag(bits[0]), flag(bits[-1])]).astype(jnp.int32)
    scaled_one, scaled_two, grad_gate_pre, grad_up_pre, grad_live, extra = expert_rows(
        place, normed_two, cotangent, gathered, gates, w_gate, w_up, w_down, own, block
    )
    def mine(array):
        return lax.dynamic_slice_in_dim(array, me * own, own, 0)

    products = lambda e, dtype: expert_products(
        normed_two, grad_gate_pre, grad_up_pre, scaled_one, scaled_two, grad_live, e, dtype
    )
    grad_rows, out_rows = expert_sums(
        place, scaled_one, grad_gate_pre, grad_up_pre, extra, w_gate, w_up, w_down, block
    )
    grad_two_sum = lax.psum_scatter(grad_rows, "ctx", scatter_dimension=0, tiled=True)
    normed_two, grad_live = after((normed_two, grad_live), grad_rows)
    chains = [Chain(bits), Chain(bits[::-1])]
    for chain, sent in zip(chains, products(0, jnp.bfloat16)):
        chain.send(sent)
    normed_two, grad_live = after((normed_two, grad_live), *[chain.sent for chain in chains])
    for chain, kept in zip(chains, products(1, jnp.float32)):
        chain.kept = kept

    grad_middle, grad_branch, grad_mixed, grad_logits, gain_two_grad = turn_rows(
        place,
        after(grad_two_sum, *[(c.kept, c.flying) for c in chains]),
        gates,
        router_all,
        gain_two,
        middle,
        grad_live,
        w_out_halves,
    )
    grad_branch_all = lax.all_gather(grad_branch, "ctx", axis=0, tiled=True)

    def deal(blocks, *others):
        blocks = blocks.reshape((chips, 2) + blocks.shape[1:])
        got = [blocks[(chip - k) % chips] for k in range(chips)]
        got = jnp.stack([got[0]] + [from_chip(got[k], k) for k in range(1, chips)])
        got = after(got, *others)
        stay = jnp.where(odd, got[:, 1], got[:, 0])
        go = from_core(jnp.where(odd, got[:, 0], got[:, 1]))
        both = cores(stay[:, None], go[:, None], 1)
        both = jnp.concatenate([both, both], 0)
        both = lax.dynamic_slice_in_dim(both, (chips - chip) % chips, chips, 0)
        return both.reshape((size,) + both.shape[2:])

    sent = [grad_mixed]
    while chains[0].stage <= len(bits):
        sent = [chain.step(*sent) for chain in chains]
    grad_mixed_all = deal(jnp.repeat(grad_mixed, copies, 0), *sent).reshape(tokens, query_width)
    grad_query, grad_pair = attend_back(
        query,
        grad_mixed_all,
        log_total,
        cosine_table,
        sine_table,
        gathered,
        segment_rows,
        key,
        value,
        own,
    )
    if copies > 1:
        places = jnp.arange(tokens, dtype=jnp.int32)
        counted = (places // part == copy_index)[:, None]
        grad_query = jnp.where(counted, grad_query, jnp.zeros((), jnp.bfloat16))
        grad_pair = jnp.where(counted, grad_pair, jnp.zeros((), jnp.bfloat16))
    both_rows, *halves = close_rows(
        place,
        grad_query,
        grad_pair,
        head_all,
        gathered,
        normed_one,
        gain_two_grad,
        normed_two,
        grad_logits,
        out_rows,
        lax.dynamic_slice_in_dim(mixed, copy_index * rows_own, rows_own, 1),
        grad_branch_all,
        reps,
        side_width,
        block,
    )
    both_sums = lax.psum_scatter(
        both_rows, "ctx", scatter_dimension=0, tiled=True
    ).astype(jnp.float32)
    grad_one, out_sum = both_sums[:, :MODEL_WIDTH], both_sums[:, MODEL_WIDTH:]

    line = size // 2 * side_width
    cubes = [
        Cube(halves[h], halves[2 + h], order, share)
        for h, order in enumerate((bits, bits[::-1]))
    ]
    while chains[0].stage < chains[0].steps:
        sent = [chain.step(*halves, *[cube.flying for cube in cubes]) for chain in chains]
    while cubes[0].stage < len(bits):
        for cube in cubes:
            cube.add(*sent)
        sent = [cube.halve() for cube in cubes]
    first = [chain.piece(0, 3) for chain in chains]
    second = [chain.piece(1, 3, *sent) for chain in chains]
    for cube in cubes:
        cube.add()
    totals = [cube.value.astype(jnp.bfloat16) for cube in cubes]
    blocks = jnp.concatenate(
        [
            jnp.transpose(
                total.reshape(share, -1)[:, :line].reshape(share, size // 2, side_width), (1, 0, 2)
            )
            for total in totals
        ],
        0,
    )
    head_sums = deal(after(blocks, *first))
    for h, cube in enumerate(cubes):
        rows = jnp.transpose(head_sums[h * (size // 2) : (h + 1) * (size // 2)], (1, 0, 2))
        rows = jnp.concatenate(
            [rows.reshape(share, line), totals[h].reshape(share, -1)[:, line:]], 1
        )
        cube.value = rows.reshape(totals[h].shape)
    sent = [cube.back(*second) for cube in cubes]
    third = [chain.piece(2, 3, *sent) for chain in chains]
    keeps = place[2:]
    grad_gate, grad_up = [
        into_output(keeps, side, *after((chain.sent, first[side], second[side]), *sent))
        for side, chain in enumerate(chains)
    ]
    for cube in cubes:
        cube.join(grad_gate, grad_up)
    while cubes[0].stage > 0:
        sent = [cube.back() for cube in cubes]
        if cubes[0].stage > 0:
            for cube in cubes:
                cube.join(*sent)
    output = jnp.where((segments[0] != 0)[:, None], mine(after(middle, grad_mixed)) + out_sum, 0.0)
    own_hidden = inputs[0].astype(jnp.float32)
    own_scale = lax.rsqrt(jnp.mean(own_hidden * own_hidden, -1, keepdims=True) + EPS)
    grad_in = grad_middle + norm_back(grad_one * gain_one, own_hidden * own_scale, own_scale)
    grad_down = down_output(
        keeps,
        *after((chains[0].sent, third[0], chains[1].sent, third[1]), *sent),
    )
    for cube in cubes:
        cube.join(grad_down)
    head_outs = head_outputs(
        *[cube.value.reshape(rows_own, -1) for cube in cubes], copies, side_width
    )
    small = head_outs[4]
    return (
        output.astype(jnp.bfloat16)[None],
        grad_in[None],
        small[:, 0],
        *head_outs[:4],
        small[:, 1],
        small[:, 8 : 8 + experts_all],
        grad_gate,
        grad_up,
        grad_down,
    )


def solution(mesh):
    return jax.shard_map(
        per_device,
        mesh=mesh,
        in_specs=(
            P("rep", "ctx", None),
            P("rep", "ctx"),
            P("rep", "ctx"),
            P("rep", "ctx", None),
            P("ctx"),
            P("ctx", None),
            P("ctx", None),
            P("ctx", None),
            P("ctx", None),
            P("ctx"),
            P("ctx", None),
            P("ctx", None, None),
            P("ctx", None, None),
            P("ctx", None, None),
            P("rep", "ctx", None),
        ),
        out_specs=(
            P("rep", "ctx", None),
            P("rep", "ctx", None),
            P("ctx"),
            P("ctx", None),
            P("ctx", None),
            P("ctx", None),
            P("ctx", None),
            P("ctx"),
            P("ctx", None),
            P("ctx", None, None),
            P("ctx", None, None),
            P("ctx", None, None),
        ),
        check_vma=False,
    )
```

```python
import jax
import jax.numpy as jnp
from jax import lax
from jax.experimental import pallas as pl
from jax.experimental.pallas import tpu as pltpu
from jax.sharding import PartitionSpec as P

MODEL_WIDTH = 1536
QUERY_HEADS = 24
KEY_VALUE_HEADS = 8
HEAD_GROUP = QUERY_HEADS // KEY_VALUE_HEADS
HEAD_SIZE = 64
TOPK = 8

EPS = 1e-06
THETA = 10000.0
MASK_FLOOR = -1e30

ROWS = (((0,), (0,)), ((), ()))
COLUMNS = (((1,), (1,)), ((), ()))


def dot(left, right, contract=(((1,), (0,)), ((), ()))):
    return lax.dot_general(left, right, contract, preferred_element_type=jnp.float32)


def norm_back(grad_base, base, scale):
    return scale * (grad_base - base * jnp.mean(grad_base * base, -1, keepdims=True))


def turn(rows):
    half = HEAD_SIZE // 2
    return jnp.concatenate([-rows[:, half:], rows[:, :half]], 1)


def turn_back(rows):
    half = HEAD_SIZE // 2
    return jnp.concatenate([rows[:, half:], -rows[:, :half]], 1)


def stack_heads(rows):
    return jnp.concatenate(
        [rows[:, h * HEAD_SIZE : (h + 1) * HEAD_SIZE] for h in range(HEAD_GROUP)], 0
    )


def side_heads(rows):
    block = rows.shape[0] // HEAD_GROUP
    return jnp.concatenate([rows[h * block : (h + 1) * block] for h in range(HEAD_GROUP)], 1)


def lanes(values, combine):
    total = values[:, :128]
    for start in range(128, values.shape[1], 128):
        total = combine(total, values[:, start : start + 128])
    return total


def masked_scores(stacked, keys, row_segments, key_segments, row_start, key_start):
    block = row_segments.shape[0]
    scores = dot(stacked, keys, COLUMNS) * HEAD_SIZE ** (-0.5)
    row_place = row_start + lax.broadcasted_iota(jnp.int32, (block, block), 0)
    key_place = key_start + lax.broadcasted_iota(jnp.int32, (block, block), 1)
    allowed = (row_segments == key_segments) & (key_place <= row_place)
    scores = scores.reshape(HEAD_GROUP, block, block)
    return jnp.where(allowed[None], scores, MASK_FLOOR).reshape(HEAD_GROUP * block, block)


def first_block(row_segments, segment_ref, step):
    here = jnp.max(row_segments[:1, :1])
    segments = segment_ref[...]
    number = lax.broadcasted_iota(jnp.int32, segments.shape, 0)
    return jnp.min(jnp.where((segments == here) & (number <= step), number, step))


def token_rows(block, own, features):
    count = block // own
    return (
        pl.BlockSpec((count, own, features), lambda i, *_: (i, 0, 0)),
        pl.BlockSpec((count, own, 128), lambda i, *_: (i, 0, features // 128)),
    )


def flat(ref):
    return ref[...].reshape(-1, ref.shape[-1])


def whole_block(*shape):
    return pl.BlockSpec(shape, lambda *i: (0,) * len(shape), pipeline_mode=pl.Buffered(1))


def attend_kernel(
    hidden_ref,
    column_ref,
    gain_ref,
    low_ref,
    high_ref,
    rate_ref,
    normed_ref,
    query_ref,
    key_ref,
    value_ref,
    mixed_ref,
    packed_ref,
    log_ref,
    cosine_ref,
    sine_ref,
    segment_ref,
    score_ref,
):
    step = pl.program_id(0)
    block = query_ref.shape[0]
    query_width = query_ref.shape[1]
    width = query_width + 2 * HEAD_SIZE
    here = pl.ds(pl.multiple_of(step * block, block), block)
    columns = flat(column_ref).astype(jnp.float32)
    row_segments = columns[:, :1]
    segment_ref[step] = jnp.transpose(columns)[:1, :]
    angles = (columns[:, 1:2] * 64.0 + columns[:, 2:3]) * rate_ref[...]
    cosine = jnp.cos(angles)
    sine = jnp.sin(angles)
    cosine_ref[...] = cosine
    sine_ref[...] = sine
    hidden = flat(hidden_ref).astype(jnp.float32)
    scale = lax.rsqrt(jnp.mean(hidden * hidden, -1, keepdims=True) + EPS)
    normed = (hidden * scale * gain_ref[...]).astype(jnp.bfloat16)
    normed_ref[...] = normed
    middle = low_ref.shape[0]
    raw = dot(normed[:, :middle], low_ref[:, :width]) + dot(
        normed[:, middle:], high_ref[:, :width]
    )
    key_raw = raw[:, query_width : query_width + HEAD_SIZE]
    key_ref[here, :] = (key_raw * cosine + turn(key_raw) * sine).astype(jnp.bfloat16)
    value_ref[here, :] = raw[:, query_width + HEAD_SIZE :].astype(jnp.bfloat16)
    query_raw = stack_heads(raw[:, :query_width])
    cosine = jnp.concatenate([cosine] * HEAD_GROUP, 0)
    sine = jnp.concatenate([sine] * HEAD_GROUP, 0)
    query = (query_raw * cosine + turn(query_raw) * sine).astype(jnp.bfloat16)
    query_ref[...] = side_heads(query)
    rows = HEAD_GROUP * block
    first = first_block(row_segments, segment_ref, step)

    def first_pass(index, top):
        there = pl.ds(pl.multiple_of(index * block, block), block)
        scores = masked_scores(
            query,
            key_ref[there, :],
            row_segments,
            segment_ref[index],
            step * block,
            index * block,
        )
        score_ref[index] = scores
        return jnp.maximum(top, lanes(scores, jnp.maximum))

    top = lax.fori_loop(
        first, step + 1, first_pass, jnp.full((rows, 128), MASK_FLOOR, jnp.float32)
    )
    top = jnp.max(top, -1, keepdims=True)

    def second_pass(index, carry):
        total, mixed = carry
        there = pl.ds(pl.multiple_of(index * block, block), block)
        weights = jnp.exp(score_ref[index] - top)
        mixed = mixed + dot(weights.astype(jnp.bfloat16), value_ref[there, :])
        return total + lanes(weights, jnp.add), mixed

    total, mixed = lax.fori_loop(
        first,
        step + 1,
        second_pass,
        (
            jnp.zeros((rows, 128), jnp.float32),
            jnp.zeros((rows, HEAD_SIZE), jnp.float32),
        ),
    )
    total = jnp.sum(total, -1, keepdims=True)
    mixed = side_heads((mixed / total).astype(jnp.bfloat16))
    mixed_ref[...] = mixed
    packed_ref[...] = jnp.concatenate([mixed[: block // 2], mixed[block // 2 :]], 1)
    log_ref[...] = (top + jnp.log(total)).reshape(HEAD_GROUP, block, 1)


def attend(gathered, gain, weights, own, block):
    tokens, features = gathered.shape[0] * own, gain.shape[0]
    query_width = HEAD_GROUP * HEAD_SIZE
    steps = tokens // block
    half = jnp.arange(HEAD_SIZE // 2, dtype=jnp.float32)
    rate = THETA ** (-(2.0 * half) / HEAD_SIZE)
    rate = jnp.concatenate([rate, rate])[None, :]
    rows = lambda width: pl.BlockSpec((block, width), lambda i: (i, 0))
    resident = lambda *shape: pl.BlockSpec(shape, lambda i: (0,) * len(shape))
    shaped = jax.ShapeDtypeStruct
    return pl.pallas_call(
        attend_kernel,
        out_shape=(
            shaped((tokens, features), jnp.bfloat16),
            shaped((tokens, query_width), jnp.bfloat16),
            shaped((tokens, HEAD_SIZE), jnp.bfloat16),
            shaped((tokens, HEAD_SIZE), jnp.bfloat16),
            shaped((tokens, query_width), jnp.bfloat16),
            shaped((tokens // 2, 2 * query_width), jnp.bfloat16),
            shaped((HEAD_GROUP, tokens, 1), jnp.float32),
            shaped((tokens, HEAD_SIZE), jnp.float32),
            shaped((tokens, HEAD_SIZE), jnp.float32),
            shaped((steps, 1, block), jnp.float32),
        ),
        grid=(steps,),
        in_specs=[
            *token_rows(block, own, features),
            whole_block(1, features),
            whole_block(*weights[0].shape),
            whole_block(*weights[1].shape),
            whole_block(1, HEAD_SIZE),
        ],
        out_specs=[
            rows(features),
            rows(query_width),
            resident(tokens, HEAD_SIZE),
            resident(tokens, HEAD_SIZE),
            rows(query_width),
            pl.BlockSpec((block // 2, 2 * query_width), lambda i: (i, 0)),
            pl.BlockSpec((HEAD_GROUP, block, 1), lambda i: (0, i, 0)),
            rows(HEAD_SIZE),
            rows(HEAD_SIZE),
            resident(steps, 1, block),
        ],
        scratch_shapes=[pltpu.VMEM((steps, HEAD_GROUP * block, block), jnp.float32)],
        compiler_params=pltpu.CompilerParams(vmem_limit_bytes=48 << 20),
        cost_estimate=pl.CostEstimate(flops=0, bytes_accessed=tokens, transcendentals=0),
    )(gathered, gathered, gain[None, :], *weights, rate)


def attend_back_kernel(
    query_ref,
    grad_ref,
    log_ref,
    cosine_ref,
    sine_ref,
    column_ref,
    segment_ref,
    key_ref,
    value_ref,
    key_cosine_ref,
    key_sine_ref,
    grad_query_ref,
    grad_pair_ref,
    probs_ref,
    grad_probs_ref,
    grad_key_ref,
    grad_value_ref,
):
    step = pl.program_id(0)
    block = query_ref.shape[0]
    rows = HEAD_GROUP * block

    @pl.when(step == 0)
    def _():
        grad_key_ref[...] = jnp.zeros_like(grad_key_ref)
        grad_value_ref[...] = jnp.zeros_like(grad_value_ref)

    query = stack_heads(query_ref[...])
    grad = stack_heads(grad_ref[...])
    log_total = log_ref[...].reshape(rows, 1)
    row_segments = flat(column_ref).astype(jnp.float32)[:, :1]
    first = first_block(row_segments, segment_ref, step)

    def first_pass(index, delta):
        there = pl.ds(pl.multiple_of(index * block, block), block)
        scores = masked_scores(
            query,
            key_ref[there, :],
            row_segments,
            segment_ref[index],
            step * block,
            index * block,
        )
        probs = jnp.exp(scores - log_total)
        grad_probs = dot(grad, value_ref[there, :], COLUMNS)
        probs_ref[index] = probs
        grad_probs_ref[index] = grad_probs
        grad_value_ref[there, :] += dot(probs.astype(jnp.bfloat16), grad, ROWS)
        return delta + lanes(probs * grad_probs, jnp.add)

    delta = lax.fori_loop(first, step + 1, first_pass, jnp.zeros((rows, 128), jnp.float32))
    delta = jnp.sum(delta, -1, keepdims=True)

    def second_pass(index, grad_query):
        there = pl.ds(pl.multiple_of(index * block, block), block)
        grad_scores = (probs_ref[index] * (grad_probs_ref[index] - delta)).astype(jnp.bfloat16)
        grad_key_ref[there, :] += dot(grad_scores, query, ROWS)
        return grad_query + dot(grad_scores, key_ref[there, :])

    grad_query = lax.fori_loop(
        first, step + 1, second_pass, jnp.zeros((rows, HEAD_SIZE), jnp.float32)
    )
    score_scale = HEAD_SIZE ** (-0.5)
    cosine = jnp.concatenate([cosine_ref[...]] * HEAD_GROUP, 0)
    sine = jnp.concatenate([sine_ref[...]] * HEAD_GROUP, 0)
    grad_query = grad_query * score_scale
    grad_query = grad_query * cosine + turn_back(grad_query * sine)
    grad_query_ref[...] = side_heads(grad_query.astype(jnp.bfloat16))

    @pl.when(step == pl.num_programs(0) - 1)
    def _():
        @pl.loop(0, pl.num_programs(0))
        def _(index):
            there = pl.ds(pl.multiple_of(index * block, block), block)
            grad_key = grad_key_ref[there, :] * score_scale
            turned = turn_back(grad_key * key_sine_ref[there, :])
            grad_key = grad_key * key_cosine_ref[there, :] + turned
            grad_pair_ref[there, :] = jnp.concatenate(
                [grad_key, grad_value_ref[there, :]], 1
            ).astype(jnp.bfloat16)


def attend_back(query, grad, log_total, cosine, sine, gathered, segments, key, value, own):
    tokens, query_width = query.shape
    steps, _, block = segments.shape
    features = gathered.shape[2] - 128
    rows = lambda width: pl.BlockSpec((block, width), lambda i: (i, 0))
    resident = lambda *shape: pl.BlockSpec(shape, lambda i: (0,) * len(shape))
    return pl.pallas_call(
        attend_back_kernel,
        out_shape=(
            jax.ShapeDtypeStruct((tokens, query_width), jnp.bfloat16),
            jax.ShapeDtypeStruct((tokens, 2 * HEAD_SIZE), jnp.bfloat16),
        ),
        grid=(steps,),
        in_specs=[
            rows(query_width),
            rows(query_width),
            pl.BlockSpec((HEAD_GROUP, block, 1), lambda i: (0, i, 0)),
            rows(HEAD_SIZE),
            rows(HEAD_SIZE),
            token_rows(block, own, features)[1],
            whole_block(steps, 1, block),
            whole_block(tokens, HEAD_SIZE),
            whole_block(tokens, HEAD_SIZE),
            whole_block(tokens, HEAD_SIZE),
            whole_block(tokens, HEAD_SIZE),
        ],
        out_specs=[rows(query_width), resident(tokens, 2 * HEAD_SIZE)],
        scratch_shapes=[
            pltpu.VMEM((steps, HEAD_GROUP * block, block), jnp.float32),
            pltpu.VMEM((steps, HEAD_GROUP * block, block), jnp.float32),
            pltpu.VMEM((tokens, HEAD_SIZE), jnp.float32),
            pltpu.VMEM((tokens, HEAD_SIZE), jnp.float32),
        ],
        compiler_params=pltpu.CompilerParams(vmem_limit_bytes=48 << 20),
        cost_estimate=pl.CostEstimate(flops=0, bytes_accessed=tokens, transcendentals=0),
    )(query, grad, log_total, cosine, sine, gathered, segments, key, value, cosine, sine)


def middle_kernel(
    mixed_ref,
    low_ref,
    high_ref,
    hidden_ref,
    column_ref,
    gain_ref,
    router_ref,
    middle_ref,
    normed_ref,
    gates_ref,
):
    groups = mixed_ref.shape[0]
    width = mixed_ref.shape[2] // 2
    mixed = jnp.concatenate(
        [
            jnp.concatenate([mixed_ref[g, :, side : side + width] for g in range(groups)], 1)
            for side in (0, width)
        ],
        0,
    )
    half = low_ref.shape[0]
    middle = dot(mixed[:, :half], low_ref[...]) + dot(mixed[:, half:], high_ref[...])
    middle = flat(hidden_ref).astype(jnp.float32) + middle
    middle_ref[...] = middle
    scale = lax.rsqrt(jnp.mean(middle * middle, -1, keepdims=True) + EPS)
    normed = (middle * scale * gain_ref[...]).astype(jnp.bfloat16)
    normed_ref[...] = normed
    logits = dot(normed, router_ref[...])
    columns = flat(column_ref).astype(jnp.float32)
    number = lax.broadcasted_iota(jnp.int32, logits.shape, 1).astype(jnp.float32)
    named = columns[:, 3:4] == number
    for slot in range(1, TOPK):
        named = named | (columns[:, 3 + slot : 4 + slot] == number)
    logits = jnp.where(named, logits, MASK_FLOOR)
    shifted = jnp.exp(logits - jnp.max(logits, -1, keepdims=True))
    shifted = jnp.where(named, shifted, 0.0)
    gates_ref[...] = shifted / jnp.sum(shifted, -1, keepdims=True)


def middle_rows(mixed, weights, gathered, gain, router, own, block):
    groups, _, width = mixed.shape
    tokens = gathered.shape[0] * own
    features = gain.shape[0]
    experts = router.shape[1]
    rows = lambda columns: pl.BlockSpec((block, columns), lambda i: (i, 0))
    return pl.pallas_call(
        middle_kernel,
        out_shape=(
            jax.ShapeDtypeStruct((tokens, features), jnp.float32),
            jax.ShapeDtypeStruct((tokens, features), jnp.bfloat16),
            jax.ShapeDtypeStruct((tokens, experts), jnp.float32),
        ),
        grid=(tokens // block,),
        in_specs=[
            pl.BlockSpec((groups, block // 2, width), lambda i: (0, i, 0)),
            whole_block(*weights[0].shape),
            whole_block(*weights[1].shape),
            *token_rows(block, own, features),
            whole_block(1, features),
            whole_block(features, experts),
        ],
        out_specs=[rows(features), rows(features), rows(experts)],
        compiler_params=pltpu.CompilerParams(vmem_limit_bytes=48 << 20),
        cost_estimate=pl.CostEstimate(
            flops=tokens * features * groups * width,
            bytes_accessed=12 * tokens * features,
            transcendentals=0,
        ),
    )(mixed, *weights, gathered, gathered, gain[None, :], router)


def slot_of(e, keeps, experts_own):
    pick = experts_own // 2
    high, low = e // pick, e % pick
    return (1 - (high ^ keeps)) * pick + low


def expert_kernel(
    place_ref,
    normed_ref,
    cotangent_ref,
    column_ref,
    gates_ref,
    gate_weight_ref,
    up_weight_ref,
    down_weight_ref,
    scaled_one_ref,
    scaled_two_ref,
    grad_gate_ref,
    grad_up_ref,
    grad_live_ref,
    extra_ref,
):
    experts_own = gate_weight_ref.shape[0]
    experts_all = gates_ref.shape[1]
    first = place_ref[1] * experts_own
    live = flat(column_ref).astype(jnp.float32)[:, :1] > 0
    grad_live_ref[...] = jnp.where(live, cotangent_ref[...], jnp.zeros((), jnp.bfloat16))
    gates = gates_ref[...]
    number = lax.broadcasted_iota(jnp.int32, gates.shape, 1)

    def one_expert(e, grad_gates):
        one = slot_of(e, place_ref[2], experts_own)
        two = slot_of(e, place_ref[3], experts_own)
        gate = jnp.sum(jnp.where(number == first + e, gates, 0.0), -1, keepdims=True)
        gate_pre = dot(normed_ref[...], gate_weight_ref[e])
        up_pre = dot(normed_ref[...], up_weight_ref[e])
        grad_plain = dot(grad_live_ref[...], down_weight_ref[e], COLUMNS)
        sigma = jax.nn.sigmoid(gate_pre)
        silu = gate_pre * sigma
        acted = silu * up_pre
        grad_acted = gate * grad_plain
        scaled = (gate * acted).astype(jnp.bfloat16)
        scaled_one_ref[one] = scaled
        scaled_two_ref[two] = scaled
        grad_gate_ref[one] = (
            grad_acted * up_pre * (sigma * (1.0 + gate_pre * (1.0 - sigma)))
        ).astype(jnp.bfloat16)
        grad_up_ref[two] = (grad_acted * silu).astype(jnp.bfloat16)
        return grad_gates + jnp.where(
            number == first + e, jnp.sum(acted * grad_plain, -1, keepdims=True), 0.0
        )

    grad_gates = lax.fori_loop(
        0, experts_own, one_expert, jnp.zeros(gates.shape, jnp.float32)
    )
    rough = grad_gates.astype(jnp.bfloat16)
    fine = (grad_gates - rough.astype(jnp.float32)).astype(jnp.bfloat16)
    rest = jnp.zeros((gates.shape[0], extra_ref.shape[1] - 2 * experts_all), jnp.bfloat16)
    extra_ref[...] = jnp.concatenate([rough, fine, rest], 1)


def expert_rows(place, normed, cotangent, gathered, gates, w_gate, w_up, w_down, own, block):
    tokens, features = normed.shape
    experts_own, _, hidden = w_gate.shape
    experts_all = gates.shape[1]
    rows = lambda columns: pl.BlockSpec((block, columns), lambda i, p: (i, 0))
    spread = pl.BlockSpec((experts_own, block, hidden), lambda i, p: (0, i, 0))
    wide = jax.ShapeDtypeStruct((experts_own, tokens, hidden), jnp.bfloat16)
    return pl.pallas_call(
        expert_kernel,
        out_shape=(
            wide,
            wide,
            wide,
            wide,
            jax.ShapeDtypeStruct((tokens, features), jnp.bfloat16),
            jax.ShapeDtypeStruct((tokens, 128), jnp.bfloat16),
        ),
        grid_spec=pltpu.PrefetchScalarGridSpec(
            num_scalar_prefetch=1,
            grid=(tokens // block,),
            in_specs=[
                rows(features),
                rows(features),
                token_rows(block, own, features)[1],
                rows(experts_all),
                whole_block(*w_gate.shape),
                whole_block(*w_up.shape),
                whole_block(*w_down.shape),
            ],
            out_specs=[spread, spread, spread, spread, rows(features), rows(128)],
        ),
        compiler_params=pltpu.CompilerParams(vmem_limit_bytes=52 << 20),
        cost_estimate=pl.CostEstimate(
            flops=6 * tokens * features * hidden * experts_own,
            bytes_accessed=6 * features * hidden * experts_own + 10 * tokens * features,
            transcendentals=tokens * hidden * experts_own,
        ),
    )(place, normed, cotangent, gathered, gates, w_gate, w_up, w_down)


def product_kernel(
    left_ref,
    gate_ref,
    up_ref,
    scaled_one_ref,
    scaled_two_ref,
    live_one_ref,
    live_two_ref,
    out_one_ref,
    out_two_ref,
):
    step = pl.program_id(0)
    tile, hidden = left_ref.shape[1], gate_ref.shape[1]
    narrow = live_one_ref.shape[1]
    tops = pl.num_programs(0) - 3
    top = tops * tile

    @pl.when(step < tops)
    def _():
        here = pl.ds(pl.multiple_of(step * tile, tile), tile)
        both = dot(left_ref[...], jnp.concatenate([gate_ref[...], up_ref[...]], 1), ROWS)
        out_one_ref[here, :] = both[:, :hidden].astype(out_one_ref.dtype)
        out_two_ref[here, :] = both[:, hidden:].astype(out_two_ref.dtype)

    @pl.when(step >= tops)
    def _():
        part = step - tops
        for scaled_ref, live_ref, out_ref in (
            (scaled_one_ref, live_one_ref, out_one_ref),
            (scaled_two_ref, live_two_ref, out_two_ref),
        ):
            product = dot(scaled_ref[...], live_ref[...], ROWS).astype(out_ref.dtype)

            @pl.when(part < 2)
            def _():
                there = pl.ds(pl.multiple_of(part * narrow, narrow), narrow)
                out_ref[top : top + hidden, there] = product

            @pl.when(part == 2)
            def _():
                out_ref[top + hidden :, :narrow] = product[:narrow]
                out_ref[top + hidden :, narrow:] = product[narrow:]


def expert_products(left, gate, up, scaled_one, scaled_two, live, e, dtype):
    tokens, features = left.shape
    hidden = gate.shape[2]
    narrow = hidden // 2
    tile = 512
    tops = features // tile
    rows = features + features // 2
    stack = pl.BlockSpec((None, tokens, hidden), lambda i: (e, 0, 0), pipeline_mode=pl.Buffered(1))
    lives = [
        pl.BlockSpec((tokens, narrow), lambda i, side=side: (0, 3 * side + jnp.maximum(i - tops, 0)))
        for side in range(2)
    ]
    out = pl.BlockSpec((rows, hidden), lambda i: (0, 0), pipeline_mode=pl.Buffered(1))
    return pl.pallas_call(
        product_kernel,
        out_shape=(jax.ShapeDtypeStruct((rows, hidden), dtype),) * 2,
        grid=(tops + 3,),
        in_specs=[
            pl.BlockSpec((tokens, tile), lambda i: (0, jnp.minimum(i, tops - 1))),
            stack,
            stack,
            stack,
            stack,
            *lives,
        ],
        out_specs=[out, out],
        compiler_params=pltpu.CompilerParams(vmem_limit_bytes=58 << 20),
        cost_estimate=pl.CostEstimate(flops=0, bytes_accessed=tokens, transcendentals=0),
    )(left, gate, up, scaled_one, scaled_two, live, live)


def gradient_kernel(
    place_ref, grad_gate_ref, grad_up_ref, extra_ref, gate_weight_ref, up_weight_ref, grad_ref
):
    experts_own, features = gate_weight_ref.shape[:2]
    one = [slot_of(e, place_ref[2], experts_own) for e in range(experts_own)]
    two = [slot_of(e, place_ref[3], experts_own) for e in range(experts_own)]
    size = 512

    @pl.loop(0, features // size)
    def _(index):
        part = pl.ds(pl.multiple_of(index * size, size), size)
        grad = 0.0
        for e in range(experts_own):
            grad = grad + dot(grad_gate_ref[one[e]], gate_weight_ref[e, part, :], COLUMNS)
            grad = grad + dot(grad_up_ref[two[e]], up_weight_ref[e, part, :], COLUMNS)
        grad_ref[:, part] = grad.astype(jnp.bfloat16)

    grad_ref[:, features:] = extra_ref[...]


def gradient_rows(place, grad_gate_pre, grad_up_pre, extra, w_gate, w_up, block):
    experts_own, tokens, hidden = grad_gate_pre.shape
    features = w_gate.shape[1]
    rows = lambda columns: pl.BlockSpec((block, columns), lambda i, p: (i, 0))
    spread = pl.BlockSpec((experts_own, block, hidden), lambda i, p: (0, i, 0))
    return pl.pallas_call(
        gradient_kernel,
        out_shape=jax.ShapeDtypeStruct((tokens, features + extra.shape[1]), jnp.bfloat16),
        grid_spec=pltpu.PrefetchScalarGridSpec(
            num_scalar_prefetch=1,
            grid=(tokens // block,),
            in_specs=[
                spread,
                spread,
                rows(extra.shape[1]),
                whole_block(*w_gate.shape),
                whole_block(*w_up.shape),
            ],
            out_specs=rows(features + extra.shape[1]),
        ),
        compiler_params=pltpu.CompilerParams(vmem_limit_bytes=52 << 20),
        cost_estimate=pl.CostEstimate(flops=0, bytes_accessed=tokens, transcendentals=0),
    )(place, grad_gate_pre, grad_up_pre, extra, w_gate, w_up)


def output_kernel(place_ref, scaled_ref, down_weight_ref, out_ref):
    experts_own, _, features = down_weight_ref.shape
    size = 512

    @pl.loop(0, features // size)
    def _(index):
        part = pl.ds(pl.multiple_of(index * size, size), size)
        out = 0.0
        for e in range(experts_own):
            slot = slot_of(e, place_ref[2], experts_own)
            out = out + dot(scaled_ref[slot], down_weight_ref[e, :, part])
        out_ref[:, part] = out.astype(jnp.bfloat16)


def output_rows(place, scaled, w_down, block):
    experts_own, tokens, hidden = scaled.shape
    features = w_down.shape[2]
    return pl.pallas_call(
        output_kernel,
        out_shape=jax.ShapeDtypeStruct((tokens, features), jnp.bfloat16),
        grid_spec=pltpu.PrefetchScalarGridSpec(
            num_scalar_prefetch=1,
            grid=(tokens // block,),
            in_specs=[
                pl.BlockSpec((experts_own, block, hidden), lambda i, p: (0, i, 0)),
                whole_block(*w_down.shape),
            ],
            out_specs=pl.BlockSpec((block, features), lambda i, p: (i, 0)),
        ),
        compiler_params=pltpu.CompilerParams(vmem_limit_bytes=52 << 20),
        cost_estimate=pl.CostEstimate(flops=0, bytes_accessed=tokens, transcendentals=0),
    )(place, scaled, w_down)


def turn_kernel(
    place_ref,
    sum_ref,
    gates_ref,
    router_ref,
    gain_ref,
    middle_ref,
    live_ref,
    low_ref,
    high_ref,
    grad_middle_ref,
    branch_ref,
    mixed_ref,
    logits_ref,
    gain_grad_ref,
):
    features = middle_ref.shape[1]
    experts = gates_ref.shape[1]
    groups, _, width = mixed_ref.shape
    extra = sum_ref[:, features:].astype(jnp.float32)
    grad_gates = extra[:, :experts] + extra[:, experts : 2 * experts]
    gates = gates_ref[...]
    grad_logits = gates * (grad_gates - jnp.sum(gates * grad_gates, -1, keepdims=True))
    grad_logits = grad_logits.astype(jnp.bfloat16)
    logits_ref[...] = grad_logits
    grad = sum_ref[:, :features].astype(jnp.float32) + dot(grad_logits, router_ref[...], COLUMNS)
    middle = middle_ref[...]
    scale = lax.rsqrt(jnp.mean(middle * middle, -1, keepdims=True) + EPS)
    base = middle * scale
    gain_grad_ref[...] = jnp.sum(grad * base, 0, keepdims=True)
    grad_middle = live_ref[...].astype(jnp.float32) + norm_back(grad * gain_ref[...], base, scale)
    grad_middle_ref[...] = grad_middle
    branch = grad_middle.astype(jnp.bfloat16)
    branch_ref[...] = branch
    for half, weight_ref in enumerate((low_ref, high_ref)):
        mixed = dot(branch, weight_ref[...], COLUMNS).astype(jnp.bfloat16)
        for g in range(groups // 2):
            mixed_ref[half * (groups // 2) + g] = mixed[:, g * width : (g + 1) * width]


def turn_rows(place, sums, gates, router, gain, middle, live, weights):
    own, features = sums.shape[0], middle.shape[1]
    experts = gates.shape[1]
    groups = KEY_VALUE_HEADS
    shaped = jax.ShapeDtypeStruct
    rows = lambda width: pl.BlockSpec((own, width), lambda i, p: (p[1], 0))
    resident = lambda *shape: pl.BlockSpec(shape, lambda i, p: (0,) * len(shape))
    outs = (
        shaped((own, features), jnp.float32),
        shaped((own, features), jnp.bfloat16),
        shaped((groups, own, features // groups), jnp.bfloat16),
        shaped((own, experts), jnp.bfloat16),
        shaped((1, features), jnp.float32),
    )
    return pl.pallas_call(
        turn_kernel,
        out_shape=outs,
        grid_spec=pltpu.PrefetchScalarGridSpec(
            num_scalar_prefetch=1,
            grid=(1,),
            in_specs=[
                whole_block(*sums.shape),
                rows(experts),
                whole_block(*router.shape),
                whole_block(1, features),
                rows(features),
                rows(features),
                whole_block(*weights[0].shape),
                whole_block(*weights[1].shape),
            ],
            out_specs=[resident(*out.shape) for out in outs],
        ),
        compiler_params=pltpu.CompilerParams(vmem_limit_bytes=58 << 20),
        cost_estimate=pl.CostEstimate(flops=0, bytes_accessed=own, transcendentals=0),
    )(place, sums, gates, router, gain[None, :], middle, live, *weights)


def close_kernel(
    reps,
    place_ref,
    query_ref,
    pair_ref,
    weight_ref,
    hidden_ref,
    normed_ref,
    gain_two_ref,
    normed_own_ref,
    logits_ref,
    rows_ref,
    mixed_ref,
    branch_ref,
    grad_ref,
    kept_one_ref,
    kept_two_ref,
    sent_one_ref,
    sent_two_ref,
    product_ref,
    gain_ref,
    out_ref,
    head_ref,
):
    step = pl.program_id(0)
    both = query_ref.shape[1] + pair_ref.shape[1]
    heads = jnp.concatenate([query_ref[...], pair_ref[...]], 1)
    grad = dot(heads, weight_ref[:, :both], COLUMNS)
    grad_ref[:, : grad.shape[1]] = grad.astype(jnp.bfloat16)
    grad_ref[:, grad.shape[1] :] = rows_ref[...]
    hidden = flat(hidden_ref).astype(jnp.float32)
    scale = lax.rsqrt(jnp.mean(hidden * hidden, -1, keepdims=True) + EPS)
    normed = normed_ref[...]

    @pl.when(step == 0)
    def _():
        gain_ref[...] = jnp.zeros_like(gain_ref)
        product_ref[...] = jnp.zeros_like(product_ref)
        out_ref[...] = jnp.zeros_like(out_ref)

    gain_ref[...] += jnp.sum(grad * (hidden * scale), 0, keepdims=True)
    product_ref[...] += dot(normed, heads, ROWS)
    out_ref[...] += dot(mixed_ref[...], branch_ref[...], ROWS)

    @pl.when(step == pl.num_programs(0) - 1)
    def _():
        features = product_ref.shape[0]
        rows = out_ref.shape[0]
        share = rows // reps
        experts = logits_ref.shape[1]
        line = kept_one_ref.shape[1]
        count = features // rows
        side = (line - features // 2) // (count // 2)
        gains = jnp.concatenate(
            [gain_ref[...], gain_two_ref[...], jnp.zeros((6, features), jnp.float32)], 0
        )
        gains = jnp.transpose(gains)
        router = dot(normed_own_ref[...], logits_ref[...], ROWS)
        rest = jnp.zeros((rows, side - both - 8 - experts), jnp.float32)
        for h in range(2):
            for c in range(count // 2):
                place = h * (count // 2) + c
                part = slice(place * rows, (place + 1) * rows)
                head_ref[h, :, c * side : (c + 1) * side] = jnp.concatenate(
                    [product_ref[part, :], gains[part], router[part], rest], 1
                )
            half = features // 2
            head_ref[h, :, count // 2 * side :] = out_ref[:, h * half : (h + 1) * half]
        sides = ((0, kept_one_ref, sent_one_ref), (1, kept_two_ref, sent_two_ref))
        for h, kept_ref, sent_ref in sides:
            bit = 1 if h == 0 else reps // 2
            for index in range(reps // 2):
                base = index // bit * 2 * bit + index % bit
                here = slice(index * share, (index + 1) * share)
                lower = head_ref[h, base * share : (base + 1) * share, :]
                upper = head_ref[h, (base + bit) * share : (base + bit + 1) * share, :]
                kept_ref[here, :] = jnp.where(place_ref[2 + h] > 0, upper, lower)
                sent_ref[here, :] = jnp.where(place_ref[2 + h] > 0, lower, upper).astype(jnp.bfloat16)


def close_rows(
    place,
    query,
    pair,
    weight,
    gathered,
    normed,
    gain_two_grad,
    normed_two,
    logits,
    out_rows,
    mixed,
    branch,
    reps,
    side,
    block,
):
    tokens, features = normed.shape
    own = logits.shape[0]
    both = query.shape[1] + pair.shape[1]
    rows_own = mixed.shape[1]
    rows = lambda width: pl.BlockSpec((block, width), lambda i, k: (i, 0))
    resident = lambda *shape: pl.BlockSpec(shape, lambda i, k: (0,) * len(shape))
    shaped = jax.ShapeDtypeStruct
    line = features // rows_own // 2 * side + features // 2
    half = (rows_own // 2, line)
    return pl.pallas_call(
        lambda *refs: close_kernel(reps, *refs),
        name="close",
        out_shape=(
            shaped((tokens, 2 * features), jnp.bfloat16),
            shaped(half, jnp.float32),
            shaped(half, jnp.float32),
            shaped(half, jnp.bfloat16),
            shaped(half, jnp.bfloat16),
        ),
        grid_spec=pltpu.PrefetchScalarGridSpec(
            num_scalar_prefetch=1,
            grid=(tokens // block,),
            in_specs=[
                rows(query.shape[1]),
                rows(pair.shape[1]),
                whole_block(*weight.shape),
                token_rows(block, own, features)[0],
                rows(features),
                whole_block(1, features),
                pl.BlockSpec((own, features), lambda i, p: (p[1], 0)),
                whole_block(*logits.shape),
                rows(features),
                rows(rows_own),
                rows(features),
            ],
            out_specs=[rows(2 * features), *[resident(*half)] * 4],
            scratch_shapes=[
                pltpu.VMEM((features, both), jnp.float32),
                pltpu.VMEM((1, features), jnp.float32),
                pltpu.VMEM((rows_own, features), jnp.float32),
                pltpu.VMEM((2, rows_own, line), jnp.float32),
            ],
        ),
        compiler_params=pltpu.CompilerParams(vmem_limit_bytes=56 << 20),
        cost_estimate=pl.CostEstimate(flops=0, bytes_accessed=tokens, transcendentals=0),
    )(
        place,
        query,
        pair,
        weight,
        gathered,
        normed,
        gain_two_grad,
        normed_two,
        logits,
        out_rows,
        mixed,
        branch,
    )


def head_kernel(copies, side, low_ref, high_ref, query_ref, key_ref, value_ref, out_ref, small_ref):
    groups = KEY_VALUE_HEADS
    count = groups * copies
    halves = [low_ref[...].astype(jnp.float32), high_ref[...].astype(jnp.float32)]
    width = query_ref.shape[1] // groups
    parts = []
    for c in range(count):
        place = c % (count // 2) * side
        parts.append(halves[c // (count // 2)][:, place : place + side])
    heads = []
    small = 0.0
    for g in range(groups):
        total = parts[g * copies]
        for p in range(1, copies):
            total = total + parts[g * copies + p]
        heads.append(total)
        small = small + total[:, width + 2 * HEAD_SIZE :]
    small_ref[...] = small
    query_ref[...] = jnp.concatenate([head[:, :width] for head in heads], 1)
    key_ref[...] = jnp.concatenate([head[:, width : width + HEAD_SIZE] for head in heads], 1)
    value_ref[...] = jnp.concatenate(
        [head[:, width + HEAD_SIZE : width + 2 * HEAD_SIZE] for head in heads], 1
    )
    out_ref[...] = jnp.concatenate([half[:, count // 2 * side :] for half in halves], 1)


def head_outputs(low, high, copies, side):
    rows = low.shape[0]
    groups = KEY_VALUE_HEADS
    query_width = QUERY_HEADS * HEAD_SIZE
    shaped = lambda width: jax.ShapeDtypeStruct((rows, width), jnp.float32)
    return pl.pallas_call(
        lambda *refs: head_kernel(copies, side, *refs),
        name="head_outputs",
        out_shape=(
            shaped(query_width),
            shaped(groups * HEAD_SIZE),
            shaped(groups * HEAD_SIZE),
            shaped(MODEL_WIDTH),
            shaped(side - (query_width // groups + 2 * HEAD_SIZE)),
        ),
        compiler_params=pltpu.CompilerParams(vmem_limit_bytes=40 << 20),
        cost_estimate=pl.CostEstimate(flops=0, bytes_accessed=rows, transcendentals=0),
    )(low, high)


def into_kernel(keeps_ref, side, sent_ref, first_ref, second_ref, out_ref):
    kept = pl.program_id(0) == keeps_ref[side]
    came = jnp.where(pl.program_id(1) == 0, first_ref[...], second_ref[...])
    out_ref[...] = jnp.where(kept, sent_ref[...], came).astype(jnp.float32)


def into_output(keeps, side, sent, first, second):
    rows, hidden = first.shape
    part = lambda index: pl.BlockSpec((rows, hidden), index)
    return pl.pallas_call(
        lambda k, *refs: into_kernel(k, side, *refs),
        name="into_output",
        out_shape=jax.ShapeDtypeStruct((2, 2 * rows, hidden), jnp.float32),
        grid_spec=pltpu.PrefetchScalarGridSpec(
            num_scalar_prefetch=1,
            grid=(2, 2),
            in_specs=[
                part(lambda e, h, k: (h, 0)),
                part(lambda e, h, k: (0, 0)),
                part(lambda e, h, k: (0, 0)),
            ],
            out_specs=pl.BlockSpec((None, rows, hidden), lambda e, h, k: (e, h, 0)),
        ),
        compiler_params=pltpu.CompilerParams(vmem_limit_bytes=32 << 20),
        cost_estimate=pl.CostEstimate(flops=0, bytes_accessed=rows, transcendentals=0),
    )(keeps, sent, first, second)


def down_kernel(keeps_ref, sent_low_ref, came_low_ref, sent_high_ref, came_high_ref, out_ref):
    rows, hidden = came_low_ref.shape
    narrow = hidden // 2
    pairs = ((sent_low_ref, came_low_ref), (sent_high_ref, came_high_ref))
    for side, (sent_ref, came_ref) in enumerate(pairs):
        kept = pl.program_id(0) == keeps_ref[side]
        value = jnp.where(kept, sent_ref[...], came_ref[...]).astype(jnp.float32)
        start = side * rows
        out_ref[:, start : start + hidden] = value[:hidden]
        out_ref[:narrow, start + hidden : start + rows] = value[hidden:, :narrow]
        out_ref[narrow:, start + hidden : start + rows] = value[hidden:, narrow:]


def down_output(keeps, sent_low, came_low, sent_high, came_high):
    rows, hidden = came_low.shape
    place = sent_low.shape[0] // rows - 1
    sent = pl.BlockSpec((rows, hidden), lambda e, k: (place, 0))
    came = pl.BlockSpec((rows, hidden), lambda e, k: (0, 0))
    return pl.pallas_call(
        down_kernel,
        out_shape=jax.ShapeDtypeStruct((2, hidden, 2 * rows), jnp.float32),
        grid_spec=pltpu.PrefetchScalarGridSpec(
            num_scalar_prefetch=1,
            grid=(2,),
            in_specs=[sent, came, sent, came],
            out_specs=pl.BlockSpec((None, hidden, 2 * rows), lambda e, k: (e, 0, 0)),
        ),
        compiler_params=pltpu.CompilerParams(vmem_limit_bytes=32 << 20),
        cost_estimate=pl.CostEstimate(flops=0, bytes_accessed=rows, transcendentals=0),
    )(keeps, sent_low, came_low, sent_high, came_high)


def after(values, *others):
    values, _ = lax.optimization_barrier((values, others))
    return values


def swap(value, bit):
    size = lax.axis_size("rep")
    return lax.ppermute(value, "rep", [(i, i ^ bit) for i in range(size)])


def has(bit):
    return (lax.axis_index("rep") & bit) != 0


def join(value, came, bit, axis):
    upper = has(bit)
    return jnp.concatenate(
        [jnp.where(upper, came, value), jnp.where(upper, value, came)], axis
    )


class Chain:
    def __init__(self, order):
        self.order = order
        self.stage = 0
        self.steps = 2 * len(order)

    def send(self, sent):
        bit = self.order[min(self.stage, self.steps - 1 - self.stage)]
        self.sent = sent
        self.stage += 1
        if self.stage < self.steps:
            self.flying = swap(sent, bit)

    def step(self, *others):
        came = after(self.flying, *others)
        if self.stage == len(self.order):
            self.send((self.kept + came.astype(jnp.float32)).astype(jnp.bfloat16))
        else:
            self.send(join(self.sent, came, self.order[self.steps - self.stage], 0))
        return self.sent

    def piece(self, number, count, *others):
        rows = self.sent.shape[0] // count
        part = after(self.sent[number * rows : (number + 1) * rows], *others)
        return swap(part, self.order[0])


def halve_kernel(keeps_ref, *refs):
    for chain in range(2):
        kept_ref, other_ref, came_ref, rest_ref = refs[4 * chain : 4 * chain + 4]
        out_ref, sent_ref = refs[8 + 2 * chain : 10 + 2 * chain]
        out_ref[...] = kept_ref[...] + came_ref[...].astype(jnp.float32)
        sent = other_ref[...] + rest_ref[...].astype(jnp.float32)
        sent_ref[...] = sent.astype(jnp.bfloat16)


def halve_chains(chains, *others):
    order = [chain.order[chain.stage] for chain in chains]
    keeps = jnp.stack([has(bit) for bit in order]).astype(jnp.int32)
    rows, hidden = chains[0].kept.shape
    count = 4
    part = rows // 2 // count
    operands, specs = [], []
    for c, chain in enumerate(chains):
        came = after(chain.flying, *others)
        for array in (chain.kept, came):
            for flip in range(2):
                operands.append(array)
                specs.append(
                    pl.BlockSpec(
                        (part, hidden), lambda i, k, c=c, flip=flip: ((k[c] ^ flip) * count + i, 0)
                    )
                )
    block = pl.BlockSpec((part, hidden), lambda i, k: (i, 0))
    shaped = lambda dtype: jax.ShapeDtypeStruct((rows // 2, hidden), dtype)
    outs = pl.pallas_call(
        halve_kernel,
        out_shape=[shaped(jnp.float32), shaped(jnp.bfloat16)] * 2,
        grid_spec=pltpu.PrefetchScalarGridSpec(
            num_scalar_prefetch=1, grid=(count,), in_specs=specs, out_specs=[block] * 4
        ),
        compiler_params=pltpu.CompilerParams(vmem_limit_bytes=58 << 20),
        cost_estimate=pl.CostEstimate(
            flops=60000 * rows * hidden, bytes_accessed=24 * rows * hidden, transcendentals=0
        ),
    )(keeps, *operands)
    for chain, kept, sent in zip(chains, outs[::2], outs[1::2]):
        chain.kept = kept
        chain.send(sent)
    return [chain.sent for chain in chains]


class Cube:
    def __init__(self, kept, sent, order, share):
        shape = [2] * len(order)
        shape[len(order) - order[0].bit_length()] = 1
        self.value, sent = [array.reshape(*shape, share, -1) for array in (kept, sent)]
        self.order = order
        self.flying = swap(sent, order[0])
        self.stage = 1

    def axis(self, bit):
        return len(self.order) - bit.bit_length()

    def halve(self, *others):
        bit = self.order[self.stage]
        keep = has(bit).astype(jnp.int32)
        part = lambda index: lax.dynamic_slice_in_dim(self.value, index, 1, self.axis(bit))
        self.value, sent = part(keep), part(1 - keep).astype(jnp.bfloat16)
        self.flying = swap(after(sent, *others), bit)
        self.stage += 1
        return sent

    def add(self, *others):
        self.value = self.value + after(self.flying, *others).astype(jnp.float32)

    def back(self, *others):
        self.stage -= 1
        self.flying = swap(after(self.value, *others), self.order[self.stage])
        return self.value

    def join(self, *others):
        bit = self.order[self.stage]
        self.value = join(self.value, after(self.flying, *others), bit, self.axis(bit))


class Exchange:
    def __init__(self, fetched, bits):
        size = fetched.shape[0]
        fetched = fetched.reshape((size,) + (1,) * len(bits) + fetched.shape[1:])
        self.values = [fetched[: size // 2], fetched[size // 2 :]]
        self.orders = (bits, bits[::-1])
        self.stage = 0
        self.fly()

    def fly(self):
        self.flying = [
            swap(value, order[self.stage]) for value, order in zip(self.values, self.orders)
        ]

    def step(self, *others):
        bits = len(self.orders[0])
        for h, order in enumerate(self.orders):
            bit = order[self.stage]
            came = after(self.flying[h], *others)
            self.values[h] = join(self.values[h], came, bit, bits - (bit.bit_length() - 1))
        self.stage += 1
        if self.stage < bits:
            self.fly()
        return list(self.values)

    def finish(self, *others):
        while self.stage < len(self.orders[0]):
            self.step(*others)
        return [value.reshape(-1, value.shape[-1]) for value in self.values]


def per_device(
    inputs,
    segments,
    positions,
    expert_ids,
    attn_gain,
    w_query,
    key_weight,
    value_weight,
    w_out,
    ffn_gain,
    router,
    w_gate,
    w_up,
    w_down,
    grad_out,
):
    size = lax.axis_size("ctx")
    me = lax.axis_index("ctx")
    reps = lax.axis_size("rep")
    bits = [1 << i for i in range(reps.bit_length() - 1)]
    own = inputs.shape[1]
    tokens = size * own
    groups = KEY_VALUE_HEADS
    copies = size // groups
    query_width = HEAD_GROUP * HEAD_SIZE
    width = query_width + 2 * HEAD_SIZE
    copy_index = me % copies
    rows_own = w_out.shape[0]
    experts_own = w_gate.shape[0]
    experts_all = size * experts_own
    block = 2 * own
    chips = size // 2
    chip = me // 2
    odd = me % 2 == 1
    share = rows_own // reps
    share_start = lax.axis_index("rep") * share

    columns = jnp.concatenate(
        [
            segments[0][:, None],
            positions[0][:, None] // 64,
            positions[0][:, None] % 64,
            expert_ids[0],
        ],
        1,
    ).astype(jnp.bfloat16)
    columns = jnp.pad(columns, ((0, 0), (0, 128 - columns.shape[1])))
    shared = lambda array: lax.dynamic_slice_in_dim(array, share_start, share, 0)

    rows = jnp.concatenate(
        [
            jnp.concatenate([inputs[0], columns], 1),
            jnp.pad(shared(w_out), ((0, 0), (0, 128))),
        ],
        0,
    )
    gathered = lax.all_gather(rows, "ctx", axis=0)
    cotangent = lax.all_gather(after(grad_out[0], rows), "ctx", axis=0, tiled=True)

    def from_chip(value, k):
        return lax.ppermute(value, "ctx", [(i, (i - 2 * k) % size) for i in range(size)])

    def from_core(value):
        return lax.ppermute(value, "ctx", [(i, i ^ 1) for i in range(size)])

    def cores(mine, others, axis):
        return jnp.concatenate(
            [jnp.where(odd, others, mine), jnp.where(odd, mine, others)], axis
        )

    side_width = -(-(width + 2 + router.shape[1]) // 128) * 128
    head_columns = jnp.concatenate(
        [
            shared(w_query).reshape(share, groups, query_width),
            shared(key_weight).reshape(share, groups, HEAD_SIZE),
            shared(value_weight).reshape(share, groups, HEAD_SIZE),
            jnp.broadcast_to(shared(attn_gain)[:, None, None], (share, groups, 1)),
            jnp.broadcast_to(shared(ffn_gain)[:, None, None], (share, groups, 1)),
            jnp.broadcast_to(shared(router)[:, None, :], (share, groups, router.shape[1])),
        ],
        -1,
    )
    used = head_columns.shape[-1]
    head_columns = jnp.pad(head_columns, ((0, 0), (0, 0), (0, side_width - used)))
    head_columns = jnp.repeat(jnp.transpose(head_columns, (1, 0, 2)), copies, 0)
    head_columns = lax.all_to_all(head_columns, "ctx", split_axis=0, concat_axis=0, tiled=True)
    head_halves = Exchange(head_columns, bits).finish()
    head_all = jnp.concatenate(head_halves, 0)
    gain_one = head_all[:, width].astype(jnp.float32)
    gain_two = head_all[:, width + 1].astype(jnp.float32)
    router_all = head_all[:, width + 2 : used]

    (
        normed_one,
        query,
        key,
        value,
        mixed,
        packed,
        log_total,
        cosine_table,
        sine_table,
        segment_rows,
    ) = attend(gathered, gain_one, head_halves, own, block)
    out_exchange = Exchange(gathered[:, own:, :MODEL_WIDTH], bits)

    part = tokens // copies
    mixed_all = lax.all_gather(
        after(
            lax.dynamic_slice_in_dim(packed, copy_index * part // 2, part // 2, 0),
            cotangent,
            out_exchange.step(),
        ),
        "ctx",
        axis=0,
    ).reshape(groups, tokens // 2, 2 * query_width)
    w_out_halves = out_exchange.finish()

    middle, normed_two, gates = middle_rows(
        mixed_all, w_out_halves, gathered, gain_two, router_all, own, block
    )
    flag = lambda bit: has(bit).astype(jnp.int32)
    place = jnp.stack([chip, me, flag(bits[0]), flag(bits[-1])]).astype(jnp.int32)
    scaled_one, scaled_two, grad_gate_pre, grad_up_pre, grad_live, extra = expert_rows(
        place, normed_two, cotangent, gathered, gates, w_gate, w_up, w_down, own, block
    )
    def mine(array):
        return lax.dynamic_slice_in_dim(array, me * own, own, 0)

    products = lambda e, dtype: expert_products(
        normed_two, grad_gate_pre, grad_up_pre, scaled_one, scaled_two, grad_live, e, dtype
    )
    grad_rows = gradient_rows(place, grad_gate_pre, grad_up_pre, extra, w_gate, w_up, block)
    grad_two_sum = lax.psum_scatter(grad_rows, "ctx", scatter_dimension=0, tiled=True)
    normed_two, grad_live = after((normed_two, grad_live), grad_rows)
    chains = [Chain(bits), Chain(bits[::-1])]
    for chain, sent in zip(chains, products(0, jnp.bfloat16)):
        chain.send(sent)
    normed_two, grad_live = after((normed_two, grad_live), *[chain.sent for chain in chains])
    for chain, kept in zip(chains, products(1, jnp.float32)):
        chain.kept = kept
    out_rows = output_rows(place, after(scaled_one, *[c.kept for c in chains]), w_down, block)

    grad_middle, grad_branch, grad_mixed, grad_logits, gain_two_grad = turn_rows(
        place,
        after(grad_two_sum, out_rows),
        gates,
        router_all,
        gain_two,
        middle,
        grad_live,
        w_out_halves,
    )
    grad_branch_all = lax.all_gather(grad_branch, "ctx", axis=0, tiled=True)

    def deal_chips(blocks):
        blocks = blocks.reshape((chips, 2) + blocks.shape[1:])
        got = [blocks[(chip - k) % chips] for k in range(chips)]
        return jnp.stack([got[0]] + [from_chip(got[k], k) for k in range(1, chips)])

    def deal_cores(got):
        stay = jnp.where(odd, got[:, 1], got[:, 0])
        go = from_core(jnp.where(odd, got[:, 0], got[:, 1]))
        both = cores(stay[:, None], go[:, None], 1)
        both = jnp.concatenate([both, both], 0)
        both = lax.dynamic_slice_in_dim(both, (chips - chip) % chips, chips, 0)
        return both.reshape((size,) + both.shape[2:])

    got = deal_chips(jnp.repeat(grad_mixed, copies, 0))
    sent = [got]
    while chains[0].stage < len(bits):
        sent = halve_chains(chains, *sent)
    grad_mixed_all = deal_cores(after(got, *sent)).reshape(tokens, query_width)
    grad_query, grad_pair = attend_back(
        query,
        grad_mixed_all,
        log_total,
        cosine_table,
        sine_table,
        gathered,
        segment_rows,
        key,
        value,
        own,
    )
    if copies > 1:
        places = jnp.arange(tokens, dtype=jnp.int32)
        counted = (places // part == copy_index)[:, None]
        grad_query = jnp.where(counted, grad_query, jnp.zeros((), jnp.bfloat16))
        grad_pair = jnp.where(counted, grad_pair, jnp.zeros((), jnp.bfloat16))
    sent = [chain.step(grad_pair) for chain in chains]
    both_rows, *halves = close_rows(
        place,
        after(grad_query, *sent),
        grad_pair,
        head_all,
        gathered,
        normed_one,
        gain_two_grad,
        normed_two,
        grad_logits,
        out_rows,
        lax.dynamic_slice_in_dim(mixed, copy_index * rows_own, rows_own, 1),
        grad_branch_all,
        reps,
        side_width,
        block,
    )
    both_sums = lax.psum_scatter(
        both_rows, "ctx", scatter_dimension=0, tiled=True
    ).astype(jnp.float32)
    grad_one, out_sum = both_sums[:, :MODEL_WIDTH], both_sums[:, MODEL_WIDTH:]

    line = size // 2 * side_width
    cubes = [
        Cube(halves[h], halves[2 + h], order, share)
        for h, order in enumerate((bits, bits[::-1]))
    ]
    while chains[0].stage < chains[0].steps:
        sent = [chain.step(*halves) for chain in chains]
    while cubes[0].stage < len(bits):
        for cube in cubes:
            cube.add(*sent)
        sent = [cube.halve() for cube in cubes]
    first = [chain.piece(0, 3) for chain in chains]
    second = [chain.piece(1, 3, *sent) for chain in chains]
    for cube in cubes:
        cube.add()
    totals = [cube.value.astype(jnp.bfloat16) for cube in cubes]
    blocks = jnp.concatenate(
        [
            jnp.transpose(
                total.reshape(share, -1)[:, :line].reshape(share, size // 2, side_width), (1, 0, 2)
            )
            for total in totals
        ],
        0,
    )
    got = deal_chips(after(blocks, *first))
    head_sums = deal_cores(after(got, *second))
    for h, cube in enumerate(cubes):
        rows = jnp.transpose(head_sums[h * (size // 2) : (h + 1) * (size // 2)], (1, 0, 2))
        rows = jnp.concatenate(
            [rows.reshape(share, line), totals[h].reshape(share, -1)[:, line:]], 1
        )
        cube.value = rows.reshape(totals[h].shape)
    sent = [cube.back() for cube in cubes]
    third = [chain.piece(2, 3, *sent) for chain in chains]
    keeps = place[2:]
    grad_gate, grad_up = [
        into_output(keeps, side, *after((chain.sent, first[side], second[side]), *sent))
        for side, chain in enumerate(chains)
    ]
    for cube in cubes:
        cube.join(grad_gate, grad_up)
    while cubes[0].stage > 0:
        sent = [cube.back() for cube in cubes]
        if cubes[0].stage > 0:
            for cube in cubes:
                cube.join(*sent)
    output = jnp.where((segments[0] != 0)[:, None], mine(after(middle, grad_mixed)) + out_sum, 0.0)
    own_hidden = inputs[0].astype(jnp.float32)
    own_scale = lax.rsqrt(jnp.mean(own_hidden * own_hidden, -1, keepdims=True) + EPS)
    grad_in = grad_middle + norm_back(grad_one * gain_one, own_hidden * own_scale, own_scale)
    grad_down = down_output(
        keeps,
        *after((chains[0].sent, third[0], chains[1].sent, third[1]), *sent),
    )
    for cube in cubes:
        cube.join(grad_down)
    head_outs = head_outputs(
        *[cube.value.reshape(rows_own, -1) for cube in cubes], copies, side_width
    )
    small = head_outs[4]
    return (
        output.astype(jnp.bfloat16)[None],
        grad_in[None],
        small[:, 0],
        *head_outs[:4],
        small[:, 1],
        small[:, 8 : 8 + experts_all],
        grad_gate,
        grad_up,
        grad_down,
    )


def solution(mesh):
    return jax.shard_map(
        per_device,
        mesh=mesh,
        in_specs=(
            P("rep", "ctx", None),
            P("rep", "ctx"),
            P("rep", "ctx"),
            P("rep", "ctx", None),
            P("ctx"),
            P("ctx", None),
            P("ctx", None),
            P("ctx", None),
            P("ctx", None),
            P("ctx"),
            P("ctx", None),
            P("ctx", None, None),
            P("ctx", None, None),
            P("ctx", None, None),
            P("rep", "ctx", None),
        ),
        out_specs=(
            P("rep", "ctx", None),
            P("rep", "ctx", None),
            P("ctx"),
            P("ctx", None),
            P("ctx", None),
            P("ctx", None),
            P("ctx", None),
            P("ctx"),
            P("ctx", None),
            P("ctx", None, None),
            P("ctx", None, None),
            P("ctx", None, None),
        ),
        check_vma=False,
    )
```

```python
import jax
import jax.numpy as jnp
from jax import lax
from jax.experimental import pallas as pl
from jax.experimental.pallas import tpu as pltpu
from jax.sharding import PartitionSpec as P

MODEL_WIDTH = 1536
QUERY_HEADS = 24
KEY_VALUE_HEADS = 8
HEAD_GROUP = QUERY_HEADS // KEY_VALUE_HEADS
HEAD_SIZE = 64
TOPK = 8

EPS = 1e-06
THETA = 10000.0
MASK_FLOOR = -1e30

ROWS = (((0,), (0,)), ((), ()))
COLUMNS = (((1,), (1,)), ((), ()))


def dot(left, right, contract=(((1,), (0,)), ((), ()))):
    return lax.dot_general(left, right, contract, preferred_element_type=jnp.float32)


def norm_back(grad_base, base, scale):
    return scale * (grad_base - base * jnp.mean(grad_base * base, -1, keepdims=True))


def turn(rows):
    half = HEAD_SIZE // 2
    return jnp.concatenate([-rows[:, half:], rows[:, :half]], 1)


def turn_back(rows):
    half = HEAD_SIZE // 2
    return jnp.concatenate([rows[:, half:], -rows[:, :half]], 1)


def stack_heads(rows):
    return jnp.concatenate(
        [rows[:, h * HEAD_SIZE : (h + 1) * HEAD_SIZE] for h in range(HEAD_GROUP)], 0
    )


def side_heads(rows):
    block = rows.shape[0] // HEAD_GROUP
    return jnp.concatenate([rows[h * block : (h + 1) * block] for h in range(HEAD_GROUP)], 1)


def lanes(values, combine):
    total = values[:, :128]
    for start in range(128, values.shape[1], 128):
        total = combine(total, values[:, start : start + 128])
    return total


def masked_scores(stacked, keys, row_segments, key_segments, row_start, key_start):
    block = row_segments.shape[0]
    scores = dot(stacked, keys, COLUMNS) * HEAD_SIZE ** (-0.5)
    row_place = row_start + lax.broadcasted_iota(jnp.int32, (block, block), 0)
    key_place = key_start + lax.broadcasted_iota(jnp.int32, (block, block), 1)
    allowed = (row_segments == key_segments) & (key_place <= row_place)
    scores = scores.reshape(HEAD_GROUP, block, block)
    return jnp.where(allowed[None], scores, MASK_FLOOR).reshape(HEAD_GROUP * block, block)


def first_block(row_segments, segment_ref, step):
    here = jnp.max(row_segments[:1, :1])
    segments = segment_ref[...]
    number = lax.broadcasted_iota(jnp.int32, segments.shape, 0)
    return jnp.min(jnp.where((segments == here) & (number <= step), number, step))


def token_rows(block, own, features):
    count = block // own
    return (
        pl.BlockSpec((count, own, features), lambda i, *_: (i, 0, 0)),
        pl.BlockSpec((count, own, 128), lambda i, *_: (i, 0, features // 128)),
    )


def flat(ref):
    return ref[...].reshape(-1, ref.shape[-1])


def whole_block(*shape):
    return pl.BlockSpec(shape, lambda *i: (0,) * len(shape), pipeline_mode=pl.Buffered(1))


def attend_kernel(
    hidden_ref,
    column_ref,
    gain_ref,
    low_ref,
    high_ref,
    rate_ref,
    normed_ref,
    query_ref,
    key_ref,
    value_ref,
    mixed_ref,
    packed_ref,
    log_ref,
    cosine_ref,
    sine_ref,
    segment_ref,
    score_ref,
):
    step = pl.program_id(0)
    block = query_ref.shape[0]
    query_width = query_ref.shape[1]
    width = query_width + 2 * HEAD_SIZE
    here = pl.ds(pl.multiple_of(step * block, block), block)
    columns = flat(column_ref).astype(jnp.float32)
    row_segments = columns[:, :1]
    segment_ref[step] = jnp.transpose(columns)[:1, :]
    angles = (columns[:, 1:2] * 64.0 + columns[:, 2:3]) * rate_ref[...]
    cosine = jnp.cos(angles)
    sine = jnp.sin(angles)
    cosine_ref[...] = cosine
    sine_ref[...] = sine
    hidden = flat(hidden_ref).astype(jnp.float32)
    scale = lax.rsqrt(jnp.mean(hidden * hidden, -1, keepdims=True) + EPS)
    normed = (hidden * scale * gain_ref[...]).astype(jnp.bfloat16)
    normed_ref[...] = normed
    middle = low_ref.shape[0]
    raw = dot(normed[:, :middle], low_ref[:, :width]) + dot(
        normed[:, middle:], high_ref[:, :width]
    )
    key_raw = raw[:, query_width : query_width + HEAD_SIZE]
    key_ref[here, :] = (key_raw * cosine + turn(key_raw) * sine).astype(jnp.bfloat16)
    value_ref[here, :] = raw[:, query_width + HEAD_SIZE :].astype(jnp.bfloat16)
    query_raw = stack_heads(raw[:, :query_width])
    cosine = jnp.concatenate([cosine] * HEAD_GROUP, 0)
    sine = jnp.concatenate([sine] * HEAD_GROUP, 0)
    query = (query_raw * cosine + turn(query_raw) * sine).astype(jnp.bfloat16)
    query_ref[...] = side_heads(query)
    rows = HEAD_GROUP * block
    first = first_block(row_segments, segment_ref, step)

    def first_pass(index, top):
        there = pl.ds(pl.multiple_of(index * block, block), block)
        scores = masked_scores(
            query,
            key_ref[there, :],
            row_segments,
            segment_ref[index],
            step * block,
            index * block,
        )
        score_ref[index] = scores
        return jnp.maximum(top, lanes(scores, jnp.maximum))

    top = lax.fori_loop(
        first, step + 1, first_pass, jnp.full((rows, 128), MASK_FLOOR, jnp.float32)
    )
    top = jnp.max(top, -1, keepdims=True)

    def second_pass(index, carry):
        total, mixed = carry
        there = pl.ds(pl.multiple_of(index * block, block), block)
        weights = jnp.exp(score_ref[index] - top)
        mixed = mixed + dot(weights.astype(jnp.bfloat16), value_ref[there, :])
        return total + lanes(weights, jnp.add), mixed

    total, mixed = lax.fori_loop(
        first,
        step + 1,
        second_pass,
        (
            jnp.zeros((rows, 128), jnp.float32),
            jnp.zeros((rows, HEAD_SIZE), jnp.float32),
        ),
    )
    total = jnp.sum(total, -1, keepdims=True)
    mixed = side_heads((mixed / total).astype(jnp.bfloat16))
    mixed_ref[...] = mixed
    packed_ref[...] = jnp.concatenate([mixed[: block // 2], mixed[block // 2 :]], 1)
    log_ref[...] = (top + jnp.log(total)).reshape(HEAD_GROUP, block, 1)


def attend(gathered, gain, weights, own, block):
    tokens, features = gathered.shape[0] * own, gain.shape[0]
    query_width = HEAD_GROUP * HEAD_SIZE
    steps = tokens // block
    half = jnp.arange(HEAD_SIZE // 2, dtype=jnp.float32)
    rate = THETA ** (-(2.0 * half) / HEAD_SIZE)
    rate = jnp.concatenate([rate, rate])[None, :]
    rows = lambda width: pl.BlockSpec((block, width), lambda i: (i, 0))
    resident = lambda *shape: pl.BlockSpec(shape, lambda i: (0,) * len(shape))
    shaped = jax.ShapeDtypeStruct
    return pl.pallas_call(
        attend_kernel,
        out_shape=(
            shaped((tokens, features), jnp.bfloat16),
            shaped((tokens, query_width), jnp.bfloat16),
            shaped((tokens, HEAD_SIZE), jnp.bfloat16),
            shaped((tokens, HEAD_SIZE), jnp.bfloat16),
            shaped((tokens, query_width), jnp.bfloat16),
            shaped((tokens // 2, 2 * query_width), jnp.bfloat16),
            shaped((HEAD_GROUP, tokens, 1), jnp.float32),
            shaped((tokens, HEAD_SIZE), jnp.float32),
            shaped((tokens, HEAD_SIZE), jnp.float32),
            shaped((steps, 1, block), jnp.float32),
        ),
        grid=(steps,),
        in_specs=[
            *token_rows(block, own, features),
            whole_block(1, features),
            whole_block(*weights[0].shape),
            whole_block(*weights[1].shape),
            whole_block(1, HEAD_SIZE),
        ],
        out_specs=[
            rows(features),
            rows(query_width),
            resident(tokens, HEAD_SIZE),
            resident(tokens, HEAD_SIZE),
            rows(query_width),
            pl.BlockSpec((block // 2, 2 * query_width), lambda i: (i, 0)),
            pl.BlockSpec((HEAD_GROUP, block, 1), lambda i: (0, i, 0)),
            rows(HEAD_SIZE),
            rows(HEAD_SIZE),
            resident(steps, 1, block),
        ],
        scratch_shapes=[pltpu.VMEM((steps, HEAD_GROUP * block, block), jnp.float32)],
        compiler_params=pltpu.CompilerParams(vmem_limit_bytes=48 << 20),
        cost_estimate=pl.CostEstimate(flops=0, bytes_accessed=tokens, transcendentals=0),
    )(gathered, gathered, gain[None, :], *weights, rate)


def attend_back_kernel(
    query_ref,
    grad_ref,
    log_ref,
    cosine_ref,
    sine_ref,
    column_ref,
    segment_ref,
    key_ref,
    value_ref,
    key_cosine_ref,
    key_sine_ref,
    grad_query_ref,
    grad_pair_ref,
    probs_ref,
    grad_probs_ref,
    grad_key_ref,
    grad_value_ref,
):
    step = pl.program_id(0)
    block = query_ref.shape[0]
    rows = HEAD_GROUP * block

    @pl.when(step == 0)
    def _():
        grad_key_ref[...] = jnp.zeros_like(grad_key_ref)
        grad_value_ref[...] = jnp.zeros_like(grad_value_ref)

    query = stack_heads(query_ref[...])
    grad = stack_heads(grad_ref[...])
    log_total = log_ref[...].reshape(rows, 1)
    row_segments = flat(column_ref).astype(jnp.float32)[:, :1]
    first = first_block(row_segments, segment_ref, step)

    def first_pass(index, delta):
        there = pl.ds(pl.multiple_of(index * block, block), block)
        scores = masked_scores(
            query,
            key_ref[there, :],
            row_segments,
            segment_ref[index],
            step * block,
            index * block,
        )
        probs = jnp.exp(scores - log_total)
        grad_probs = dot(grad, value_ref[there, :], COLUMNS)
        probs_ref[index] = probs
        grad_probs_ref[index] = grad_probs
        grad_value_ref[there, :] += dot(probs.astype(jnp.bfloat16), grad, ROWS)
        return delta + lanes(probs * grad_probs, jnp.add)

    delta = lax.fori_loop(first, step + 1, first_pass, jnp.zeros((rows, 128), jnp.float32))
    delta = jnp.sum(delta, -1, keepdims=True)

    def second_pass(index, grad_query):
        there = pl.ds(pl.multiple_of(index * block, block), block)
        grad_scores = (probs_ref[index] * (grad_probs_ref[index] - delta)).astype(jnp.bfloat16)
        grad_key_ref[there, :] += dot(grad_scores, query, ROWS)
        return grad_query + dot(grad_scores, key_ref[there, :])

    grad_query = lax.fori_loop(
        first, step + 1, second_pass, jnp.zeros((rows, HEAD_SIZE), jnp.float32)
    )
    score_scale = HEAD_SIZE ** (-0.5)
    cosine = jnp.concatenate([cosine_ref[...]] * HEAD_GROUP, 0)
    sine = jnp.concatenate([sine_ref[...]] * HEAD_GROUP, 0)
    grad_query = grad_query * score_scale
    grad_query = grad_query * cosine + turn_back(grad_query * sine)
    grad_query_ref[...] = side_heads(grad_query.astype(jnp.bfloat16))

    @pl.when(step == pl.num_programs(0) - 1)
    def _():
        @pl.loop(0, pl.num_programs(0))
        def _(index):
            there = pl.ds(pl.multiple_of(index * block, block), block)
            grad_key = grad_key_ref[there, :] * score_scale
            turned = turn_back(grad_key * key_sine_ref[there, :])
            grad_key = grad_key * key_cosine_ref[there, :] + turned
            grad_pair_ref[there, :] = jnp.concatenate(
                [grad_key, grad_value_ref[there, :]], 1
            ).astype(jnp.bfloat16)


def attend_back(query, grad, log_total, cosine, sine, gathered, segments, key, value, own):
    tokens, query_width = query.shape
    steps, _, block = segments.shape
    features = gathered.shape[2] - 128
    rows = lambda width: pl.BlockSpec((block, width), lambda i: (i, 0))
    resident = lambda *shape: pl.BlockSpec(shape, lambda i: (0,) * len(shape))
    return pl.pallas_call(
        attend_back_kernel,
        out_shape=(
            jax.ShapeDtypeStruct((tokens, query_width), jnp.bfloat16),
            jax.ShapeDtypeStruct((tokens, 2 * HEAD_SIZE), jnp.bfloat16),
        ),
        grid=(steps,),
        in_specs=[
            rows(query_width),
            rows(query_width),
            pl.BlockSpec((HEAD_GROUP, block, 1), lambda i: (0, i, 0)),
            rows(HEAD_SIZE),
            rows(HEAD_SIZE),
            token_rows(block, own, features)[1],
            whole_block(steps, 1, block),
            whole_block(tokens, HEAD_SIZE),
            whole_block(tokens, HEAD_SIZE),
            whole_block(tokens, HEAD_SIZE),
            whole_block(tokens, HEAD_SIZE),
        ],
        out_specs=[rows(query_width), resident(tokens, 2 * HEAD_SIZE)],
        scratch_shapes=[
            pltpu.VMEM((steps, HEAD_GROUP * block, block), jnp.float32),
            pltpu.VMEM((steps, HEAD_GROUP * block, block), jnp.float32),
            pltpu.VMEM((tokens, HEAD_SIZE), jnp.float32),
            pltpu.VMEM((tokens, HEAD_SIZE), jnp.float32),
        ],
        compiler_params=pltpu.CompilerParams(vmem_limit_bytes=48 << 20),
        cost_estimate=pl.CostEstimate(flops=0, bytes_accessed=tokens, transcendentals=0),
    )(query, grad, log_total, cosine, sine, gathered, segments, key, value, cosine, sine)


def middle_kernel(
    mixed_ref,
    low_ref,
    high_ref,
    hidden_ref,
    column_ref,
    gain_ref,
    router_ref,
    middle_ref,
    normed_ref,
    gates_ref,
):
    groups = mixed_ref.shape[0]
    width = mixed_ref.shape[2] // 2
    mixed = jnp.concatenate(
        [
            jnp.concatenate([mixed_ref[g, :, side : side + width] for g in range(groups)], 1)
            for side in (0, width)
        ],
        0,
    )
    half = low_ref.shape[0]
    middle = dot(mixed[:, :half], low_ref[...]) + dot(mixed[:, half:], high_ref[...])
    middle = flat(hidden_ref).astype(jnp.float32) + middle
    middle_ref[...] = middle
    scale = lax.rsqrt(jnp.mean(middle * middle, -1, keepdims=True) + EPS)
    normed = (middle * scale * gain_ref[...]).astype(jnp.bfloat16)
    normed_ref[...] = normed
    logits = dot(normed, router_ref[...])
    columns = flat(column_ref).astype(jnp.float32)
    number = lax.broadcasted_iota(jnp.int32, logits.shape, 1).astype(jnp.float32)
    named = columns[:, 3:4] == number
    for slot in range(1, TOPK):
        named = named | (columns[:, 3 + slot : 4 + slot] == number)
    logits = jnp.where(named, logits, MASK_FLOOR)
    shifted = jnp.exp(logits - jnp.max(logits, -1, keepdims=True))
    shifted = jnp.where(named, shifted, 0.0)
    gates_ref[...] = shifted / jnp.sum(shifted, -1, keepdims=True)


def middle_rows(mixed, weights, gathered, gain, router, own, block):
    groups, _, width = mixed.shape
    tokens = gathered.shape[0] * own
    features = gain.shape[0]
    experts = router.shape[1]
    rows = lambda columns: pl.BlockSpec((block, columns), lambda i: (i, 0))
    return pl.pallas_call(
        middle_kernel,
        out_shape=(
            jax.ShapeDtypeStruct((tokens, features), jnp.float32),
            jax.ShapeDtypeStruct((tokens, features), jnp.bfloat16),
            jax.ShapeDtypeStruct((tokens, experts), jnp.float32),
        ),
        grid=(tokens // block,),
        in_specs=[
            pl.BlockSpec((groups, block // 2, width), lambda i: (0, i, 0)),
            whole_block(*weights[0].shape),
            whole_block(*weights[1].shape),
            *token_rows(block, own, features),
            whole_block(1, features),
            whole_block(features, experts),
        ],
        out_specs=[rows(features), rows(features), rows(experts)],
        compiler_params=pltpu.CompilerParams(vmem_limit_bytes=48 << 20),
        cost_estimate=pl.CostEstimate(
            flops=tokens * features * groups * width,
            bytes_accessed=12 * tokens * features,
            transcendentals=0,
        ),
    )(mixed, *weights, gathered, gathered, gain[None, :], router)


def slot_of(e, keeps, experts_own):
    pick = experts_own // 2
    high, low = e // pick, e % pick
    return (1 - (high ^ keeps)) * pick + low


def expert_kernel(
    place_ref,
    normed_ref,
    cotangent_ref,
    column_ref,
    gates_ref,
    gate_weight_ref,
    up_weight_ref,
    down_weight_ref,
    scaled_one_ref,
    scaled_two_ref,
    grad_gate_ref,
    grad_up_ref,
    grad_live_ref,
    extra_ref,
):
    experts_own = gate_weight_ref.shape[0]
    experts_all = gates_ref.shape[1]
    first = place_ref[1] * experts_own
    live = flat(column_ref).astype(jnp.float32)[:, :1] > 0
    grad_live_ref[...] = jnp.where(live, cotangent_ref[...], jnp.zeros((), jnp.bfloat16))
    gates = gates_ref[...]
    number = lax.broadcasted_iota(jnp.int32, gates.shape, 1)

    def one_expert(e, grad_gates):
        one = slot_of(e, place_ref[2], experts_own)
        two = slot_of(e, place_ref[3], experts_own)
        gate = jnp.sum(jnp.where(number == first + e, gates, 0.0), -1, keepdims=True)
        gate_pre = dot(normed_ref[...], gate_weight_ref[e])
        up_pre = dot(normed_ref[...], up_weight_ref[e])
        grad_plain = dot(grad_live_ref[...], down_weight_ref[e], COLUMNS)
        sigma = jax.nn.sigmoid(gate_pre)
        silu = gate_pre * sigma
        acted = silu * up_pre
        grad_acted = gate * grad_plain
        scaled = (gate * acted).astype(jnp.bfloat16)
        scaled_one_ref[one] = scaled
        scaled_two_ref[two] = scaled
        grad_gate_ref[one] = (
            grad_acted * up_pre * (sigma * (1.0 + gate_pre * (1.0 - sigma)))
        ).astype(jnp.bfloat16)
        grad_up_ref[two] = (grad_acted * silu).astype(jnp.bfloat16)
        return grad_gates + jnp.where(
            number == first + e, jnp.sum(acted * grad_plain, -1, keepdims=True), 0.0
        )

    grad_gates = lax.fori_loop(
        0, experts_own, one_expert, jnp.zeros(gates.shape, jnp.float32)
    )
    rough = grad_gates.astype(jnp.bfloat16)
    fine = (grad_gates - rough.astype(jnp.float32)).astype(jnp.bfloat16)
    rest = jnp.zeros((gates.shape[0], extra_ref.shape[1] - 2 * experts_all), jnp.bfloat16)
    extra_ref[...] = jnp.concatenate([rough, fine, rest], 1)


def expert_rows(place, normed, cotangent, gathered, gates, w_gate, w_up, w_down, own, block):
    tokens, features = normed.shape
    experts_own, _, hidden = w_gate.shape
    experts_all = gates.shape[1]
    rows = lambda columns: pl.BlockSpec((block, columns), lambda i, p: (i, 0))
    spread = pl.BlockSpec((experts_own, block, hidden), lambda i, p: (0, i, 0))
    wide = jax.ShapeDtypeStruct((experts_own, tokens, hidden), jnp.bfloat16)
    return pl.pallas_call(
        expert_kernel,
        out_shape=(
            wide,
            wide,
            wide,
            wide,
            jax.ShapeDtypeStruct((tokens, features), jnp.bfloat16),
            jax.ShapeDtypeStruct((tokens, 128), jnp.bfloat16),
        ),
        grid_spec=pltpu.PrefetchScalarGridSpec(
            num_scalar_prefetch=1,
            grid=(tokens // block,),
            in_specs=[
                rows(features),
                rows(features),
                token_rows(block, own, features)[1],
                rows(experts_all),
                whole_block(*w_gate.shape),
                whole_block(*w_up.shape),
                whole_block(*w_down.shape),
            ],
            out_specs=[spread, spread, spread, spread, rows(features), rows(128)],
        ),
        compiler_params=pltpu.CompilerParams(vmem_limit_bytes=52 << 20),
        cost_estimate=pl.CostEstimate(
            flops=6 * tokens * features * hidden * experts_own,
            bytes_accessed=6 * features * hidden * experts_own + 10 * tokens * features,
            transcendentals=tokens * hidden * experts_own,
        ),
    )(place, normed, cotangent, gathered, gates, w_gate, w_up, w_down)


def product_kernel(
    left_ref,
    gate_ref,
    up_ref,
    scaled_one_ref,
    scaled_two_ref,
    live_one_ref,
    live_two_ref,
    out_one_ref,
    out_two_ref,
):
    step = pl.program_id(0)
    tile, hidden = left_ref.shape[1], gate_ref.shape[1]
    narrow = live_one_ref.shape[1]
    tops = pl.num_programs(0) - 3
    top = tops * tile

    @pl.when(step < tops)
    def _():
        here = pl.ds(pl.multiple_of(step * tile, tile), tile)
        both = dot(left_ref[...], jnp.concatenate([gate_ref[...], up_ref[...]], 1), ROWS)
        out_one_ref[here, :] = both[:, :hidden].astype(out_one_ref.dtype)
        out_two_ref[here, :] = both[:, hidden:].astype(out_two_ref.dtype)

    @pl.when(step >= tops)
    def _():
        part = step - tops
        for scaled_ref, live_ref, out_ref in (
            (scaled_one_ref, live_one_ref, out_one_ref),
            (scaled_two_ref, live_two_ref, out_two_ref),
        ):
            product = dot(scaled_ref[...], live_ref[...], ROWS).astype(out_ref.dtype)

            @pl.when(part < 2)
            def _():
                there = pl.ds(pl.multiple_of(part * narrow, narrow), narrow)
                out_ref[top : top + hidden, there] = product

            @pl.when(part == 2)
            def _():
                out_ref[top + hidden :, :narrow] = product[:narrow]
                out_ref[top + hidden :, narrow:] = product[narrow:]


def expert_products(left, gate, up, scaled_one, scaled_two, live, e, dtype):
    tokens, features = left.shape
    hidden = gate.shape[2]
    narrow = hidden // 2
    tile = 512
    tops = features // tile
    rows = features + features // 2
    stack = pl.BlockSpec((None, tokens, hidden), lambda i: (e, 0, 0), pipeline_mode=pl.Buffered(1))
    lives = [
        pl.BlockSpec((tokens, narrow), lambda i, side=side: (0, 3 * side + jnp.maximum(i - tops, 0)))
        for side in range(2)
    ]
    out = pl.BlockSpec((rows, hidden), lambda i: (0, 0), pipeline_mode=pl.Buffered(1))
    return pl.pallas_call(
        product_kernel,
        out_shape=(jax.ShapeDtypeStruct((rows, hidden), dtype),) * 2,
        grid=(tops + 3,),
        in_specs=[
            pl.BlockSpec((tokens, tile), lambda i: (0, jnp.minimum(i, tops - 1))),
            stack,
            stack,
            stack,
            stack,
            *lives,
        ],
        out_specs=[out, out],
        compiler_params=pltpu.CompilerParams(vmem_limit_bytes=58 << 20),
        cost_estimate=pl.CostEstimate(flops=0, bytes_accessed=tokens, transcendentals=0),
    )(left, gate, up, scaled_one, scaled_two, live, live)


def gradient_kernel(
    place_ref, grad_gate_ref, grad_up_ref, extra_ref, gate_weight_ref, up_weight_ref, grad_ref
):
    experts_own, features = gate_weight_ref.shape[:2]
    one = [slot_of(e, place_ref[2], experts_own) for e in range(experts_own)]
    two = [slot_of(e, place_ref[3], experts_own) for e in range(experts_own)]
    size = 512

    @pl.loop(0, features // size)
    def _(index):
        part = pl.ds(pl.multiple_of(index * size, size), size)
        grad = 0.0
        for e in range(experts_own):
            grad = grad + dot(grad_gate_ref[one[e]], gate_weight_ref[e, part, :], COLUMNS)
            grad = grad + dot(grad_up_ref[two[e]], up_weight_ref[e, part, :], COLUMNS)
        grad_ref[:, part] = grad.astype(jnp.bfloat16)

    grad_ref[:, features:] = extra_ref[...]


def gradient_rows(place, grad_gate_pre, grad_up_pre, extra, w_gate, w_up, block):
    experts_own, tokens, hidden = grad_gate_pre.shape
    features = w_gate.shape[1]
    rows = lambda columns: pl.BlockSpec((block, columns), lambda i, p: (i, 0))
    spread = pl.BlockSpec((experts_own, block, hidden), lambda i, p: (0, i, 0))
    return pl.pallas_call(
        gradient_kernel,
        out_shape=jax.ShapeDtypeStruct((tokens, features + extra.shape[1]), jnp.bfloat16),
        grid_spec=pltpu.PrefetchScalarGridSpec(
            num_scalar_prefetch=1,
            grid=(tokens // block,),
            in_specs=[
                spread,
                spread,
                rows(extra.shape[1]),
                whole_block(*w_gate.shape),
                whole_block(*w_up.shape),
            ],
            out_specs=rows(features + extra.shape[1]),
        ),
        compiler_params=pltpu.CompilerParams(vmem_limit_bytes=52 << 20),
        cost_estimate=pl.CostEstimate(flops=0, bytes_accessed=tokens, transcendentals=0),
    )(place, grad_gate_pre, grad_up_pre, extra, w_gate, w_up)


def output_kernel(place_ref, scaled_ref, down_weight_ref, out_ref):
    experts_own, _, features = down_weight_ref.shape
    size = 512

    @pl.loop(0, features // size)
    def _(index):
        part = pl.ds(pl.multiple_of(index * size, size), size)
        out = 0.0
        for e in range(experts_own):
            slot = slot_of(e, place_ref[2], experts_own)
            out = out + dot(scaled_ref[slot], down_weight_ref[e, :, part])
        out_ref[:, part] = out.astype(jnp.bfloat16)


def output_rows(place, scaled, w_down, block):
    experts_own, tokens, hidden = scaled.shape
    features = w_down.shape[2]
    return pl.pallas_call(
        output_kernel,
        out_shape=jax.ShapeDtypeStruct((tokens, features), jnp.bfloat16),
        grid_spec=pltpu.PrefetchScalarGridSpec(
            num_scalar_prefetch=1,
            grid=(tokens // block,),
            in_specs=[
                pl.BlockSpec((experts_own, block, hidden), lambda i, p: (0, i, 0)),
                whole_block(*w_down.shape),
            ],
            out_specs=pl.BlockSpec((block, features), lambda i, p: (i, 0)),
        ),
        compiler_params=pltpu.CompilerParams(vmem_limit_bytes=52 << 20),
        cost_estimate=pl.CostEstimate(flops=0, bytes_accessed=tokens, transcendentals=0),
    )(place, scaled, w_down)


def turn_kernel(
    place_ref,
    sum_ref,
    gates_ref,
    router_ref,
    gain_ref,
    middle_ref,
    live_ref,
    low_ref,
    high_ref,
    grad_middle_ref,
    branch_ref,
    mixed_ref,
    logits_ref,
    gain_grad_ref,
):
    features = middle_ref.shape[1]
    experts = gates_ref.shape[1]
    groups, _, width = mixed_ref.shape
    extra = sum_ref[:, features:].astype(jnp.float32)
    grad_gates = extra[:, :experts] + extra[:, experts : 2 * experts]
    gates = gates_ref[...]
    grad_logits = gates * (grad_gates - jnp.sum(gates * grad_gates, -1, keepdims=True))
    grad_logits = grad_logits.astype(jnp.bfloat16)
    logits_ref[...] = grad_logits
    grad = sum_ref[:, :features].astype(jnp.float32) + dot(grad_logits, router_ref[...], COLUMNS)
    middle = middle_ref[...]
    scale = lax.rsqrt(jnp.mean(middle * middle, -1, keepdims=True) + EPS)
    base = middle * scale
    gain_grad_ref[...] = jnp.sum(grad * base, 0, keepdims=True)
    grad_middle = live_ref[...].astype(jnp.float32) + norm_back(grad * gain_ref[...], base, scale)
    grad_middle_ref[...] = grad_middle
    branch = grad_middle.astype(jnp.bfloat16)
    branch_ref[...] = branch
    for half, weight_ref in enumerate((low_ref, high_ref)):
        mixed = dot(branch, weight_ref[...], COLUMNS).astype(jnp.bfloat16)
        for g in range(groups // 2):
            mixed_ref[half * (groups // 2) + g] = mixed[:, g * width : (g + 1) * width]


def turn_rows(place, sums, gates, router, gain, middle, live, weights):
    own, features = sums.shape[0], middle.shape[1]
    experts = gates.shape[1]
    groups = KEY_VALUE_HEADS
    shaped = jax.ShapeDtypeStruct
    rows = lambda width: pl.BlockSpec((own, width), lambda i, p: (p[1], 0))
    resident = lambda *shape: pl.BlockSpec(shape, lambda i, p: (0,) * len(shape))
    outs = (
        shaped((own, features), jnp.float32),
        shaped((own, features), jnp.bfloat16),
        shaped((groups, own, features // groups), jnp.bfloat16),
        shaped((own, experts), jnp.bfloat16),
        shaped((1, features), jnp.float32),
    )
    return pl.pallas_call(
        turn_kernel,
        out_shape=outs,
        grid_spec=pltpu.PrefetchScalarGridSpec(
            num_scalar_prefetch=1,
            grid=(1,),
            in_specs=[
                whole_block(*sums.shape),
                rows(experts),
                whole_block(*router.shape),
                whole_block(1, features),
                rows(features),
                rows(features),
                whole_block(*weights[0].shape),
                whole_block(*weights[1].shape),
            ],
            out_specs=[resident(*out.shape) for out in outs],
        ),
        compiler_params=pltpu.CompilerParams(vmem_limit_bytes=58 << 20),
        cost_estimate=pl.CostEstimate(flops=0, bytes_accessed=own, transcendentals=0),
    )(place, sums, gates, router, gain[None, :], middle, live, *weights)


def close_kernel(
    reps,
    place_ref,
    query_ref,
    pair_ref,
    weight_ref,
    hidden_ref,
    normed_ref,
    gain_two_ref,
    normed_own_ref,
    logits_ref,
    rows_ref,
    mixed_ref,
    branch_ref,
    grad_ref,
    kept_one_ref,
    kept_two_ref,
    sent_one_ref,
    sent_two_ref,
    product_ref,
    gain_ref,
    out_ref,
    head_ref,
):
    step = pl.program_id(0)
    both = query_ref.shape[1] + pair_ref.shape[1]
    heads = jnp.concatenate([query_ref[...], pair_ref[...]], 1)
    grad = dot(heads, weight_ref[:, :both], COLUMNS)
    grad_ref[:, : grad.shape[1]] = grad.astype(jnp.bfloat16)
    grad_ref[:, grad.shape[1] :] = rows_ref[...]
    hidden = flat(hidden_ref).astype(jnp.float32)
    scale = lax.rsqrt(jnp.mean(hidden * hidden, -1, keepdims=True) + EPS)
    normed = normed_ref[...]

    @pl.when(step == 0)
    def _():
        gain_ref[...] = jnp.zeros_like(gain_ref)
        product_ref[...] = jnp.zeros_like(product_ref)
        out_ref[...] = jnp.zeros_like(out_ref)

    gain_ref[...] += jnp.sum(grad * (hidden * scale), 0, keepdims=True)
    product_ref[...] += dot(normed, heads, ROWS)
    out_ref[...] += dot(mixed_ref[...], branch_ref[...], ROWS)

    @pl.when(step == pl.num_programs(0) - 1)
    def _():
        features = product_ref.shape[0]
        rows = out_ref.shape[0]
        share = rows // reps
        experts = logits_ref.shape[1]
        line = kept_one_ref.shape[1]
        count = features // rows
        side = (line - features // 2) // (count // 2)
        gains = jnp.concatenate(
            [gain_ref[...], gain_two_ref[...], jnp.zeros((6, features), jnp.float32)], 0
        )
        gains = jnp.transpose(gains)
        router = dot(normed_own_ref[...], logits_ref[...], ROWS)
        rest = jnp.zeros((rows, side - both - 8 - experts), jnp.float32)
        for h in range(2):
            for c in range(count // 2):
                place = h * (count // 2) + c
                part = slice(place * rows, (place + 1) * rows)
                head_ref[h, :, c * side : (c + 1) * side] = jnp.concatenate(
                    [product_ref[part, :], gains[part], router[part], rest], 1
                )
            half = features // 2
            head_ref[h, :, count // 2 * side :] = out_ref[:, h * half : (h + 1) * half]
        sides = ((0, kept_one_ref, sent_one_ref), (1, kept_two_ref, sent_two_ref))
        for h, kept_ref, sent_ref in sides:
            bit = 1 if h == 0 else reps // 2
            for index in range(reps // 2):
                base = index // bit * 2 * bit + index % bit
                here = slice(index * share, (index + 1) * share)
                lower = head_ref[h, base * share : (base + 1) * share, :]
                upper = head_ref[h, (base + bit) * share : (base + bit + 1) * share, :]
                kept_ref[here, :] = jnp.where(place_ref[2 + h] > 0, upper, lower)
                sent_ref[here, :] = jnp.where(place_ref[2 + h] > 0, lower, upper).astype(jnp.bfloat16)


def close_rows(
    place,
    query,
    pair,
    weight,
    gathered,
    normed,
    gain_two_grad,
    normed_two,
    logits,
    out_rows,
    mixed,
    branch,
    reps,
    side,
    block,
):
    tokens, features = normed.shape
    own = logits.shape[0]
    both = query.shape[1] + pair.shape[1]
    rows_own = mixed.shape[1]
    rows = lambda width: pl.BlockSpec((block, width), lambda i, k: (i, 0))
    resident = lambda *shape: pl.BlockSpec(shape, lambda i, k: (0,) * len(shape))
    shaped = jax.ShapeDtypeStruct
    line = features // rows_own // 2 * side + features // 2
    half = (rows_own // 2, line)
    return pl.pallas_call(
        lambda *refs: close_kernel(reps, *refs),
        name="close",
        out_shape=(
            shaped((tokens, 2 * features), jnp.bfloat16),
            shaped(half, jnp.float32),
            shaped(half, jnp.float32),
            shaped(half, jnp.bfloat16),
            shaped(half, jnp.bfloat16),
        ),
        grid_spec=pltpu.PrefetchScalarGridSpec(
            num_scalar_prefetch=1,
            grid=(tokens // block,),
            in_specs=[
                rows(query.shape[1]),
                rows(pair.shape[1]),
                whole_block(*weight.shape),
                token_rows(block, own, features)[0],
                rows(features),
                whole_block(1, features),
                pl.BlockSpec((own, features), lambda i, p: (p[1], 0)),
                whole_block(*logits.shape),
                rows(features),
                rows(rows_own),
                rows(features),
            ],
            out_specs=[rows(2 * features), *[resident(*half)] * 4],
            scratch_shapes=[
                pltpu.VMEM((features, both), jnp.float32),
                pltpu.VMEM((1, features), jnp.float32),
                pltpu.VMEM((rows_own, features), jnp.float32),
                pltpu.VMEM((2, rows_own, line), jnp.float32),
            ],
        ),
        compiler_params=pltpu.CompilerParams(vmem_limit_bytes=56 << 20),
        cost_estimate=pl.CostEstimate(flops=0, bytes_accessed=tokens, transcendentals=0),
    )(
        place,
        query,
        pair,
        weight,
        gathered,
        normed,
        gain_two_grad,
        normed_two,
        logits,
        out_rows,
        mixed,
        branch,
    )


def head_kernel(
    copies,
    side,
    low_ref,
    high_ref,
    query_ref,
    key_ref,
    value_ref,
    out_ref,
    gains_ref,
    router_ref,
):
    groups = KEY_VALUE_HEADS
    count = groups * copies
    halves = [low_ref[...].astype(jnp.float32), high_ref[...].astype(jnp.float32)]
    width = query_ref.shape[1] // groups
    parts = []
    for c in range(count):
        place = c % (count // 2) * side
        parts.append(halves[c // (count // 2)][:, place : place + side])
    heads = []
    small = 0.0
    for g in range(groups):
        total = parts[g * copies]
        for p in range(1, copies):
            total = total + parts[g * copies + p]
        heads.append(total)
        small = small + total[:, width + 2 * HEAD_SIZE :]
    gains_ref[...] = jnp.transpose(small[:, :8])
    router_ref[...] = small[:, 8 : 8 + router_ref.shape[1]]
    query_ref[...] = jnp.concatenate([head[:, :width] for head in heads], 1)
    key_ref[...] = jnp.concatenate([head[:, width : width + HEAD_SIZE] for head in heads], 1)
    value_ref[...] = jnp.concatenate(
        [head[:, width + HEAD_SIZE : width + 2 * HEAD_SIZE] for head in heads], 1
    )
    out_ref[...] = jnp.concatenate([half[:, count // 2 * side :] for half in halves], 1)


def head_outputs(low, high, copies, side, experts):
    rows = low.shape[0]
    groups = KEY_VALUE_HEADS
    query_width = QUERY_HEADS * HEAD_SIZE
    shaped = lambda width: jax.ShapeDtypeStruct((rows, width), jnp.float32)
    return pl.pallas_call(
        lambda *refs: head_kernel(copies, side, *refs),
        name="head_outputs",
        out_shape=(
            shaped(query_width),
            shaped(groups * HEAD_SIZE),
            shaped(groups * HEAD_SIZE),
            shaped(MODEL_WIDTH),
            jax.ShapeDtypeStruct((8, rows), jnp.float32),
            shaped(experts),
        ),
        compiler_params=pltpu.CompilerParams(vmem_limit_bytes=40 << 20),
        cost_estimate=pl.CostEstimate(flops=0, bytes_accessed=rows, transcendentals=0),
    )(low, high)


def into_kernel(keeps_ref, side, sent_ref, first_ref, second_ref, out_ref):
    kept = pl.program_id(0) == keeps_ref[side]
    came = jnp.where(pl.program_id(1) == 0, first_ref[...], second_ref[...])
    out_ref[...] = jnp.where(kept, sent_ref[...], came).astype(jnp.float32)


def into_output(keeps, side, sent, first, second):
    rows, hidden = first.shape
    part = lambda index: pl.BlockSpec((rows, hidden), index)
    return pl.pallas_call(
        lambda k, *refs: into_kernel(k, side, *refs),
        name="into_output",
        out_shape=jax.ShapeDtypeStruct((2, 2 * rows, hidden), jnp.float32),
        grid_spec=pltpu.PrefetchScalarGridSpec(
            num_scalar_prefetch=1,
            grid=(2, 2),
            in_specs=[
                part(lambda e, h, k: (h, 0)),
                part(lambda e, h, k: (0, 0)),
                part(lambda e, h, k: (0, 0)),
            ],
            out_specs=pl.BlockSpec((None, rows, hidden), lambda e, h, k: (e, h, 0)),
        ),
        compiler_params=pltpu.CompilerParams(vmem_limit_bytes=32 << 20),
        cost_estimate=pl.CostEstimate(flops=0, bytes_accessed=rows, transcendentals=0),
    )(keeps, sent, first, second)


def down_kernel(keeps_ref, sent_low_ref, came_low_ref, sent_high_ref, came_high_ref, out_ref):
    rows, hidden = came_low_ref.shape
    narrow = hidden // 2
    pairs = ((sent_low_ref, came_low_ref), (sent_high_ref, came_high_ref))
    for side, (sent_ref, came_ref) in enumerate(pairs):
        kept = pl.program_id(0) == keeps_ref[side]
        value = jnp.where(kept, sent_ref[...], came_ref[...]).astype(jnp.float32)
        start = side * rows
        out_ref[:, start : start + hidden] = value[:hidden]
        out_ref[:narrow, start + hidden : start + rows] = value[hidden:, :narrow]
        out_ref[narrow:, start + hidden : start + rows] = value[hidden:, narrow:]


def down_output(keeps, sent_low, came_low, sent_high, came_high):
    rows, hidden = came_low.shape
    place = sent_low.shape[0] // rows - 1
    sent = pl.BlockSpec((rows, hidden), lambda e, k: (place, 0))
    came = pl.BlockSpec((rows, hidden), lambda e, k: (0, 0))
    return pl.pallas_call(
        down_kernel,
        out_shape=jax.ShapeDtypeStruct((2, hidden, 2 * rows), jnp.float32),
        grid_spec=pltpu.PrefetchScalarGridSpec(
            num_scalar_prefetch=1,
            grid=(2,),
            in_specs=[sent, came, sent, came],
            out_specs=pl.BlockSpec((None, hidden, 2 * rows), lambda e, k: (e, 0, 0)),
        ),
        compiler_params=pltpu.CompilerParams(vmem_limit_bytes=32 << 20),
        cost_estimate=pl.CostEstimate(flops=0, bytes_accessed=rows, transcendentals=0),
    )(keeps, sent_low, came_low, sent_high, came_high)


def after(values, *others):
    values, _ = lax.optimization_barrier((values, others))
    return values


def swap(value, bit):
    size = lax.axis_size("rep")
    return lax.ppermute(value, "rep", [(i, i ^ bit) for i in range(size)])


def has(bit):
    return (lax.axis_index("rep") & bit) != 0


def join(value, came, bit, axis):
    upper = has(bit)
    return jnp.concatenate(
        [jnp.where(upper, came, value), jnp.where(upper, value, came)], axis
    )


class Chain:
    def __init__(self, order):
        self.order = order
        self.stage = 0
        self.steps = 2 * len(order)

    def send(self, sent):
        bit = self.order[min(self.stage, self.steps - 1 - self.stage)]
        self.sent = sent
        self.stage += 1
        if self.stage < self.steps:
            self.flying = swap(sent, bit)

    def step(self, *others):
        came = after(self.flying, *others)
        self.send(join(self.sent, came, self.order[self.steps - self.stage], 0))
        return self.sent

    def piece(self, number, count, *others):
        rows = self.sent.shape[0] // count
        part = after(self.sent[number * rows : (number + 1) * rows], *others)
        return swap(part, self.order[0])


def halve_kernel(keeps_ref, *refs):
    count = len(refs) // 3
    for chain in range(2):
        for place in range(0, count, 2):
            value_ref, came_ref = refs[count * chain + place : count * chain + place + 2]
            out_ref = refs[2 * count + chain * (count // 2) + place // 2]
            out_ref[...] = (value_ref[...] + came_ref[...].astype(jnp.float32)).astype(
                out_ref.dtype
            )


def halve_chains(chains, *others):
    order = [chain.order[chain.stage] for chain in chains]
    last = chains[0].stage == len(chains[0].order) - 1
    keeps = jnp.stack([has(bit) for bit in order]).astype(jnp.int32)
    rows, hidden = chains[0].kept.shape
    count = 4
    part = rows // 2 // count
    operands, specs = [], []
    for c, chain in enumerate(chains):
        chain.came = after(chain.flying, *others)
        for flip in (1,) if last else (1, 0):
            index = lambda i, k, c=c, flip=flip: ((k[c] ^ flip) * count + i, 0)
            operands += [chain.kept, chain.came]
            specs += [pl.BlockSpec((part, hidden), index)] * 2
    block = pl.BlockSpec((part, hidden), lambda i, k: (i, 0))
    shaped = lambda dtype: jax.ShapeDtypeStruct((rows // 2, hidden), dtype)
    each = [shaped(jnp.bfloat16)] if last else [shaped(jnp.bfloat16), shaped(jnp.float32)]
    outs = pl.pallas_call(
        halve_kernel,
        out_shape=each * 2,
        grid_spec=pltpu.PrefetchScalarGridSpec(
            num_scalar_prefetch=1,
            grid=(count,),
            in_specs=specs,
            out_specs=[block] * (2 * len(each)),
        ),
        compiler_params=pltpu.CompilerParams(vmem_limit_bytes=58 << 20),
        cost_estimate=pl.CostEstimate(
            flops=60000 * rows * hidden, bytes_accessed=12 * rows * hidden, transcendentals=0
        ),
    )(keeps, *operands)
    for c, chain in enumerate(chains):
        if not last:
            chain.kept = outs[2 * c + 1]
        chain.send(outs[len(each) * c])
    return [chain.sent for chain in chains]


def total_kernel(keeps_ref, *refs):
    for chain in range(2):
        kept_ref, first_ref, second_ref = refs[3 * chain : 3 * chain + 3]
        total = kept_ref[...] + first_ref[...].astype(jnp.float32)
        refs[6 + chain][...] = (total + second_ref[...].astype(jnp.float32)).astype(jnp.bfloat16)


def total_chains(chains, *others):
    keeps = jnp.stack([has(chain.order[-1]) for chain in chains]).astype(jnp.int32)
    rows, hidden = chains[0].kept.shape
    count = 4
    part = rows // 2 // count
    block = pl.BlockSpec((part, hidden), lambda i, k: (i, 0))
    operands, specs = [], []
    for c, chain in enumerate(chains):
        stay = pl.BlockSpec((part, hidden), lambda i, k, c=c: (k[c] * count + i, 0))
        operands += [chain.kept, chain.came, after(chain.flying, *others)]
        specs += [stay, stay, block]
    outs = pl.pallas_call(
        total_kernel,
        out_shape=[jax.ShapeDtypeStruct((rows // 2, hidden), jnp.bfloat16)] * 2,
        grid_spec=pltpu.PrefetchScalarGridSpec(
            num_scalar_prefetch=1, grid=(count,), in_specs=specs, out_specs=[block] * 2
        ),
        compiler_params=pltpu.CompilerParams(vmem_limit_bytes=58 << 20),
        cost_estimate=pl.CostEstimate(flops=0, bytes_accessed=rows, transcendentals=0),
    )(keeps, *operands)
    for chain, out in zip(chains, outs):
        chain.send(out)
    return list(outs)


class Cube:
    def __init__(self, kept, sent, order, share):
        shape = [2] * len(order)
        shape[len(order) - order[0].bit_length()] = 1
        self.value, sent = [array.reshape(*shape, share, -1) for array in (kept, sent)]
        self.order = order
        self.flying = swap(sent, order[0])
        self.stage = 1

    def axis(self, bit):
        return len(self.order) - bit.bit_length()

    def halve(self, *others):
        bit = self.order[self.stage]
        keep = has(bit).astype(jnp.int32)
        part = lambda index: lax.dynamic_slice_in_dim(self.value, index, 1, self.axis(bit))
        self.value, sent = part(keep), part(1 - keep).astype(jnp.bfloat16)
        self.flying = swap(after(sent, *others), bit)
        self.stage += 1
        return sent

    def add(self, *others):
        self.value = self.value + after(self.flying, *others).astype(jnp.float32)

    def back(self, *others):
        self.stage -= 1
        self.flying = swap(after(self.value, *others), self.order[self.stage])
        return self.value

    def join(self, *others):
        bit = self.order[self.stage]
        self.value = join(self.value, after(self.flying, *others), bit, self.axis(bit))


def halve_cubes_kernel(keeps_ref, *refs):
    for h in range(2):
        value_ref, came_ref = refs[2 * h : 2 * h + 2]
        kept_ref, sent_ref = refs[4 + 2 * h : 6 + 2 * h]
        keep = keeps_ref[h]
        kept_ref[...] = value_ref[keep] + came_ref[keep].astype(jnp.float32)
        sent = value_ref[1 - keep] + came_ref[1 - keep].astype(jnp.float32)
        sent_ref[...] = sent.astype(jnp.bfloat16)


def scalar_call(kernel, outs, scalars, *operands, scratch=(), flops=0):
    whole = lambda array: pl.BlockSpec(array.shape, lambda i, p: (0,) * len(array.shape))
    return pl.pallas_call(
        kernel,
        out_shape=outs,
        grid_spec=pltpu.PrefetchScalarGridSpec(
            num_scalar_prefetch=1,
            grid=(1,),
            in_specs=[whole(array) for array in operands],
            out_specs=[whole(out) for out in outs],
            scratch_shapes=scratch,
        ),
        name="scalar_call",
        compiler_params=pltpu.CompilerParams(vmem_limit_bytes=58 << 20),
        cost_estimate=pl.CostEstimate(flops=flops, bytes_accessed=1024, transcendentals=0),
    )(scalars, *operands)


def halve_cubes(cubes, *others):
    share, line = cubes[0].value.shape[-2:]
    if cubes[0].stage < len(cubes[0].order) - 1:
        for cube in cubes:
            cube.add(*others)
        return [cube.halve() for cube in cubes]
    order = [cube.order[cube.stage] for cube in cubes]
    keeps = jnp.stack([has(bit) for bit in order]).astype(jnp.int32)
    shaped = lambda dtype: jax.ShapeDtypeStruct((share, line), dtype)
    operands = []
    for cube in cubes:
        operands += [cube.value.reshape(2, share, line)]
        operands += [after(cube.flying, *others).reshape(2, share, line)]
    outs = scalar_call(
        halve_cubes_kernel, [shaped(jnp.float32), shaped(jnp.bfloat16)] * 2, keeps, *operands
    )
    for h, cube in enumerate(cubes):
        cube.value, sent = outs[2 * h : 2 * h + 2]
        cube.flying = swap(sent, order[h])
        cube.stage += 1
    return outs[1::2]


def pack_kernel(size, side, place_ref, *refs):
    chips = size // 2
    values = refs[:4]
    out_ref = refs[4 + chips]
    all_ref = refs[5 + chips]
    for h in range(2):
        total = values[2 * h][...] + values[2 * h + 1][...].astype(jnp.float32)
        total = total.astype(jnp.bfloat16)
        for c in range(chips):
            all_ref[h * chips + c] = total[:, c * side : (c + 1) * side]
        out_ref[h] = total[:, chips * side :]
    for k in range(chips):
        chip = lax.rem(place_ref[0] - k + chips, chips)
        for core in range(2):
            refs[4 + k][core] = all_ref[2 * chip + core]


def pack_heads(place, cubes, size, side):
    chips = size // 2
    share, line = cubes[0].value.shape[-2:]
    low = jnp.bfloat16
    outs = [jax.ShapeDtypeStruct((2, share, side), low)] * chips
    outs.append(jax.ShapeDtypeStruct((2, share, line - chips * side), low))
    operands = []
    for cube in cubes:
        operands += [cube.value.reshape(share, line), cube.flying.reshape(share, line)]
    *parcels, out_sums = scalar_call(
        lambda *refs: pack_kernel(size, side, *refs),
        outs,
        place,
        *operands,
        scratch=[pltpu.VMEM((size, share, side), low)],
        flops=200000000000,
    )
    return parcels, out_sums


def split_kernel(place_ref, *refs):
    chips = len(refs) - 2
    core = lax.rem(place_ref[1], 2)
    for k in range(chips):
        refs[chips][k] = refs[k][core]
        refs[chips + 1][k] = refs[k][1 - core]


def split_cores(place, got):
    out = jax.ShapeDtypeStruct((len(got),) + got[0].shape[1:], got[0].dtype)
    return scalar_call(split_kernel, [out, out], place, *got)


def unpack_kernel(place_ref, stay_ref, came_ref, out_ref, low_ref, high_ref, all_ref):
    chips, _, side = stay_ref.shape
    core = lax.rem(place_ref[1], 2)
    for k in range(chips):
        chip = lax.rem(place_ref[0] + k, chips)
        all_ref[2 * chip + core] = stay_ref[k]
        all_ref[2 * chip + 1 - core] = came_ref[k]
    for h, rows_ref in enumerate((low_ref, high_ref)):
        for c in range(chips):
            rows_ref[:, c * side : (c + 1) * side] = all_ref[h * chips + c]
        rows_ref[:, chips * side :] = out_ref[h]


def unpack_heads(place, stay, came, out_sums):
    chips, share, side = stay.shape
    line = chips * side + out_sums.shape[2]
    out = jax.ShapeDtypeStruct((share, line), stay.dtype)
    return scalar_call(
        unpack_kernel,
        [out, out],
        place,
        stay,
        came,
        out_sums,
        scratch=[pltpu.VMEM((2 * chips, share, side), stay.dtype)],
    )


class Exchange:
    def __init__(self, fetched, bits):
        size = fetched.shape[0]
        fetched = fetched.reshape((size,) + (1,) * len(bits) + fetched.shape[1:])
        self.values = [fetched[: size // 2], fetched[size // 2 :]]
        self.orders = (bits, bits[::-1])
        self.stage = 0
        self.fly()

    def fly(self):
        self.flying = [
            swap(value, order[self.stage]) for value, order in zip(self.values, self.orders)
        ]

    def step(self, *others):
        bits = len(self.orders[0])
        for h, order in enumerate(self.orders):
            bit = order[self.stage]
            came = after(self.flying[h], *others)
            self.values[h] = join(self.values[h], came, bit, bits - (bit.bit_length() - 1))
        self.stage += 1
        if self.stage < bits:
            self.fly()
        return list(self.values)

    def finish(self, *others):
        while self.stage < len(self.orders[0]):
            self.step(*others)
        return [value.reshape(-1, value.shape[-1]) for value in self.values]


def per_device(
    inputs,
    segments,
    positions,
    expert_ids,
    attn_gain,
    w_query,
    key_weight,
    value_weight,
    w_out,
    ffn_gain,
    router,
    w_gate,
    w_up,
    w_down,
    grad_out,
):
    size = lax.axis_size("ctx")
    me = lax.axis_index("ctx")
    reps = lax.axis_size("rep")
    bits = [1 << i for i in range(reps.bit_length() - 1)]
    own = inputs.shape[1]
    tokens = size * own
    groups = KEY_VALUE_HEADS
    copies = size // groups
    query_width = HEAD_GROUP * HEAD_SIZE
    width = query_width + 2 * HEAD_SIZE
    copy_index = me % copies
    rows_own = w_out.shape[0]
    experts_own = w_gate.shape[0]
    experts_all = size * experts_own
    block = 2 * own
    chips = size // 2
    chip = me // 2
    odd = me % 2 == 1
    share = rows_own // reps
    share_start = lax.axis_index("rep") * share

    columns = jnp.concatenate(
        [
            segments[0][:, None],
            positions[0][:, None] // 64,
            positions[0][:, None] % 64,
            expert_ids[0],
        ],
        1,
    ).astype(jnp.bfloat16)
    columns = jnp.pad(columns, ((0, 0), (0, 128 - columns.shape[1])))
    shared = lambda array: lax.dynamic_slice_in_dim(array, share_start, share, 0)

    rows = jnp.concatenate(
        [
            jnp.concatenate([inputs[0], columns], 1),
            jnp.pad(shared(w_out), ((0, 0), (0, 128))),
        ],
        0,
    )
    gathered = lax.all_gather(rows, "ctx", axis=0)
    cotangent = lax.all_gather(after(grad_out[0], rows), "ctx", axis=0, tiled=True)

    def from_chip(value, k):
        return lax.ppermute(value, "ctx", [(i, (i - 2 * k) % size) for i in range(size)])

    def from_core(value):
        return lax.ppermute(value, "ctx", [(i, i ^ 1) for i in range(size)])

    def cores(mine, others, axis):
        return jnp.concatenate(
            [jnp.where(odd, others, mine), jnp.where(odd, mine, others)], axis
        )

    side_width = -(-(width + 2 + router.shape[1]) // 128) * 128
    head_columns = jnp.concatenate(
        [
            shared(w_query).reshape(share, groups, query_width),
            shared(key_weight).reshape(share, groups, HEAD_SIZE),
            shared(value_weight).reshape(share, groups, HEAD_SIZE),
            jnp.broadcast_to(shared(attn_gain)[:, None, None], (share, groups, 1)),
            jnp.broadcast_to(shared(ffn_gain)[:, None, None], (share, groups, 1)),
            jnp.broadcast_to(shared(router)[:, None, :], (share, groups, router.shape[1])),
        ],
        -1,
    )
    used = head_columns.shape[-1]
    head_columns = jnp.pad(head_columns, ((0, 0), (0, 0), (0, side_width - used)))
    head_columns = jnp.repeat(jnp.transpose(head_columns, (1, 0, 2)), copies, 0)
    head_columns = lax.all_to_all(head_columns, "ctx", split_axis=0, concat_axis=0, tiled=True)
    head_halves = Exchange(head_columns, bits).finish()
    head_all = jnp.concatenate(head_halves, 0)
    gain_one = head_all[:, width].astype(jnp.float32)
    gain_two = head_all[:, width + 1].astype(jnp.float32)
    router_all = head_all[:, width + 2 : used]

    (
        normed_one,
        query,
        key,
        value,
        mixed,
        packed,
        log_total,
        cosine_table,
        sine_table,
        segment_rows,
    ) = attend(gathered, gain_one, head_halves, own, block)
    out_exchange = Exchange(gathered[:, own:, :MODEL_WIDTH], bits)

    part = tokens // copies
    mixed_all = lax.all_gather(
        after(
            lax.dynamic_slice_in_dim(packed, copy_index * part // 2, part // 2, 0),
            cotangent,
            out_exchange.step(),
        ),
        "ctx",
        axis=0,
    ).reshape(groups, tokens // 2, 2 * query_width)
    w_out_halves = out_exchange.finish()

    middle, normed_two, gates = middle_rows(
        mixed_all, w_out_halves, gathered, gain_two, router_all, own, block
    )
    flag = lambda bit: has(bit).astype(jnp.int32)
    place = jnp.stack([chip, me, flag(bits[0]), flag(bits[-1])]).astype(jnp.int32)
    scaled_one, scaled_two, grad_gate_pre, grad_up_pre, grad_live, extra = expert_rows(
        place, normed_two, cotangent, gathered, gates, w_gate, w_up, w_down, own, block
    )
    def mine(array):
        return lax.dynamic_slice_in_dim(array, me * own, own, 0)

    products = lambda e, dtype: expert_products(
        normed_two, grad_gate_pre, grad_up_pre, scaled_one, scaled_two, grad_live, e, dtype
    )
    grad_rows = gradient_rows(place, grad_gate_pre, grad_up_pre, extra, w_gate, w_up, block)
    grad_two_sum = lax.psum_scatter(grad_rows, "ctx", scatter_dimension=0, tiled=True)
    normed_two, grad_live = after((normed_two, grad_live), grad_rows)
    chains = [Chain(bits), Chain(bits[::-1])]
    for chain, sent in zip(chains, products(0, jnp.bfloat16)):
        chain.send(sent)
    normed_two, grad_live = after((normed_two, grad_live), *[chain.sent for chain in chains])
    for chain, kept in zip(chains, products(1, jnp.float32)):
        chain.kept = kept
    out_rows = output_rows(place, after(scaled_one, *[c.kept for c in chains]), w_down, block)

    grad_middle, grad_branch, grad_mixed, grad_logits, gain_two_grad = turn_rows(
        place,
        after(grad_two_sum, out_rows),
        gates,
        router_all,
        gain_two,
        middle,
        grad_live,
        w_out_halves,
    )
    grad_branch_all = lax.all_gather(grad_branch, "ctx", axis=0, tiled=True)

    def deal_chips(blocks):
        blocks = blocks.reshape((chips, 2) + blocks.shape[1:])
        got = [blocks[(chip - k) % chips] for k in range(chips)]
        return jnp.stack([got[0]] + [from_chip(got[k], k) for k in range(1, chips)])

    def deal_cores(got):
        stay = jnp.where(odd, got[:, 1], got[:, 0])
        go = from_core(jnp.where(odd, got[:, 0], got[:, 1]))
        both = cores(stay[:, None], go[:, None], 1)
        both = jnp.concatenate([both, both], 0)
        both = lax.dynamic_slice_in_dim(both, (chips - chip) % chips, chips, 0)
        return both.reshape((size,) + both.shape[2:])

    got = deal_chips(jnp.repeat(grad_mixed, copies, 0))
    sent = [got]
    while chains[0].stage < len(bits):
        sent = halve_chains(chains, *sent)
    grad_mixed_all = deal_cores(after(got, *sent)).reshape(tokens, query_width)
    grad_query, grad_pair = attend_back(
        query,
        grad_mixed_all,
        log_total,
        cosine_table,
        sine_table,
        gathered,
        segment_rows,
        key,
        value,
        own,
    )
    if copies > 1:
        places = jnp.arange(tokens, dtype=jnp.int32)
        counted = (places // part == copy_index)[:, None]
        grad_query = jnp.where(counted, grad_query, jnp.zeros((), jnp.bfloat16))
        grad_pair = jnp.where(counted, grad_pair, jnp.zeros((), jnp.bfloat16))
    sent = total_chains(chains, grad_pair)
    both_rows, *halves = close_rows(
        place,
        after(grad_query, *sent),
        grad_pair,
        head_all,
        gathered,
        normed_one,
        gain_two_grad,
        normed_two,
        grad_logits,
        out_rows,
        lax.dynamic_slice_in_dim(mixed, copy_index * rows_own, rows_own, 1),
        grad_branch_all,
        reps,
        side_width,
        block,
    )
    both_sums = lax.psum_scatter(
        both_rows, "ctx", scatter_dimension=0, tiled=True
    ).astype(jnp.float32)
    grad_one, out_sum = both_sums[:, :MODEL_WIDTH], both_sums[:, MODEL_WIDTH:]

    line = size // 2 * side_width
    cubes = [
        Cube(halves[h], halves[2 + h], order, share)
        for h, order in enumerate((bits, bits[::-1]))
    ]
    while chains[0].stage < chains[0].steps:
        sent = [chain.step(*halves) for chain in chains]
    while cubes[0].stage < len(bits):
        sent = halve_cubes(cubes, *sent)
    first = [chain.piece(0, 3) for chain in chains]
    second = [chain.piece(1, 3, *sent) for chain in chains]
    for cube in cubes:
        cube.flying = after(cube.flying, *sent)
    parcels, out_sums = pack_heads(place, cubes, size, side_width)
    parcels = after(parcels, *first)
    got = [parcels[0]] + [from_chip(parcels[k], k) for k in range(1, chips)]
    stay, go = split_cores(place, got)
    came = from_core(after(go, *second))
    for cube, value in zip(cubes, unpack_heads(place, stay, came, out_sums)):
        cube.value = value.reshape((1,) * len(bits) + value.shape)
    sent = [cube.back() for cube in cubes]
    third = [chain.piece(2, 3, *sent, *[cube.flying for cube in cubes]) for chain in chains]
    keeps = place[2:]
    grad_gate, grad_up = [
        into_output(keeps, side, *after((chain.sent, first[side], second[side]), *sent))
        for side, chain in enumerate(chains)
    ]
    for cube in cubes:
        cube.join(grad_gate, grad_up)
    while cubes[0].stage > 0:
        sent = [cube.back() for cube in cubes]
        if cubes[0].stage > 0:
            for cube in cubes:
                cube.join(*sent)
    output = jnp.where((segments[0] != 0)[:, None], mine(after(middle, grad_mixed)) + out_sum, 0.0)
    own_hidden = inputs[0].astype(jnp.float32)
    own_scale = lax.rsqrt(jnp.mean(own_hidden * own_hidden, -1, keepdims=True) + EPS)
    grad_in = grad_middle + norm_back(grad_one * gain_one, own_hidden * own_scale, own_scale)
    grad_down = down_output(
        keeps,
        *after((chains[0].sent, third[0], chains[1].sent, third[1]), *sent),
    )
    for cube in cubes:
        cube.join(grad_down, output, grad_in)
    head_outs = head_outputs(
        *[cube.value.reshape(rows_own, -1) for cube in cubes], copies, side_width, experts_all
    )
    return (
        output.astype(jnp.bfloat16)[None],
        grad_in[None],
        head_outs[4][0],
        *head_outs[:4],
        head_outs[4][1],
        head_outs[5],
        grad_gate,
        grad_up,
        grad_down,
    )


def solution(mesh):
    return jax.shard_map(
        per_device,
        mesh=mesh,
        in_specs=(
            P("rep", "ctx", None),
            P("rep", "ctx"),
            P("rep", "ctx"),
            P("rep", "ctx", None),
            P("ctx"),
            P("ctx", None),
            P("ctx", None),
            P("ctx", None),
            P("ctx", None),
            P("ctx"),
            P("ctx", None),
            P("ctx", None, None),
            P("ctx", None, None),
            P("ctx", None, None),
            P("rep", "ctx", None),
        ),
        out_specs=(
            P("rep", "ctx", None),
            P("rep", "ctx", None),
            P("ctx"),
            P("ctx", None),
            P("ctx", None),
            P("ctx", None),
            P("ctx", None),
            P("ctx"),
            P("ctx", None),
            P("ctx", None, None),
            P("ctx", None, None),
            P("ctx", None, None),
        ),
        check_vma=False,
    )
```

```python
import jax
import jax.numpy as jnp
from jax import lax
from jax.experimental import pallas as pl
from jax.experimental.pallas import tpu as pltpu
from jax.sharding import PartitionSpec as P

MODEL_WIDTH = 1536
QUERY_HEADS = 24
KEY_VALUE_HEADS = 8
HEAD_GROUP = QUERY_HEADS // KEY_VALUE_HEADS
HEAD_SIZE = 64
TOPK = 8

EPS = 1e-06
THETA = 10000.0
MASK_FLOOR = -1e30

ROWS = (((0,), (0,)), ((), ()))
COLUMNS = (((1,), (1,)), ((), ()))


def dot(left, right, contract=(((1,), (0,)), ((), ()))):
    return lax.dot_general(left, right, contract, preferred_element_type=jnp.float32)


def norm_back(grad_base, base, scale):
    return scale * (grad_base - base * jnp.mean(grad_base * base, -1, keepdims=True))


def turn(rows):
    half = HEAD_SIZE // 2
    return jnp.concatenate([-rows[:, half:], rows[:, :half]], 1)


def turn_back(rows):
    half = HEAD_SIZE // 2
    return jnp.concatenate([rows[:, half:], -rows[:, :half]], 1)


def stack_heads(rows):
    return jnp.concatenate(
        [rows[:, h * HEAD_SIZE : (h + 1) * HEAD_SIZE] for h in range(HEAD_GROUP)], 0
    )


def side_heads(rows):
    block = rows.shape[0] // HEAD_GROUP
    return jnp.concatenate([rows[h * block : (h + 1) * block] for h in range(HEAD_GROUP)], 1)


def lanes(values, combine):
    total = values[:, :128]
    for start in range(128, values.shape[1], 128):
        total = combine(total, values[:, start : start + 128])
    return total


def masked_scores(stacked, keys, row_segments, key_segments, row_start, key_start):
    block = row_segments.shape[0]
    scores = dot(stacked, keys, COLUMNS) * HEAD_SIZE ** (-0.5)
    row_place = row_start + lax.broadcasted_iota(jnp.int32, (block, block), 0)
    key_place = key_start + lax.broadcasted_iota(jnp.int32, (block, block), 1)
    allowed = (row_segments == key_segments) & (key_place <= row_place)
    scores = scores.reshape(HEAD_GROUP, block, block)
    return jnp.where(allowed[None], scores, MASK_FLOOR).reshape(HEAD_GROUP * block, block)


def first_block(row_segments, segment_ref, step):
    here = jnp.max(row_segments[:1, :1])
    segments = segment_ref[...]
    number = lax.broadcasted_iota(jnp.int32, segments.shape, 0)
    return jnp.min(jnp.where((segments == here) & (number <= step), number, step))


def token_rows(block, own, features):
    count = block // own
    return (
        pl.BlockSpec((count, own, features), lambda i, *_: (i, 0, 0)),
        pl.BlockSpec((count, own, 128), lambda i, *_: (i, 0, features // 128)),
    )


def flat(ref):
    return ref[...].reshape(-1, ref.shape[-1])


def whole_block(*shape):
    return pl.BlockSpec(shape, lambda *i: (0,) * len(shape), pipeline_mode=pl.Buffered(1))


def attend_kernel(
    hidden_ref,
    column_ref,
    gain_ref,
    low_ref,
    high_ref,
    rate_ref,
    normed_ref,
    query_ref,
    key_ref,
    value_ref,
    mixed_ref,
    packed_ref,
    log_ref,
    cosine_ref,
    sine_ref,
    segment_ref,
    score_ref,
):
    step = pl.program_id(0)
    block = query_ref.shape[0]
    query_width = query_ref.shape[1]
    width = query_width + 2 * HEAD_SIZE
    here = pl.ds(pl.multiple_of(step * block, block), block)
    columns = flat(column_ref).astype(jnp.float32)
    row_segments = columns[:, :1]
    segment_ref[step] = jnp.transpose(columns)[:1, :]
    angles = (columns[:, 1:2] * 64.0 + columns[:, 2:3]) * rate_ref[...]
    cosine = jnp.cos(angles)
    sine = jnp.sin(angles)
    cosine_ref[...] = cosine
    sine_ref[...] = sine
    hidden = flat(hidden_ref).astype(jnp.float32)
    scale = lax.rsqrt(jnp.mean(hidden * hidden, -1, keepdims=True) + EPS)
    normed = (hidden * scale * gain_ref[...]).astype(jnp.bfloat16)
    normed_ref[...] = normed
    middle = low_ref.shape[0]
    raw = dot(normed[:, :middle], low_ref[:, :width]) + dot(
        normed[:, middle:], high_ref[:, :width]
    )
    key_raw = raw[:, query_width : query_width + HEAD_SIZE]
    key_ref[here, :] = (key_raw * cosine + turn(key_raw) * sine).astype(jnp.bfloat16)
    value_ref[here, :] = raw[:, query_width + HEAD_SIZE :].astype(jnp.bfloat16)
    query_raw = stack_heads(raw[:, :query_width])
    cosine = jnp.concatenate([cosine] * HEAD_GROUP, 0)
    sine = jnp.concatenate([sine] * HEAD_GROUP, 0)
    query = (query_raw * cosine + turn(query_raw) * sine).astype(jnp.bfloat16)
    query_ref[...] = side_heads(query)
    rows = HEAD_GROUP * block
    first = first_block(row_segments, segment_ref, step)

    def first_pass(index, top):
        there = pl.ds(pl.multiple_of(index * block, block), block)
        scores = masked_scores(
            query,
            key_ref[there, :],
            row_segments,
            segment_ref[index],
            step * block,
            index * block,
        )
        score_ref[index] = scores
        return jnp.maximum(top, lanes(scores, jnp.maximum))

    top = lax.fori_loop(
        first, step + 1, first_pass, jnp.full((rows, 128), MASK_FLOOR, jnp.float32)
    )
    top = jnp.max(top, -1, keepdims=True)

    def second_pass(index, carry):
        total, mixed = carry
        there = pl.ds(pl.multiple_of(index * block, block), block)
        weights = jnp.exp(score_ref[index] - top)
        mixed = mixed + dot(weights.astype(jnp.bfloat16), value_ref[there, :])
        return total + lanes(weights, jnp.add), mixed

    total, mixed = lax.fori_loop(
        first,
        step + 1,
        second_pass,
        (
            jnp.zeros((rows, 128), jnp.float32),
            jnp.zeros((rows, HEAD_SIZE), jnp.float32),
        ),
    )
    total = jnp.sum(total, -1, keepdims=True)
    mixed = side_heads((mixed / total).astype(jnp.bfloat16))
    mixed_ref[...] = mixed
    packed_ref[...] = jnp.concatenate([mixed[: block // 2], mixed[block // 2 :]], 1)
    log_ref[...] = (top + jnp.log(total)).reshape(HEAD_GROUP, block, 1)


def attend(gathered, gain, weights, own, block):
    tokens, features = gathered.shape[0] * own, gain.shape[0]
    query_width = HEAD_GROUP * HEAD_SIZE
    steps = tokens // block
    half = jnp.arange(HEAD_SIZE // 2, dtype=jnp.float32)
    rate = THETA ** (-(2.0 * half) / HEAD_SIZE)
    rate = jnp.concatenate([rate, rate])[None, :]
    rows = lambda width: pl.BlockSpec((block, width), lambda i: (i, 0))
    resident = lambda *shape: pl.BlockSpec(shape, lambda i: (0,) * len(shape))
    shaped = jax.ShapeDtypeStruct
    return pl.pallas_call(
        attend_kernel,
        out_shape=(
            shaped((tokens, features), jnp.bfloat16),
            shaped((tokens, query_width), jnp.bfloat16),
            shaped((tokens, HEAD_SIZE), jnp.bfloat16),
            shaped((tokens, HEAD_SIZE), jnp.bfloat16),
            shaped((tokens, query_width), jnp.bfloat16),
            shaped((tokens // 2, 2 * query_width), jnp.bfloat16),
            shaped((HEAD_GROUP, tokens, 1), jnp.float32),
            shaped((tokens, HEAD_SIZE), jnp.float32),
            shaped((tokens, HEAD_SIZE), jnp.float32),
            shaped((steps, 1, block), jnp.float32),
        ),
        grid=(steps,),
        in_specs=[
            *token_rows(block, own, features),
            whole_block(1, features),
            whole_block(*weights[0].shape),
            whole_block(*weights[1].shape),
            whole_block(1, HEAD_SIZE),
        ],
        out_specs=[
            rows(features),
            rows(query_width),
            resident(tokens, HEAD_SIZE),
            resident(tokens, HEAD_SIZE),
            rows(query_width),
            pl.BlockSpec((block // 2, 2 * query_width), lambda i: (i, 0)),
            pl.BlockSpec((HEAD_GROUP, block, 1), lambda i: (0, i, 0)),
            rows(HEAD_SIZE),
            rows(HEAD_SIZE),
            resident(steps, 1, block),
        ],
        scratch_shapes=[pltpu.VMEM((steps, HEAD_GROUP * block, block), jnp.float32)],
        compiler_params=pltpu.CompilerParams(vmem_limit_bytes=48 << 20),
        cost_estimate=pl.CostEstimate(flops=0, bytes_accessed=tokens, transcendentals=0),
    )(gathered, gathered, gain[None, :], *weights, rate)


def attend_back_kernel(
    query_ref,
    grad_ref,
    log_ref,
    cosine_ref,
    sine_ref,
    column_ref,
    segment_ref,
    key_ref,
    value_ref,
    key_cosine_ref,
    key_sine_ref,
    grad_query_ref,
    grad_pair_ref,
    probs_ref,
    grad_probs_ref,
    grad_key_ref,
    grad_value_ref,
):
    step = pl.program_id(0)
    block = query_ref.shape[0]
    rows = HEAD_GROUP * block

    @pl.when(step == 0)
    def _():
        grad_key_ref[...] = jnp.zeros_like(grad_key_ref)
        grad_value_ref[...] = jnp.zeros_like(grad_value_ref)

    query = stack_heads(query_ref[...])
    grad = stack_heads(grad_ref[...])
    log_total = log_ref[...].reshape(rows, 1)
    row_segments = flat(column_ref).astype(jnp.float32)[:, :1]
    first = first_block(row_segments, segment_ref, step)

    def first_pass(index, delta):
        there = pl.ds(pl.multiple_of(index * block, block), block)
        scores = masked_scores(
            query,
            key_ref[there, :],
            row_segments,
            segment_ref[index],
            step * block,
            index * block,
        )
        probs = jnp.exp(scores - log_total)
        grad_probs = dot(grad, value_ref[there, :], COLUMNS)
        probs_ref[index] = probs
        grad_probs_ref[index] = grad_probs
        grad_value_ref[there, :] += dot(probs.astype(jnp.bfloat16), grad, ROWS)
        return delta + lanes(probs * grad_probs, jnp.add)

    delta = lax.fori_loop(first, step + 1, first_pass, jnp.zeros((rows, 128), jnp.float32))
    delta = jnp.sum(delta, -1, keepdims=True)

    def second_pass(index, grad_query):
        there = pl.ds(pl.multiple_of(index * block, block), block)
        grad_scores = (probs_ref[index] * (grad_probs_ref[index] - delta)).astype(jnp.bfloat16)
        grad_key_ref[there, :] += dot(grad_scores, query, ROWS)
        return grad_query + dot(grad_scores, key_ref[there, :])

    grad_query = lax.fori_loop(
        first, step + 1, second_pass, jnp.zeros((rows, HEAD_SIZE), jnp.float32)
    )
    score_scale = HEAD_SIZE ** (-0.5)
    cosine = jnp.concatenate([cosine_ref[...]] * HEAD_GROUP, 0)
    sine = jnp.concatenate([sine_ref[...]] * HEAD_GROUP, 0)
    grad_query = grad_query * score_scale
    grad_query = grad_query * cosine + turn_back(grad_query * sine)
    grad_query_ref[...] = side_heads(grad_query.astype(jnp.bfloat16))

    @pl.when(step == pl.num_programs(0) - 1)
    def _():
        @pl.loop(0, pl.num_programs(0))
        def _(index):
            there = pl.ds(pl.multiple_of(index * block, block), block)
            grad_key = grad_key_ref[there, :] * score_scale
            turned = turn_back(grad_key * key_sine_ref[there, :])
            grad_key = grad_key * key_cosine_ref[there, :] + turned
            grad_pair_ref[there, :] = jnp.concatenate(
                [grad_key, grad_value_ref[there, :]], 1
            ).astype(jnp.bfloat16)


def attend_back(query, grad, log_total, cosine, sine, gathered, segments, key, value, own):
    tokens, query_width = query.shape
    steps, _, block = segments.shape
    features = gathered.shape[2] - 128
    rows = lambda width: pl.BlockSpec((block, width), lambda i: (i, 0))
    resident = lambda *shape: pl.BlockSpec(shape, lambda i: (0,) * len(shape))
    return pl.pallas_call(
        attend_back_kernel,
        out_shape=(
            jax.ShapeDtypeStruct((tokens, query_width), jnp.bfloat16),
            jax.ShapeDtypeStruct((tokens, 2 * HEAD_SIZE), jnp.bfloat16),
        ),
        grid=(steps,),
        in_specs=[
            rows(query_width),
            rows(query_width),
            pl.BlockSpec((HEAD_GROUP, block, 1), lambda i: (0, i, 0)),
            rows(HEAD_SIZE),
            rows(HEAD_SIZE),
            token_rows(block, own, features)[1],
            whole_block(steps, 1, block),
            whole_block(tokens, HEAD_SIZE),
            whole_block(tokens, HEAD_SIZE),
            whole_block(tokens, HEAD_SIZE),
            whole_block(tokens, HEAD_SIZE),
        ],
        out_specs=[rows(query_width), resident(tokens, 2 * HEAD_SIZE)],
        scratch_shapes=[
            pltpu.VMEM((steps, HEAD_GROUP * block, block), jnp.float32),
            pltpu.VMEM((steps, HEAD_GROUP * block, block), jnp.float32),
            pltpu.VMEM((tokens, HEAD_SIZE), jnp.float32),
            pltpu.VMEM((tokens, HEAD_SIZE), jnp.float32),
        ],
        compiler_params=pltpu.CompilerParams(vmem_limit_bytes=48 << 20),
        cost_estimate=pl.CostEstimate(flops=0, bytes_accessed=tokens, transcendentals=0),
    )(query, grad, log_total, cosine, sine, gathered, segments, key, value, cosine, sine)


def middle_kernel(
    mixed_ref,
    low_ref,
    high_ref,
    hidden_ref,
    column_ref,
    gain_ref,
    router_ref,
    middle_ref,
    normed_ref,
    gates_ref,
):
    groups = mixed_ref.shape[0]
    width = mixed_ref.shape[2] // 2
    mixed = jnp.concatenate(
        [
            jnp.concatenate([mixed_ref[g, :, side : side + width] for g in range(groups)], 1)
            for side in (0, width)
        ],
        0,
    )
    half = low_ref.shape[0]
    middle = dot(mixed[:, :half], low_ref[...]) + dot(mixed[:, half:], high_ref[...])
    middle = flat(hidden_ref).astype(jnp.float32) + middle
    middle_ref[...] = middle
    scale = lax.rsqrt(jnp.mean(middle * middle, -1, keepdims=True) + EPS)
    normed = (middle * scale * gain_ref[...]).astype(jnp.bfloat16)
    normed_ref[...] = normed
    logits = dot(normed, router_ref[...])
    columns = flat(column_ref).astype(jnp.float32)
    number = lax.broadcasted_iota(jnp.int32, logits.shape, 1).astype(jnp.float32)
    named = columns[:, 3:4] == number
    for slot in range(1, TOPK):
        named = named | (columns[:, 3 + slot : 4 + slot] == number)
    logits = jnp.where(named, logits, MASK_FLOOR)
    shifted = jnp.exp(logits - jnp.max(logits, -1, keepdims=True))
    shifted = jnp.where(named, shifted, 0.0)
    gates_ref[...] = shifted / jnp.sum(shifted, -1, keepdims=True)


def middle_rows(mixed, weights, gathered, gain, router, own, block):
    groups, _, width = mixed.shape
    tokens = gathered.shape[0] * own
    features = gain.shape[0]
    experts = router.shape[1]
    rows = lambda columns: pl.BlockSpec((block, columns), lambda i: (i, 0))
    return pl.pallas_call(
        middle_kernel,
        out_shape=(
            jax.ShapeDtypeStruct((tokens, features), jnp.float32),
            jax.ShapeDtypeStruct((tokens, features), jnp.bfloat16),
            jax.ShapeDtypeStruct((tokens, experts), jnp.float32),
        ),
        grid=(tokens // block,),
        in_specs=[
            pl.BlockSpec((groups, block // 2, width), lambda i: (0, i, 0)),
            whole_block(*weights[0].shape),
            whole_block(*weights[1].shape),
            *token_rows(block, own, features),
            whole_block(1, features),
            whole_block(features, experts),
        ],
        out_specs=[rows(features), rows(features), rows(experts)],
        compiler_params=pltpu.CompilerParams(vmem_limit_bytes=48 << 20),
        cost_estimate=pl.CostEstimate(
            flops=tokens * features * groups * width,
            bytes_accessed=12 * tokens * features,
            transcendentals=0,
        ),
    )(mixed, *weights, gathered, gathered, gain[None, :], router)


def slot_of(e, keeps, experts_own):
    pick = experts_own // 2
    high, low = e // pick, e % pick
    return (1 - (high ^ keeps)) * pick + low


def expert_kernel(
    place_ref,
    normed_ref,
    cotangent_ref,
    column_ref,
    gates_ref,
    gate_weight_ref,
    up_weight_ref,
    down_weight_ref,
    scaled_one_ref,
    scaled_two_ref,
    grad_gate_ref,
    grad_up_ref,
    grad_live_ref,
    extra_ref,
):
    experts_own = gate_weight_ref.shape[0]
    experts_all = gates_ref.shape[1]
    first = place_ref[1] * experts_own
    live = flat(column_ref).astype(jnp.float32)[:, :1] > 0
    grad_live_ref[...] = jnp.where(live, cotangent_ref[...], jnp.zeros((), jnp.bfloat16))
    gates = gates_ref[...]
    number = lax.broadcasted_iota(jnp.int32, gates.shape, 1)

    def one_expert(e, grad_gates):
        one = slot_of(e, place_ref[2], experts_own)
        two = slot_of(e, place_ref[3], experts_own)
        gate = jnp.sum(jnp.where(number == first + e, gates, 0.0), -1, keepdims=True)
        gate_pre = dot(normed_ref[...], gate_weight_ref[e])
        up_pre = dot(normed_ref[...], up_weight_ref[e])
        grad_plain = dot(grad_live_ref[...], down_weight_ref[e], COLUMNS)
        sigma = jax.nn.sigmoid(gate_pre)
        silu = gate_pre * sigma
        acted = silu * up_pre
        grad_acted = gate * grad_plain
        scaled = (gate * acted).astype(jnp.bfloat16)
        scaled_one_ref[one] = scaled
        scaled_two_ref[two] = scaled
        grad_gate_ref[one] = (
            grad_acted * up_pre * (sigma * (1.0 + gate_pre * (1.0 - sigma)))
        ).astype(jnp.bfloat16)
        grad_up_ref[two] = (grad_acted * silu).astype(jnp.bfloat16)
        return grad_gates + jnp.where(
            number == first + e, jnp.sum(acted * grad_plain, -1, keepdims=True), 0.0
        )

    grad_gates = lax.fori_loop(
        0, experts_own, one_expert, jnp.zeros(gates.shape, jnp.float32)
    )
    rough = grad_gates.astype(jnp.bfloat16)
    fine = (grad_gates - rough.astype(jnp.float32)).astype(jnp.bfloat16)
    rest = jnp.zeros((gates.shape[0], extra_ref.shape[1] - 2 * experts_all), jnp.bfloat16)
    extra_ref[...] = jnp.concatenate([rough, fine, rest], 1)


def expert_rows(place, normed, cotangent, gathered, gates, w_gate, w_up, w_down, own, block):
    tokens, features = normed.shape
    experts_own, _, hidden = w_gate.shape
    experts_all = gates.shape[1]
    rows = lambda columns: pl.BlockSpec((block, columns), lambda i, p: (i, 0))
    spread = pl.BlockSpec((experts_own, block, hidden), lambda i, p: (0, i, 0))
    wide = jax.ShapeDtypeStruct((experts_own, tokens, hidden), jnp.bfloat16)
    return pl.pallas_call(
        expert_kernel,
        out_shape=(
            wide,
            wide,
            wide,
            wide,
            jax.ShapeDtypeStruct((tokens, features), jnp.bfloat16),
            jax.ShapeDtypeStruct((tokens, 128), jnp.bfloat16),
        ),
        grid_spec=pltpu.PrefetchScalarGridSpec(
            num_scalar_prefetch=1,
            grid=(tokens // block,),
            in_specs=[
                rows(features),
                rows(features),
                token_rows(block, own, features)[1],
                rows(experts_all),
                whole_block(*w_gate.shape),
                whole_block(*w_up.shape),
                whole_block(*w_down.shape),
            ],
            out_specs=[spread, spread, spread, spread, rows(features), rows(128)],
        ),
        compiler_params=pltpu.CompilerParams(vmem_limit_bytes=52 << 20),
        cost_estimate=pl.CostEstimate(
            flops=6 * tokens * features * hidden * experts_own,
            bytes_accessed=6 * features * hidden * experts_own + 10 * tokens * features,
            transcendentals=tokens * hidden * experts_own,
        ),
    )(place, normed, cotangent, gathered, gates, w_gate, w_up, w_down)


def product_kernel(
    left_ref,
    gate_ref,
    up_ref,
    scaled_one_ref,
    scaled_two_ref,
    live_one_ref,
    live_two_ref,
    out_one_ref,
    out_two_ref,
):
    step = pl.program_id(0)
    tile, hidden = left_ref.shape[1], gate_ref.shape[1]
    narrow = live_one_ref.shape[1]
    tops = pl.num_programs(0) - 3
    top = tops * tile

    @pl.when(step < tops)
    def _():
        here = pl.ds(pl.multiple_of(step * tile, tile), tile)
        both = dot(left_ref[...], jnp.concatenate([gate_ref[...], up_ref[...]], 1), ROWS)
        out_one_ref[here, :] = both[:, :hidden].astype(out_one_ref.dtype)
        out_two_ref[here, :] = both[:, hidden:].astype(out_two_ref.dtype)

    @pl.when(step >= tops)
    def _():
        part = step - tops
        for scaled_ref, live_ref, out_ref in (
            (scaled_one_ref, live_one_ref, out_one_ref),
            (scaled_two_ref, live_two_ref, out_two_ref),
        ):
            product = dot(scaled_ref[...], live_ref[...], ROWS).astype(out_ref.dtype)

            @pl.when(part < 2)
            def _():
                there = pl.ds(pl.multiple_of(part * narrow, narrow), narrow)
                out_ref[top : top + hidden, there] = product

            @pl.when(part == 2)
            def _():
                out_ref[top + hidden :, :narrow] = product[:narrow]
                out_ref[top + hidden :, narrow:] = product[narrow:]


def expert_products(left, gate, up, scaled_one, scaled_two, live, e, dtype):
    tokens, features = left.shape
    hidden = gate.shape[2]
    narrow = hidden // 2
    tile = 512
    tops = features // tile
    rows = features + features // 2
    stack = pl.BlockSpec((None, tokens, hidden), lambda i: (e, 0, 0), pipeline_mode=pl.Buffered(1))
    lives = [
        pl.BlockSpec((tokens, narrow), lambda i, side=side: (0, 3 * side + jnp.maximum(i - tops, 0)))
        for side in range(2)
    ]
    out = pl.BlockSpec((rows, hidden), lambda i: (0, 0), pipeline_mode=pl.Buffered(1))
    return pl.pallas_call(
        product_kernel,
        out_shape=(jax.ShapeDtypeStruct((rows, hidden), dtype),) * 2,
        grid=(tops + 3,),
        in_specs=[
            pl.BlockSpec((tokens, tile), lambda i: (0, jnp.minimum(i, tops - 1))),
            stack,
            stack,
            stack,
            stack,
            *lives,
        ],
        out_specs=[out, out],
        compiler_params=pltpu.CompilerParams(vmem_limit_bytes=58 << 20),
        cost_estimate=pl.CostEstimate(flops=0, bytes_accessed=tokens, transcendentals=0),
    )(left, gate, up, scaled_one, scaled_two, live, live)


def gradient_kernel(
    place_ref, grad_gate_ref, grad_up_ref, extra_ref, gate_weight_ref, up_weight_ref, grad_ref
):
    experts_own, features = gate_weight_ref.shape[:2]
    one = [slot_of(e, place_ref[2], experts_own) for e in range(experts_own)]
    two = [slot_of(e, place_ref[3], experts_own) for e in range(experts_own)]
    size = 512

    @pl.loop(0, features // size)
    def _(index):
        part = pl.ds(pl.multiple_of(index * size, size), size)
        grad = 0.0
        for e in range(experts_own):
            grad = grad + dot(grad_gate_ref[one[e]], gate_weight_ref[e, part, :], COLUMNS)
            grad = grad + dot(grad_up_ref[two[e]], up_weight_ref[e, part, :], COLUMNS)
        grad_ref[:, part] = grad.astype(jnp.bfloat16)

    grad_ref[:, features:] = extra_ref[...]


def gradient_rows(place, grad_gate_pre, grad_up_pre, extra, w_gate, w_up, block):
    experts_own, tokens, hidden = grad_gate_pre.shape
    features = w_gate.shape[1]
    rows = lambda columns: pl.BlockSpec((block, columns), lambda i, p: (i, 0))
    spread = pl.BlockSpec((experts_own, block, hidden), lambda i, p: (0, i, 0))
    return pl.pallas_call(
        gradient_kernel,
        out_shape=jax.ShapeDtypeStruct((tokens, features + extra.shape[1]), jnp.bfloat16),
        grid_spec=pltpu.PrefetchScalarGridSpec(
            num_scalar_prefetch=1,
            grid=(tokens // block,),
            in_specs=[
                spread,
                spread,
                rows(extra.shape[1]),
                whole_block(*w_gate.shape),
                whole_block(*w_up.shape),
            ],
            out_specs=rows(features + extra.shape[1]),
        ),
        compiler_params=pltpu.CompilerParams(vmem_limit_bytes=52 << 20),
        cost_estimate=pl.CostEstimate(flops=0, bytes_accessed=tokens, transcendentals=0),
    )(place, grad_gate_pre, grad_up_pre, extra, w_gate, w_up)


def output_kernel(place_ref, scaled_ref, down_weight_ref, out_ref):
    experts_own, _, features = down_weight_ref.shape
    size = 512

    @pl.loop(0, features // size)
    def _(index):
        part = pl.ds(pl.multiple_of(index * size, size), size)
        out = 0.0
        for e in range(experts_own):
            slot = slot_of(e, place_ref[2], experts_own)
            out = out + dot(scaled_ref[slot], down_weight_ref[e, :, part])
        out_ref[:, part] = out.astype(jnp.bfloat16)


def output_rows(place, scaled, w_down, block):
    experts_own, tokens, hidden = scaled.shape
    features = w_down.shape[2]
    return pl.pallas_call(
        output_kernel,
        out_shape=jax.ShapeDtypeStruct((tokens, features), jnp.bfloat16),
        grid_spec=pltpu.PrefetchScalarGridSpec(
            num_scalar_prefetch=1,
            grid=(tokens // block,),
            in_specs=[
                pl.BlockSpec((experts_own, block, hidden), lambda i, p: (0, i, 0)),
                whole_block(*w_down.shape),
            ],
            out_specs=pl.BlockSpec((block, features), lambda i, p: (i, 0)),
        ),
        compiler_params=pltpu.CompilerParams(vmem_limit_bytes=52 << 20),
        cost_estimate=pl.CostEstimate(flops=0, bytes_accessed=tokens, transcendentals=0),
    )(place, scaled, w_down)


def turn_kernel(
    place_ref,
    sum_ref,
    gates_ref,
    router_ref,
    gain_ref,
    middle_ref,
    live_ref,
    low_ref,
    high_ref,
    grad_middle_ref,
    branch_ref,
    mixed_ref,
    logits_ref,
    gain_grad_ref,
):
    features = middle_ref.shape[1]
    experts = gates_ref.shape[1]
    groups, _, width = mixed_ref.shape
    extra = sum_ref[:, features:].astype(jnp.float32)
    grad_gates = extra[:, :experts] + extra[:, experts : 2 * experts]
    gates = gates_ref[...]
    grad_logits = gates * (grad_gates - jnp.sum(gates * grad_gates, -1, keepdims=True))
    grad_logits = grad_logits.astype(jnp.bfloat16)
    logits_ref[...] = grad_logits
    grad = sum_ref[:, :features].astype(jnp.float32) + dot(grad_logits, router_ref[...], COLUMNS)
    middle = middle_ref[...]
    scale = lax.rsqrt(jnp.mean(middle * middle, -1, keepdims=True) + EPS)
    base = middle * scale
    gain_grad_ref[...] = jnp.sum(grad * base, 0, keepdims=True)
    grad_middle = live_ref[...].astype(jnp.float32) + norm_back(grad * gain_ref[...], base, scale)
    grad_middle_ref[...] = grad_middle
    branch = grad_middle.astype(jnp.bfloat16)
    branch_ref[...] = branch
    for half, weight_ref in enumerate((low_ref, high_ref)):
        mixed = dot(branch, weight_ref[...], COLUMNS).astype(jnp.bfloat16)
        for g in range(groups // 2):
            mixed_ref[half * (groups // 2) + g] = mixed[:, g * width : (g + 1) * width]


def turn_rows(place, sums, gates, router, gain, middle, live, weights):
    own, features = sums.shape[0], middle.shape[1]
    experts = gates.shape[1]
    groups = KEY_VALUE_HEADS
    shaped = jax.ShapeDtypeStruct
    rows = lambda width: pl.BlockSpec((own, width), lambda i, p: (p[1], 0))
    resident = lambda *shape: pl.BlockSpec(shape, lambda i, p: (0,) * len(shape))
    outs = (
        shaped((own, features), jnp.float32),
        shaped((own, features), jnp.bfloat16),
        shaped((groups, own, features // groups), jnp.bfloat16),
        shaped((own, experts), jnp.bfloat16),
        shaped((1, features), jnp.float32),
    )
    return pl.pallas_call(
        turn_kernel,
        out_shape=outs,
        grid_spec=pltpu.PrefetchScalarGridSpec(
            num_scalar_prefetch=1,
            grid=(1,),
            in_specs=[
                whole_block(*sums.shape),
                rows(experts),
                whole_block(*router.shape),
                whole_block(1, features),
                rows(features),
                rows(features),
                whole_block(*weights[0].shape),
                whole_block(*weights[1].shape),
            ],
            out_specs=[resident(*out.shape) for out in outs],
        ),
        compiler_params=pltpu.CompilerParams(vmem_limit_bytes=58 << 20),
        cost_estimate=pl.CostEstimate(flops=0, bytes_accessed=own, transcendentals=0),
    )(place, sums, gates, router, gain[None, :], middle, live, *weights)


def close_kernel(
    reps,
    place_ref,
    query_ref,
    pair_ref,
    weight_ref,
    hidden_ref,
    normed_ref,
    gain_two_ref,
    normed_own_ref,
    logits_ref,
    rows_ref,
    mixed_ref,
    branch_ref,
    grad_ref,
    kept_one_ref,
    kept_two_ref,
    sent_one_ref,
    sent_two_ref,
    product_ref,
    gain_ref,
    out_ref,
    head_ref,
):
    step = pl.program_id(0)
    both = query_ref.shape[1] + pair_ref.shape[1]
    heads = jnp.concatenate([query_ref[...], pair_ref[...]], 1)
    grad = dot(heads, weight_ref[:, :both], COLUMNS)
    grad_ref[:, : grad.shape[1]] = grad.astype(jnp.bfloat16)
    grad_ref[:, grad.shape[1] :] = rows_ref[...]
    hidden = flat(hidden_ref).astype(jnp.float32)
    scale = lax.rsqrt(jnp.mean(hidden * hidden, -1, keepdims=True) + EPS)
    normed = normed_ref[...]

    @pl.when(step == 0)
    def _():
        gain_ref[...] = jnp.zeros_like(gain_ref)
        product_ref[...] = jnp.zeros_like(product_ref)
        out_ref[...] = jnp.zeros_like(out_ref)

    gain_ref[...] += jnp.sum(grad * (hidden * scale), 0, keepdims=True)
    product_ref[...] += dot(normed, heads, ROWS)
    out_ref[...] += dot(mixed_ref[...], branch_ref[...], ROWS)

    @pl.when(step == pl.num_programs(0) - 1)
    def _():
        features = product_ref.shape[0]
        rows = out_ref.shape[0]
        share = rows // reps
        experts = logits_ref.shape[1]
        line = kept_one_ref.shape[1]
        count = features // rows
        side = (line - features // 2) // (count // 2)
        gains = jnp.concatenate(
            [gain_ref[...], gain_two_ref[...], jnp.zeros((6, features), jnp.float32)], 0
        )
        gains = jnp.transpose(gains)
        router = dot(normed_own_ref[...], logits_ref[...], ROWS)
        rest = jnp.zeros((rows, side - both - 8 - experts), jnp.float32)
        for h in range(2):
            for c in range(count // 2):
                place = h * (count // 2) + c
                part = slice(place * rows, (place + 1) * rows)
                head_ref[h, :, c * side : (c + 1) * side] = jnp.concatenate(
                    [product_ref[part, :], gains[part], router[part], rest], 1
                )
            half = features // 2
            head_ref[h, :, count // 2 * side :] = out_ref[:, h * half : (h + 1) * half]
        sides = ((0, kept_one_ref, sent_one_ref), (1, kept_two_ref, sent_two_ref))
        for h, kept_ref, sent_ref in sides:
            bit = 1 if h == 0 else reps // 2
            for index in range(reps // 2):
                base = index // bit * 2 * bit + index % bit
                here = slice(index * share, (index + 1) * share)
                lower = head_ref[h, base * share : (base + 1) * share, :]
                upper = head_ref[h, (base + bit) * share : (base + bit + 1) * share, :]
                kept_ref[here, :] = jnp.where(place_ref[2 + h] > 0, upper, lower)
                sent_ref[here, :] = jnp.where(place_ref[2 + h] > 0, lower, upper).astype(jnp.bfloat16)


def close_rows(
    place,
    query,
    pair,
    weight,
    gathered,
    normed,
    gain_two_grad,
    normed_two,
    logits,
    out_rows,
    mixed,
    branch,
    reps,
    side,
    block,
):
    tokens, features = normed.shape
    own = logits.shape[0]
    both = query.shape[1] + pair.shape[1]
    rows_own = mixed.shape[1]
    rows = lambda width: pl.BlockSpec((block, width), lambda i, k: (i, 0))
    resident = lambda *shape: pl.BlockSpec(shape, lambda i, k: (0,) * len(shape))
    shaped = jax.ShapeDtypeStruct
    line = features // rows_own // 2 * side + features // 2
    half = (rows_own // 2, line)
    return pl.pallas_call(
        lambda *refs: close_kernel(reps, *refs),
        name="close",
        out_shape=(
            shaped((tokens, 2 * features), jnp.bfloat16),
            shaped(half, jnp.float32),
            shaped(half, jnp.float32),
            shaped(half, jnp.bfloat16),
            shaped(half, jnp.bfloat16),
        ),
        grid_spec=pltpu.PrefetchScalarGridSpec(
            num_scalar_prefetch=1,
            grid=(tokens // block,),
            in_specs=[
                rows(query.shape[1]),
                rows(pair.shape[1]),
                whole_block(*weight.shape),
                token_rows(block, own, features)[0],
                rows(features),
                whole_block(1, features),
                pl.BlockSpec((own, features), lambda i, p: (p[1], 0)),
                whole_block(*logits.shape),
                rows(features),
                rows(rows_own),
                rows(features),
            ],
            out_specs=[rows(2 * features), *[resident(*half)] * 4],
            scratch_shapes=[
                pltpu.VMEM((features, both), jnp.float32),
                pltpu.VMEM((1, features), jnp.float32),
                pltpu.VMEM((rows_own, features), jnp.float32),
                pltpu.VMEM((2, rows_own, line), jnp.float32),
            ],
        ),
        compiler_params=pltpu.CompilerParams(vmem_limit_bytes=56 << 20),
        cost_estimate=pl.CostEstimate(flops=0, bytes_accessed=tokens, transcendentals=0),
    )(
        place,
        query,
        pair,
        weight,
        gathered,
        normed,
        gain_two_grad,
        normed_two,
        logits,
        out_rows,
        mixed,
        branch,
    )


def head_kernel(
    copies,
    side,
    low_ref,
    high_ref,
    query_ref,
    key_ref,
    value_ref,
    out_ref,
    gains_ref,
    router_ref,
):
    groups = KEY_VALUE_HEADS
    count = groups * copies
    halves = [low_ref[...].astype(jnp.float32), high_ref[...].astype(jnp.float32)]
    width = query_ref.shape[1] // groups
    parts = []
    for c in range(count):
        place = c % (count // 2) * side
        parts.append(halves[c // (count // 2)][:, place : place + side])
    heads = []
    small = 0.0
    for g in range(groups):
        total = parts[g * copies]
        for p in range(1, copies):
            total = total + parts[g * copies + p]
        heads.append(total)
        small = small + total[:, width + 2 * HEAD_SIZE :]
    gains_ref[...] = jnp.transpose(small[:, :8])
    router_ref[...] = small[:, 8 : 8 + router_ref.shape[1]]
    query_ref[...] = jnp.concatenate([head[:, :width] for head in heads], 1)
    key_ref[...] = jnp.concatenate([head[:, width : width + HEAD_SIZE] for head in heads], 1)
    value_ref[...] = jnp.concatenate(
        [head[:, width + HEAD_SIZE : width + 2 * HEAD_SIZE] for head in heads], 1
    )
    out_ref[...] = jnp.concatenate([half[:, count // 2 * side :] for half in halves], 1)


def head_outputs(low, high, copies, side, experts):
    rows = low.shape[0]
    groups = KEY_VALUE_HEADS
    query_width = QUERY_HEADS * HEAD_SIZE
    shaped = lambda width: jax.ShapeDtypeStruct((rows, width), jnp.float32)
    return pl.pallas_call(
        lambda *refs: head_kernel(copies, side, *refs),
        name="head_outputs",
        out_shape=(
            shaped(query_width),
            shaped(groups * HEAD_SIZE),
            shaped(groups * HEAD_SIZE),
            shaped(MODEL_WIDTH),
            jax.ShapeDtypeStruct((8, rows), jnp.float32),
            shaped(experts),
        ),
        compiler_params=pltpu.CompilerParams(vmem_limit_bytes=40 << 20),
        cost_estimate=pl.CostEstimate(flops=0, bytes_accessed=rows, transcendentals=0),
    )(low, high)


def upper_rows(flags_ref, side, own_ref, came_ref, rows):
    return jnp.where(flags_ref[2 + side] > 0, own_ref[rows, :], came_ref[rows, :])


def into_kernel(flags_ref, side, own_ref, came_ref, low_ref, high_ref, out_ref):
    rows = own_ref.shape[0]
    rest = out_ref.shape[0] - rows
    kept = pl.program_id(0) == flags_ref[side]

    @pl.when(kept)
    def _():
        low = jnp.where(flags_ref[2 + side] > 0, came_ref[...], own_ref[...])
        out_ref[:rows, :] = low.astype(jnp.float32)
        high = upper_rows(flags_ref, side, own_ref, came_ref, slice(0, rest))
        out_ref[rows:, :] = high.astype(jnp.float32)

    @pl.when(jnp.logical_not(kept))
    def _():
        out_ref[:rows, :] = low_ref[...].astype(jnp.float32)
        out_ref[rows:, :] = high_ref[:rest, :].astype(jnp.float32)


def into_output(flags, side, own, came, low, high):
    rows, hidden = own.shape
    total = 2 * rows * 2 // 3
    whole = lambda array: pl.BlockSpec(array.shape, lambda e, k: (0, 0))
    return pl.pallas_call(
        lambda k, *refs: into_kernel(k, side, *refs),
        name="into_output",
        out_shape=jax.ShapeDtypeStruct((2, total, hidden), jnp.float32),
        grid_spec=pltpu.PrefetchScalarGridSpec(
            num_scalar_prefetch=1,
            grid=(2,),
            in_specs=[whole(own), whole(came), whole(low), whole(high)],
            out_specs=pl.BlockSpec((None, total, hidden), lambda e, k: (e, 0, 0)),
        ),
        compiler_params=pltpu.CompilerParams(vmem_limit_bytes=40 << 20),
        cost_estimate=pl.CostEstimate(flops=0, bytes_accessed=rows, transcendentals=0),
    )(flags, own, came, low, high)


def down_kernel(flags_ref, *refs):
    out_ref = refs[8]
    hidden = out_ref.shape[0]
    narrow = hidden // 2
    for side in range(2):
        own_ref, came_ref, high_ref, last_ref = refs[4 * side : 4 * side + 4]
        rows = own_ref.shape[0]
        rest = rows - out_ref.shape[1] // 2
        mine = upper_rows(flags_ref, side, own_ref, came_ref, slice(rest, rows))
        theirs = jnp.concatenate([high_ref[rest:, :], last_ref[...]], 0)
        kept = pl.program_id(0) == flags_ref[side]
        value = jnp.where(kept, mine, theirs).astype(jnp.float32)
        start = side * value.shape[0]
        out_ref[:, start : start + hidden] = value[:hidden]
        middle, end = start + hidden, start + value.shape[0]
        out_ref[:narrow, middle:end] = value[hidden:, :narrow]
        out_ref[narrow:, middle:end] = value[hidden:, narrow:]


def down_output(flags, *operands):
    rows, hidden = operands[0].shape
    whole = lambda array: pl.BlockSpec(array.shape, lambda e, k: (0, 0))
    return pl.pallas_call(
        down_kernel,
        out_shape=jax.ShapeDtypeStruct((2, hidden, 3 * hidden), jnp.float32),
        grid_spec=pltpu.PrefetchScalarGridSpec(
            num_scalar_prefetch=1,
            grid=(2,),
            in_specs=[whole(array) for array in operands],
            out_specs=pl.BlockSpec((None, hidden, 3 * hidden), lambda e, k: (e, 0, 0)),
        ),
        compiler_params=pltpu.CompilerParams(vmem_limit_bytes=40 << 20),
        cost_estimate=pl.CostEstimate(flops=0, bytes_accessed=rows, transcendentals=0),
    )(flags, *operands)


def after(values, *others):
    values, _ = lax.optimization_barrier((values, others))
    return values


def swap(value, bit):
    size = lax.axis_size("rep")
    return lax.ppermute(value, "rep", [(i, i ^ bit) for i in range(size)])


def has(bit):
    return (lax.axis_index("rep") & bit) != 0


def join(value, came, bit, axis):
    upper = has(bit)
    return jnp.concatenate(
        [jnp.where(upper, came, value), jnp.where(upper, value, came)], axis
    )


class Chain:
    def __init__(self, order):
        self.order = order
        self.stage = 0
        self.steps = 2 * len(order)

    def send(self, sent):
        bit = self.order[min(self.stage, self.steps - 1 - self.stage)]
        self.sent = sent
        self.stage += 1
        if self.stage < self.steps:
            self.flying = swap(sent, bit)

    def step(self, *others):
        came = after(self.flying, *others)
        self.send(join(self.sent, came, self.order[self.steps - self.stage], 0))
        return self.sent

    def ends(self, *others):
        self.own = self.sent
        self.came = after(self.flying, *others)
        bit = self.order[1]
        half = self.own.shape[0] // 2
        low = jnp.where(has(bit), self.came, self.own)
        pieces = [low] + [
            jnp.where(has(bit), self.own[rows], self.came[rows])
            for rows in (slice(0, half), slice(half, 2 * half))
        ]
        return pieces

    def last(self, piece):
        return swap(piece, self.order[0])


def halve_kernel(keeps_ref, *refs):
    count = len(refs) // 3
    for chain in range(2):
        for place in range(0, count, 2):
            value_ref, came_ref = refs[count * chain + place : count * chain + place + 2]
            out_ref = refs[2 * count + chain * (count // 2) + place // 2]
            out_ref[...] = (value_ref[...] + came_ref[...].astype(jnp.float32)).astype(
                out_ref.dtype
            )


def halve_chains(chains, *others):
    order = [chain.order[chain.stage] for chain in chains]
    last = chains[0].stage == len(chains[0].order) - 1
    keeps = jnp.stack([has(bit) for bit in order]).astype(jnp.int32)
    rows, hidden = chains[0].kept.shape
    count = 4
    part = rows // 2 // count
    operands, specs = [], []
    for c, chain in enumerate(chains):
        chain.came = after(chain.flying, *others)
        for flip in (1,) if last else (1, 0):
            index = lambda i, k, c=c, flip=flip: ((k[c] ^ flip) * count + i, 0)
            operands += [chain.kept, chain.came]
            specs += [pl.BlockSpec((part, hidden), index)] * 2
    block = pl.BlockSpec((part, hidden), lambda i, k: (i, 0))
    shaped = lambda dtype: jax.ShapeDtypeStruct((rows // 2, hidden), dtype)
    each = [shaped(jnp.bfloat16)] if last else [shaped(jnp.bfloat16), shaped(jnp.float32)]
    outs = pl.pallas_call(
        halve_kernel,
        out_shape=each * 2,
        grid_spec=pltpu.PrefetchScalarGridSpec(
            num_scalar_prefetch=1,
            grid=(count,),
            in_specs=specs,
            out_specs=[block] * (2 * len(each)),
        ),
        compiler_params=pltpu.CompilerParams(vmem_limit_bytes=58 << 20),
        cost_estimate=pl.CostEstimate(
            flops=60000 * rows * hidden, bytes_accessed=12 * rows * hidden, transcendentals=0
        ),
    )(keeps, *operands)
    for c, chain in enumerate(chains):
        if not last:
            chain.kept = outs[2 * c + 1]
        chain.send(outs[len(each) * c])
    return [chain.sent for chain in chains]


def total_kernel(keeps_ref, *refs):
    for chain in range(2):
        kept_ref, first_ref, second_ref = refs[3 * chain : 3 * chain + 3]
        total = kept_ref[...] + first_ref[...].astype(jnp.float32)
        refs[6 + chain][...] = (total + second_ref[...].astype(jnp.float32)).astype(jnp.bfloat16)


def total_chains(chains, *others):
    keeps = jnp.stack([has(chain.order[-1]) for chain in chains]).astype(jnp.int32)
    rows, hidden = chains[0].kept.shape
    count = 4
    part = rows // 2 // count
    block = pl.BlockSpec((part, hidden), lambda i, k: (i, 0))
    operands, specs = [], []
    for c, chain in enumerate(chains):
        stay = pl.BlockSpec((part, hidden), lambda i, k, c=c: (k[c] * count + i, 0))
        operands += [chain.kept, chain.came, after(chain.flying, *others)]
        specs += [stay, stay, block]
    outs = pl.pallas_call(
        total_kernel,
        out_shape=[jax.ShapeDtypeStruct((rows // 2, hidden), jnp.bfloat16)] * 2,
        grid_spec=pltpu.PrefetchScalarGridSpec(
            num_scalar_prefetch=1, grid=(count,), in_specs=specs, out_specs=[block] * 2
        ),
        compiler_params=pltpu.CompilerParams(vmem_limit_bytes=58 << 20),
        cost_estimate=pl.CostEstimate(flops=0, bytes_accessed=rows, transcendentals=0),
    )(keeps, *operands)
    for chain, out in zip(chains, outs):
        chain.send(out)
    return list(outs)


class Cube:
    def __init__(self, kept, sent, order, share):
        shape = [2] * len(order)
        shape[len(order) - order[0].bit_length()] = 1
        self.value, sent = [array.reshape(*shape, share, -1) for array in (kept, sent)]
        self.order = order
        self.flying = swap(sent, order[0])
        self.stage = 1

    def axis(self, bit):
        return len(self.order) - bit.bit_length()

    def halve(self, *others):
        bit = self.order[self.stage]
        keep = has(bit).astype(jnp.int32)
        part = lambda index: lax.dynamic_slice_in_dim(self.value, index, 1, self.axis(bit))
        self.value, sent = part(keep), part(1 - keep).astype(jnp.bfloat16)
        self.flying = swap(after(sent, *others), bit)
        self.stage += 1
        return sent

    def add(self, *others):
        self.value = self.value + after(self.flying, *others).astype(jnp.float32)

    def back(self, *others):
        self.stage -= 1
        self.flying = swap(after(self.value, *others), self.order[self.stage])
        return self.value

    def join(self, *others):
        bit = self.order[self.stage]
        self.value = join(self.value, after(self.flying, *others), bit, self.axis(bit))


class Exchange:
    def __init__(self, fetched, bits):
        size = fetched.shape[0]
        fetched = fetched.reshape((size,) + (1,) * len(bits) + fetched.shape[1:])
        self.values = [fetched[: size // 2], fetched[size // 2 :]]
        self.orders = (bits, bits[::-1])
        self.stage = 0
        self.fly()

    def fly(self):
        self.flying = [
            swap(value, order[self.stage]) for value, order in zip(self.values, self.orders)
        ]

    def step(self, *others):
        bits = len(self.orders[0])
        for h, order in enumerate(self.orders):
            bit = order[self.stage]
            came = after(self.flying[h], *others)
            self.values[h] = join(self.values[h], came, bit, bits - (bit.bit_length() - 1))
        self.stage += 1
        if self.stage < bits:
            self.fly()
        return list(self.values)

    def finish(self, *others):
        while self.stage < len(self.orders[0]):
            self.step(*others)
        return [value.reshape(-1, value.shape[-1]) for value in self.values]


def per_device(
    inputs,
    segments,
    positions,
    expert_ids,
    attn_gain,
    w_query,
    key_weight,
    value_weight,
    w_out,
    ffn_gain,
    router,
    w_gate,
    w_up,
    w_down,
    grad_out,
):
    size = lax.axis_size("ctx")
    me = lax.axis_index("ctx")
    reps = lax.axis_size("rep")
    bits = [1 << i for i in range(reps.bit_length() - 1)]
    own = inputs.shape[1]
    tokens = size * own
    groups = KEY_VALUE_HEADS
    copies = size // groups
    query_width = HEAD_GROUP * HEAD_SIZE
    width = query_width + 2 * HEAD_SIZE
    copy_index = me % copies
    rows_own = w_out.shape[0]
    experts_own = w_gate.shape[0]
    experts_all = size * experts_own
    block = 2 * own
    chips = size // 2
    chip = me // 2
    odd = me % 2 == 1
    share = rows_own // reps
    share_start = lax.axis_index("rep") * share

    columns = jnp.concatenate(
        [
            segments[0][:, None],
            positions[0][:, None] // 64,
            positions[0][:, None] % 64,
            expert_ids[0],
        ],
        1,
    ).astype(jnp.bfloat16)
    columns = jnp.pad(columns, ((0, 0), (0, 128 - columns.shape[1])))
    shared = lambda array: lax.dynamic_slice_in_dim(array, share_start, share, 0)

    rows = jnp.concatenate(
        [
            jnp.concatenate([inputs[0], columns], 1),
            jnp.pad(shared(w_out), ((0, 0), (0, 128))),
        ],
        0,
    )
    gathered = lax.all_gather(rows, "ctx", axis=0)
    cotangent = lax.all_gather(after(grad_out[0], rows), "ctx", axis=0, tiled=True)

    def from_chip(value, k):
        return lax.ppermute(value, "ctx", [(i, (i - 2 * k) % size) for i in range(size)])

    def from_core(value):
        return lax.ppermute(value, "ctx", [(i, i ^ 1) for i in range(size)])

    def cores(mine, others, axis):
        return jnp.concatenate(
            [jnp.where(odd, others, mine), jnp.where(odd, mine, others)], axis
        )

    side_width = -(-(width + 2 + router.shape[1]) // 128) * 128
    head_columns = jnp.concatenate(
        [
            shared(w_query).reshape(share, groups, query_width),
            shared(key_weight).reshape(share, groups, HEAD_SIZE),
            shared(value_weight).reshape(share, groups, HEAD_SIZE),
            jnp.broadcast_to(shared(attn_gain)[:, None, None], (share, groups, 1)),
            jnp.broadcast_to(shared(ffn_gain)[:, None, None], (share, groups, 1)),
            jnp.broadcast_to(shared(router)[:, None, :], (share, groups, router.shape[1])),
        ],
        -1,
    )
    used = head_columns.shape[-1]
    head_columns = jnp.pad(head_columns, ((0, 0), (0, 0), (0, side_width - used)))
    head_columns = jnp.repeat(jnp.transpose(head_columns, (1, 0, 2)), copies, 0)
    head_columns = lax.all_to_all(head_columns, "ctx", split_axis=0, concat_axis=0, tiled=True)
    head_halves = Exchange(head_columns, bits).finish()
    head_all = jnp.concatenate(head_halves, 0)
    gain_one = head_all[:, width].astype(jnp.float32)
    gain_two = head_all[:, width + 1].astype(jnp.float32)
    router_all = head_all[:, width + 2 : used]

    (
        normed_one,
        query,
        key,
        value,
        mixed,
        packed,
        log_total,
        cosine_table,
        sine_table,
        segment_rows,
    ) = attend(gathered, gain_one, head_halves, own, block)
    out_exchange = Exchange(gathered[:, own:, :MODEL_WIDTH], bits)

    part = tokens // copies
    mixed_all = lax.all_gather(
        after(
            lax.dynamic_slice_in_dim(packed, copy_index * part // 2, part // 2, 0),
            cotangent,
            out_exchange.step(),
        ),
        "ctx",
        axis=0,
    ).reshape(groups, tokens // 2, 2 * query_width)
    w_out_halves = out_exchange.finish()

    middle, normed_two, gates = middle_rows(
        mixed_all, w_out_halves, gathered, gain_two, router_all, own, block
    )
    flag = lambda bit: has(bit).astype(jnp.int32)
    place = jnp.stack([chip, me, flag(bits[0]), flag(bits[-1])]).astype(jnp.int32)
    scaled_one, scaled_two, grad_gate_pre, grad_up_pre, grad_live, extra = expert_rows(
        place, normed_two, cotangent, gathered, gates, w_gate, w_up, w_down, own, block
    )
    def mine(array):
        return lax.dynamic_slice_in_dim(array, me * own, own, 0)

    products = lambda e, dtype: expert_products(
        normed_two, grad_gate_pre, grad_up_pre, scaled_one, scaled_two, grad_live, e, dtype
    )
    grad_rows = gradient_rows(place, grad_gate_pre, grad_up_pre, extra, w_gate, w_up, block)
    grad_two_sum = lax.psum_scatter(grad_rows, "ctx", scatter_dimension=0, tiled=True)
    normed_two, grad_live = after((normed_two, grad_live), grad_rows)
    chains = [Chain(bits), Chain(bits[::-1])]
    for chain, sent in zip(chains, products(0, jnp.bfloat16)):
        chain.send(sent)
    normed_two, grad_live = after((normed_two, grad_live), *[chain.sent for chain in chains])
    for chain, kept in zip(chains, products(1, jnp.float32)):
        chain.kept = kept
    out_rows = output_rows(place, after(scaled_one, *[c.kept for c in chains]), w_down, block)

    grad_middle, grad_branch, grad_mixed, grad_logits, gain_two_grad = turn_rows(
        place,
        after(grad_two_sum, out_rows),
        gates,
        router_all,
        gain_two,
        middle,
        grad_live,
        w_out_halves,
    )
    grad_branch_all = lax.all_gather(grad_branch, "ctx", axis=0, tiled=True)

    def deal_chips(blocks):
        blocks = blocks.reshape((chips, 2) + blocks.shape[1:])
        got = [blocks[(chip - k) % chips] for k in range(chips)]
        return jnp.stack([got[0]] + [from_chip(got[k], k) for k in range(1, chips)])

    def deal_cores(got):
        stay = jnp.where(odd, got[:, 1], got[:, 0])
        go = from_core(jnp.where(odd, got[:, 0], got[:, 1]))
        both = cores(stay[:, None], go[:, None], 1)
        both = jnp.concatenate([both, both], 0)
        both = lax.dynamic_slice_in_dim(both, (chips - chip) % chips, chips, 0)
        return both.reshape((size,) + both.shape[2:])

    got = deal_chips(jnp.repeat(grad_mixed, copies, 0))
    sent = [got]
    while chains[0].stage < len(bits):
        sent = halve_chains(chains, *sent)
    grad_mixed_all = deal_cores(after(got, *sent)).reshape(tokens, query_width)
    grad_query, grad_pair = attend_back(
        query,
        grad_mixed_all,
        log_total,
        cosine_table,
        sine_table,
        gathered,
        segment_rows,
        key,
        value,
        own,
    )
    if copies > 1:
        places = jnp.arange(tokens, dtype=jnp.int32)
        counted = (places // part == copy_index)[:, None]
        grad_query = jnp.where(counted, grad_query, jnp.zeros((), jnp.bfloat16))
        grad_pair = jnp.where(counted, grad_pair, jnp.zeros((), jnp.bfloat16))
    sent = total_chains(chains, grad_pair)
    both_rows, *halves = close_rows(
        place,
        after(grad_query, *sent),
        grad_pair,
        head_all,
        gathered,
        normed_one,
        gain_two_grad,
        normed_two,
        grad_logits,
        out_rows,
        lax.dynamic_slice_in_dim(mixed, copy_index * rows_own, rows_own, 1),
        grad_branch_all,
        reps,
        side_width,
        block,
    )
    both_sums = lax.psum_scatter(
        both_rows, "ctx", scatter_dimension=0, tiled=True
    ).astype(jnp.float32)
    grad_one, out_sum = both_sums[:, :MODEL_WIDTH], both_sums[:, MODEL_WIDTH:]

    line = size // 2 * side_width
    cubes = [
        Cube(halves[h], halves[2 + h], order, share)
        for h, order in enumerate((bits, bits[::-1]))
    ]
    while chains[0].stage < chains[0].steps - 1:
        sent = [chain.step(*halves) for chain in chains]
    pieces = [chain.ends(*halves) for chain in chains]
    sent = [part[0] for part in pieces]
    while cubes[0].stage < len(bits):
        for cube in cubes:
            cube.add(*sent)
        sent = [cube.halve() for cube in cubes]
    first = [chain.last(part[0]) for chain, part in zip(chains, pieces)]
    second = [chain.last(after(part[1], *sent)) for chain, part in zip(chains, pieces)]
    for cube in cubes:
        cube.add()
    totals = [cube.value.astype(jnp.bfloat16) for cube in cubes]
    blocks = jnp.concatenate(
        [
            jnp.transpose(
                total.reshape(share, -1)[:, :line].reshape(share, size // 2, side_width), (1, 0, 2)
            )
            for total in totals
        ],
        0,
    )
    got = deal_chips(after(blocks, *first))
    head_sums = deal_cores(after(got, *second))
    for h, cube in enumerate(cubes):
        rows = jnp.transpose(head_sums[h * (size // 2) : (h + 1) * (size // 2)], (1, 0, 2))
        rows = jnp.concatenate(
            [rows.reshape(share, line), totals[h].reshape(share, -1)[:, line:]], 1
        )
        cube.value = rows.reshape(totals[h].shape)
    sent = [cube.back() for cube in cubes]
    third = [
        chain.last(after(part[2], *sent)) for chain, part in zip(chains, pieces)
    ]
    flags = jnp.stack([flag(chain.order[n]) for n in range(2) for chain in chains])
    came = [cube.flying for cube in cubes]
    grad_gate, grad_up = [
        into_output(flags, side, *after((chain.own, chain.came, first[side], second[side]), *came))
        for side, chain in enumerate(chains)
    ]
    for cube in cubes:
        cube.join(*sent)
    while cubes[0].stage > 0:
        sent = [cube.back() for cube in cubes]
        if cubes[0].stage > 0:
            for cube in cubes:
                cube.join(*sent)
    output = jnp.where((segments[0] != 0)[:, None], mine(after(middle, grad_mixed)) + out_sum, 0.0)
    own_hidden = inputs[0].astype(jnp.float32)
    own_scale = lax.rsqrt(jnp.mean(own_hidden * own_hidden, -1, keepdims=True) + EPS)
    grad_in = grad_middle + norm_back(grad_one * gain_one, own_hidden * own_scale, own_scale)
    operands = []
    for side, chain in enumerate(chains):
        operands += [chain.own, chain.came, second[side], third[side]]
    grad_down = down_output(flags, *after(operands, *sent))
    for cube in cubes:
        cube.join(grad_down)
    head_outs = head_outputs(
        *[cube.value.reshape(rows_own, -1) for cube in cubes], copies, side_width, experts_all
    )
    return (
        output.astype(jnp.bfloat16)[None],
        grad_in[None],
        head_outs[4][0],
        *head_outs[:4],
        head_outs[4][1],
        head_outs[5],
        grad_gate,
        grad_up,
        grad_down,
    )


def solution(mesh):
    return jax.shard_map(
        per_device,
        mesh=mesh,
        in_specs=(
            P("rep", "ctx", None),
            P("rep", "ctx"),
            P("rep", "ctx"),
            P("rep", "ctx", None),
            P("ctx"),
            P("ctx", None),
            P("ctx", None),
            P("ctx", None),
            P("ctx", None),
            P("ctx"),
            P("ctx", None),
            P("ctx", None, None),
            P("ctx", None, None),
            P("ctx", None, None),
            P("rep", "ctx", None),
        ),
        out_specs=(
            P("rep", "ctx", None),
            P("rep", "ctx", None),
            P("ctx"),
            P("ctx", None),
            P("ctx", None),
            P("ctx", None),
            P("ctx", None),
            P("ctx"),
            P("ctx", None),
            P("ctx", None, None),
            P("ctx", None, None),
            P("ctx", None, None),
        ),
        check_vma=False,
    )
```

```python
import jax
import jax.numpy as jnp
from jax import lax
from jax.experimental import pallas as pl
from jax.experimental.pallas import tpu as pltpu
from jax.sharding import PartitionSpec as P

MODEL_WIDTH = 1536
QUERY_HEADS = 24
KEY_VALUE_HEADS = 8
HEAD_GROUP = QUERY_HEADS // KEY_VALUE_HEADS
HEAD_SIZE = 64
TOPK = 8

EPS = 1e-06
THETA = 10000.0
MASK_FLOOR = -1e30

ROWS = (((0,), (0,)), ((), ()))
COLUMNS = (((1,), (1,)), ((), ()))


def dot(left, right, contract=(((1,), (0,)), ((), ()))):
    return lax.dot_general(left, right, contract, preferred_element_type=jnp.float32)


def norm_back(grad_base, base, scale):
    return scale * (grad_base - base * jnp.mean(grad_base * base, -1, keepdims=True))


def turn(rows):
    half = HEAD_SIZE // 2
    return jnp.concatenate([-rows[:, half:], rows[:, :half]], 1)


def turn_back(rows):
    half = HEAD_SIZE // 2
    return jnp.concatenate([rows[:, half:], -rows[:, :half]], 1)


def stack_heads(rows):
    return jnp.concatenate(
        [rows[:, h * HEAD_SIZE : (h + 1) * HEAD_SIZE] for h in range(HEAD_GROUP)], 0
    )


def side_heads(rows):
    block = rows.shape[0] // HEAD_GROUP
    return jnp.concatenate([rows[h * block : (h + 1) * block] for h in range(HEAD_GROUP)], 1)


def lanes(values, combine):
    total = values[:, :128]
    for start in range(128, values.shape[1], 128):
        total = combine(total, values[:, start : start + 128])
    return total


def masked_scores(stacked, keys, row_segments, key_segments, row_start, key_start):
    block = row_segments.shape[0]
    scores = dot(stacked, keys, COLUMNS) * HEAD_SIZE ** (-0.5)
    row_place = row_start + lax.broadcasted_iota(jnp.int32, (block, block), 0)
    key_place = key_start + lax.broadcasted_iota(jnp.int32, (block, block), 1)
    allowed = (row_segments == key_segments) & (key_place <= row_place)
    scores = scores.reshape(HEAD_GROUP, block, block)
    return jnp.where(allowed[None], scores, MASK_FLOOR).reshape(HEAD_GROUP * block, block)


def first_block(row_segments, segment_ref, step):
    here = jnp.max(row_segments[:1, :1])
    segments = segment_ref[...]
    number = lax.broadcasted_iota(jnp.int32, segments.shape, 0)
    return jnp.min(jnp.where((segments == here) & (number <= step), number, step))


def token_rows(block, own, features):
    count = block // own
    return (
        pl.BlockSpec((count, own, features), lambda i, *_: (i, 0, 0)),
        pl.BlockSpec((count, own, 128), lambda i, *_: (i, 0, features // 128)),
    )


def flat(ref):
    return ref[...].reshape(-1, ref.shape[-1])


def whole_block(*shape):
    return pl.BlockSpec(shape, lambda *i: (0,) * len(shape), pipeline_mode=pl.Buffered(1))


def attend_kernel(
    hidden_ref,
    column_ref,
    gain_ref,
    low_ref,
    high_ref,
    rate_ref,
    normed_ref,
    query_ref,
    key_ref,
    value_ref,
    mixed_ref,
    packed_ref,
    log_ref,
    cosine_ref,
    sine_ref,
    segment_ref,
    score_ref,
):
    step = pl.program_id(0)
    block = query_ref.shape[0]
    query_width = query_ref.shape[1]
    width = query_width + 2 * HEAD_SIZE
    here = pl.ds(pl.multiple_of(step * block, block), block)
    columns = flat(column_ref).astype(jnp.float32)
    row_segments = columns[:, :1]
    segment_ref[step] = jnp.transpose(columns)[:1, :]
    angles = (columns[:, 1:2] * 64.0 + columns[:, 2:3]) * rate_ref[...]
    cosine = jnp.cos(angles)
    sine = jnp.sin(angles)
    cosine_ref[...] = cosine
    sine_ref[...] = sine
    hidden = flat(hidden_ref).astype(jnp.float32)
    scale = lax.rsqrt(jnp.mean(hidden * hidden, -1, keepdims=True) + EPS)
    normed = (hidden * scale * gain_ref[...]).astype(jnp.bfloat16)
    normed_ref[...] = normed
    middle = low_ref.shape[0]
    raw = dot(normed[:, :middle], low_ref[:, :width]) + dot(
        normed[:, middle:], high_ref[:, :width]
    )
    key_raw = raw[:, query_width : query_width + HEAD_SIZE]
    key_ref[here, :] = (key_raw * cosine + turn(key_raw) * sine).astype(jnp.bfloat16)
    value_ref[here, :] = raw[:, query_width + HEAD_SIZE :].astype(jnp.bfloat16)
    query_raw = stack_heads(raw[:, :query_width])
    cosine = jnp.concatenate([cosine] * HEAD_GROUP, 0)
    sine = jnp.concatenate([sine] * HEAD_GROUP, 0)
    query = (query_raw * cosine + turn(query_raw) * sine).astype(jnp.bfloat16)
    query_ref[...] = side_heads(query)
    rows = HEAD_GROUP * block
    first = first_block(row_segments, segment_ref, step)

    def first_pass(index, top):
        there = pl.ds(pl.multiple_of(index * block, block), block)
        scores = masked_scores(
            query,
            key_ref[there, :],
            row_segments,
            segment_ref[index],
            step * block,
            index * block,
        )
        score_ref[index] = scores
        return jnp.maximum(top, lanes(scores, jnp.maximum))

    top = lax.fori_loop(
        first, step + 1, first_pass, jnp.full((rows, 128), MASK_FLOOR, jnp.float32)
    )
    top = jnp.max(top, -1, keepdims=True)

    def second_pass(index, carry):
        total, mixed = carry
        there = pl.ds(pl.multiple_of(index * block, block), block)
        weights = jnp.exp(score_ref[index] - top)
        mixed = mixed + dot(weights.astype(jnp.bfloat16), value_ref[there, :])
        return total + lanes(weights, jnp.add), mixed

    total, mixed = lax.fori_loop(
        first,
        step + 1,
        second_pass,
        (
            jnp.zeros((rows, 128), jnp.float32),
            jnp.zeros((rows, HEAD_SIZE), jnp.float32),
        ),
    )
    total = jnp.sum(total, -1, keepdims=True)
    mixed = side_heads((mixed / total).astype(jnp.bfloat16))
    mixed_ref[...] = mixed
    packed_ref[...] = jnp.concatenate([mixed[: block // 2], mixed[block // 2 :]], 1)
    log_ref[...] = (top + jnp.log(total)).reshape(HEAD_GROUP, block, 1)


def attend(gathered, gain, weights, own, block):
    tokens, features = gathered.shape[0] * own, gain.shape[0]
    query_width = HEAD_GROUP * HEAD_SIZE
    steps = tokens // block
    half = jnp.arange(HEAD_SIZE // 2, dtype=jnp.float32)
    rate = THETA ** (-(2.0 * half) / HEAD_SIZE)
    rate = jnp.concatenate([rate, rate])[None, :]
    rows = lambda width: pl.BlockSpec((block, width), lambda i: (i, 0))
    resident = lambda *shape: pl.BlockSpec(shape, lambda i: (0,) * len(shape))
    shaped = jax.ShapeDtypeStruct
    return pl.pallas_call(
        attend_kernel,
        out_shape=(
            shaped((tokens, features), jnp.bfloat16),
            shaped((tokens, query_width), jnp.bfloat16),
            shaped((tokens, HEAD_SIZE), jnp.bfloat16),
            shaped((tokens, HEAD_SIZE), jnp.bfloat16),
            shaped((tokens, query_width), jnp.bfloat16),
            shaped((tokens // 2, 2 * query_width), jnp.bfloat16),
            shaped((HEAD_GROUP, tokens, 1), jnp.float32),
            shaped((tokens, HEAD_SIZE), jnp.float32),
            shaped((tokens, HEAD_SIZE), jnp.float32),
            shaped((steps, 1, block), jnp.float32),
        ),
        grid=(steps,),
        in_specs=[
            *token_rows(block, own, features),
            whole_block(1, features),
            whole_block(*weights[0].shape),
            whole_block(*weights[1].shape),
            whole_block(1, HEAD_SIZE),
        ],
        out_specs=[
            rows(features),
            rows(query_width),
            resident(tokens, HEAD_SIZE),
            resident(tokens, HEAD_SIZE),
            rows(query_width),
            pl.BlockSpec((block // 2, 2 * query_width), lambda i: (i, 0)),
            pl.BlockSpec((HEAD_GROUP, block, 1), lambda i: (0, i, 0)),
            rows(HEAD_SIZE),
            rows(HEAD_SIZE),
            resident(steps, 1, block),
        ],
        scratch_shapes=[pltpu.VMEM((steps, HEAD_GROUP * block, block), jnp.float32)],
        compiler_params=pltpu.CompilerParams(vmem_limit_bytes=48 << 20),
        cost_estimate=pl.CostEstimate(flops=0, bytes_accessed=tokens, transcendentals=0),
    )(gathered, gathered, gain[None, :], *weights, rate)


def attend_back_kernel(
    query_ref,
    grad_ref,
    log_ref,
    cosine_ref,
    sine_ref,
    column_ref,
    segment_ref,
    key_ref,
    value_ref,
    key_cosine_ref,
    key_sine_ref,
    grad_query_ref,
    grad_pair_ref,
    probs_ref,
    grad_probs_ref,
    grad_key_ref,
    grad_value_ref,
):
    step = pl.program_id(0)
    block = query_ref.shape[0]
    rows = HEAD_GROUP * block

    @pl.when(step == 0)
    def _():
        grad_key_ref[...] = jnp.zeros_like(grad_key_ref)
        grad_value_ref[...] = jnp.zeros_like(grad_value_ref)

    query = stack_heads(query_ref[...])
    grad = stack_heads(grad_ref[...])
    log_total = log_ref[...].reshape(rows, 1)
    row_segments = flat(column_ref).astype(jnp.float32)[:, :1]
    first = first_block(row_segments, segment_ref, step)

    def first_pass(index, delta):
        there = pl.ds(pl.multiple_of(index * block, block), block)
        scores = masked_scores(
            query,
            key_ref[there, :],
            row_segments,
            segment_ref[index],
            step * block,
            index * block,
        )
        probs = jnp.exp(scores - log_total)
        grad_probs = dot(grad, value_ref[there, :], COLUMNS)
        probs_ref[index] = probs
        grad_probs_ref[index] = grad_probs
        grad_value_ref[there, :] += dot(probs.astype(jnp.bfloat16), grad, ROWS)
        return delta + lanes(probs * grad_probs, jnp.add)

    delta = lax.fori_loop(first, step + 1, first_pass, jnp.zeros((rows, 128), jnp.float32))
    delta = jnp.sum(delta, -1, keepdims=True)

    def second_pass(index, grad_query):
        there = pl.ds(pl.multiple_of(index * block, block), block)
        grad_scores = (probs_ref[index] * (grad_probs_ref[index] - delta)).astype(jnp.bfloat16)
        grad_key_ref[there, :] += dot(grad_scores, query, ROWS)
        return grad_query + dot(grad_scores, key_ref[there, :])

    grad_query = lax.fori_loop(
        first, step + 1, second_pass, jnp.zeros((rows, HEAD_SIZE), jnp.float32)
    )
    score_scale = HEAD_SIZE ** (-0.5)
    cosine = jnp.concatenate([cosine_ref[...]] * HEAD_GROUP, 0)
    sine = jnp.concatenate([sine_ref[...]] * HEAD_GROUP, 0)
    grad_query = grad_query * score_scale
    grad_query = grad_query * cosine + turn_back(grad_query * sine)
    grad_query_ref[...] = side_heads(grad_query.astype(jnp.bfloat16))

    @pl.when(step == pl.num_programs(0) - 1)
    def _():
        @pl.loop(0, pl.num_programs(0))
        def _(index):
            there = pl.ds(pl.multiple_of(index * block, block), block)
            grad_key = grad_key_ref[there, :] * score_scale
            turned = turn_back(grad_key * key_sine_ref[there, :])
            grad_key = grad_key * key_cosine_ref[there, :] + turned
            grad_pair_ref[there, :] = jnp.concatenate(
                [grad_key, grad_value_ref[there, :]], 1
            ).astype(jnp.bfloat16)


def attend_back(query, grad, log_total, cosine, sine, gathered, segments, key, value, own):
    tokens, query_width = query.shape
    steps, _, block = segments.shape
    features = gathered.shape[2] - 128
    rows = lambda width: pl.BlockSpec((block, width), lambda i: (i, 0))
    resident = lambda *shape: pl.BlockSpec(shape, lambda i: (0,) * len(shape))
    return pl.pallas_call(
        attend_back_kernel,
        out_shape=(
            jax.ShapeDtypeStruct((tokens, query_width), jnp.bfloat16),
            jax.ShapeDtypeStruct((tokens, 2 * HEAD_SIZE), jnp.bfloat16),
        ),
        grid=(steps,),
        in_specs=[
            rows(query_width),
            rows(query_width),
            pl.BlockSpec((HEAD_GROUP, block, 1), lambda i: (0, i, 0)),
            rows(HEAD_SIZE),
            rows(HEAD_SIZE),
            token_rows(block, own, features)[1],
            whole_block(steps, 1, block),
            whole_block(tokens, HEAD_SIZE),
            whole_block(tokens, HEAD_SIZE),
            whole_block(tokens, HEAD_SIZE),
            whole_block(tokens, HEAD_SIZE),
        ],
        out_specs=[rows(query_width), resident(tokens, 2 * HEAD_SIZE)],
        scratch_shapes=[
            pltpu.VMEM((steps, HEAD_GROUP * block, block), jnp.float32),
            pltpu.VMEM((steps, HEAD_GROUP * block, block), jnp.float32),
            pltpu.VMEM((tokens, HEAD_SIZE), jnp.float32),
            pltpu.VMEM((tokens, HEAD_SIZE), jnp.float32),
        ],
        compiler_params=pltpu.CompilerParams(vmem_limit_bytes=48 << 20),
        cost_estimate=pl.CostEstimate(flops=0, bytes_accessed=tokens, transcendentals=0),
    )(query, grad, log_total, cosine, sine, gathered, segments, key, value, cosine, sine)


def slot_of(e, keeps, experts_own):
    pick = experts_own // 2
    high, low = e // pick, e % pick
    return (1 - (high ^ keeps)) * pick + low


def layer_kernel(
    place_ref,
    mixed_ref,
    low_ref,
    high_ref,
    hidden_ref,
    column_ref,
    gain_ref,
    router_ref,
    cotangent_ref,
    gate_any,
    up_any,
    down_any,
    normed_ref,
    scaled_one_ref,
    scaled_two_ref,
    grad_gate_ref,
    grad_up_ref,
    grad_live_ref,
    grad_rows_ref,
    middle_own_ref,
    normed_own_ref,
    gates_own_ref,
    gate_weight_ref,
    up_weight_ref,
    down_weight_ref,
    middle_ref,
    gates_ref,
    semaphores,
):
    step = pl.program_id(0)
    block, features = cotangent_ref.shape
    own = middle_own_ref.shape[0]
    groups = mixed_ref.shape[0]
    experts_own = gate_weight_ref.shape[0]
    experts_all = router_ref.shape[1]
    copies = [
        pltpu.make_async_copy(source, target, semaphores.at[n])
        for n, (source, target) in enumerate(
            (
                (gate_any, gate_weight_ref),
                (up_any, up_weight_ref),
                (down_any, down_weight_ref),
            )
        )
    ]

    @pl.when(step == 0)
    def _():
        for copy in copies:
            copy.start()

    width = mixed_ref.shape[2] // 2
    mixed = jnp.concatenate(
        [
            jnp.concatenate([mixed_ref[g, :, side : side + width] for g in range(groups)], 1)
            for side in (0, width)
        ],
        0,
    )
    half = low_ref.shape[0]
    middle = dot(mixed[:, :half], low_ref[...]) + dot(mixed[:, half:], high_ref[...])
    middle = flat(hidden_ref).astype(jnp.float32) + middle
    middle_ref[...] = middle
    scale = lax.rsqrt(jnp.mean(middle * middle, -1, keepdims=True) + EPS)
    normed = (middle * scale * gain_ref[...]).astype(jnp.bfloat16)
    normed_ref[...] = normed
    logits = dot(normed, router_ref[...])
    columns = flat(column_ref).astype(jnp.float32)
    number = lax.broadcasted_iota(jnp.int32, logits.shape, 1)
    named = columns[:, 3:4] == number.astype(jnp.float32)
    for slot in range(1, TOPK):
        named = named | (columns[:, 3 + slot : 4 + slot] == number.astype(jnp.float32))
    logits = jnp.where(named, logits, MASK_FLOOR)
    shifted = jnp.exp(logits - jnp.max(logits, -1, keepdims=True))
    shifted = jnp.where(named, shifted, 0.0)
    gates = shifted / jnp.sum(shifted, -1, keepdims=True)
    gates_ref[...] = gates
    grad_live_ref[...] = jnp.where(
        columns[:, :1] > 0, cotangent_ref[...], jnp.zeros((), jnp.bfloat16)
    )

    @pl.when(place_ref[0] == step)
    def _():
        there = pl.ds(pl.multiple_of(lax.rem(place_ref[1], 2) * own, own), own)
        middle_own_ref[...] = middle_ref[there, :]
        normed_own_ref[...] = normed_ref[there, :]
        gates_own_ref[...] = gates_ref[there, :]

    @pl.when(step == 0)
    def _():
        for copy in copies:
            copy.wait()

    first = place_ref[1] * experts_own

    def one_expert(e, grad_gates):
        one = slot_of(e, place_ref[2], experts_own)
        two = slot_of(e, place_ref[3], experts_own)
        gates = gates_ref[...]
        gate = jnp.sum(jnp.where(number == first + e, gates, 0.0), -1, keepdims=True)
        gate_pre = dot(normed_ref[...], gate_weight_ref[e])
        up_pre = dot(normed_ref[...], up_weight_ref[e])
        grad_plain = dot(grad_live_ref[...], down_weight_ref[e], COLUMNS)
        sigma = jax.nn.sigmoid(gate_pre)
        silu = gate_pre * sigma
        acted = silu * up_pre
        grad_acted = gate * grad_plain
        scaled = (gate * acted).astype(jnp.bfloat16)
        scaled_one_ref[one] = scaled
        scaled_two_ref[two] = scaled
        grad_gate_ref[one] = (
            grad_acted * up_pre * (sigma * (1.0 + gate_pre * (1.0 - sigma)))
        ).astype(jnp.bfloat16)
        grad_up_ref[two] = (grad_acted * silu).astype(jnp.bfloat16)
        return grad_gates + jnp.where(
            number == first + e, jnp.sum(acted * grad_plain, -1, keepdims=True), 0.0
        )

    grad_gates = lax.fori_loop(
        0, experts_own, one_expert, jnp.zeros(gates.shape, jnp.float32)
    )
    one = [slot_of(e, place_ref[2], experts_own) for e in range(experts_own)]
    two = [slot_of(e, place_ref[3], experts_own) for e in range(experts_own)]
    size = 512

    @pl.loop(0, features // size)
    def _(index):
        part = pl.ds(pl.multiple_of(index * size, size), size)
        grad = 0.0
        for e in range(experts_own):
            grad = grad + dot(grad_gate_ref[one[e]], gate_weight_ref[e, part, :], COLUMNS)
            grad = grad + dot(grad_up_ref[two[e]], up_weight_ref[e, part, :], COLUMNS)
        grad_rows_ref[:, part] = grad.astype(jnp.bfloat16)

    rough = grad_gates.astype(jnp.bfloat16)
    fine = (grad_gates - rough.astype(jnp.float32)).astype(jnp.bfloat16)
    rest = jnp.zeros((block, 128 - 2 * experts_all), jnp.bfloat16)
    grad_rows_ref[:, features:] = jnp.concatenate([rough, fine, rest], 1)


def layer_rows(place, mixed, weights, gathered, gain, router, cotangent, experts, own, block):
    groups, _, width = mixed.shape
    tokens, features = cotangent.shape
    experts_all = router.shape[1]
    experts_own, _, hidden = experts[0].shape
    rows = lambda columns: pl.BlockSpec((block, columns), lambda i, p: (i, 0))
    resident = lambda *shape: pl.BlockSpec(shape, lambda i, p: (0,) * len(shape))
    spread = pl.BlockSpec((experts_own, block, hidden), lambda i, p: (0, i, 0))
    low = jnp.bfloat16
    shaped = jax.ShapeDtypeStruct
    wide = shaped((experts_own, tokens, hidden), low)
    return pl.pallas_call(
        layer_kernel,
        out_shape=(
            shaped((tokens, features), low),
            wide,
            wide,
            wide,
            wide,
            shaped((tokens, features), low),
            shaped((tokens, features + 128), low),
            shaped((own, features), jnp.float32),
            shaped((own, features), low),
            shaped((own, experts_all), jnp.float32),
        ),
        grid_spec=pltpu.PrefetchScalarGridSpec(
            num_scalar_prefetch=1,
            grid=(tokens // block,),
            in_specs=[
                pl.BlockSpec((groups, block // 2, width), lambda i, p: (0, i, 0)),
                whole_block(*weights[0].shape),
                whole_block(*weights[1].shape),
                *token_rows(block, own, features),
                whole_block(1, features),
                whole_block(features, experts_all),
                rows(features),
                *[pl.BlockSpec(memory_space=pl.ANY)] * 3,
            ],
            out_specs=[
                rows(features),
                spread,
                spread,
                spread,
                spread,
                rows(features),
                rows(features + 128),
                resident(own, features),
                resident(own, features),
                resident(own, experts_all),
            ],
            scratch_shapes=[
                *[pltpu.VMEM(array.shape, low) for array in experts],
                pltpu.VMEM((block, features), jnp.float32),
                pltpu.VMEM((block, experts_all), jnp.float32),
                pltpu.SemaphoreType.DMA((3,)),
            ],
        ),
        compiler_params=pltpu.CompilerParams(vmem_limit_bytes=58 << 20),
        cost_estimate=pl.CostEstimate(
            flops=12 * tokens * features * hidden * experts_own,
            bytes_accessed=6 * features * hidden * experts_own + 20 * tokens * features,
            transcendentals=tokens * hidden * experts_own,
        ),
    )(
        place,
        mixed,
        *weights,
        gathered,
        gathered,
        gain[None, :],
        router,
        cotangent,
        *experts,
    )


def product_kernel(
    left_ref,
    gate_ref,
    up_ref,
    scaled_one_ref,
    scaled_two_ref,
    live_one_ref,
    live_two_ref,
    out_one_ref,
    out_two_ref,
):
    step = pl.program_id(0)
    tile, hidden = left_ref.shape[1], gate_ref.shape[1]
    narrow = live_one_ref.shape[1]
    tops = pl.num_programs(0) - 3
    top = tops * tile

    @pl.when(step < tops)
    def _():
        here = pl.ds(pl.multiple_of(step * tile, tile), tile)
        both = dot(left_ref[...], jnp.concatenate([gate_ref[...], up_ref[...]], 1), ROWS)
        out_one_ref[here, :] = both[:, :hidden].astype(out_one_ref.dtype)
        out_two_ref[here, :] = both[:, hidden:].astype(out_two_ref.dtype)

    @pl.when(step >= tops)
    def _():
        part = step - tops
        for scaled_ref, live_ref, out_ref in (
            (scaled_one_ref, live_one_ref, out_one_ref),
            (scaled_two_ref, live_two_ref, out_two_ref),
        ):
            product = dot(scaled_ref[...], live_ref[...], ROWS).astype(out_ref.dtype)

            @pl.when(part < 2)
            def _():
                there = pl.ds(pl.multiple_of(part * narrow, narrow), narrow)
                out_ref[top : top + hidden, there] = product

            @pl.when(part == 2)
            def _():
                out_ref[top + hidden :, :narrow] = product[:narrow]
                out_ref[top + hidden :, narrow:] = product[narrow:]


def expert_products(left, gate, up, scaled_one, scaled_two, live, e, dtype):
    tokens, features = left.shape
    hidden = gate.shape[2]
    narrow = hidden // 2
    tile = 512
    tops = features // tile
    rows = features + features // 2
    stack = pl.BlockSpec((None, tokens, hidden), lambda i: (e, 0, 0), pipeline_mode=pl.Buffered(1))
    lives = [
        pl.BlockSpec((tokens, narrow), lambda i, side=side: (0, 3 * side + jnp.maximum(i - tops, 0)))
        for side in range(2)
    ]
    out = pl.BlockSpec((rows, hidden), lambda i: (0, 0), pipeline_mode=pl.Buffered(1))
    return pl.pallas_call(
        product_kernel,
        out_shape=(jax.ShapeDtypeStruct((rows, hidden), dtype),) * 2,
        grid=(tops + 3,),
        in_specs=[
            pl.BlockSpec((tokens, tile), lambda i: (0, jnp.minimum(i, tops - 1))),
            stack,
            stack,
            stack,
            stack,
            *lives,
        ],
        out_specs=[out, out],
        compiler_params=pltpu.CompilerParams(vmem_limit_bytes=58 << 20),
        cost_estimate=pl.CostEstimate(flops=0, bytes_accessed=tokens, transcendentals=0),
    )(left, gate, up, scaled_one, scaled_two, live, live)


def output_kernel(place_ref, scaled_ref, down_weight_ref, out_ref):
    experts_own, _, features = down_weight_ref.shape
    size = 512

    @pl.loop(0, features // size)
    def _(index):
        part = pl.ds(pl.multiple_of(index * size, size), size)
        out = 0.0
        for e in range(experts_own):
            slot = slot_of(e, place_ref[2], experts_own)
            out = out + dot(scaled_ref[slot], down_weight_ref[e, :, part])
        out_ref[:, part] = out.astype(jnp.bfloat16)


def output_rows(place, scaled, w_down, block):
    experts_own, tokens, hidden = scaled.shape
    features = w_down.shape[2]
    return pl.pallas_call(
        output_kernel,
        out_shape=jax.ShapeDtypeStruct((tokens, features), jnp.bfloat16),
        grid_spec=pltpu.PrefetchScalarGridSpec(
            num_scalar_prefetch=1,
            grid=(tokens // block,),
            in_specs=[
                pl.BlockSpec((experts_own, block, hidden), lambda i, p: (0, i, 0)),
                whole_block(*w_down.shape),
            ],
            out_specs=pl.BlockSpec((block, features), lambda i, p: (i, 0)),
        ),
        compiler_params=pltpu.CompilerParams(vmem_limit_bytes=52 << 20),
        cost_estimate=pl.CostEstimate(flops=0, bytes_accessed=tokens, transcendentals=0),
    )(place, scaled, w_down)


def turn_kernel(
    place_ref,
    sum_ref,
    gates_ref,
    router_ref,
    gain_ref,
    middle_ref,
    live_ref,
    low_ref,
    high_ref,
    grad_middle_ref,
    branch_ref,
    mixed_ref,
    logits_ref,
    gain_grad_ref,
):
    features = middle_ref.shape[1]
    experts = gates_ref.shape[1]
    groups, _, width = mixed_ref.shape
    extra = sum_ref[:, features:].astype(jnp.float32)
    grad_gates = extra[:, :experts] + extra[:, experts : 2 * experts]
    gates = gates_ref[...]
    grad_logits = gates * (grad_gates - jnp.sum(gates * grad_gates, -1, keepdims=True))
    grad_logits = grad_logits.astype(jnp.bfloat16)
    logits_ref[...] = grad_logits
    grad = sum_ref[:, :features].astype(jnp.float32) + dot(grad_logits, router_ref[...], COLUMNS)
    middle = middle_ref[...]
    scale = lax.rsqrt(jnp.mean(middle * middle, -1, keepdims=True) + EPS)
    base = middle * scale
    gain_grad_ref[...] = jnp.sum(grad * base, 0, keepdims=True)
    grad_middle = live_ref[...].astype(jnp.float32) + norm_back(grad * gain_ref[...], base, scale)
    grad_middle_ref[...] = grad_middle
    branch = grad_middle.astype(jnp.bfloat16)
    branch_ref[...] = branch
    for half, weight_ref in enumerate((low_ref, high_ref)):
        mixed = dot(branch, weight_ref[...], COLUMNS).astype(jnp.bfloat16)
        for g in range(groups // 2):
            mixed_ref[half * (groups // 2) + g] = mixed[:, g * width : (g + 1) * width]


def turn_rows(place, sums, gates, router, gain, middle, live, weights):
    own, features = sums.shape[0], middle.shape[1]
    experts = gates.shape[1]
    groups = KEY_VALUE_HEADS
    shaped = jax.ShapeDtypeStruct
    rows = lambda width: pl.BlockSpec((own, width), lambda i, p: (p[1], 0))
    resident = lambda *shape: pl.BlockSpec(shape, lambda i, p: (0,) * len(shape))
    outs = (
        shaped((own, features), jnp.float32),
        shaped((own, features), jnp.bfloat16),
        shaped((groups, own, features // groups), jnp.bfloat16),
        shaped((own, experts), jnp.bfloat16),
        shaped((1, features), jnp.float32),
    )
    return pl.pallas_call(
        turn_kernel,
        out_shape=outs,
        grid_spec=pltpu.PrefetchScalarGridSpec(
            num_scalar_prefetch=1,
            grid=(1,),
            in_specs=[
                whole_block(*sums.shape),
                whole_block(*gates.shape),
                whole_block(*router.shape),
                whole_block(1, features),
                whole_block(*middle.shape),
                rows(features),
                whole_block(*weights[0].shape),
                whole_block(*weights[1].shape),
            ],
            out_specs=[resident(*out.shape) for out in outs],
        ),
        compiler_params=pltpu.CompilerParams(vmem_limit_bytes=58 << 20),
        cost_estimate=pl.CostEstimate(flops=0, bytes_accessed=own, transcendentals=0),
    )(place, sums, gates, router, gain[None, :], middle, live, *weights)


def close_kernel(
    reps,
    place_ref,
    query_ref,
    pair_ref,
    weight_ref,
    hidden_ref,
    normed_ref,
    gain_two_ref,
    normed_own_ref,
    logits_ref,
    rows_ref,
    mixed_ref,
    branch_ref,
    grad_ref,
    kept_one_ref,
    kept_two_ref,
    sent_one_ref,
    sent_two_ref,
    product_ref,
    gain_ref,
    out_ref,
    head_ref,
):
    step = pl.program_id(0)
    both = query_ref.shape[1] + pair_ref.shape[1]
    heads = jnp.concatenate([query_ref[...], pair_ref[...]], 1)
    grad = dot(heads, weight_ref[:, :both], COLUMNS)
    grad_ref[:, : grad.shape[1]] = grad.astype(jnp.bfloat16)
    grad_ref[:, grad.shape[1] :] = rows_ref[...]
    hidden = flat(hidden_ref).astype(jnp.float32)
    scale = lax.rsqrt(jnp.mean(hidden * hidden, -1, keepdims=True) + EPS)
    normed = normed_ref[...]

    @pl.when(step == 0)
    def _():
        gain_ref[...] = jnp.zeros_like(gain_ref)
        product_ref[...] = jnp.zeros_like(product_ref)
        out_ref[...] = jnp.zeros_like(out_ref)

    gain_ref[...] += jnp.sum(grad * (hidden * scale), 0, keepdims=True)
    product_ref[...] += dot(normed, heads, ROWS)
    out_ref[...] += dot(mixed_ref[...], branch_ref[...], ROWS)

    @pl.when(step == pl.num_programs(0) - 1)
    def _():
        features = product_ref.shape[0]
        rows = out_ref.shape[0]
        share = rows // reps
        experts = logits_ref.shape[1]
        line = kept_one_ref.shape[1]
        count = features // rows
        side = (line - features // 2) // (count // 2)
        gains = jnp.concatenate(
            [gain_ref[...], gain_two_ref[...], jnp.zeros((6, features), jnp.float32)], 0
        )
        gains = jnp.transpose(gains)
        router = dot(normed_own_ref[...], logits_ref[...], ROWS)
        rest = jnp.zeros((rows, side - both - 8 - experts), jnp.float32)
        for h in range(2):
            for c in range(count // 2):
                place = h * (count // 2) + c
                part = slice(place * rows, (place + 1) * rows)
                head_ref[h, :, c * side : (c + 1) * side] = jnp.concatenate(
                    [product_ref[part, :], gains[part], router[part], rest], 1
                )
            half = features // 2
            head_ref[h, :, count // 2 * side :] = out_ref[:, h * half : (h + 1) * half]
        sides = ((0, kept_one_ref, sent_one_ref), (1, kept_two_ref, sent_two_ref))
        for h, kept_ref, sent_ref in sides:
            bit = 1 if h == 0 else reps // 2
            for index in range(reps // 2):
                base = index // bit * 2 * bit + index % bit
                here = slice(index * share, (index + 1) * share)
                lower = head_ref[h, base * share : (base + 1) * share, :]
                upper = head_ref[h, (base + bit) * share : (base + bit + 1) * share, :]
                kept_ref[here, :] = jnp.where(place_ref[2 + h] > 0, upper, lower)
                sent_ref[here, :] = jnp.where(place_ref[2 + h] > 0, lower, upper).astype(jnp.bfloat16)


def close_rows(
    place,
    query,
    pair,
    weight,
    gathered,
    normed,
    gain_two_grad,
    normed_two,
    logits,
    out_rows,
    mixed,
    branch,
    reps,
    side,
    block,
):
    tokens, features = normed.shape
    own = logits.shape[0]
    both = query.shape[1] + pair.shape[1]
    rows_own = mixed.shape[1]
    rows = lambda width: pl.BlockSpec((block, width), lambda i, k: (i, 0))
    resident = lambda *shape: pl.BlockSpec(shape, lambda i, k: (0,) * len(shape))
    shaped = jax.ShapeDtypeStruct
    line = features // rows_own // 2 * side + features // 2
    half = (rows_own // 2, line)
    return pl.pallas_call(
        lambda *refs: close_kernel(reps, *refs),
        name="close",
        out_shape=(
            shaped((tokens, 2 * features), jnp.bfloat16),
            shaped(half, jnp.float32),
            shaped(half, jnp.float32),
            shaped(half, jnp.bfloat16),
            shaped(half, jnp.bfloat16),
        ),
        grid_spec=pltpu.PrefetchScalarGridSpec(
            num_scalar_prefetch=1,
            grid=(tokens // block,),
            in_specs=[
                rows(query.shape[1]),
                rows(pair.shape[1]),
                whole_block(*weight.shape),
                token_rows(block, own, features)[0],
                rows(features),
                whole_block(1, features),
                whole_block(own, features),
                whole_block(*logits.shape),
                rows(features),
                rows(rows_own),
                rows(features),
            ],
            out_specs=[rows(2 * features), *[resident(*half)] * 4],
            scratch_shapes=[
                pltpu.VMEM((features, both), jnp.float32),
                pltpu.VMEM((1, features), jnp.float32),
                pltpu.VMEM((rows_own, features), jnp.float32),
                pltpu.VMEM((2, rows_own, line), jnp.float32),
            ],
        ),
        compiler_params=pltpu.CompilerParams(vmem_limit_bytes=56 << 20),
        cost_estimate=pl.CostEstimate(flops=0, bytes_accessed=tokens, transcendentals=0),
    )(
        place,
        query,
        pair,
        weight,
        gathered,
        normed,
        gain_two_grad,
        normed_two,
        logits,
        out_rows,
        mixed,
        branch,
    )


def head_kernel(
    copies,
    side,
    low_ref,
    high_ref,
    query_ref,
    key_ref,
    value_ref,
    out_ref,
    gains_ref,
    router_ref,
):
    groups = KEY_VALUE_HEADS
    count = groups * copies
    halves = [low_ref[...].astype(jnp.float32), high_ref[...].astype(jnp.float32)]
    width = query_ref.shape[1] // groups
    parts = []
    for c in range(count):
        place = c % (count // 2) * side
        parts.append(halves[c // (count // 2)][:, place : place + side])
    heads = []
    small = 0.0
    for g in range(groups):
        total = parts[g * copies]
        for p in range(1, copies):
            total = total + parts[g * copies + p]
        heads.append(total)
        small = small + total[:, width + 2 * HEAD_SIZE :]
    gains_ref[...] = jnp.transpose(small[:, :8])
    router_ref[...] = small[:, 8 : 8 + router_ref.shape[1]]
    query_ref[...] = jnp.concatenate([head[:, :width] for head in heads], 1)
    key_ref[...] = jnp.concatenate([head[:, width : width + HEAD_SIZE] for head in heads], 1)
    value_ref[...] = jnp.concatenate(
        [head[:, width + HEAD_SIZE : width + 2 * HEAD_SIZE] for head in heads], 1
    )
    out_ref[...] = jnp.concatenate([half[:, count // 2 * side :] for half in halves], 1)


def head_outputs(low, high, copies, side, experts):
    rows = low.shape[0]
    groups = KEY_VALUE_HEADS
    query_width = QUERY_HEADS * HEAD_SIZE
    shaped = lambda width: jax.ShapeDtypeStruct((rows, width), jnp.float32)
    return pl.pallas_call(
        lambda *refs: head_kernel(copies, side, *refs),
        name="head_outputs",
        out_shape=(
            shaped(query_width),
            shaped(groups * HEAD_SIZE),
            shaped(groups * HEAD_SIZE),
            shaped(MODEL_WIDTH),
            jax.ShapeDtypeStruct((8, rows), jnp.float32),
            shaped(experts),
        ),
        compiler_params=pltpu.CompilerParams(vmem_limit_bytes=40 << 20),
        cost_estimate=pl.CostEstimate(flops=0, bytes_accessed=rows, transcendentals=0),
    )(low, high)


def upper_rows(flags_ref, side, own_ref, came_ref, rows):
    return jnp.where(flags_ref[2 + side] > 0, own_ref[rows, :], came_ref[rows, :])


def into_kernel(flags_ref, side, own_ref, came_ref, first_ref, second_ref, third_ref, out_ref):
    rows = own_ref.shape[0]
    rest = out_ref.shape[0] - rows
    half = first_ref.shape[0]
    kept = pl.program_id(0) == flags_ref[side]

    @pl.when(kept)
    def _():
        low = jnp.where(flags_ref[2 + side] > 0, came_ref[...], own_ref[...])
        out_ref[:rows, :] = low.astype(jnp.float32)
        high = upper_rows(flags_ref, side, own_ref, came_ref, slice(0, rest))
        out_ref[rows:, :] = high.astype(jnp.float32)

    @pl.when(jnp.logical_not(kept))
    def _():
        out_ref[:half, :] = first_ref[...].astype(jnp.float32)
        out_ref[half:rows, :] = second_ref[...].astype(jnp.float32)
        out_ref[rows:, :] = third_ref[:rest, :].astype(jnp.float32)


def into_output(flags, side, own, came, first, second, third):
    rows, hidden = own.shape
    total = 2 * rows * 2 // 3
    whole = lambda array: pl.BlockSpec(array.shape, lambda e, k: (0, 0))
    return pl.pallas_call(
        lambda k, *refs: into_kernel(k, side, *refs),
        name="into_output",
        out_shape=jax.ShapeDtypeStruct((2, total, hidden), jnp.float32),
        grid_spec=pltpu.PrefetchScalarGridSpec(
            num_scalar_prefetch=1,
            grid=(2,),
            in_specs=[whole(own), whole(came), whole(first), whole(second), whole(third)],
            out_specs=pl.BlockSpec((None, total, hidden), lambda e, k: (e, 0, 0)),
        ),
        compiler_params=pltpu.CompilerParams(vmem_limit_bytes=40 << 20),
        cost_estimate=pl.CostEstimate(flops=0, bytes_accessed=rows, transcendentals=0),
    )(flags, own, came, first, second, third)


def down_kernel(flags_ref, *refs):
    out_ref = refs[8]
    hidden = out_ref.shape[0]
    narrow = hidden // 2
    for side in range(2):
        own_ref, came_ref, third_ref, last_ref = refs[4 * side : 4 * side + 4]
        rows = own_ref.shape[0]
        rest = rows - out_ref.shape[1] // 2
        mine = upper_rows(flags_ref, side, own_ref, came_ref, slice(rest, rows))
        theirs = jnp.concatenate([third_ref[rest:, :], last_ref[...]], 0)
        kept = pl.program_id(0) == flags_ref[side]
        value = jnp.where(kept, mine, theirs).astype(jnp.float32)
        start = side * value.shape[0]
        out_ref[:, start : start + hidden] = value[:hidden]
        middle, end = start + hidden, start + value.shape[0]
        out_ref[:narrow, middle:end] = value[hidden:, :narrow]
        out_ref[narrow:, middle:end] = value[hidden:, narrow:]


def down_output(flags, *operands):
    rows, hidden = operands[0].shape
    whole = lambda array: pl.BlockSpec(array.shape, lambda e, k: (0, 0))
    return pl.pallas_call(
        down_kernel,
        out_shape=jax.ShapeDtypeStruct((2, hidden, 3 * hidden), jnp.float32),
        grid_spec=pltpu.PrefetchScalarGridSpec(
            num_scalar_prefetch=1,
            grid=(2,),
            in_specs=[whole(array) for array in operands],
            out_specs=pl.BlockSpec((None, hidden, 3 * hidden), lambda e, k: (e, 0, 0)),
        ),
        compiler_params=pltpu.CompilerParams(vmem_limit_bytes=40 << 20),
        cost_estimate=pl.CostEstimate(flops=0, bytes_accessed=rows, transcendentals=0),
    )(flags, *operands)


def after(values, *others):
    values, _ = lax.optimization_barrier((values, others))
    return values


def swap(value, bit):
    size = lax.axis_size("rep")
    return lax.ppermute(value, "rep", [(i, i ^ bit) for i in range(size)])


def has(bit):
    return (lax.axis_index("rep") & bit) != 0


def join(value, came, bit, axis):
    upper = has(bit)
    return jnp.concatenate(
        [jnp.where(upper, came, value), jnp.where(upper, value, came)], axis
    )


class Chain:
    def __init__(self, order):
        self.order = order
        self.stage = 0
        self.steps = 2 * len(order)

    def send(self, sent):
        bit = self.order[min(self.stage, self.steps - 1 - self.stage)]
        self.sent = sent
        self.stage += 1
        if self.stage < self.steps:
            self.flying = swap(sent, bit)

    def step(self, *others):
        came = after(self.flying, *others)
        self.send(join(self.sent, came, self.order[self.steps - self.stage], 0))
        return self.sent

    def ends(self, *others):
        self.own = self.sent
        self.came = after(self.flying, *others)
        upper = has(self.order[1])
        half = self.own.shape[0] // 2
        begin, end = slice(0, half), slice(half, 2 * half)
        low = lambda rows: jnp.where(upper, self.came[rows], self.own[rows])
        high = lambda rows: jnp.where(upper, self.own[rows], self.came[rows])
        return [low(begin), low(end), high(begin), high(end)]

    def last(self, piece):
        return swap(piece, self.order[0])


def halve_kernel(keeps_ref, *refs):
    count = len(refs) // 3
    for chain in range(2):
        for place in range(0, count, 2):
            value_ref, came_ref = refs[count * chain + place : count * chain + place + 2]
            out_ref = refs[2 * count + chain * (count // 2) + place // 2]
            out_ref[...] = (value_ref[...] + came_ref[...].astype(jnp.float32)).astype(
                out_ref.dtype
            )


def halve_chains(chains, *others):
    order = [chain.order[chain.stage] for chain in chains]
    last = chains[0].stage == len(chains[0].order) - 1
    keeps = jnp.stack([has(bit) for bit in order]).astype(jnp.int32)
    rows, hidden = chains[0].kept.shape
    count = 4
    part = rows // 2 // count
    operands, specs = [], []
    for c, chain in enumerate(chains):
        chain.came = after(chain.flying, *others)
        for flip in (1,) if last else (1, 0):
            index = lambda i, k, c=c, flip=flip: ((k[c] ^ flip) * count + i, 0)
            operands += [chain.kept, chain.came]
            specs += [pl.BlockSpec((part, hidden), index)] * 2
    block = pl.BlockSpec((part, hidden), lambda i, k: (i, 0))
    shaped = lambda dtype: jax.ShapeDtypeStruct((rows // 2, hidden), dtype)
    each = [shaped(jnp.bfloat16)] if last else [shaped(jnp.bfloat16), shaped(jnp.float32)]
    outs = pl.pallas_call(
        halve_kernel,
        out_shape=each * 2,
        grid_spec=pltpu.PrefetchScalarGridSpec(
            num_scalar_prefetch=1,
            grid=(count,),
            in_specs=specs,
            out_specs=[block] * (2 * len(each)),
        ),
        compiler_params=pltpu.CompilerParams(vmem_limit_bytes=58 << 20),
        cost_estimate=pl.CostEstimate(
            flops=60000 * rows * hidden, bytes_accessed=12 * rows * hidden, transcendentals=0
        ),
    )(keeps, *operands)
    for c, chain in enumerate(chains):
        if not last:
            chain.kept = outs[2 * c + 1]
        chain.send(outs[len(each) * c])
    return [chain.sent for chain in chains]


def total_kernel(keeps_ref, *refs):
    for chain in range(2):
        kept_ref, first_ref, second_ref = refs[3 * chain : 3 * chain + 3]
        total = kept_ref[...] + first_ref[...].astype(jnp.float32)
        refs[6 + chain][...] = (total + second_ref[...].astype(jnp.float32)).astype(jnp.bfloat16)


def total_chains(chains, *others):
    keeps = jnp.stack([has(chain.order[-1]) for chain in chains]).astype(jnp.int32)
    rows, hidden = chains[0].kept.shape
    count = 4
    part = rows // 2 // count
    block = pl.BlockSpec((part, hidden), lambda i, k: (i, 0))
    operands, specs = [], []
    for c, chain in enumerate(chains):
        stay = pl.BlockSpec((part, hidden), lambda i, k, c=c: (k[c] * count + i, 0))
        operands += [chain.kept, chain.came, after(chain.flying, *others)]
        specs += [stay, stay, block]
    outs = pl.pallas_call(
        total_kernel,
        out_shape=[jax.ShapeDtypeStruct((rows // 2, hidden), jnp.bfloat16)] * 2,
        grid_spec=pltpu.PrefetchScalarGridSpec(
            num_scalar_prefetch=1, grid=(count,), in_specs=specs, out_specs=[block] * 2
        ),
        compiler_params=pltpu.CompilerParams(vmem_limit_bytes=58 << 20),
        cost_estimate=pl.CostEstimate(flops=0, bytes_accessed=rows, transcendentals=0),
    )(keeps, *operands)
    for chain, out in zip(chains, outs):
        chain.send(out)
    return list(outs)


class Cube:
    def __init__(self, kept, sent, order, share):
        shape = [2] * len(order)
        shape[len(order) - order[0].bit_length()] = 1
        self.value, sent = [array.reshape(*shape, share, -1) for array in (kept, sent)]
        self.order = order
        self.flying = swap(sent, order[0])
        self.stage = 1

    def axis(self, bit):
        return len(self.order) - bit.bit_length()

    def halve(self, *others):
        bit = self.order[self.stage]
        keep = has(bit).astype(jnp.int32)
        part = lambda index: lax.dynamic_slice_in_dim(self.value, index, 1, self.axis(bit))
        self.value, sent = part(keep), part(1 - keep).astype(jnp.bfloat16)
        self.flying = swap(after(sent, *others), bit)
        self.stage += 1
        return sent

    def add(self, *others):
        self.value = self.value + after(self.flying, *others).astype(jnp.float32)

    def back(self, *others):
        self.stage -= 1
        self.flying = swap(after(self.value, *others), self.order[self.stage])
        return self.value

    def join(self, *others):
        bit = self.order[self.stage]
        self.value = join(self.value, after(self.flying, *others), bit, self.axis(bit))


def scalar_call(kernel, outs, scalars, *operands, scratch=(), flops=0):
    whole = lambda array: pl.BlockSpec(array.shape, lambda i, p: (0,) * len(array.shape))
    return pl.pallas_call(
        kernel,
        out_shape=outs,
        grid_spec=pltpu.PrefetchScalarGridSpec(
            num_scalar_prefetch=1,
            grid=(1,),
            in_specs=[whole(array) for array in operands],
            out_specs=[whole(out) for out in outs],
            scratch_shapes=scratch,
        ),
        name="scalar_call",
        compiler_params=pltpu.CompilerParams(vmem_limit_bytes=58 << 20),
        cost_estimate=pl.CostEstimate(flops=flops, bytes_accessed=1024, transcendentals=0),
    )(scalars, *operands)


def pack_kernel(size, side, place_ref, *refs):
    chips = size // 2
    values = refs[:4]
    out_ref = refs[4 + chips]
    all_ref = refs[5 + chips]
    for h in range(2):
        total = values[2 * h][...] + values[2 * h + 1][...].astype(jnp.float32)
        total = total.astype(jnp.bfloat16)
        for c in range(chips):
            all_ref[h * chips + c] = total[:, c * side : (c + 1) * side]
        out_ref[h] = total[:, chips * side :]
    for k in range(chips):
        chip = lax.rem(place_ref[0] - k + chips, chips)
        for core in range(2):
            refs[4 + k][core] = all_ref[2 * chip + core]


def pack_heads(place, cubes, size, side):
    chips = size // 2
    share, line = cubes[0].value.shape[-2:]
    low = jnp.bfloat16
    outs = [jax.ShapeDtypeStruct((2, share, side), low)] * chips
    outs.append(jax.ShapeDtypeStruct((2, share, line - chips * side), low))
    operands = []
    for cube in cubes:
        operands += [cube.value.reshape(share, line), cube.flying.reshape(share, line)]
    *parcels, out_sums = scalar_call(
        lambda *refs: pack_kernel(size, side, *refs),
        outs,
        place,
        *operands,
        scratch=[pltpu.VMEM((size, share, side), low)],
        flops=200000000000,
    )
    return parcels, out_sums


def split_kernel(place_ref, *refs):
    chips = len(refs) - 2
    core = lax.rem(place_ref[1], 2)
    for k in range(chips):
        refs[chips][k] = refs[k][core]
        refs[chips + 1][k] = refs[k][1 - core]


def split_cores(place, got):
    out = jax.ShapeDtypeStruct((len(got),) + got[0].shape[1:], got[0].dtype)
    return scalar_call(split_kernel, [out, out], place, *got)


def unpack_kernel(place_ref, stay_ref, came_ref, out_ref, low_ref, high_ref, all_ref):
    chips, _, side = stay_ref.shape
    core = lax.rem(place_ref[1], 2)
    for k in range(chips):
        chip = lax.rem(place_ref[0] + k, chips)
        all_ref[2 * chip + core] = stay_ref[k]
        all_ref[2 * chip + 1 - core] = came_ref[k]
    for h, rows_ref in enumerate((low_ref, high_ref)):
        for c in range(chips):
            rows_ref[:, c * side : (c + 1) * side] = all_ref[h * chips + c]
        rows_ref[:, chips * side :] = out_ref[h]


def unpack_heads(place, stay, came, out_sums):
    chips, share, side = stay.shape
    line = chips * side + out_sums.shape[2]
    out = jax.ShapeDtypeStruct((share, line), stay.dtype)
    return scalar_call(
        unpack_kernel,
        [out, out],
        place,
        stay,
        came,
        out_sums,
        scratch=[pltpu.VMEM((2 * chips, share, side), stay.dtype)],
    )


class Exchange:
    def __init__(self, fetched, bits):
        size = fetched.shape[0]
        fetched = fetched.reshape((size,) + (1,) * len(bits) + fetched.shape[1:])
        self.values = [fetched[: size // 2], fetched[size // 2 :]]
        self.orders = (bits, bits[::-1])
        self.stage = 0
        self.fly()

    def fly(self):
        self.flying = [
            swap(value, order[self.stage]) for value, order in zip(self.values, self.orders)
        ]

    def step(self, *others):
        bits = len(self.orders[0])
        for h, order in enumerate(self.orders):
            bit = order[self.stage]
            came = after(self.flying[h], *others)
            self.values[h] = join(self.values[h], came, bit, bits - (bit.bit_length() - 1))
        self.stage += 1
        if self.stage < bits:
            self.fly()
        return list(self.values)

    def finish(self, *others):
        while self.stage < len(self.orders[0]):
            self.step(*others)
        return [value.reshape(-1, value.shape[-1]) for value in self.values]


def per_device(
    inputs,
    segments,
    positions,
    expert_ids,
    attn_gain,
    w_query,
    key_weight,
    value_weight,
    w_out,
    ffn_gain,
    router,
    w_gate,
    w_up,
    w_down,
    grad_out,
):
    size = lax.axis_size("ctx")
    me = lax.axis_index("ctx")
    reps = lax.axis_size("rep")
    bits = [1 << i for i in range(reps.bit_length() - 1)]
    own = inputs.shape[1]
    tokens = size * own
    groups = KEY_VALUE_HEADS
    copies = size // groups
    query_width = HEAD_GROUP * HEAD_SIZE
    width = query_width + 2 * HEAD_SIZE
    copy_index = me % copies
    rows_own = w_out.shape[0]
    experts_own = w_gate.shape[0]
    experts_all = size * experts_own
    block = 2 * own
    chips = size // 2
    chip = me // 2
    odd = me % 2 == 1
    share = rows_own // reps
    share_start = lax.axis_index("rep") * share

    columns = jnp.concatenate(
        [
            segments[0][:, None],
            positions[0][:, None] // 64,
            positions[0][:, None] % 64,
            expert_ids[0],
        ],
        1,
    ).astype(jnp.bfloat16)
    columns = jnp.pad(columns, ((0, 0), (0, 128 - columns.shape[1])))
    shared = lambda array: lax.dynamic_slice_in_dim(array, share_start, share, 0)

    rows = jnp.concatenate(
        [
            jnp.concatenate([inputs[0], columns], 1),
            jnp.pad(shared(w_out), ((0, 0), (0, 128))),
        ],
        0,
    )
    gathered = lax.all_gather(rows, "ctx", axis=0)
    cotangent = lax.all_gather(after(grad_out[0], rows), "ctx", axis=0, tiled=True)

    def from_chip(value, k):
        return lax.ppermute(value, "ctx", [(i, (i - 2 * k) % size) for i in range(size)])

    def from_core(value):
        return lax.ppermute(value, "ctx", [(i, i ^ 1) for i in range(size)])

    def cores(mine, others, axis):
        return jnp.concatenate(
            [jnp.where(odd, others, mine), jnp.where(odd, mine, others)], axis
        )

    side_width = -(-(width + 2 + router.shape[1]) // 128) * 128
    head_columns = jnp.concatenate(
        [
            shared(w_query).reshape(share, groups, query_width),
            shared(key_weight).reshape(share, groups, HEAD_SIZE),
            shared(value_weight).reshape(share, groups, HEAD_SIZE),
            jnp.broadcast_to(shared(attn_gain)[:, None, None], (share, groups, 1)),
            jnp.broadcast_to(shared(ffn_gain)[:, None, None], (share, groups, 1)),
            jnp.broadcast_to(shared(router)[:, None, :], (share, groups, router.shape[1])),
        ],
        -1,
    )
    used = head_columns.shape[-1]
    head_columns = jnp.pad(head_columns, ((0, 0), (0, 0), (0, side_width - used)))
    head_columns = jnp.repeat(jnp.transpose(head_columns, (1, 0, 2)), copies, 0)
    head_columns = lax.all_to_all(head_columns, "ctx", split_axis=0, concat_axis=0, tiled=True)
    head_halves = Exchange(head_columns, bits).finish()
    head_all = jnp.concatenate(head_halves, 0)
    gain_one = head_all[:, width].astype(jnp.float32)
    gain_two = head_all[:, width + 1].astype(jnp.float32)
    router_all = head_all[:, width + 2 : used]

    (
        normed_one,
        query,
        key,
        value,
        mixed,
        packed,
        log_total,
        cosine_table,
        sine_table,
        segment_rows,
    ) = attend(gathered, gain_one, head_halves, own, block)
    out_exchange = Exchange(gathered[:, own:, :MODEL_WIDTH], bits)

    part = tokens // copies
    mixed_all = lax.all_gather(
        after(
            lax.dynamic_slice_in_dim(packed, copy_index * part // 2, part // 2, 0),
            cotangent,
            out_exchange.step(),
        ),
        "ctx",
        axis=0,
    ).reshape(groups, tokens // 2, 2 * query_width)
    w_out_halves = out_exchange.finish()

    flag = lambda bit: has(bit).astype(jnp.int32)
    place = jnp.stack([chip, me, flag(bits[0]), flag(bits[-1])]).astype(jnp.int32)
    (
        normed_two,
        scaled_one,
        scaled_two,
        grad_gate_pre,
        grad_up_pre,
        grad_live,
        grad_rows,
        middle_own,
        normed_own,
        gates_own,
    ) = layer_rows(
        place,
        mixed_all,
        w_out_halves,
        gathered,
        gain_two,
        router_all,
        cotangent,
        (w_gate, w_up, w_down),
        own,
        block,
    )

    products = lambda e, dtype: expert_products(
        normed_two, grad_gate_pre, grad_up_pre, scaled_one, scaled_two, grad_live, e, dtype
    )
    grad_two_sum = lax.psum_scatter(grad_rows, "ctx", scatter_dimension=0, tiled=True)
    normed_two, grad_live = after((normed_two, grad_live), grad_rows)
    chains = [Chain(bits), Chain(bits[::-1])]
    for chain, sent in zip(chains, products(0, jnp.bfloat16)):
        chain.send(sent)
    normed_two, grad_live = after((normed_two, grad_live), *[chain.sent for chain in chains])
    for chain, kept in zip(chains, products(1, jnp.float32)):
        chain.kept = kept
    out_rows = output_rows(place, after(scaled_one, *[c.kept for c in chains]), w_down, block)

    grad_middle, grad_branch, grad_mixed, grad_logits, gain_two_grad = turn_rows(
        place,
        after(grad_two_sum, out_rows),
        gates_own,
        router_all,
        gain_two,
        middle_own,
        grad_live,
        w_out_halves,
    )
    grad_branch_all = lax.all_gather(grad_branch, "ctx", axis=0, tiled=True)

    def deal_chips(blocks):
        blocks = blocks.reshape((chips, 2) + blocks.shape[1:])
        got = [blocks[(chip - k) % chips] for k in range(chips)]
        return jnp.stack([got[0]] + [from_chip(got[k], k) for k in range(1, chips)])

    def deal_cores(got):
        stay = jnp.where(odd, got[:, 1], got[:, 0])
        go = from_core(jnp.where(odd, got[:, 0], got[:, 1]))
        both = cores(stay[:, None], go[:, None], 1)
        both = jnp.concatenate([both, both], 0)
        both = lax.dynamic_slice_in_dim(both, (chips - chip) % chips, chips, 0)
        return both.reshape((size,) + both.shape[2:])

    got = deal_chips(jnp.repeat(grad_mixed, copies, 0))
    sent = [got]
    while chains[0].stage < len(bits):
        sent = halve_chains(chains, *sent)
    grad_mixed_all = deal_cores(after(got, *sent)).reshape(tokens, query_width)
    grad_query, grad_pair = attend_back(
        query,
        grad_mixed_all,
        log_total,
        cosine_table,
        sine_table,
        gathered,
        segment_rows,
        key,
        value,
        own,
    )
    if copies > 1:
        places = jnp.arange(tokens, dtype=jnp.int32)
        counted = (places // part == copy_index)[:, None]
        grad_query = jnp.where(counted, grad_query, jnp.zeros((), jnp.bfloat16))
        grad_pair = jnp.where(counted, grad_pair, jnp.zeros((), jnp.bfloat16))
    sent = total_chains(chains, grad_pair)
    both_rows, *halves = close_rows(
        place,
        after(grad_query, *sent),
        grad_pair,
        head_all,
        gathered,
        normed_one,
        gain_two_grad,
        normed_own,
        grad_logits,
        out_rows,
        lax.dynamic_slice_in_dim(mixed, copy_index * rows_own, rows_own, 1),
        grad_branch_all,
        reps,
        side_width,
        block,
    )
    both_sums = lax.psum_scatter(
        both_rows, "ctx", scatter_dimension=0, tiled=True
    ).astype(jnp.float32)
    grad_one, out_sum = both_sums[:, :MODEL_WIDTH], both_sums[:, MODEL_WIDTH:]

    line = size // 2 * side_width
    cubes = [
        Cube(halves[h], halves[2 + h], order, share)
        for h, order in enumerate((bits, bits[::-1]))
    ]
    while chains[0].stage < chains[0].steps - 1:
        sent = [chain.step(*halves) for chain in chains]
    pieces = [chain.ends(*halves) for chain in chains]
    sent = [part[0] for part in pieces]
    while cubes[0].stage < len(bits):
        for cube in cubes:
            cube.add(*sent)
        sent = [cube.halve() for cube in cubes]
    first = [chain.last(part[0]) for chain, part in zip(chains, pieces)]
    second = [chain.last(after(part[1], *sent)) for chain, part in zip(chains, pieces)]
    for cube in cubes:
        cube.flying = after(cube.flying, *sent)
    parcels, out_sums = pack_heads(place, cubes, size, side_width)
    parcels = after(parcels, *first)
    got = [parcels[0]] + [from_chip(parcels[k], k) for k in range(1, chips)]
    stay, go = split_cores(place, got)
    came = from_core(after(go, *second))
    third = [chain.last(after(part[2], *second)) for chain, part in zip(chains, pieces)]
    for cube, value in zip(cubes, unpack_heads(place, stay, came, out_sums)):
        cube.value = value.reshape((1,) * len(bits) + value.shape)
    sent = [cube.back() for cube in cubes]
    fourth = [chain.last(after(part[3], *third)) for chain, part in zip(chains, pieces)]
    flags = jnp.stack([flag(chain.order[n]) for n in range(2) for chain in chains])
    while cubes[0].stage > 0:
        for cube in cubes:
            cube.join(*third)
        sent = [cube.back() for cube in cubes]
    grad_gate, grad_up = [
        into_output(
            flags,
            side,
            *after((chain.own, chain.came, first[side], second[side], third[side]), *sent),
        )
        for side, chain in enumerate(chains)
    ]
    output = jnp.where((segments[0] != 0)[:, None], middle_own + out_sum, 0.0)
    own_hidden = inputs[0].astype(jnp.float32)
    own_scale = lax.rsqrt(jnp.mean(own_hidden * own_hidden, -1, keepdims=True) + EPS)
    grad_in = grad_middle + norm_back(grad_one * gain_one, own_hidden * own_scale, own_scale)
    for cube in cubes:
        cube.join(grad_gate, grad_up, output, grad_in)
    head_outs = head_outputs(
        *[cube.value.reshape(rows_own, -1) for cube in cubes], copies, side_width, experts_all
    )
    operands = []
    for side, chain in enumerate(chains):
        operands += [chain.own, chain.came, third[side], fourth[side]]
    grad_down = down_output(flags, *after(operands, head_outs))

    return (
        output.astype(jnp.bfloat16)[None],
        grad_in[None],
        head_outs[4][0],
        *head_outs[:4],
        head_outs[4][1],
        head_outs[5],
        grad_gate,
        grad_up,
        grad_down,
    )


def solution(mesh):
    return jax.shard_map(
        per_device,
        mesh=mesh,
        in_specs=(
            P("rep", "ctx", None),
            P("rep", "ctx"),
            P("rep", "ctx"),
            P("rep", "ctx", None),
            P("ctx"),
            P("ctx", None),
            P("ctx", None),
            P("ctx", None),
            P("ctx", None),
            P("ctx"),
            P("ctx", None),
            P("ctx", None, None),
            P("ctx", None, None),
            P("ctx", None, None),
            P("rep", "ctx", None),
        ),
        out_specs=(
            P("rep", "ctx", None),
            P("rep", "ctx", None),
            P("ctx"),
            P("ctx", None),
            P("ctx", None),
            P("ctx", None),
            P("ctx", None),
            P("ctx"),
            P("ctx", None),
            P("ctx", None, None),
            P("ctx", None, None),
            P("ctx", None, None),
        ),
        check_vma=False,
    )
```

```python
import jax
import jax.numpy as jnp
from jax import lax
from jax.experimental import pallas as pl
from jax.experimental.pallas import tpu as pltpu
from jax.sharding import PartitionSpec as P

MODEL_WIDTH = 1536
QUERY_HEADS = 24
KEY_VALUE_HEADS = 8
HEAD_GROUP = QUERY_HEADS // KEY_VALUE_HEADS
HEAD_SIZE = 64
TOPK = 8

EPS = 1e-06
THETA = 10000.0
MASK_FLOOR = -1e30

ROWS = (((0,), (0,)), ((), ()))
COLUMNS = (((1,), (1,)), ((), ()))


def dot(left, right, contract=(((1,), (0,)), ((), ()))):
    return lax.dot_general(left, right, contract, preferred_element_type=jnp.float32)


def norm_back(grad_base, base, scale):
    return scale * (grad_base - base * jnp.mean(grad_base * base, -1, keepdims=True))


def turn(rows):
    half = HEAD_SIZE // 2
    return jnp.concatenate([-rows[:, half:], rows[:, :half]], 1)


def turn_back(rows):
    half = HEAD_SIZE // 2
    return jnp.concatenate([rows[:, half:], -rows[:, :half]], 1)


def stack_heads(rows):
    return jnp.concatenate(
        [rows[:, h * HEAD_SIZE : (h + 1) * HEAD_SIZE] for h in range(HEAD_GROUP)], 0
    )


def side_heads(rows):
    block = rows.shape[0] // HEAD_GROUP
    return jnp.concatenate([rows[h * block : (h + 1) * block] for h in range(HEAD_GROUP)], 1)


def lanes(values, combine):
    total = values[:, :128]
    for start in range(128, values.shape[1], 128):
        total = combine(total, values[:, start : start + 128])
    return total


def masked_scores(stacked, keys, row_segments, key_segments, row_start, key_start):
    block = row_segments.shape[0]
    scores = dot(stacked, keys, COLUMNS) * HEAD_SIZE ** (-0.5)
    row_place = row_start + lax.broadcasted_iota(jnp.int32, (block, block), 0)
    key_place = key_start + lax.broadcasted_iota(jnp.int32, (block, block), 1)
    allowed = (row_segments == key_segments) & (key_place <= row_place)
    scores = scores.reshape(HEAD_GROUP, block, block)
    return jnp.where(allowed[None], scores, MASK_FLOOR).reshape(HEAD_GROUP * block, block)


def first_block(row_segments, segment_ref, step):
    here = jnp.max(row_segments[:1, :1])
    segments = segment_ref[...]
    number = lax.broadcasted_iota(jnp.int32, segments.shape, 0)
    return jnp.min(jnp.where((segments == here) & (number <= step), number, step))


def token_rows(block, own, features):
    count = block // own
    return (
        pl.BlockSpec((count, own, features), lambda i, *_: (i, 0, 0)),
        pl.BlockSpec((count, own, 128), lambda i, *_: (i, 0, features // 128)),
    )


def flat(ref):
    return ref[...].reshape(-1, ref.shape[-1])


def whole_block(*shape):
    return pl.BlockSpec(shape, lambda *i: (0,) * len(shape), pipeline_mode=pl.Buffered(1))


def attend_kernel(
    hidden_ref,
    column_ref,
    gain_ref,
    low_ref,
    high_ref,
    rate_ref,
    normed_ref,
    query_ref,
    key_ref,
    value_ref,
    mixed_ref,
    packed_ref,
    log_ref,
    cosine_ref,
    sine_ref,
    segment_ref,
    score_ref,
):
    step = pl.program_id(0)
    block = query_ref.shape[0]
    query_width = query_ref.shape[1]
    width = query_width + 2 * HEAD_SIZE
    here = pl.ds(pl.multiple_of(step * block, block), block)
    columns = flat(column_ref).astype(jnp.float32)
    row_segments = columns[:, :1]
    segment_ref[step] = jnp.transpose(columns)[:1, :]
    angles = (columns[:, 1:2] * 64.0 + columns[:, 2:3]) * rate_ref[...]
    cosine = jnp.cos(angles)
    sine = jnp.sin(angles)
    cosine_ref[...] = cosine
    sine_ref[...] = sine
    hidden = flat(hidden_ref).astype(jnp.float32)
    scale = lax.rsqrt(jnp.mean(hidden * hidden, -1, keepdims=True) + EPS)
    normed = (hidden * scale * gain_ref[...]).astype(jnp.bfloat16)
    normed_ref[...] = normed
    middle = low_ref.shape[0]
    raw = dot(normed[:, :middle], low_ref[:, :width]) + dot(
        normed[:, middle:], high_ref[:, :width]
    )
    key_raw = raw[:, query_width : query_width + HEAD_SIZE]
    key_ref[here, :] = (key_raw * cosine + turn(key_raw) * sine).astype(jnp.bfloat16)
    value_ref[here, :] = raw[:, query_width + HEAD_SIZE :].astype(jnp.bfloat16)
    query_raw = stack_heads(raw[:, :query_width])
    cosine = jnp.concatenate([cosine] * HEAD_GROUP, 0)
    sine = jnp.concatenate([sine] * HEAD_GROUP, 0)
    query = (query_raw * cosine + turn(query_raw) * sine).astype(jnp.bfloat16)
    query_ref[...] = side_heads(query)
    rows = HEAD_GROUP * block
    first = first_block(row_segments, segment_ref, step)

    def first_pass(index, top):
        there = pl.ds(pl.multiple_of(index * block, block), block)
        scores = masked_scores(
            query,
            key_ref[there, :],
            row_segments,
            segment_ref[index],
            step * block,
            index * block,
        )
        score_ref[index] = scores
        return jnp.maximum(top, lanes(scores, jnp.maximum))

    top = lax.fori_loop(
        first, step + 1, first_pass, jnp.full((rows, 128), MASK_FLOOR, jnp.float32)
    )
    top = jnp.max(top, -1, keepdims=True)

    def second_pass(index, carry):
        total, mixed = carry
        there = pl.ds(pl.multiple_of(index * block, block), block)
        weights = jnp.exp(score_ref[index] - top)
        mixed = mixed + dot(weights.astype(jnp.bfloat16), value_ref[there, :])
        return total + lanes(weights, jnp.add), mixed

    total, mixed = lax.fori_loop(
        first,
        step + 1,
        second_pass,
        (
            jnp.zeros((rows, 128), jnp.float32),
            jnp.zeros((rows, HEAD_SIZE), jnp.float32),
        ),
    )
    total = jnp.sum(total, -1, keepdims=True)
    mixed = side_heads((mixed / total).astype(jnp.bfloat16))
    mixed_ref[...] = mixed
    packed_ref[...] = jnp.concatenate([mixed[: block // 2], mixed[block // 2 :]], 1)
    log_ref[...] = (top + jnp.log(total)).reshape(HEAD_GROUP, block, 1)


def attend(gathered, gain, weights, own, block):
    tokens, features = gathered.shape[0] * own, gain.shape[0]
    query_width = HEAD_GROUP * HEAD_SIZE
    steps = tokens // block
    half = jnp.arange(HEAD_SIZE // 2, dtype=jnp.float32)
    rate = THETA ** (-(2.0 * half) / HEAD_SIZE)
    rate = jnp.concatenate([rate, rate])[None, :]
    rows = lambda width: pl.BlockSpec((block, width), lambda i: (i, 0))
    resident = lambda *shape: pl.BlockSpec(shape, lambda i: (0,) * len(shape))
    shaped = jax.ShapeDtypeStruct
    return pl.pallas_call(
        attend_kernel,
        out_shape=(
            shaped((tokens, features), jnp.bfloat16),
            shaped((tokens, query_width), jnp.bfloat16),
            shaped((tokens, HEAD_SIZE), jnp.bfloat16),
            shaped((tokens, HEAD_SIZE), jnp.bfloat16),
            shaped((tokens, query_width), jnp.bfloat16),
            shaped((tokens // 2, 2 * query_width), jnp.bfloat16),
            shaped((HEAD_GROUP, tokens, 1), jnp.float32),
            shaped((tokens, HEAD_SIZE), jnp.float32),
            shaped((tokens, HEAD_SIZE), jnp.float32),
            shaped((steps, 1, block), jnp.float32),
        ),
        grid=(steps,),
        in_specs=[
            *token_rows(block, own, features),
            whole_block(1, features),
            whole_block(*weights[0].shape),
            whole_block(*weights[1].shape),
            whole_block(1, HEAD_SIZE),
        ],
        out_specs=[
            rows(features),
            rows(query_width),
            resident(tokens, HEAD_SIZE),
            resident(tokens, HEAD_SIZE),
            rows(query_width),
            pl.BlockSpec((block // 2, 2 * query_width), lambda i: (i, 0)),
            pl.BlockSpec((HEAD_GROUP, block, 1), lambda i: (0, i, 0)),
            rows(HEAD_SIZE),
            rows(HEAD_SIZE),
            resident(steps, 1, block),
        ],
        scratch_shapes=[pltpu.VMEM((steps, HEAD_GROUP * block, block), jnp.float32)],
        compiler_params=pltpu.CompilerParams(vmem_limit_bytes=48 << 20),
        cost_estimate=pl.CostEstimate(flops=0, bytes_accessed=tokens, transcendentals=0),
    )(gathered, gathered, gain[None, :], *weights, rate)


def attend_back_kernel(
    query_ref,
    grad_ref,
    log_ref,
    cosine_ref,
    sine_ref,
    column_ref,
    segment_ref,
    key_ref,
    value_ref,
    key_cosine_ref,
    key_sine_ref,
    grad_query_ref,
    grad_pair_ref,
    probs_ref,
    grad_probs_ref,
    grad_key_ref,
    grad_value_ref,
):
    step = pl.program_id(0)
    block = query_ref.shape[0]
    rows = HEAD_GROUP * block

    @pl.when(step == 0)
    def _():
        grad_key_ref[...] = jnp.zeros_like(grad_key_ref)
        grad_value_ref[...] = jnp.zeros_like(grad_value_ref)

    query = stack_heads(query_ref[...])
    grad = stack_heads(grad_ref[...])
    log_total = log_ref[...].reshape(rows, 1)
    row_segments = flat(column_ref).astype(jnp.float32)[:, :1]
    first = first_block(row_segments, segment_ref, step)

    def first_pass(index, delta):
        there = pl.ds(pl.multiple_of(index * block, block), block)
        scores = masked_scores(
            query,
            key_ref[there, :],
            row_segments,
            segment_ref[index],
            step * block,
            index * block,
        )
        probs = jnp.exp(scores - log_total)
        grad_probs = dot(grad, value_ref[there, :], COLUMNS)
        probs_ref[index] = probs
        grad_probs_ref[index] = grad_probs
        grad_value_ref[there, :] += dot(probs.astype(jnp.bfloat16), grad, ROWS)
        return delta + lanes(probs * grad_probs, jnp.add)

    delta = lax.fori_loop(first, step + 1, first_pass, jnp.zeros((rows, 128), jnp.float32))
    delta = jnp.sum(delta, -1, keepdims=True)

    def second_pass(index, grad_query):
        there = pl.ds(pl.multiple_of(index * block, block), block)
        grad_scores = (probs_ref[index] * (grad_probs_ref[index] - delta)).astype(jnp.bfloat16)
        grad_key_ref[there, :] += dot(grad_scores, query, ROWS)
        return grad_query + dot(grad_scores, key_ref[there, :])

    grad_query = lax.fori_loop(
        first, step + 1, second_pass, jnp.zeros((rows, HEAD_SIZE), jnp.float32)
    )
    score_scale = HEAD_SIZE ** (-0.5)
    cosine = jnp.concatenate([cosine_ref[...]] * HEAD_GROUP, 0)
    sine = jnp.concatenate([sine_ref[...]] * HEAD_GROUP, 0)
    grad_query = grad_query * score_scale
    grad_query = grad_query * cosine + turn_back(grad_query * sine)
    grad_query_ref[...] = side_heads(grad_query.astype(jnp.bfloat16))

    @pl.when(step == pl.num_programs(0) - 1)
    def _():
        @pl.loop(0, pl.num_programs(0))
        def _(index):
            there = pl.ds(pl.multiple_of(index * block, block), block)
            grad_key = grad_key_ref[there, :] * score_scale
            turned = turn_back(grad_key * key_sine_ref[there, :])
            grad_key = grad_key * key_cosine_ref[there, :] + turned
            grad_pair_ref[there, :] = jnp.concatenate(
                [grad_key, grad_value_ref[there, :]], 1
            ).astype(jnp.bfloat16)


def attend_back(query, grad, log_total, cosine, sine, gathered, segments, key, value, own):
    tokens, query_width = query.shape
    steps, _, block = segments.shape
    features = gathered.shape[2] - 128
    rows = lambda width: pl.BlockSpec((block, width), lambda i: (i, 0))
    resident = lambda *shape: pl.BlockSpec(shape, lambda i: (0,) * len(shape))
    return pl.pallas_call(
        attend_back_kernel,
        out_shape=(
            jax.ShapeDtypeStruct((tokens, query_width), jnp.bfloat16),
            jax.ShapeDtypeStruct((tokens, 2 * HEAD_SIZE), jnp.bfloat16),
        ),
        grid=(steps,),
        in_specs=[
            rows(query_width),
            rows(query_width),
            pl.BlockSpec((HEAD_GROUP, block, 1), lambda i: (0, i, 0)),
            rows(HEAD_SIZE),
            rows(HEAD_SIZE),
            token_rows(block, own, features)[1],
            whole_block(steps, 1, block),
            whole_block(tokens, HEAD_SIZE),
            whole_block(tokens, HEAD_SIZE),
            whole_block(tokens, HEAD_SIZE),
            whole_block(tokens, HEAD_SIZE),
        ],
        out_specs=[rows(query_width), resident(tokens, 2 * HEAD_SIZE)],
        scratch_shapes=[
            pltpu.VMEM((steps, HEAD_GROUP * block, block), jnp.float32),
            pltpu.VMEM((steps, HEAD_GROUP * block, block), jnp.float32),
            pltpu.VMEM((tokens, HEAD_SIZE), jnp.float32),
            pltpu.VMEM((tokens, HEAD_SIZE), jnp.float32),
        ],
        compiler_params=pltpu.CompilerParams(vmem_limit_bytes=48 << 20),
        cost_estimate=pl.CostEstimate(flops=0, bytes_accessed=tokens, transcendentals=0),
    )(query, grad, log_total, cosine, sine, gathered, segments, key, value, cosine, sine)


def slot_of(e, keeps, experts_own):
    pick = experts_own // 2
    high, low = e // pick, e % pick
    return (1 - (high ^ keeps)) * pick + low


def layer_kernel(
    place_ref,
    mixed_ref,
    low_ref,
    high_ref,
    hidden_ref,
    column_ref,
    gain_ref,
    router_ref,
    cotangent_ref,
    gate_any,
    up_any,
    down_any,
    normed_ref,
    scaled_one_ref,
    scaled_two_ref,
    grad_gate_ref,
    grad_up_ref,
    grad_live_ref,
    grad_rows_ref,
    middle_own_ref,
    normed_own_ref,
    gates_own_ref,
    gate_weight_ref,
    up_weight_ref,
    down_weight_ref,
    middle_ref,
    gates_ref,
    semaphores,
):
    step = pl.program_id(0)
    block, features = cotangent_ref.shape
    own = middle_own_ref.shape[0]
    groups = mixed_ref.shape[0]
    experts_own = gate_weight_ref.shape[0]
    experts_all = router_ref.shape[1]
    copies = [
        pltpu.make_async_copy(source, target, semaphores.at[n])
        for n, (source, target) in enumerate(
            (
                (gate_any, gate_weight_ref),
                (up_any, up_weight_ref),
                (down_any, down_weight_ref),
            )
        )
    ]

    @pl.when(step == 0)
    def _():
        for copy in copies:
            copy.start()

    width = mixed_ref.shape[2] // 2
    mixed = jnp.concatenate(
        [
            jnp.concatenate([mixed_ref[g, :, side : side + width] for g in range(groups)], 1)
            for side in (0, width)
        ],
        0,
    )
    half = low_ref.shape[0]
    middle = dot(mixed[:, :half], low_ref[...]) + dot(mixed[:, half:], high_ref[...])
    middle = flat(hidden_ref).astype(jnp.float32) + middle
    middle_ref[...] = middle
    scale = lax.rsqrt(jnp.mean(middle * middle, -1, keepdims=True) + EPS)
    normed = (middle * scale * gain_ref[...]).astype(jnp.bfloat16)
    normed_ref[...] = normed
    logits = dot(normed, router_ref[...])
    columns = flat(column_ref).astype(jnp.float32)
    number = lax.broadcasted_iota(jnp.int32, logits.shape, 1)
    named = columns[:, 3:4] == number.astype(jnp.float32)
    for slot in range(1, TOPK):
        named = named | (columns[:, 3 + slot : 4 + slot] == number.astype(jnp.float32))
    logits = jnp.where(named, logits, MASK_FLOOR)
    shifted = jnp.exp(logits - jnp.max(logits, -1, keepdims=True))
    shifted = jnp.where(named, shifted, 0.0)
    gates = shifted / jnp.sum(shifted, -1, keepdims=True)
    gates_ref[...] = gates
    grad_live_ref[...] = jnp.where(
        columns[:, :1] > 0, cotangent_ref[...], jnp.zeros((), jnp.bfloat16)
    )

    @pl.when(place_ref[0] == step)
    def _():
        there = pl.ds(pl.multiple_of(lax.rem(place_ref[1], 2) * own, own), own)
        middle_own_ref[...] = middle_ref[there, :]
        normed_own_ref[...] = normed_ref[there, :]
        gates_own_ref[...] = gates_ref[there, :]

    @pl.when(step == 0)
    def _():
        for copy in copies:
            copy.wait()

    first = place_ref[1] * experts_own

    def one_expert(e, grad_gates):
        one = slot_of(e, place_ref[2], experts_own)
        two = slot_of(e, place_ref[3], experts_own)
        gates = gates_ref[...]
        gate = jnp.sum(jnp.where(number == first + e, gates, 0.0), -1, keepdims=True)
        gate_pre = dot(normed_ref[...], gate_weight_ref[e])
        up_pre = dot(normed_ref[...], up_weight_ref[e])
        grad_plain = dot(grad_live_ref[...], down_weight_ref[e], COLUMNS)
        sigma = jax.nn.sigmoid(gate_pre)
        silu = gate_pre * sigma
        acted = silu * up_pre
        grad_acted = gate * grad_plain
        scaled = (gate * acted).astype(jnp.bfloat16)
        scaled_one_ref[one] = scaled
        scaled_two_ref[two] = scaled
        grad_gate_ref[one] = (
            grad_acted * up_pre * (sigma * (1.0 + gate_pre * (1.0 - sigma)))
        ).astype(jnp.bfloat16)
        grad_up_ref[two] = (grad_acted * silu).astype(jnp.bfloat16)
        return grad_gates + jnp.where(
            number == first + e, jnp.sum(acted * grad_plain, -1, keepdims=True), 0.0
        )

    grad_gates = lax.fori_loop(
        0, experts_own, one_expert, jnp.zeros(gates.shape, jnp.float32)
    )
    one = [slot_of(e, place_ref[2], experts_own) for e in range(experts_own)]
    two = [slot_of(e, place_ref[3], experts_own) for e in range(experts_own)]
    size = 512

    @pl.loop(0, features // size)
    def _(index):
        part = pl.ds(pl.multiple_of(index * size, size), size)
        grad = 0.0
        for e in range(experts_own):
            grad = grad + dot(grad_gate_ref[one[e]], gate_weight_ref[e, part, :], COLUMNS)
            grad = grad + dot(grad_up_ref[two[e]], up_weight_ref[e, part, :], COLUMNS)
        grad_rows_ref[:, part] = grad.astype(jnp.bfloat16)

    rough = grad_gates.astype(jnp.bfloat16)
    fine = (grad_gates - rough.astype(jnp.float32)).astype(jnp.bfloat16)
    rest = jnp.zeros((block, 128 - 2 * experts_all), jnp.bfloat16)
    grad_rows_ref[:, features:] = jnp.concatenate([rough, fine, rest], 1)


def layer_rows(place, mixed, weights, gathered, gain, router, cotangent, experts, own, block):
    groups, _, width = mixed.shape
    tokens, features = cotangent.shape
    experts_all = router.shape[1]
    experts_own, _, hidden = experts[0].shape
    rows = lambda columns: pl.BlockSpec((block, columns), lambda i, p: (i, 0))
    resident = lambda *shape: pl.BlockSpec(shape, lambda i, p: (0,) * len(shape))
    spread = pl.BlockSpec((experts_own, block, hidden), lambda i, p: (0, i, 0))
    low = jnp.bfloat16
    shaped = jax.ShapeDtypeStruct
    wide = shaped((experts_own, tokens, hidden), low)
    return pl.pallas_call(
        layer_kernel,
        out_shape=(
            shaped((tokens, features), low),
            wide,
            wide,
            wide,
            wide,
            shaped((tokens, features), low),
            shaped((tokens, features + 128), low),
            shaped((own, features), jnp.float32),
            shaped((own, features), low),
            shaped((own, experts_all), jnp.float32),
        ),
        grid_spec=pltpu.PrefetchScalarGridSpec(
            num_scalar_prefetch=1,
            grid=(tokens // block,),
            in_specs=[
                pl.BlockSpec((groups, block // 2, width), lambda i, p: (0, i, 0)),
                whole_block(*weights[0].shape),
                whole_block(*weights[1].shape),
                *token_rows(block, own, features),
                whole_block(1, features),
                whole_block(features, experts_all),
                rows(features),
                *[pl.BlockSpec(memory_space=pl.ANY)] * 3,
            ],
            out_specs=[
                rows(features),
                spread,
                spread,
                spread,
                spread,
                rows(features),
                rows(features + 128),
                resident(own, features),
                resident(own, features),
                resident(own, experts_all),
            ],
            scratch_shapes=[
                *[pltpu.VMEM(array.shape, low) for array in experts],
                pltpu.VMEM((block, features), jnp.float32),
                pltpu.VMEM((block, experts_all), jnp.float32),
                pltpu.SemaphoreType.DMA((3,)),
            ],
        ),
        compiler_params=pltpu.CompilerParams(vmem_limit_bytes=58 << 20),
        cost_estimate=pl.CostEstimate(
            flops=12 * tokens * features * hidden * experts_own,
            bytes_accessed=6 * features * hidden * experts_own + 20 * tokens * features,
            transcendentals=tokens * hidden * experts_own,
        ),
    )(
        place,
        mixed,
        *weights,
        gathered,
        gathered,
        gain[None, :],
        router,
        cotangent,
        *experts,
    )


def product_kernel(
    e,
    left_any,
    gate_any,
    up_any,
    scaled_one_any,
    scaled_two_any,
    live_any,
    out_one_any,
    out_two_any,
    left_ref,
    right_ref,
    scaled_ref,
    live_ref,
    out_ref,
    came,
    gone,
):
    tiles, _, tile = left_ref.shape
    hidden = scaled_ref.shape[2]
    half = live_ref.shape[2]
    narrow = half - hidden
    top = tiles * tile
    copy = pltpu.make_async_copy
    rights = [
        copy(source.at[e], right_ref.at[:, n * hidden : (n + 1) * hidden], came.at[n])
        for n, source in enumerate((gate_any, up_any))
    ]
    lefts = [
        copy(left_any.at[:, i * tile : (i + 1) * tile], left_ref.at[i], came.at[2 + i])
        for i in range(tiles)
    ]

    def result(n, rows, place):
        target = (out_one_any, out_two_any)[n]
        return copy(out_ref.at[n, rows, :], target.at[rows, :], gone.at[place])

    def tile_rows(i):
        return pl.ds(pl.multiple_of(i * tile, tile), tile)

    downs = []
    for n, source in enumerate((scaled_one_any, scaled_two_any)):
        place = 2 + tiles + 2 * n
        downs.append(copy(source.at[e], scaled_ref.at[n], came.at[place]))
        downs.append(
            copy(
                live_any.at[:, n * half : (n + 1) * half], live_ref.at[n], came.at[place + 1]
            )
        )
    for each in rights + lefts + downs:
        each.start()
    for each in rights:
        each.wait()

    @pl.loop(0, tiles)
    def _(i):
        copy(left_any.at[:, tile_rows(i)], left_ref.at[i], came.at[2 + i]).wait()
        both = dot(left_ref[i], right_ref[...], ROWS).astype(out_ref.dtype)
        for n in range(2):
            out_ref[n, tile_rows(i), :] = both[:, n * hidden : (n + 1) * hidden]
            result(n, tile_rows(i), 2 * i + n).start()

    rest = slice(top, top + half)
    for n in range(2):
        downs[2 * n].wait()
        downs[2 * n + 1].wait()
        product = dot(scaled_ref[n], live_ref[n], ROWS).astype(out_ref.dtype)
        out_ref[n, top : top + hidden, :] = product[:, :hidden]
        out_ref[n, top + hidden : top + half, :narrow] = product[:narrow, hidden:]
        out_ref[n, top + hidden : top + half, narrow:] = product[narrow:, hidden:]
        result(n, rest, 2 * tiles + n).start()

    @pl.loop(0, tiles)
    def _(i):
        for n in range(2):
            result(n, tile_rows(i), 2 * i + n).wait()

    for n in range(2):
        result(n, rest, 2 * tiles + n).wait()


def expert_products(left, gate, up, scaled_one, scaled_two, live, e, dtype):
    tokens, features = left.shape
    hidden = gate.shape[2]
    half = features // 2
    tile = 512
    tiles = features // tile
    rows = features + half
    low = jnp.bfloat16
    anywhere = pl.BlockSpec(memory_space=pl.ANY)
    return pl.pallas_call(
        lambda *refs: product_kernel(e, *refs),
        name="expert_products",
        out_shape=(jax.ShapeDtypeStruct((rows, hidden), dtype),) * 2,
        in_specs=[anywhere] * 6,
        out_specs=[anywhere] * 2,
        scratch_shapes=[
            pltpu.VMEM((tiles, tokens, tile), low),
            pltpu.VMEM((tokens, 2 * hidden), low),
            pltpu.VMEM((2, tokens, hidden), low),
            pltpu.VMEM((2, tokens, half), low),
            pltpu.VMEM((2, rows, hidden), dtype),
            pltpu.SemaphoreType.DMA((6 + tiles,)),
            pltpu.SemaphoreType.DMA((2 * tiles + 2,)),
        ],
        compiler_params=pltpu.CompilerParams(vmem_limit_bytes=58 << 20),
        cost_estimate=pl.CostEstimate(flops=0, bytes_accessed=tokens, transcendentals=0),
    )(left, gate, up, scaled_one, scaled_two, live)


def output_kernel(place_ref, scaled_ref, down_weight_ref, out_ref):
    experts_own, _, features = down_weight_ref.shape
    size = 512

    @pl.loop(0, features // size)
    def _(index):
        part = pl.ds(pl.multiple_of(index * size, size), size)
        out = 0.0
        for e in range(experts_own):
            slot = slot_of(e, place_ref[2], experts_own)
            out = out + dot(scaled_ref[slot], down_weight_ref[e, :, part])
        out_ref[:, part] = out.astype(jnp.bfloat16)


def output_rows(place, scaled, w_down, block):
    experts_own, tokens, hidden = scaled.shape
    features = w_down.shape[2]
    return pl.pallas_call(
        output_kernel,
        out_shape=jax.ShapeDtypeStruct((tokens, features), jnp.bfloat16),
        grid_spec=pltpu.PrefetchScalarGridSpec(
            num_scalar_prefetch=1,
            grid=(tokens // block,),
            in_specs=[
                pl.BlockSpec((experts_own, block, hidden), lambda i, p: (0, i, 0)),
                whole_block(*w_down.shape),
            ],
            out_specs=pl.BlockSpec((block, features), lambda i, p: (i, 0)),
        ),
        compiler_params=pltpu.CompilerParams(vmem_limit_bytes=52 << 20),
        cost_estimate=pl.CostEstimate(flops=0, bytes_accessed=tokens, transcendentals=0),
    )(place, scaled, w_down)


def turn_kernel(
    place_ref,
    sum_ref,
    gates_ref,
    router_ref,
    gain_ref,
    middle_ref,
    live_ref,
    low_ref,
    high_ref,
    grad_middle_ref,
    branch_ref,
    mixed_ref,
    logits_ref,
    gain_grad_ref,
):
    features = middle_ref.shape[1]
    experts = gates_ref.shape[1]
    groups, _, width = mixed_ref.shape
    extra = sum_ref[:, features:].astype(jnp.float32)
    grad_gates = extra[:, :experts] + extra[:, experts : 2 * experts]
    gates = gates_ref[...]
    grad_logits = gates * (grad_gates - jnp.sum(gates * grad_gates, -1, keepdims=True))
    grad_logits = grad_logits.astype(jnp.bfloat16)
    logits_ref[...] = grad_logits
    grad = sum_ref[:, :features].astype(jnp.float32) + dot(grad_logits, router_ref[...], COLUMNS)
    middle = middle_ref[...]
    scale = lax.rsqrt(jnp.mean(middle * middle, -1, keepdims=True) + EPS)
    base = middle * scale
    gain_grad_ref[...] = jnp.sum(grad * base, 0, keepdims=True)
    grad_middle = live_ref[...].astype(jnp.float32) + norm_back(grad * gain_ref[...], base, scale)
    grad_middle_ref[...] = grad_middle
    branch = grad_middle.astype(jnp.bfloat16)
    branch_ref[...] = branch
    for half, weight_ref in enumerate((low_ref, high_ref)):
        mixed = dot(branch, weight_ref[...], COLUMNS).astype(jnp.bfloat16)
        for g in range(groups // 2):
            mixed_ref[half * (groups // 2) + g] = mixed[:, g * width : (g + 1) * width]


def turn_rows(place, sums, gates, router, gain, middle, live, weights):
    own, features = sums.shape[0], middle.shape[1]
    experts = gates.shape[1]
    groups = KEY_VALUE_HEADS
    shaped = jax.ShapeDtypeStruct
    rows = lambda width: pl.BlockSpec((own, width), lambda i, p: (p[1], 0))
    resident = lambda *shape: pl.BlockSpec(shape, lambda i, p: (0,) * len(shape))
    outs = (
        shaped((own, features), jnp.float32),
        shaped((own, features), jnp.bfloat16),
        shaped((groups, own, features // groups), jnp.bfloat16),
        shaped((own, experts), jnp.bfloat16),
        shaped((1, features), jnp.float32),
    )
    return pl.pallas_call(
        turn_kernel,
        out_shape=outs,
        grid_spec=pltpu.PrefetchScalarGridSpec(
            num_scalar_prefetch=1,
            grid=(1,),
            in_specs=[
                whole_block(*sums.shape),
                whole_block(*gates.shape),
                whole_block(*router.shape),
                whole_block(1, features),
                whole_block(*middle.shape),
                rows(features),
                whole_block(*weights[0].shape),
                whole_block(*weights[1].shape),
            ],
            out_specs=[resident(*out.shape) for out in outs],
        ),
        compiler_params=pltpu.CompilerParams(vmem_limit_bytes=58 << 20),
        cost_estimate=pl.CostEstimate(flops=0, bytes_accessed=own, transcendentals=0),
    )(place, sums, gates, router, gain[None, :], middle, live, *weights)


def close_kernel(
    reps,
    place_ref,
    query_ref,
    pair_ref,
    weight_ref,
    hidden_ref,
    normed_ref,
    gain_two_ref,
    normed_own_ref,
    logits_ref,
    rows_ref,
    mixed_ref,
    branch_ref,
    grad_ref,
    kept_one_ref,
    kept_two_ref,
    sent_one_ref,
    sent_two_ref,
    product_ref,
    gain_ref,
    out_ref,
    head_ref,
):
    step = pl.program_id(0)
    both = query_ref.shape[1] + pair_ref.shape[1]
    heads = jnp.concatenate([query_ref[...], pair_ref[...]], 1)
    grad = dot(heads, weight_ref[:, :both], COLUMNS)
    grad_ref[:, : grad.shape[1]] = grad.astype(jnp.bfloat16)
    grad_ref[:, grad.shape[1] :] = rows_ref[...]
    hidden = flat(hidden_ref).astype(jnp.float32)
    scale = lax.rsqrt(jnp.mean(hidden * hidden, -1, keepdims=True) + EPS)
    normed = normed_ref[...]

    @pl.when(step == 0)
    def _():
        gain_ref[...] = jnp.zeros_like(gain_ref)
        product_ref[...] = jnp.zeros_like(product_ref)
        out_ref[...] = jnp.zeros_like(out_ref)

    gain_ref[...] += jnp.sum(grad * (hidden * scale), 0, keepdims=True)
    product_ref[...] += dot(normed, heads, ROWS)
    out_ref[...] += dot(mixed_ref[...], branch_ref[...], ROWS)

    @pl.when(step == pl.num_programs(0) - 1)
    def _():
        features = product_ref.shape[0]
        rows = out_ref.shape[0]
        share = rows // reps
        experts = logits_ref.shape[1]
        line = kept_one_ref.shape[1]
        count = features // rows
        side = (line - features // 2) // (count // 2)
        gains = jnp.concatenate(
            [gain_ref[...], gain_two_ref[...], jnp.zeros((6, features), jnp.float32)], 0
        )
        gains = jnp.transpose(gains)
        router = dot(normed_own_ref[...], logits_ref[...], ROWS)
        rest = jnp.zeros((rows, side - both - 8 - experts), jnp.float32)
        for h in range(2):
            for c in range(count // 2):
                place = h * (count // 2) + c
                part = slice(place * rows, (place + 1) * rows)
                head_ref[h, :, c * side : (c + 1) * side] = jnp.concatenate(
                    [product_ref[part, :], gains[part], router[part], rest], 1
                )
            half = features // 2
            head_ref[h, :, count // 2 * side :] = out_ref[:, h * half : (h + 1) * half]
        sides = ((0, kept_one_ref, sent_one_ref), (1, kept_two_ref, sent_two_ref))
        for h, kept_ref, sent_ref in sides:
            bit = 1 if h == 0 else reps // 2
            for index in range(reps // 2):
                base = index // bit * 2 * bit + index % bit
                here = slice(index * share, (index + 1) * share)
                lower = head_ref[h, base * share : (base + 1) * share, :]
                upper = head_ref[h, (base + bit) * share : (base + bit + 1) * share, :]
                kept_ref[here, :] = jnp.where(place_ref[2 + h] > 0, upper, lower)
                sent_ref[here, :] = jnp.where(place_ref[2 + h] > 0, lower, upper).astype(jnp.bfloat16)


def close_rows(
    place,
    query,
    pair,
    weight,
    gathered,
    normed,
    gain_two_grad,
    normed_two,
    logits,
    out_rows,
    mixed,
    branch,
    reps,
    side,
    block,
):
    tokens, features = normed.shape
    own = logits.shape[0]
    both = query.shape[1] + pair.shape[1]
    rows_own = mixed.shape[1]
    rows = lambda width: pl.BlockSpec((block, width), lambda i, k: (i, 0))
    resident = lambda *shape: pl.BlockSpec(shape, lambda i, k: (0,) * len(shape))
    shaped = jax.ShapeDtypeStruct
    line = features // rows_own // 2 * side + features // 2
    half = (rows_own // 2, line)
    return pl.pallas_call(
        lambda *refs: close_kernel(reps, *refs),
        name="close",
        out_shape=(
            shaped((tokens, 2 * features), jnp.bfloat16),
            shaped(half, jnp.float32),
            shaped(half, jnp.float32),
            shaped(half, jnp.bfloat16),
            shaped(half, jnp.bfloat16),
        ),
        grid_spec=pltpu.PrefetchScalarGridSpec(
            num_scalar_prefetch=1,
            grid=(tokens // block,),
            in_specs=[
                rows(query.shape[1]),
                rows(pair.shape[1]),
                whole_block(*weight.shape),
                token_rows(block, own, features)[0],
                rows(features),
                whole_block(1, features),
                whole_block(own, features),
                whole_block(*logits.shape),
                rows(features),
                rows(rows_own),
                rows(features),
            ],
            out_specs=[rows(2 * features), *[resident(*half)] * 4],
            scratch_shapes=[
                pltpu.VMEM((features, both), jnp.float32),
                pltpu.VMEM((1, features), jnp.float32),
                pltpu.VMEM((rows_own, features), jnp.float32),
                pltpu.VMEM((2, rows_own, line), jnp.float32),
            ],
        ),
        compiler_params=pltpu.CompilerParams(vmem_limit_bytes=56 << 20),
        cost_estimate=pl.CostEstimate(flops=0, bytes_accessed=tokens, transcendentals=0),
    )(
        place,
        query,
        pair,
        weight,
        gathered,
        normed,
        gain_two_grad,
        normed_two,
        logits,
        out_rows,
        mixed,
        branch,
    )


def head_kernel(
    copies,
    side,
    low_ref,
    high_ref,
    query_ref,
    key_ref,
    value_ref,
    out_ref,
    gains_ref,
    router_ref,
):
    groups = KEY_VALUE_HEADS
    count = groups * copies
    halves = [low_ref[...].astype(jnp.float32), high_ref[...].astype(jnp.float32)]
    width = query_ref.shape[1] // groups
    parts = []
    for c in range(count):
        place = c % (count // 2) * side
        parts.append(halves[c // (count // 2)][:, place : place + side])
    heads = []
    small = 0.0
    for g in range(groups):
        total = parts[g * copies]
        for p in range(1, copies):
            total = total + parts[g * copies + p]
        heads.append(total)
        small = small + total[:, width + 2 * HEAD_SIZE :]
    gains_ref[...] = jnp.transpose(small[:, :8])
    router_ref[...] = small[:, 8 : 8 + router_ref.shape[1]]
    query_ref[...] = jnp.concatenate([head[:, :width] for head in heads], 1)
    key_ref[...] = jnp.concatenate([head[:, width : width + HEAD_SIZE] for head in heads], 1)
    value_ref[...] = jnp.concatenate(
        [head[:, width + HEAD_SIZE : width + 2 * HEAD_SIZE] for head in heads], 1
    )
    out_ref[...] = jnp.concatenate([half[:, count // 2 * side :] for half in halves], 1)


def head_outputs(low, high, copies, side, experts):
    rows = low.shape[0]
    groups = KEY_VALUE_HEADS
    query_width = QUERY_HEADS * HEAD_SIZE
    shaped = lambda width: jax.ShapeDtypeStruct((rows, width), jnp.float32)
    return pl.pallas_call(
        lambda *refs: head_kernel(copies, side, *refs),
        name="head_outputs",
        out_shape=(
            shaped(query_width),
            shaped(groups * HEAD_SIZE),
            shaped(groups * HEAD_SIZE),
            shaped(MODEL_WIDTH),
            jax.ShapeDtypeStruct((8, rows), jnp.float32),
            shaped(experts),
        ),
        compiler_params=pltpu.CompilerParams(vmem_limit_bytes=58 << 20),
        cost_estimate=pl.CostEstimate(flops=0, bytes_accessed=rows, transcendentals=0),
    )(low, high)


def fold_down(out_ref, value):
    hidden = out_ref.shape[0]
    narrow = hidden // 2
    out_ref[:, :hidden] = value[:hidden]
    out_ref[:narrow, hidden:] = value[hidden:, :narrow]
    out_ref[narrow:, hidden:] = value[hidden:, narrow:]


def own_kernel(flags_ref, *refs):
    down_ref = refs[6]
    for side in range(2):

        @pl.when(pl.program_id(0) == side)
        def _():
            own, came = refs[2 * side][...], refs[2 * side + 1][...]
            out_ref = refs[4 + side]
            rows = own.shape[0]
            rest = out_ref.shape[0] - rows
            late = flags_ref[2 + side] > 0
            high = jnp.where(late, own, came).astype(jnp.float32)
            out_ref[:rows, :] = jnp.where(late, came, own).astype(jnp.float32)
            out_ref[rows:, :] = high[:rest]
            fold_down(down_ref, high[rest:])


def own_outputs(flags, chains):
    rows, hidden = chains[0].own.shape
    features = 2 * rows * 2 // 3
    operands = []
    for chain in chains:
        operands += [chain.own, chain.came]
    into = lambda side: pl.BlockSpec((None, features, hidden), lambda s, k: (k[side], 0, 0))
    shaped = lambda *shape: jax.ShapeDtypeStruct((2,) + shape, jnp.float32)
    return pl.pallas_call(
        own_kernel,
        name="own_outputs",
        out_shape=(
            shaped(features, hidden),
            shaped(features, hidden),
            shaped(hidden, features),
        ),
        grid_spec=pltpu.PrefetchScalarGridSpec(
            num_scalar_prefetch=1,
            grid=(2,),
            in_specs=[whole_block(rows, hidden)] * 4,
            out_specs=[
                into(0),
                into(1),
                pl.BlockSpec((None, hidden, features // 2), lambda s, k: (k[s], 0, s)),
            ],
        ),
        compiler_params=pltpu.CompilerParams(vmem_limit_bytes=58 << 20),
        cost_estimate=pl.CostEstimate(flops=0, bytes_accessed=rows, transcendentals=0),
    )(flags, *operands)


def into_kernel(flags_ref, gate_any, up_any, *refs):
    for side in range(2):

        @pl.when(pl.program_id(0) == side)
        def _():
            first_ref, second_ref, third_ref = refs[3 * side : 3 * side + 3]
            out_ref = refs[6 + side]
            half = first_ref.shape[0]
            rest = out_ref.shape[0] - 2 * half
            out_ref[:half, :] = first_ref[...].astype(jnp.float32)
            out_ref[half : 2 * half, :] = second_ref[...].astype(jnp.float32)
            out_ref[2 * half :, :] = third_ref[:rest, :].astype(jnp.float32)


def into_outputs(flags, gate, up, pieces):
    _, features, hidden = gate.shape
    into = lambda side: pl.BlockSpec((None, features, hidden), lambda s, k: (1 - k[side], 0, 0))
    anywhere = pl.BlockSpec(memory_space=pl.ANY)
    return pl.pallas_call(
        into_kernel,
        name="into_outputs",
        out_shape=(jax.ShapeDtypeStruct(gate.shape, gate.dtype),) * 2,
        grid_spec=pltpu.PrefetchScalarGridSpec(
            num_scalar_prefetch=1,
            grid=(2,),
            in_specs=[anywhere] * 2 + [whole_block(*piece.shape) for piece in pieces],
            out_specs=[into(0), into(1)],
        ),
        input_output_aliases={1: 0, 2: 1},
        compiler_params=pltpu.CompilerParams(vmem_limit_bytes=58 << 20),
        cost_estimate=pl.CostEstimate(flops=0, bytes_accessed=features, transcendentals=0),
    )(flags, gate, up, *pieces)


def down_kernel(flags_ref, down_any, *refs):
    for side in range(2):

        @pl.when(pl.program_id(0) == side)
        def _():
            third_ref, last_ref = refs[2 * side : 2 * side + 2]
            out_ref = refs[4]
            rest = third_ref.shape[0] + last_ref.shape[0] - out_ref.shape[1]
            value = jnp.concatenate([third_ref[rest:, :], last_ref[...]], 0)
            fold_down(out_ref, value.astype(jnp.float32))


def down_outputs(flags, down, pieces):
    _, hidden, features = down.shape
    return pl.pallas_call(
        down_kernel,
        name="down_outputs",
        out_shape=jax.ShapeDtypeStruct(down.shape, down.dtype),
        grid_spec=pltpu.PrefetchScalarGridSpec(
            num_scalar_prefetch=1,
            grid=(2,),
            in_specs=[pl.BlockSpec(memory_space=pl.ANY)]
            + [whole_block(*piece.shape) for piece in pieces],
            out_specs=pl.BlockSpec(
                (None, hidden, features // 2), lambda s, k: (1 - k[s], 0, s)
            ),
        ),
        input_output_aliases={1: 0},
        compiler_params=pltpu.CompilerParams(vmem_limit_bytes=58 << 20),
        cost_estimate=pl.CostEstimate(flops=0, bytes_accessed=features, transcendentals=0),
    )(flags, down, *pieces)


def after(values, *others):
    values, _ = lax.optimization_barrier((values, others))
    return values


def swap(value, bit):
    size = lax.axis_size("rep")
    return lax.ppermute(value, "rep", [(i, i ^ bit) for i in range(size)])


def has(bit):
    return (lax.axis_index("rep") & bit) != 0


def join(value, came, bit, axis):
    upper = has(bit)
    return jnp.concatenate(
        [jnp.where(upper, came, value), jnp.where(upper, value, came)], axis
    )


class Chain:
    def __init__(self, order):
        self.order = order
        self.stage = 0
        self.steps = 2 * len(order)

    def send(self, sent):
        bit = self.order[min(self.stage, self.steps - 1 - self.stage)]
        self.sent = sent
        self.stage += 1
        if self.stage < self.steps:
            self.flying = swap(sent, bit)

    def step(self, *others):
        came = after(self.flying, *others)
        self.send(join(self.sent, came, self.order[self.steps - self.stage], 0))
        return self.sent

    def ends(self, *others):
        self.own = self.sent
        self.came = after(self.flying, *others)
        upper = has(self.order[1])
        half = self.own.shape[0] // 2
        begin, end = slice(0, half), slice(half, 2 * half)
        low = lambda rows: jnp.where(upper, self.came[rows], self.own[rows])
        high = lambda rows: jnp.where(upper, self.own[rows], self.came[rows])
        return [low(begin), low(end), high(begin), high(end)]

    def last(self, piece):
        return swap(piece, self.order[0])


def halve_kernel(keeps_ref, *refs):
    count = len(refs) // 3
    for chain in range(2):
        for place in range(0, count, 2):
            value_ref, came_ref = refs[count * chain + place : count * chain + place + 2]
            out_ref = refs[2 * count + chain * (count // 2) + place // 2]
            out_ref[...] = (value_ref[...] + came_ref[...].astype(jnp.float32)).astype(
                out_ref.dtype
            )


def halve_chains(chains, *others):
    order = [chain.order[chain.stage] for chain in chains]
    last = chains[0].stage == len(chains[0].order) - 1
    keeps = jnp.stack([has(bit) for bit in order]).astype(jnp.int32)
    rows, hidden = chains[0].kept.shape
    count = 4
    part = rows // 2 // count
    operands, specs = [], []
    for c, chain in enumerate(chains):
        chain.came = after(chain.flying, *others)
        for flip in (1,) if last else (1, 0):
            index = lambda i, k, c=c, flip=flip: ((k[c] ^ flip) * count + i, 0)
            operands += [chain.kept, chain.came]
            specs += [pl.BlockSpec((part, hidden), index)] * 2
    block = pl.BlockSpec((part, hidden), lambda i, k: (i, 0))
    shaped = lambda dtype: jax.ShapeDtypeStruct((rows // 2, hidden), dtype)
    each = [shaped(jnp.bfloat16)] if last else [shaped(jnp.bfloat16), shaped(jnp.float32)]
    outs = pl.pallas_call(
        halve_kernel,
        out_shape=each * 2,
        grid_spec=pltpu.PrefetchScalarGridSpec(
            num_scalar_prefetch=1,
            grid=(count,),
            in_specs=specs,
            out_specs=[block] * (2 * len(each)),
        ),
        compiler_params=pltpu.CompilerParams(vmem_limit_bytes=58 << 20),
        cost_estimate=pl.CostEstimate(
            flops=60000 * rows * hidden, bytes_accessed=12 * rows * hidden, transcendentals=0
        ),
    )(keeps, *operands)
    for c, chain in enumerate(chains):
        if not last:
            chain.kept = outs[2 * c + 1]
        chain.send(outs[len(each) * c])
    return [chain.sent for chain in chains]


def total_kernel(keeps_ref, *refs):
    for chain in range(2):
        kept_ref, first_ref, second_ref = refs[3 * chain : 3 * chain + 3]
        total = kept_ref[...] + first_ref[...].astype(jnp.float32)
        refs[6 + chain][...] = (total + second_ref[...].astype(jnp.float32)).astype(jnp.bfloat16)


def total_chains(chains, *others):
    keeps = jnp.stack([has(chain.order[-1]) for chain in chains]).astype(jnp.int32)
    rows, hidden = chains[0].kept.shape
    count = 4
    part = rows // 2 // count
    block = pl.BlockSpec((part, hidden), lambda i, k: (i, 0))
    operands, specs = [], []
    for c, chain in enumerate(chains):
        stay = pl.BlockSpec((part, hidden), lambda i, k, c=c: (k[c] * count + i, 0))
        operands += [chain.kept, chain.came, after(chain.flying, *others)]
        specs += [stay, stay, block]
    outs = pl.pallas_call(
        total_kernel,
        out_shape=[jax.ShapeDtypeStruct((rows // 2, hidden), jnp.bfloat16)] * 2,
        grid_spec=pltpu.PrefetchScalarGridSpec(
            num_scalar_prefetch=1, grid=(count,), in_specs=specs, out_specs=[block] * 2
        ),
        compiler_params=pltpu.CompilerParams(vmem_limit_bytes=58 << 20),
        cost_estimate=pl.CostEstimate(flops=0, bytes_accessed=rows, transcendentals=0),
    )(keeps, *operands)
    for chain, out in zip(chains, outs):
        chain.send(out)
    return list(outs)


class Cube:
    def __init__(self, kept, sent, order, share):
        shape = [2] * len(order)
        shape[len(order) - order[0].bit_length()] = 1
        self.value, sent = [array.reshape(*shape, share, -1) for array in (kept, sent)]
        self.order = order
        self.flying = swap(sent, order[0])
        self.stage = 1

    def axis(self, bit):
        return len(self.order) - bit.bit_length()

    def halve(self, *others):
        bit = self.order[self.stage]
        keep = has(bit).astype(jnp.int32)
        part = lambda index: lax.dynamic_slice_in_dim(self.value, index, 1, self.axis(bit))
        self.value, sent = part(keep), part(1 - keep).astype(jnp.bfloat16)
        self.flying = swap(after(sent, *others), bit)
        self.stage += 1
        return sent

    def add(self, *others):
        self.value = self.value + after(self.flying, *others).astype(jnp.float32)

    def back(self, *others):
        self.stage -= 1
        self.flying = swap(after(self.value, *others), self.order[self.stage])
        return self.value

    def join(self, *others):
        bit = self.order[self.stage]
        self.value = join(self.value, after(self.flying, *others), bit, self.axis(bit))


def scalar_call(kernel, outs, scalars, *operands, scratch=(), flops=0):
    whole = lambda array: pl.BlockSpec(array.shape, lambda i, p: (0,) * len(array.shape))
    return pl.pallas_call(
        kernel,
        out_shape=outs,
        grid_spec=pltpu.PrefetchScalarGridSpec(
            num_scalar_prefetch=1,
            grid=(1,),
            in_specs=[whole(array) for array in operands],
            out_specs=[whole(out) for out in outs],
            scratch_shapes=scratch,
        ),
        name="scalar_call",
        compiler_params=pltpu.CompilerParams(vmem_limit_bytes=58 << 20),
        cost_estimate=pl.CostEstimate(flops=flops, bytes_accessed=1024, transcendentals=0),
    )(scalars, *operands)


def pack_kernel(size, side, place_ref, *refs):
    chips = size // 2
    values = refs[:4]
    out_ref = refs[4 + chips]
    all_ref = refs[5 + chips]
    for h in range(2):
        total = values[2 * h][...] + values[2 * h + 1][...].astype(jnp.float32)
        total = total.astype(jnp.bfloat16)
        for c in range(chips):
            all_ref[h * chips + c] = total[:, c * side : (c + 1) * side]
        out_ref[h] = total[:, chips * side :]
    for k in range(chips):
        chip = lax.rem(place_ref[0] - k + chips, chips)
        for core in range(2):
            refs[4 + k][core] = all_ref[2 * chip + core]


def pack_heads(place, cubes, size, side):
    chips = size // 2
    share, line = cubes[0].value.shape[-2:]
    low = jnp.bfloat16
    outs = [jax.ShapeDtypeStruct((2, share, side), low)] * chips
    outs.append(jax.ShapeDtypeStruct((2, share, line - chips * side), low))
    operands = []
    for cube in cubes:
        operands += [cube.value.reshape(share, line), cube.flying.reshape(share, line)]
    *parcels, out_sums = scalar_call(
        lambda *refs: pack_kernel(size, side, *refs),
        outs,
        place,
        *operands,
        scratch=[pltpu.VMEM((size, share, side), low)],
        flops=200000000000,
    )
    return parcels, out_sums


def split_kernel(place_ref, *refs):
    chips = len(refs) - 2
    core = lax.rem(place_ref[1], 2)
    for k in range(chips):
        refs[chips][k] = refs[k][core]
        refs[chips + 1][k] = refs[k][1 - core]


def split_cores(place, got):
    out = jax.ShapeDtypeStruct((len(got),) + got[0].shape[1:], got[0].dtype)
    return scalar_call(split_kernel, [out, out], place, *got)


def unpack_kernel(place_ref, stay_ref, came_ref, out_ref, low_ref, high_ref, all_ref):
    chips, _, side = stay_ref.shape
    core = lax.rem(place_ref[1], 2)
    for k in range(chips):
        chip = lax.rem(place_ref[0] + k, chips)
        all_ref[2 * chip + core] = stay_ref[k]
        all_ref[2 * chip + 1 - core] = came_ref[k]
    for h, rows_ref in enumerate((low_ref, high_ref)):
        for c in range(chips):
            rows_ref[:, c * side : (c + 1) * side] = all_ref[h * chips + c]
        rows_ref[:, chips * side :] = out_ref[h]


def unpack_heads(place, stay, came, out_sums):
    chips, share, side = stay.shape
    line = chips * side + out_sums.shape[2]
    out = jax.ShapeDtypeStruct((share, line), stay.dtype)
    return scalar_call(
        unpack_kernel,
        [out, out],
        place,
        stay,
        came,
        out_sums,
        scratch=[pltpu.VMEM((2 * chips, share, side), stay.dtype)],
    )


class Exchange:
    def __init__(self, fetched, bits):
        size = fetched.shape[0]
        fetched = fetched.reshape((size,) + (1,) * len(bits) + fetched.shape[1:])
        self.values = [fetched[: size // 2], fetched[size // 2 :]]
        self.orders = (bits, bits[::-1])
        self.stage = 0
        self.fly()

    def fly(self):
        self.flying = [
            swap(value, order[self.stage]) for value, order in zip(self.values, self.orders)
        ]

    def step(self, *others):
        bits = len(self.orders[0])
        for h, order in enumerate(self.orders):
            bit = order[self.stage]
            came = after(self.flying[h], *others)
            self.values[h] = join(self.values[h], came, bit, bits - (bit.bit_length() - 1))
        self.stage += 1
        if self.stage < bits:
            self.fly()
        return list(self.values)

    def finish(self, *others):
        while self.stage < len(self.orders[0]):
            self.step(*others)
        return [value.reshape(-1, value.shape[-1]) for value in self.values]


def per_device(
    inputs,
    segments,
    positions,
    expert_ids,
    attn_gain,
    w_query,
    key_weight,
    value_weight,
    w_out,
    ffn_gain,
    router,
    w_gate,
    w_up,
    w_down,
    grad_out,
):
    size = lax.axis_size("ctx")
    me = lax.axis_index("ctx")
    reps = lax.axis_size("rep")
    bits = [1 << i for i in range(reps.bit_length() - 1)]
    own = inputs.shape[1]
    tokens = size * own
    groups = KEY_VALUE_HEADS
    copies = size // groups
    query_width = HEAD_GROUP * HEAD_SIZE
    width = query_width + 2 * HEAD_SIZE
    copy_index = me % copies
    rows_own = w_out.shape[0]
    experts_own = w_gate.shape[0]
    experts_all = size * experts_own
    block = 2 * own
    chips = size // 2
    chip = me // 2
    odd = me % 2 == 1
    share = rows_own // reps
    share_start = lax.axis_index("rep") * share

    columns = jnp.concatenate(
        [
            segments[0][:, None],
            positions[0][:, None] // 64,
            positions[0][:, None] % 64,
            expert_ids[0],
        ],
        1,
    ).astype(jnp.bfloat16)
    columns = jnp.pad(columns, ((0, 0), (0, 128 - columns.shape[1])))
    shared = lambda array: lax.dynamic_slice_in_dim(array, share_start, share, 0)

    rows = jnp.concatenate(
        [
            jnp.concatenate([inputs[0], columns], 1),
            jnp.pad(shared(w_out), ((0, 0), (0, 128))),
        ],
        0,
    )
    gathered = lax.all_gather(rows, "ctx", axis=0)
    cotangent = lax.all_gather(after(grad_out[0], rows), "ctx", axis=0, tiled=True)

    def from_chip(value, k):
        return lax.ppermute(value, "ctx", [(i, (i - 2 * k) % size) for i in range(size)])

    def from_core(value):
        return lax.ppermute(value, "ctx", [(i, i ^ 1) for i in range(size)])

    def cores(mine, others, axis):
        return jnp.concatenate(
            [jnp.where(odd, others, mine), jnp.where(odd, mine, others)], axis
        )

    side_width = -(-(width + 2 + router.shape[1]) // 128) * 128
    head_columns = jnp.concatenate(
        [
            shared(w_query).reshape(share, groups, query_width),
            shared(key_weight).reshape(share, groups, HEAD_SIZE),
            shared(value_weight).reshape(share, groups, HEAD_SIZE),
            jnp.broadcast_to(shared(attn_gain)[:, None, None], (share, groups, 1)),
            jnp.broadcast_to(shared(ffn_gain)[:, None, None], (share, groups, 1)),
            jnp.broadcast_to(shared(router)[:, None, :], (share, groups, router.shape[1])),
        ],
        -1,
    )
    used = head_columns.shape[-1]
    head_columns = jnp.pad(head_columns, ((0, 0), (0, 0), (0, side_width - used)))
    head_columns = jnp.repeat(jnp.transpose(head_columns, (1, 0, 2)), copies, 0)
    head_columns = lax.all_to_all(head_columns, "ctx", split_axis=0, concat_axis=0, tiled=True)
    head_halves = Exchange(head_columns, bits).finish()
    head_all = jnp.concatenate(head_halves, 0)
    gain_one = head_all[:, width].astype(jnp.float32)
    gain_two = head_all[:, width + 1].astype(jnp.float32)
    router_all = head_all[:, width + 2 : used]

    (
        normed_one,
        query,
        key,
        value,
        mixed,
        packed,
        log_total,
        cosine_table,
        sine_table,
        segment_rows,
    ) = attend(gathered, gain_one, head_halves, own, block)
    out_exchange = Exchange(gathered[:, own:, :MODEL_WIDTH], bits)

    part = tokens // copies
    mixed_all = lax.all_gather(
        after(
            lax.dynamic_slice_in_dim(packed, copy_index * part // 2, part // 2, 0),
            cotangent,
            out_exchange.step(),
        ),
        "ctx",
        axis=0,
    ).reshape(groups, tokens // 2, 2 * query_width)
    w_out_halves = out_exchange.finish()

    flag = lambda bit: has(bit).astype(jnp.int32)
    place = jnp.stack([chip, me, flag(bits[0]), flag(bits[-1])]).astype(jnp.int32)
    (
        normed_two,
        scaled_one,
        scaled_two,
        grad_gate_pre,
        grad_up_pre,
        grad_live,
        grad_rows,
        middle_own,
        normed_own,
        gates_own,
    ) = layer_rows(
        place,
        mixed_all,
        w_out_halves,
        gathered,
        gain_two,
        router_all,
        cotangent,
        (w_gate, w_up, w_down),
        own,
        block,
    )

    products = lambda e, dtype: expert_products(
        normed_two, grad_gate_pre, grad_up_pre, scaled_one, scaled_two, grad_live, e, dtype
    )
    grad_two_sum = lax.psum_scatter(grad_rows, "ctx", scatter_dimension=0, tiled=True)
    normed_two, grad_live = after((normed_two, grad_live), grad_rows)
    chains = [Chain(bits), Chain(bits[::-1])]
    for chain, sent in zip(chains, products(0, jnp.bfloat16)):
        chain.send(sent)
    normed_two, grad_live = after((normed_two, grad_live), *[chain.sent for chain in chains])
    for chain, kept in zip(chains, products(1, jnp.float32)):
        chain.kept = kept
    out_rows = output_rows(place, after(scaled_one, *[c.kept for c in chains]), w_down, block)

    grad_middle, grad_branch, grad_mixed, grad_logits, gain_two_grad = turn_rows(
        place,
        after(grad_two_sum, out_rows),
        gates_own,
        router_all,
        gain_two,
        middle_own,
        grad_live,
        w_out_halves,
    )
    grad_branch_all = lax.all_gather(grad_branch, "ctx", axis=0, tiled=True)

    def deal_chips(blocks):
        blocks = blocks.reshape((chips, 2) + blocks.shape[1:])
        got = [blocks[(chip - k) % chips] for k in range(chips)]
        return jnp.stack([got[0]] + [from_chip(got[k], k) for k in range(1, chips)])

    def deal_cores(got):
        stay = jnp.where(odd, got[:, 1], got[:, 0])
        go = from_core(jnp.where(odd, got[:, 0], got[:, 1]))
        both = cores(stay[:, None], go[:, None], 1)
        both = jnp.concatenate([both, both], 0)
        both = lax.dynamic_slice_in_dim(both, (chips - chip) % chips, chips, 0)
        return both.reshape((size,) + both.shape[2:])

    got = deal_chips(jnp.repeat(grad_mixed, copies, 0))
    sent = [got]
    while chains[0].stage < len(bits):
        sent = halve_chains(chains, *sent)
    grad_mixed_all = deal_cores(after(got, *sent)).reshape(tokens, query_width)
    grad_query, grad_pair = attend_back(
        query,
        grad_mixed_all,
        log_total,
        cosine_table,
        sine_table,
        gathered,
        segment_rows,
        key,
        value,
        own,
    )
    if copies > 1:
        places = jnp.arange(tokens, dtype=jnp.int32)
        counted = (places // part == copy_index)[:, None]
        grad_query = jnp.where(counted, grad_query, jnp.zeros((), jnp.bfloat16))
        grad_pair = jnp.where(counted, grad_pair, jnp.zeros((), jnp.bfloat16))
    sent = total_chains(chains, grad_pair)
    both_rows, *halves = close_rows(
        place,
        after(grad_query, *sent),
        grad_pair,
        head_all,
        gathered,
        normed_one,
        gain_two_grad,
        normed_own,
        grad_logits,
        out_rows,
        lax.dynamic_slice_in_dim(mixed, copy_index * rows_own, rows_own, 1),
        grad_branch_all,
        reps,
        side_width,
        block,
    )
    both_sums = lax.psum_scatter(
        both_rows, "ctx", scatter_dimension=0, tiled=True
    ).astype(jnp.float32)
    grad_one, out_sum = both_sums[:, :MODEL_WIDTH], both_sums[:, MODEL_WIDTH:]

    line = size // 2 * side_width
    cubes = [
        Cube(halves[h], halves[2 + h], order, share)
        for h, order in enumerate((bits, bits[::-1]))
    ]
    while chains[0].stage < chains[0].steps - 1:
        sent = [chain.step(*halves) for chain in chains]
    pieces = [chain.ends(*halves) for chain in chains]
    sent = [part[0] for part in pieces]
    while cubes[0].stage < len(bits):
        flying = after([cube.flying for cube in cubes], *sent)
        for cube, arrived in zip(cubes, flying):
            cube.flying = arrived
            cube.add()
        sent = [cube.halve() for cube in cubes]
    first = [chain.last(part[0]) for chain, part in zip(chains, pieces)]
    second = [chain.last(after(part[1], *sent)) for chain, part in zip(chains, pieces)]
    flags = jnp.stack([flag(chain.order[n]) for n in range(2) for chain in chains])
    for chain in chains:
        chain.own, chain.came = after((chain.own, chain.came), *sent)
    grad_gate, grad_up, grad_down = own_outputs(flags, chains)
    for cube in cubes:
        cube.flying = after(cube.flying, grad_gate, grad_up, grad_down)
    parcels, out_sums = pack_heads(place, cubes, size, side_width)
    parcels = after(parcels, *first)
    got = [parcels[0]] + [from_chip(parcels[k], k) for k in range(1, chips)]
    stay, go = split_cores(place, got)
    came = from_core(after(go, *second))
    third = [chain.last(after(part[2], *second)) for chain, part in zip(chains, pieces)]
    for cube, value in zip(cubes, unpack_heads(place, stay, came, out_sums)):
        cube.value = value.reshape((1,) * len(bits) + value.shape)
    sent = [cube.back() for cube in cubes]
    fourth = [chain.last(after(part[3], *third)) for chain, part in zip(chains, pieces)]
    while cubes[0].stage > 0:
        for cube in cubes:
            cube.join(*third)
        sent = [cube.back() for cube in cubes]
    arrived = []
    for side in range(2):
        arrived += [first[side], second[side], third[side]]
    grad_gate, grad_up = into_outputs(flags, grad_gate, grad_up, after(arrived, *sent))
    output = jnp.where((segments[0] != 0)[:, None], middle_own + out_sum, 0.0)
    own_hidden = inputs[0].astype(jnp.float32)
    own_scale = lax.rsqrt(jnp.mean(own_hidden * own_hidden, -1, keepdims=True) + EPS)
    grad_in = grad_middle + norm_back(grad_one * gain_one, own_hidden * own_scale, own_scale)
    for cube in cubes:
        cube.join(grad_gate, grad_up, output, grad_in)
    head_outs = head_outputs(
        *[cube.value.reshape(rows_own, -1) for cube in cubes], copies, side_width, experts_all
    )
    arrived = []
    for side in range(2):
        arrived += [third[side], fourth[side]]
    grad_down = down_outputs(flags, grad_down, after(arrived, head_outs))

    return (
        output.astype(jnp.bfloat16)[None],
        grad_in[None],
        head_outs[4][0],
        *head_outs[:4],
        head_outs[4][1],
        head_outs[5],
        grad_gate,
        grad_up,
        grad_down,
    )


def solution(mesh):
    return jax.shard_map(
        per_device,
        mesh=mesh,
        in_specs=(
            P("rep", "ctx", None),
            P("rep", "ctx"),
            P("rep", "ctx"),
            P("rep", "ctx", None),
            P("ctx"),
            P("ctx", None),
            P("ctx", None),
            P("ctx", None),
            P("ctx", None),
            P("ctx"),
            P("ctx", None),
            P("ctx", None, None),
            P("ctx", None, None),
            P("ctx", None, None),
            P("rep", "ctx", None),
        ),
        out_specs=(
            P("rep", "ctx", None),
            P("rep", "ctx", None),
            P("ctx"),
            P("ctx", None),
            P("ctx", None),
            P("ctx", None),
            P("ctx", None),
            P("ctx"),
            P("ctx", None),
            P("ctx", None, None),
            P("ctx", None, None),
            P("ctx", None, None),
        ),
        check_vma=False,
    )
```

```python
import jax
import jax.numpy as jnp
from jax import lax
from jax.experimental import pallas as pl
from jax.experimental.pallas import tpu as pltpu
from jax.sharding import PartitionSpec as P

MODEL_WIDTH = 1536
QUERY_HEADS = 24
KEY_VALUE_HEADS = 8
HEAD_GROUP = QUERY_HEADS // KEY_VALUE_HEADS
HEAD_SIZE = 64
TOPK = 8

EPS = 1e-06
THETA = 10000.0
MASK_FLOOR = -1e30

ROWS = (((0,), (0,)), ((), ()))
COLUMNS = (((1,), (1,)), ((), ()))


def dot(left, right, contract=(((1,), (0,)), ((), ()))):
    return lax.dot_general(left, right, contract, preferred_element_type=jnp.float32)


def norm_back(grad_base, base, scale):
    return scale * (grad_base - base * jnp.mean(grad_base * base, -1, keepdims=True))


def turn(rows):
    half = HEAD_SIZE // 2
    return jnp.concatenate([-rows[:, half:], rows[:, :half]], 1)


def turn_back(rows):
    half = HEAD_SIZE // 2
    return jnp.concatenate([rows[:, half:], -rows[:, :half]], 1)


def stack_heads(rows):
    return jnp.concatenate(
        [rows[:, h * HEAD_SIZE : (h + 1) * HEAD_SIZE] for h in range(HEAD_GROUP)], 0
    )


def side_heads(rows):
    block = rows.shape[0] // HEAD_GROUP
    return jnp.concatenate([rows[h * block : (h + 1) * block] for h in range(HEAD_GROUP)], 1)


def lanes(values, combine):
    total = values[:, :128]
    for start in range(128, values.shape[1], 128):
        total = combine(total, values[:, start : start + 128])
    return total


def masked_scores(stacked, keys, row_segments, key_segments, row_start, key_start):
    block = row_segments.shape[0]
    scores = dot(stacked, keys, COLUMNS) * HEAD_SIZE ** (-0.5)
    row_place = row_start + lax.broadcasted_iota(jnp.int32, (block, block), 0)
    key_place = key_start + lax.broadcasted_iota(jnp.int32, (block, block), 1)
    allowed = (row_segments == key_segments) & (key_place <= row_place)
    scores = scores.reshape(HEAD_GROUP, block, block)
    return jnp.where(allowed[None], scores, MASK_FLOOR).reshape(HEAD_GROUP * block, block)


def first_block(row_segments, segment_ref, step):
    here = jnp.max(row_segments[:1, :1])
    segments = segment_ref[...]
    number = lax.broadcasted_iota(jnp.int32, segments.shape, 0)
    return jnp.min(jnp.where((segments == here) & (number <= step), number, step))


def token_rows(block, own, features):
    count = block // own
    return (
        pl.BlockSpec((count, own, features), lambda i, *_: (i, 0, 0)),
        pl.BlockSpec((count, own, 128), lambda i, *_: (i, 0, features // 128)),
    )


def flat(ref):
    return ref[...].reshape(-1, ref.shape[-1])


def whole_block(*shape):
    return pl.BlockSpec(shape, lambda *i: (0,) * len(shape), pipeline_mode=pl.Buffered(1))


def attend_kernel(
    hidden_ref,
    column_ref,
    gain_ref,
    low_ref,
    high_ref,
    rate_ref,
    normed_ref,
    query_ref,
    key_ref,
    value_ref,
    mixed_ref,
    packed_ref,
    log_ref,
    cosine_ref,
    sine_ref,
    segment_ref,
    score_ref,
):
    step = pl.program_id(0)
    block = query_ref.shape[0]
    query_width = query_ref.shape[1]
    width = query_width + 2 * HEAD_SIZE
    here = pl.ds(pl.multiple_of(step * block, block), block)
    columns = flat(column_ref).astype(jnp.float32)
    row_segments = columns[:, :1]
    segment_ref[step] = jnp.transpose(columns)[:1, :]
    angles = (columns[:, 1:2] * 64.0 + columns[:, 2:3]) * rate_ref[...]
    cosine = jnp.cos(angles)
    sine = jnp.sin(angles)
    cosine_ref[...] = cosine
    sine_ref[...] = sine
    hidden = flat(hidden_ref).astype(jnp.float32)
    scale = lax.rsqrt(jnp.mean(hidden * hidden, -1, keepdims=True) + EPS)
    normed = (hidden * scale * gain_ref[...]).astype(jnp.bfloat16)
    normed_ref[...] = normed
    middle = low_ref.shape[0]
    raw = dot(normed[:, :middle], low_ref[:, :width]) + dot(
        normed[:, middle:], high_ref[:, :width]
    )
    key_raw = raw[:, query_width : query_width + HEAD_SIZE]
    key_ref[here, :] = (key_raw * cosine + turn(key_raw) * sine).astype(jnp.bfloat16)
    value_ref[here, :] = raw[:, query_width + HEAD_SIZE :].astype(jnp.bfloat16)
    query_raw = stack_heads(raw[:, :query_width])
    cosine = jnp.concatenate([cosine] * HEAD_GROUP, 0)
    sine = jnp.concatenate([sine] * HEAD_GROUP, 0)
    query = (query_raw * cosine + turn(query_raw) * sine).astype(jnp.bfloat16)
    query_ref[...] = side_heads(query)
    rows = HEAD_GROUP * block
    first = first_block(row_segments, segment_ref, step)

    def first_pass(index, top):
        there = pl.ds(pl.multiple_of(index * block, block), block)
        scores = masked_scores(
            query,
            key_ref[there, :],
            row_segments,
            segment_ref[index],
            step * block,
            index * block,
        )
        score_ref[index] = scores
        return jnp.maximum(top, lanes(scores, jnp.maximum))

    top = lax.fori_loop(
        first, step + 1, first_pass, jnp.full((rows, 128), MASK_FLOOR, jnp.float32)
    )
    top = jnp.max(top, -1, keepdims=True)

    def second_pass(index, carry):
        total, mixed = carry
        there = pl.ds(pl.multiple_of(index * block, block), block)
        weights = jnp.exp(score_ref[index] - top)
        mixed = mixed + dot(weights.astype(jnp.bfloat16), value_ref[there, :])
        return total + lanes(weights, jnp.add), mixed

    total, mixed = lax.fori_loop(
        first,
        step + 1,
        second_pass,
        (
            jnp.zeros((rows, 128), jnp.float32),
            jnp.zeros((rows, HEAD_SIZE), jnp.float32),
        ),
    )
    total = jnp.sum(total, -1, keepdims=True)
    mixed = side_heads((mixed / total).astype(jnp.bfloat16))
    mixed_ref[...] = mixed
    packed_ref[...] = jnp.concatenate([mixed[: block // 2], mixed[block // 2 :]], 1)
    log_ref[...] = (top + jnp.log(total)).reshape(HEAD_GROUP, block, 1)


def attend(gathered, gain, weights, own, block):
    tokens, features = gathered.shape[0] * own, gain.shape[0]
    query_width = HEAD_GROUP * HEAD_SIZE
    steps = tokens // block
    half = jnp.arange(HEAD_SIZE // 2, dtype=jnp.float32)
    rate = THETA ** (-(2.0 * half) / HEAD_SIZE)
    rate = jnp.concatenate([rate, rate])[None, :]
    rows = lambda width: pl.BlockSpec((block, width), lambda i: (i, 0))
    resident = lambda *shape: pl.BlockSpec(shape, lambda i: (0,) * len(shape))
    shaped = jax.ShapeDtypeStruct
    return pl.pallas_call(
        attend_kernel,
        out_shape=(
            shaped((tokens, features), jnp.bfloat16),
            shaped((tokens, query_width), jnp.bfloat16),
            shaped((tokens, HEAD_SIZE), jnp.bfloat16),
            shaped((tokens, HEAD_SIZE), jnp.bfloat16),
            shaped((tokens, query_width), jnp.bfloat16),
            shaped((tokens // 2, 2 * query_width), jnp.bfloat16),
            shaped((HEAD_GROUP, tokens, 1), jnp.float32),
            shaped((tokens, HEAD_SIZE), jnp.float32),
            shaped((tokens, HEAD_SIZE), jnp.float32),
            shaped((steps, 1, block), jnp.float32),
        ),
        grid=(steps,),
        in_specs=[
            *token_rows(block, own, features),
            whole_block(1, features),
            whole_block(*weights[0].shape),
            whole_block(*weights[1].shape),
            whole_block(1, HEAD_SIZE),
        ],
        out_specs=[
            rows(features),
            rows(query_width),
            resident(tokens, HEAD_SIZE),
            resident(tokens, HEAD_SIZE),
            rows(query_width),
            pl.BlockSpec((block // 2, 2 * query_width), lambda i: (i, 0)),
            pl.BlockSpec((HEAD_GROUP, block, 1), lambda i: (0, i, 0)),
            rows(HEAD_SIZE),
            rows(HEAD_SIZE),
            resident(steps, 1, block),
        ],
        scratch_shapes=[pltpu.VMEM((steps, HEAD_GROUP * block, block), jnp.float32)],
        compiler_params=pltpu.CompilerParams(vmem_limit_bytes=48 << 20),
        cost_estimate=pl.CostEstimate(flops=0, bytes_accessed=tokens, transcendentals=0),
    )(gathered, gathered, gain[None, :], *weights, rate)


def attend_back_kernel(
    query_ref,
    grad_ref,
    log_ref,
    cosine_ref,
    sine_ref,
    column_ref,
    segment_ref,
    key_ref,
    value_ref,
    key_cosine_ref,
    key_sine_ref,
    grad_query_ref,
    grad_pair_ref,
    probs_ref,
    grad_probs_ref,
    grad_key_ref,
    grad_value_ref,
):
    step = pl.program_id(0)
    block = query_ref.shape[0]
    rows = HEAD_GROUP * block

    @pl.when(step == 0)
    def _():
        grad_key_ref[...] = jnp.zeros_like(grad_key_ref)
        grad_value_ref[...] = jnp.zeros_like(grad_value_ref)

    query = stack_heads(query_ref[...])
    grad = stack_heads(grad_ref[...])
    log_total = log_ref[...].reshape(rows, 1)
    row_segments = flat(column_ref).astype(jnp.float32)[:, :1]
    first = first_block(row_segments, segment_ref, step)

    def first_pass(index, delta):
        there = pl.ds(pl.multiple_of(index * block, block), block)
        scores = masked_scores(
            query,
            key_ref[there, :],
            row_segments,
            segment_ref[index],
            step * block,
            index * block,
        )
        probs = jnp.exp(scores - log_total)
        grad_probs = dot(grad, value_ref[there, :], COLUMNS)
        probs_ref[index] = probs
        grad_probs_ref[index] = grad_probs
        grad_value_ref[there, :] += dot(probs.astype(jnp.bfloat16), grad, ROWS)
        return delta + lanes(probs * grad_probs, jnp.add)

    delta = lax.fori_loop(first, step + 1, first_pass, jnp.zeros((rows, 128), jnp.float32))
    delta = jnp.sum(delta, -1, keepdims=True)

    def second_pass(index, grad_query):
        there = pl.ds(pl.multiple_of(index * block, block), block)
        grad_scores = (probs_ref[index] * (grad_probs_ref[index] - delta)).astype(jnp.bfloat16)
        grad_key_ref[there, :] += dot(grad_scores, query, ROWS)
        return grad_query + dot(grad_scores, key_ref[there, :])

    grad_query = lax.fori_loop(
        first, step + 1, second_pass, jnp.zeros((rows, HEAD_SIZE), jnp.float32)
    )
    score_scale = HEAD_SIZE ** (-0.5)
    cosine = jnp.concatenate([cosine_ref[...]] * HEAD_GROUP, 0)
    sine = jnp.concatenate([sine_ref[...]] * HEAD_GROUP, 0)
    grad_query = grad_query * score_scale
    grad_query = grad_query * cosine + turn_back(grad_query * sine)
    grad_query_ref[...] = side_heads(grad_query.astype(jnp.bfloat16))

    @pl.when(step == pl.num_programs(0) - 1)
    def _():
        @pl.loop(0, pl.num_programs(0))
        def _(index):
            there = pl.ds(pl.multiple_of(index * block, block), block)
            grad_key = grad_key_ref[there, :] * score_scale
            turned = turn_back(grad_key * key_sine_ref[there, :])
            grad_key = grad_key * key_cosine_ref[there, :] + turned
            grad_pair_ref[there, :] = jnp.concatenate(
                [grad_key, grad_value_ref[there, :]], 1
            ).astype(jnp.bfloat16)


def attend_back(query, grad, log_total, cosine, sine, gathered, segments, key, value, own):
    tokens, query_width = query.shape
    steps, _, block = segments.shape
    features = gathered.shape[2] - 128
    rows = lambda width: pl.BlockSpec((block, width), lambda i: (i, 0))
    resident = lambda *shape: pl.BlockSpec(shape, lambda i: (0,) * len(shape))
    return pl.pallas_call(
        attend_back_kernel,
        out_shape=(
            jax.ShapeDtypeStruct((tokens, query_width), jnp.bfloat16),
            jax.ShapeDtypeStruct((tokens, 2 * HEAD_SIZE), jnp.bfloat16),
        ),
        grid=(steps,),
        in_specs=[
            rows(query_width),
            rows(query_width),
            pl.BlockSpec((HEAD_GROUP, block, 1), lambda i: (0, i, 0)),
            rows(HEAD_SIZE),
            rows(HEAD_SIZE),
            token_rows(block, own, features)[1],
            whole_block(steps, 1, block),
            whole_block(tokens, HEAD_SIZE),
            whole_block(tokens, HEAD_SIZE),
            whole_block(tokens, HEAD_SIZE),
            whole_block(tokens, HEAD_SIZE),
        ],
        out_specs=[rows(query_width), resident(tokens, 2 * HEAD_SIZE)],
        scratch_shapes=[
            pltpu.VMEM((steps, HEAD_GROUP * block, block), jnp.float32),
            pltpu.VMEM((steps, HEAD_GROUP * block, block), jnp.float32),
            pltpu.VMEM((tokens, HEAD_SIZE), jnp.float32),
            pltpu.VMEM((tokens, HEAD_SIZE), jnp.float32),
        ],
        compiler_params=pltpu.CompilerParams(vmem_limit_bytes=48 << 20),
        cost_estimate=pl.CostEstimate(flops=0, bytes_accessed=tokens, transcendentals=0),
    )(query, grad, log_total, cosine, sine, gathered, segments, key, value, cosine, sine)


def slot_of(e, keeps, experts_own):
    pick = experts_own // 2
    high, low = e // pick, e % pick
    return (1 - (high ^ keeps)) * pick + low


def layer_kernel(
    place_ref,
    mixed_ref,
    low_ref,
    high_ref,
    hidden_ref,
    column_ref,
    gain_ref,
    router_ref,
    cotangent_ref,
    gate_any,
    up_any,
    down_any,
    normed_ref,
    scaled_one_ref,
    scaled_two_ref,
    grad_gate_ref,
    grad_up_ref,
    grad_live_ref,
    grad_rows_ref,
    middle_own_ref,
    normed_own_ref,
    gates_own_ref,
    gate_weight_ref,
    up_weight_ref,
    down_weight_ref,
    middle_ref,
    gates_ref,
    semaphores,
):
    step = pl.program_id(0)
    block, features = cotangent_ref.shape
    own = middle_own_ref.shape[0]
    groups = mixed_ref.shape[0]
    experts_own = gate_weight_ref.shape[0]
    experts_all = router_ref.shape[1]
    copies = [
        pltpu.make_async_copy(source, target, semaphores.at[n])
        for n, (source, target) in enumerate(
            (
                (gate_any, gate_weight_ref),
                (up_any, up_weight_ref),
                (down_any, down_weight_ref),
            )
        )
    ]

    @pl.when(step == 0)
    def _():
        for copy in copies:
            copy.start()

    width = mixed_ref.shape[2] // 2
    mixed = jnp.concatenate(
        [
            jnp.concatenate([mixed_ref[g, :, side : side + width] for g in range(groups)], 1)
            for side in (0, width)
        ],
        0,
    )
    half = low_ref.shape[0]
    middle = dot(mixed[:, :half], low_ref[...]) + dot(mixed[:, half:], high_ref[...])
    middle = flat(hidden_ref).astype(jnp.float32) + middle
    middle_ref[...] = middle
    scale = lax.rsqrt(jnp.mean(middle * middle, -1, keepdims=True) + EPS)
    normed = (middle * scale * gain_ref[...]).astype(jnp.bfloat16)
    normed_ref[...] = normed
    logits = dot(normed, router_ref[...])
    columns = flat(column_ref).astype(jnp.float32)
    number = lax.broadcasted_iota(jnp.int32, logits.shape, 1)
    named = columns[:, 3:4] == number.astype(jnp.float32)
    for slot in range(1, TOPK):
        named = named | (columns[:, 3 + slot : 4 + slot] == number.astype(jnp.float32))
    logits = jnp.where(named, logits, MASK_FLOOR)
    shifted = jnp.exp(logits - jnp.max(logits, -1, keepdims=True))
    shifted = jnp.where(named, shifted, 0.0)
    gates = shifted / jnp.sum(shifted, -1, keepdims=True)
    gates_ref[...] = gates
    grad_live_ref[...] = jnp.where(
        columns[:, :1] > 0, cotangent_ref[...], jnp.zeros((), jnp.bfloat16)
    )

    @pl.when(place_ref[0] == step)
    def _():
        there = pl.ds(pl.multiple_of(lax.rem(place_ref[1], 2) * own, own), own)
        middle_own_ref[...] = middle_ref[there, :]
        normed_own_ref[...] = normed_ref[there, :]
        gates_own_ref[...] = gates_ref[there, :]

    @pl.when(step == 0)
    def _():
        for copy in copies:
            copy.wait()

    first = place_ref[1] * experts_own

    def one_expert(e, grad_gates):
        one = slot_of(e, place_ref[2], experts_own)
        two = slot_of(e, place_ref[3], experts_own)
        gates = gates_ref[...]
        gate = jnp.sum(jnp.where(number == first + e, gates, 0.0), -1, keepdims=True)
        gate_pre = dot(normed_ref[...], gate_weight_ref[e])
        up_pre = dot(normed_ref[...], up_weight_ref[e])
        grad_plain = dot(grad_live_ref[...], down_weight_ref[e], COLUMNS)
        sigma = jax.nn.sigmoid(gate_pre)
        silu = gate_pre * sigma
        acted = silu * up_pre
        grad_acted = gate * grad_plain
        scaled = (gate * acted).astype(jnp.bfloat16)
        scaled_one_ref[one] = scaled
        scaled_two_ref[two] = scaled
        grad_gate_ref[one] = (
            grad_acted * up_pre * (sigma * (1.0 + gate_pre * (1.0 - sigma)))
        ).astype(jnp.bfloat16)
        grad_up_ref[two] = (grad_acted * silu).astype(jnp.bfloat16)
        return grad_gates + jnp.where(
            number == first + e, jnp.sum(acted * grad_plain, -1, keepdims=True), 0.0
        )

    grad_gates = lax.fori_loop(
        0, experts_own, one_expert, jnp.zeros(gates.shape, jnp.float32)
    )
    one = [slot_of(e, place_ref[2], experts_own) for e in range(experts_own)]
    two = [slot_of(e, place_ref[3], experts_own) for e in range(experts_own)]
    size = 512

    @pl.loop(0, features // size)
    def _(index):
        part = pl.ds(pl.multiple_of(index * size, size), size)
        grad = 0.0
        for e in range(experts_own):
            grad = grad + dot(grad_gate_ref[one[e]], gate_weight_ref[e, part, :], COLUMNS)
            grad = grad + dot(grad_up_ref[two[e]], up_weight_ref[e, part, :], COLUMNS)
        grad_rows_ref[:, part] = grad.astype(jnp.bfloat16)

    rough = grad_gates.astype(jnp.bfloat16)
    fine = (grad_gates - rough.astype(jnp.float32)).astype(jnp.bfloat16)
    rest = jnp.zeros((block, 128 - 2 * experts_all), jnp.bfloat16)
    grad_rows_ref[:, features:] = jnp.concatenate([rough, fine, rest], 1)


def layer_rows(place, mixed, weights, gathered, gain, router, cotangent, experts, own, block):
    groups, _, width = mixed.shape
    tokens, features = cotangent.shape
    experts_all = router.shape[1]
    experts_own, _, hidden = experts[0].shape
    rows = lambda columns: pl.BlockSpec((block, columns), lambda i, p: (i, 0))
    resident = lambda *shape: pl.BlockSpec(shape, lambda i, p: (0,) * len(shape))
    spread = pl.BlockSpec((experts_own, block, hidden), lambda i, p: (0, i, 0))
    low = jnp.bfloat16
    shaped = jax.ShapeDtypeStruct
    wide = shaped((experts_own, tokens, hidden), low)
    return pl.pallas_call(
        layer_kernel,
        out_shape=(
            shaped((tokens, features), low),
            wide,
            wide,
            wide,
            wide,
            shaped((tokens, features), low),
            shaped((tokens, features + 128), low),
            shaped((own, features), jnp.float32),
            shaped((own, features), low),
            shaped((own, experts_all), jnp.float32),
        ),
        grid_spec=pltpu.PrefetchScalarGridSpec(
            num_scalar_prefetch=1,
            grid=(tokens // block,),
            in_specs=[
                pl.BlockSpec((groups, block // 2, width), lambda i, p: (0, i, 0)),
                whole_block(*weights[0].shape),
                whole_block(*weights[1].shape),
                *token_rows(block, own, features),
                whole_block(1, features),
                whole_block(features, experts_all),
                rows(features),
                *[pl.BlockSpec(memory_space=pl.ANY)] * 3,
            ],
            out_specs=[
                rows(features),
                spread,
                spread,
                spread,
                spread,
                rows(features),
                rows(features + 128),
                resident(own, features),
                resident(own, features),
                resident(own, experts_all),
            ],
            scratch_shapes=[
                *[pltpu.VMEM(array.shape, low) for array in experts],
                pltpu.VMEM((block, features), jnp.float32),
                pltpu.VMEM((block, experts_all), jnp.float32),
                pltpu.SemaphoreType.DMA((3,)),
            ],
        ),
        compiler_params=pltpu.CompilerParams(vmem_limit_bytes=58 << 20),
        cost_estimate=pl.CostEstimate(
            flops=12 * tokens * features * hidden * experts_own,
            bytes_accessed=6 * features * hidden * experts_own + 20 * tokens * features,
            transcendentals=tokens * hidden * experts_own,
        ),
    )(
        place,
        mixed,
        *weights,
        gathered,
        gathered,
        gain[None, :],
        router,
        cotangent,
        *experts,
    )


def product_kernel(
    e,
    left_any,
    gate_any,
    up_any,
    scaled_one_any,
    scaled_two_any,
    live_any,
    out_one_any,
    out_two_any,
    left_ref,
    right_ref,
    scaled_ref,
    live_ref,
    out_ref,
    came,
    gone,
):
    tiles, _, tile = left_ref.shape
    hidden = scaled_ref.shape[2]
    half = live_ref.shape[2]
    narrow = half - hidden
    top = tiles * tile
    copy = pltpu.make_async_copy
    rights = [
        copy(source.at[e], right_ref.at[:, n * hidden : (n + 1) * hidden], came.at[n])
        for n, source in enumerate((gate_any, up_any))
    ]
    lefts = [
        copy(left_any.at[:, i * tile : (i + 1) * tile], left_ref.at[i], came.at[2 + i])
        for i in range(tiles)
    ]

    def result(n, rows, place):
        target = (out_one_any, out_two_any)[n]
        return copy(out_ref.at[n, rows, :], target.at[rows, :], gone.at[place])

    def tile_rows(i):
        return pl.ds(pl.multiple_of(i * tile, tile), tile)

    downs = []
    for n, source in enumerate((scaled_one_any, scaled_two_any)):
        place = 2 + tiles + 2 * n
        downs.append(copy(source.at[e], scaled_ref.at[n], came.at[place]))
        downs.append(
            copy(
                live_any.at[:, n * half : (n + 1) * half], live_ref.at[n], came.at[place + 1]
            )
        )
    for each in rights + lefts + downs:
        each.start()
    for each in rights:
        each.wait()

    @pl.loop(0, tiles)
    def _(i):
        copy(left_any.at[:, tile_rows(i)], left_ref.at[i], came.at[2 + i]).wait()
        both = dot(left_ref[i], right_ref[...], ROWS).astype(out_ref.dtype)
        for n in range(2):
            out_ref[n, tile_rows(i), :] = both[:, n * hidden : (n + 1) * hidden]
            result(n, tile_rows(i), 2 * i + n).start()

    rest = slice(top, top + half)
    for n in range(2):
        downs[2 * n].wait()
        downs[2 * n + 1].wait()
        product = dot(scaled_ref[n], live_ref[n], ROWS).astype(out_ref.dtype)
        out_ref[n, top : top + hidden, :] = product[:, :hidden]
        out_ref[n, top + hidden : top + half, :narrow] = product[:narrow, hidden:]
        out_ref[n, top + hidden : top + half, narrow:] = product[narrow:, hidden:]
        result(n, rest, 2 * tiles + n).start()

    @pl.loop(0, tiles)
    def _(i):
        for n in range(2):
            result(n, tile_rows(i), 2 * i + n).wait()

    for n in range(2):
        result(n, rest, 2 * tiles + n).wait()


def expert_products(left, gate, up, scaled_one, scaled_two, live, e, dtype):
    tokens, features = left.shape
    hidden = gate.shape[2]
    half = features // 2
    tile = 512
    tiles = features // tile
    rows = features + half
    low = jnp.bfloat16
    anywhere = pl.BlockSpec(memory_space=pl.ANY)
    return pl.pallas_call(
        lambda *refs: product_kernel(e, *refs),
        name="expert_products",
        out_shape=(jax.ShapeDtypeStruct((rows, hidden), dtype),) * 2,
        in_specs=[anywhere] * 6,
        out_specs=[anywhere] * 2,
        scratch_shapes=[
            pltpu.VMEM((tiles, tokens, tile), low),
            pltpu.VMEM((tokens, 2 * hidden), low),
            pltpu.VMEM((2, tokens, hidden), low),
            pltpu.VMEM((2, tokens, half), low),
            pltpu.VMEM((2, rows, hidden), dtype),
            pltpu.SemaphoreType.DMA((6 + tiles,)),
            pltpu.SemaphoreType.DMA((2 * tiles + 2,)),
        ],
        compiler_params=pltpu.CompilerParams(vmem_limit_bytes=58 << 20),
        cost_estimate=pl.CostEstimate(flops=0, bytes_accessed=tokens, transcendentals=0),
    )(left, gate, up, scaled_one, scaled_two, live)


def output_kernel(place_ref, scaled_ref, down_weight_ref, out_ref):
    experts_own, _, features = down_weight_ref.shape
    size = 512

    @pl.loop(0, features // size)
    def _(index):
        part = pl.ds(pl.multiple_of(index * size, size), size)
        out = 0.0
        for e in range(experts_own):
            slot = slot_of(e, place_ref[2], experts_own)
            out = out + dot(scaled_ref[slot], down_weight_ref[e, :, part])
        out_ref[:, part] = out.astype(jnp.bfloat16)


def output_rows(place, scaled, w_down, block):
    experts_own, tokens, hidden = scaled.shape
    features = w_down.shape[2]
    return pl.pallas_call(
        output_kernel,
        out_shape=jax.ShapeDtypeStruct((tokens, features), jnp.bfloat16),
        grid_spec=pltpu.PrefetchScalarGridSpec(
            num_scalar_prefetch=1,
            grid=(tokens // block,),
            in_specs=[
                pl.BlockSpec((experts_own, block, hidden), lambda i, p: (0, i, 0)),
                whole_block(*w_down.shape),
            ],
            out_specs=pl.BlockSpec((block, features), lambda i, p: (i, 0)),
        ),
        compiler_params=pltpu.CompilerParams(vmem_limit_bytes=52 << 20),
        cost_estimate=pl.CostEstimate(flops=0, bytes_accessed=tokens, transcendentals=0),
    )(place, scaled, w_down)


def turn_kernel(
    place_ref,
    sum_ref,
    gates_ref,
    router_ref,
    gain_ref,
    middle_ref,
    live_ref,
    low_ref,
    high_ref,
    grad_middle_ref,
    branch_ref,
    mixed_ref,
    logits_ref,
    gain_grad_ref,
):
    features = middle_ref.shape[1]
    experts = gates_ref.shape[1]
    groups, _, width = mixed_ref.shape
    extra = sum_ref[:, features:].astype(jnp.float32)
    grad_gates = extra[:, :experts] + extra[:, experts : 2 * experts]
    gates = gates_ref[...]
    grad_logits = gates * (grad_gates - jnp.sum(gates * grad_gates, -1, keepdims=True))
    grad_logits = grad_logits.astype(jnp.bfloat16)
    logits_ref[...] = grad_logits
    grad = sum_ref[:, :features].astype(jnp.float32) + dot(grad_logits, router_ref[...], COLUMNS)
    middle = middle_ref[...]
    scale = lax.rsqrt(jnp.mean(middle * middle, -1, keepdims=True) + EPS)
    base = middle * scale
    gain_grad_ref[...] = jnp.sum(grad * base, 0, keepdims=True)
    grad_middle = live_ref[...].astype(jnp.float32) + norm_back(grad * gain_ref[...], base, scale)
    grad_middle_ref[...] = grad_middle
    branch = grad_middle.astype(jnp.bfloat16)
    branch_ref[...] = branch
    for half, weight_ref in enumerate((low_ref, high_ref)):
        mixed = dot(branch, weight_ref[...], COLUMNS).astype(jnp.bfloat16)
        for g in range(groups // 2):
            mixed_ref[half * (groups // 2) + g] = mixed[:, g * width : (g + 1) * width]


def turn_rows(place, sums, gates, router, gain, middle, live, weights):
    own, features = sums.shape[0], middle.shape[1]
    experts = gates.shape[1]
    groups = KEY_VALUE_HEADS
    shaped = jax.ShapeDtypeStruct
    rows = lambda width: pl.BlockSpec((own, width), lambda i, p: (p[1], 0))
    resident = lambda *shape: pl.BlockSpec(shape, lambda i, p: (0,) * len(shape))
    outs = (
        shaped((own, features), jnp.float32),
        shaped((own, features), jnp.bfloat16),
        shaped((groups, own, features // groups), jnp.bfloat16),
        shaped((own, experts), jnp.bfloat16),
        shaped((1, features), jnp.float32),
    )
    return pl.pallas_call(
        turn_kernel,
        out_shape=outs,
        grid_spec=pltpu.PrefetchScalarGridSpec(
            num_scalar_prefetch=1,
            grid=(1,),
            in_specs=[
                whole_block(*sums.shape),
                whole_block(*gates.shape),
                whole_block(*router.shape),
                whole_block(1, features),
                whole_block(*middle.shape),
                rows(features),
                whole_block(*weights[0].shape),
                whole_block(*weights[1].shape),
            ],
            out_specs=[resident(*out.shape) for out in outs],
        ),
        compiler_params=pltpu.CompilerParams(vmem_limit_bytes=58 << 20),
        cost_estimate=pl.CostEstimate(flops=0, bytes_accessed=own, transcendentals=0),
    )(place, sums, gates, router, gain[None, :], middle, live, *weights)


def close_kernel(
    reps,
    place_ref,
    query_ref,
    pair_ref,
    weight_ref,
    hidden_ref,
    normed_ref,
    gain_two_ref,
    normed_own_ref,
    logits_ref,
    rows_ref,
    mixed_ref,
    branch_ref,
    grad_ref,
    kept_one_ref,
    kept_two_ref,
    sent_one_ref,
    sent_two_ref,
    product_ref,
    gain_ref,
    out_ref,
    head_ref,
):
    step = pl.program_id(0)
    both = query_ref.shape[1] + pair_ref.shape[1]
    heads = jnp.concatenate([query_ref[...], pair_ref[...]], 1)
    grad = dot(heads, weight_ref[:, :both], COLUMNS)
    grad_ref[:, : grad.shape[1]] = grad.astype(jnp.bfloat16)
    grad_ref[:, grad.shape[1] :] = rows_ref[...]
    hidden = flat(hidden_ref).astype(jnp.float32)
    scale = lax.rsqrt(jnp.mean(hidden * hidden, -1, keepdims=True) + EPS)
    normed = normed_ref[...]

    @pl.when(step == 0)
    def _():
        gain_ref[...] = jnp.zeros_like(gain_ref)
        product_ref[...] = jnp.zeros_like(product_ref)
        out_ref[...] = jnp.zeros_like(out_ref)

    gain_ref[...] += jnp.sum(grad * (hidden * scale), 0, keepdims=True)
    product_ref[...] += dot(normed, heads, ROWS)
    out_ref[...] += dot(mixed_ref[...], branch_ref[...], ROWS)

    @pl.when(step == pl.num_programs(0) - 1)
    def _():
        features = product_ref.shape[0]
        rows = out_ref.shape[0]
        share = rows // reps
        experts = logits_ref.shape[1]
        line = kept_one_ref.shape[1]
        count = features // rows
        side = (line - features // 2) // (count // 2)
        gains = jnp.concatenate(
            [gain_ref[...], gain_two_ref[...], jnp.zeros((6, features), jnp.float32)], 0
        )
        gains = jnp.transpose(gains)
        router = dot(normed_own_ref[...], logits_ref[...], ROWS)
        rest = jnp.zeros((rows, side - both - 8 - experts), jnp.float32)
        for h in range(2):
            for c in range(count // 2):
                place = h * (count // 2) + c
                part = slice(place * rows, (place + 1) * rows)
                head_ref[h, :, c * side : (c + 1) * side] = jnp.concatenate(
                    [product_ref[part, :], gains[part], router[part], rest], 1
                )
            half = features // 2
            head_ref[h, :, count // 2 * side :] = out_ref[:, h * half : (h + 1) * half]
        sides = ((0, kept_one_ref, sent_one_ref), (1, kept_two_ref, sent_two_ref))
        for h, kept_ref, sent_ref in sides:
            bit = 1 if h == 0 else reps // 2
            for index in range(reps // 2):
                base = index // bit * 2 * bit + index % bit
                here = slice(index * share, (index + 1) * share)
                lower = head_ref[h, base * share : (base + 1) * share, :]
                upper = head_ref[h, (base + bit) * share : (base + bit + 1) * share, :]
                kept_ref[here, :] = jnp.where(place_ref[2 + h] > 0, upper, lower)
                sent_ref[here, :] = jnp.where(place_ref[2 + h] > 0, lower, upper).astype(jnp.bfloat16)


def close_rows(
    place,
    query,
    pair,
    weight,
    gathered,
    normed,
    gain_two_grad,
    normed_two,
    logits,
    out_rows,
    mixed,
    branch,
    reps,
    side,
    block,
):
    tokens, features = normed.shape
    own = logits.shape[0]
    both = query.shape[1] + pair.shape[1]
    rows_own = mixed.shape[1]
    rows = lambda width: pl.BlockSpec((block, width), lambda i, k: (i, 0))
    resident = lambda *shape: pl.BlockSpec(shape, lambda i, k: (0,) * len(shape))
    shaped = jax.ShapeDtypeStruct
    line = features // rows_own // 2 * side + features // 2
    half = (rows_own // 2, line)
    return pl.pallas_call(
        lambda *refs: close_kernel(reps, *refs),
        name="close",
        out_shape=(
            shaped((tokens, 2 * features), jnp.bfloat16),
            shaped(half, jnp.float32),
            shaped(half, jnp.float32),
            shaped(half, jnp.bfloat16),
            shaped(half, jnp.bfloat16),
        ),
        grid_spec=pltpu.PrefetchScalarGridSpec(
            num_scalar_prefetch=1,
            grid=(tokens // block,),
            in_specs=[
                rows(query.shape[1]),
                rows(pair.shape[1]),
                whole_block(*weight.shape),
                token_rows(block, own, features)[0],
                rows(features),
                whole_block(1, features),
                whole_block(own, features),
                whole_block(*logits.shape),
                rows(features),
                rows(rows_own),
                rows(features),
            ],
            out_specs=[rows(2 * features), *[resident(*half)] * 4],
            scratch_shapes=[
                pltpu.VMEM((features, both), jnp.float32),
                pltpu.VMEM((1, features), jnp.float32),
                pltpu.VMEM((rows_own, features), jnp.float32),
                pltpu.VMEM((2, rows_own, line), jnp.float32),
            ],
        ),
        compiler_params=pltpu.CompilerParams(vmem_limit_bytes=56 << 20),
        cost_estimate=pl.CostEstimate(flops=0, bytes_accessed=tokens, transcendentals=0),
    )(
        place,
        query,
        pair,
        weight,
        gathered,
        normed,
        gain_two_grad,
        normed_two,
        logits,
        out_rows,
        mixed,
        branch,
    )


def head_kernel(
    copies,
    side,
    low_ref,
    high_ref,
    query_ref,
    key_ref,
    value_ref,
    out_ref,
    gains_ref,
    router_ref,
):
    groups = KEY_VALUE_HEADS
    count = groups * copies
    halves = [low_ref[...].astype(jnp.float32), high_ref[...].astype(jnp.float32)]
    width = query_ref.shape[1] // groups
    parts = []
    for c in range(count):
        place = c % (count // 2) * side
        parts.append(halves[c // (count // 2)][:, place : place + side])
    heads = []
    small = 0.0
    for g in range(groups):
        total = parts[g * copies]
        for p in range(1, copies):
            total = total + parts[g * copies + p]
        heads.append(total)
        small = small + total[:, width + 2 * HEAD_SIZE :]
    gains_ref[...] = jnp.transpose(small[:, :8])
    router_ref[...] = small[:, 8 : 8 + router_ref.shape[1]]
    query_ref[...] = jnp.concatenate([head[:, :width] for head in heads], 1)
    key_ref[...] = jnp.concatenate([head[:, width : width + HEAD_SIZE] for head in heads], 1)
    value_ref[...] = jnp.concatenate(
        [head[:, width + HEAD_SIZE : width + 2 * HEAD_SIZE] for head in heads], 1
    )
    out_ref[...] = jnp.concatenate([half[:, count // 2 * side :] for half in halves], 1)


def head_outputs(low, high, copies, side, experts):
    rows = low.shape[0]
    groups = KEY_VALUE_HEADS
    query_width = QUERY_HEADS * HEAD_SIZE
    shaped = lambda width: jax.ShapeDtypeStruct((rows, width), jnp.float32)
    return pl.pallas_call(
        lambda *refs: head_kernel(copies, side, *refs),
        name="head_outputs",
        out_shape=(
            shaped(query_width),
            shaped(groups * HEAD_SIZE),
            shaped(groups * HEAD_SIZE),
            shaped(MODEL_WIDTH),
            jax.ShapeDtypeStruct((8, rows), jnp.float32),
            shaped(experts),
        ),
        compiler_params=pltpu.CompilerParams(vmem_limit_bytes=58 << 20),
        cost_estimate=pl.CostEstimate(flops=0, bytes_accessed=rows, transcendentals=0),
    )(low, high)


def fold_down(out_ref, value):
    hidden = out_ref.shape[0]
    narrow = hidden // 2
    out_ref[:, :hidden] = value[:hidden]
    out_ref[:narrow, hidden:] = value[hidden:, :narrow]
    out_ref[narrow:, hidden:] = value[hidden:, narrow:]


def finish_kernel(
    sum_ref, middle_ref, segment_ref, grad_ref, gain_ref, hidden_ref, out_ref, grad_in_ref
):
    features = middle_ref.shape[1]
    live = segment_ref[...] != 0
    rows = middle_ref[...] + sum_ref[:, features:].astype(jnp.float32)
    out_ref[...] = jnp.where(live, rows, 0.0).astype(jnp.bfloat16)
    grad_one = sum_ref[:, :features].astype(jnp.float32)
    hidden = hidden_ref[...].astype(jnp.float32)
    scale = lax.rsqrt(jnp.mean(hidden * hidden, -1, keepdims=True) + EPS)
    grad_in_ref[...] = grad_ref[...] + norm_back(grad_one * gain_ref[...], hidden * scale, scale)


def finish_rows(sums, middle, segments, grad_middle, gain, hidden):
    return pl.pallas_call(
        finish_kernel,
        name="finish_rows",
        out_shape=(
            jax.ShapeDtypeStruct(middle.shape, jnp.bfloat16),
            jax.ShapeDtypeStruct(middle.shape, jnp.float32),
        ),
        compiler_params=pltpu.CompilerParams(vmem_limit_bytes=58 << 20),
        cost_estimate=pl.CostEstimate(flops=0, bytes_accessed=1024, transcendentals=0),
    )(sums, middle, segments, grad_middle, gain[None, :], hidden)


def own_kernel(flags_ref, *refs):
    down_ref = refs[6]
    for side in range(2):

        @pl.when(pl.program_id(0) == side)
        def _():
            own, came = refs[2 * side][...], refs[2 * side + 1][...]
            out_ref = refs[4 + side]
            rows = own.shape[0]
            rest = out_ref.shape[0] - rows
            late = flags_ref[2 + side] > 0
            high = jnp.where(late, own, came).astype(jnp.float32)
            out_ref[:rows, :] = jnp.where(late, came, own).astype(jnp.float32)
            out_ref[rows:, :] = high[:rest]
            fold_down(down_ref, high[rest:])


def own_outputs(flags, chains):
    rows, hidden = chains[0].own.shape
    features = 2 * rows * 2 // 3
    operands = []
    for chain in chains:
        operands += [chain.own, chain.came]
    into = lambda side: pl.BlockSpec((None, features, hidden), lambda s, k: (k[side], 0, 0))
    shaped = lambda *shape: jax.ShapeDtypeStruct((2,) + shape, jnp.float32)
    return pl.pallas_call(
        own_kernel,
        name="own_outputs",
        out_shape=(
            shaped(features, hidden),
            shaped(features, hidden),
            shaped(hidden, features),
        ),
        grid_spec=pltpu.PrefetchScalarGridSpec(
            num_scalar_prefetch=1,
            grid=(2,),
            in_specs=[whole_block(rows, hidden)] * 4,
            out_specs=[
                into(0),
                into(1),
                pl.BlockSpec((None, hidden, features // 2), lambda s, k: (k[s], 0, s)),
            ],
        ),
        compiler_params=pltpu.CompilerParams(vmem_limit_bytes=58 << 20),
        cost_estimate=pl.CostEstimate(flops=0, bytes_accessed=rows, transcendentals=0),
    )(flags, *operands)


def into_kernel(flags_ref, gate_any, up_any, *refs):
    for side in range(2):

        @pl.when(pl.program_id(0) == side)
        def _():
            first_ref, second_ref, third_ref = refs[3 * side : 3 * side + 3]
            out_ref = refs[6 + side]
            half = first_ref.shape[0]
            rest = out_ref.shape[0] - 2 * half
            out_ref[:half, :] = first_ref[...].astype(jnp.float32)
            out_ref[half : 2 * half, :] = second_ref[...].astype(jnp.float32)
            out_ref[2 * half :, :] = third_ref[:rest, :].astype(jnp.float32)


def into_outputs(flags, gate, up, pieces):
    _, features, hidden = gate.shape
    into = lambda side: pl.BlockSpec((None, features, hidden), lambda s, k: (1 - k[side], 0, 0))
    anywhere = pl.BlockSpec(memory_space=pl.ANY)
    return pl.pallas_call(
        into_kernel,
        name="into_outputs",
        out_shape=(jax.ShapeDtypeStruct(gate.shape, gate.dtype),) * 2,
        grid_spec=pltpu.PrefetchScalarGridSpec(
            num_scalar_prefetch=1,
            grid=(2,),
            in_specs=[anywhere] * 2 + [whole_block(*piece.shape) for piece in pieces],
            out_specs=[into(0), into(1)],
        ),
        input_output_aliases={1: 0, 2: 1},
        compiler_params=pltpu.CompilerParams(vmem_limit_bytes=58 << 20),
        cost_estimate=pl.CostEstimate(flops=0, bytes_accessed=features, transcendentals=0),
    )(flags, gate, up, *pieces)


def down_kernel(flags_ref, down_any, *refs):
    for side in range(2):

        @pl.when(pl.program_id(0) == side)
        def _():
            third_ref, last_ref = refs[2 * side : 2 * side + 2]
            out_ref = refs[4]
            rest = third_ref.shape[0] + last_ref.shape[0] - out_ref.shape[1]
            value = jnp.concatenate([third_ref[rest:, :], last_ref[...]], 0)
            fold_down(out_ref, value.astype(jnp.float32))


def down_outputs(flags, down, pieces):
    _, hidden, features = down.shape
    return pl.pallas_call(
        down_kernel,
        name="down_outputs",
        out_shape=jax.ShapeDtypeStruct(down.shape, down.dtype),
        grid_spec=pltpu.PrefetchScalarGridSpec(
            num_scalar_prefetch=1,
            grid=(2,),
            in_specs=[pl.BlockSpec(memory_space=pl.ANY)]
            + [whole_block(*piece.shape) for piece in pieces],
            out_specs=pl.BlockSpec(
                (None, hidden, features // 2), lambda s, k: (1 - k[s], 0, s)
            ),
        ),
        input_output_aliases={1: 0},
        compiler_params=pltpu.CompilerParams(vmem_limit_bytes=58 << 20),
        cost_estimate=pl.CostEstimate(flops=0, bytes_accessed=features, transcendentals=0),
    )(flags, down, *pieces)


def after(values, *others):
    values, _ = lax.optimization_barrier((values, others))
    return values


def swap(value, bit):
    size = lax.axis_size("rep")
    return lax.ppermute(value, "rep", [(i, i ^ bit) for i in range(size)])


def has(bit):
    return (lax.axis_index("rep") & bit) != 0


def join(value, came, bit, axis):
    upper = has(bit)
    return jnp.concatenate(
        [jnp.where(upper, came, value), jnp.where(upper, value, came)], axis
    )


class Chain:
    def __init__(self, order):
        self.order = order
        self.stage = 0
        self.steps = 2 * len(order)

    def send(self, sent):
        bit = self.order[min(self.stage, self.steps - 1 - self.stage)]
        self.sent = sent
        self.stage += 1
        if self.stage < self.steps:
            self.flying = swap(sent, bit)

    def step(self, *others):
        came = after(self.flying, *others)
        self.send(join(self.sent, came, self.order[self.steps - self.stage], 0))
        return self.sent

    def ends(self, *others):
        self.own = self.sent
        self.came = after(self.flying, *others)
        upper = has(self.order[1])
        half = self.own.shape[0] // 2
        begin, end = slice(0, half), slice(half, 2 * half)
        low = lambda rows: jnp.where(upper, self.came[rows], self.own[rows])
        high = lambda rows: jnp.where(upper, self.own[rows], self.came[rows])
        return [low(begin), low(end), high(begin), high(end)]

    def last(self, piece):
        return swap(piece, self.order[0])


def halve_kernel(keeps_ref, *refs):
    count = len(refs) // 3
    for chain in range(2):
        for place in range(0, count, 2):
            value_ref, came_ref = refs[count * chain + place : count * chain + place + 2]
            out_ref = refs[2 * count + chain * (count // 2) + place // 2]
            out_ref[...] = (value_ref[...] + came_ref[...].astype(jnp.float32)).astype(
                out_ref.dtype
            )


def halve_chains(chains, *others):
    order = [chain.order[chain.stage] for chain in chains]
    last = chains[0].stage == len(chains[0].order) - 1
    keeps = jnp.stack([has(bit) for bit in order]).astype(jnp.int32)
    rows, hidden = chains[0].kept.shape
    count = 4
    part = rows // 2 // count
    operands, specs = [], []
    for c, chain in enumerate(chains):
        chain.came = after(chain.flying, *others)
        for flip in (1,) if last else (1, 0):
            index = lambda i, k, c=c, flip=flip: ((k[c] ^ flip) * count + i, 0)
            operands += [chain.kept, chain.came]
            specs += [pl.BlockSpec((part, hidden), index)] * 2
    block = pl.BlockSpec((part, hidden), lambda i, k: (i, 0))
    shaped = lambda dtype: jax.ShapeDtypeStruct((rows // 2, hidden), dtype)
    each = [shaped(jnp.bfloat16)] if last else [shaped(jnp.bfloat16), shaped(jnp.float32)]
    outs = pl.pallas_call(
        halve_kernel,
        out_shape=each * 2,
        grid_spec=pltpu.PrefetchScalarGridSpec(
            num_scalar_prefetch=1,
            grid=(count,),
            in_specs=specs,
            out_specs=[block] * (2 * len(each)),
        ),
        compiler_params=pltpu.CompilerParams(vmem_limit_bytes=58 << 20),
        cost_estimate=pl.CostEstimate(
            flops=60000 * rows * hidden, bytes_accessed=12 * rows * hidden, transcendentals=0
        ),
    )(keeps, *operands)
    for c, chain in enumerate(chains):
        if not last:
            chain.kept = outs[2 * c + 1]
        chain.send(outs[len(each) * c])
    return [chain.sent for chain in chains]


def total_kernel(keeps_ref, *refs):
    for chain in range(2):
        kept_ref, first_ref, second_ref = refs[3 * chain : 3 * chain + 3]
        total = kept_ref[...] + first_ref[...].astype(jnp.float32)
        refs[6 + chain][...] = (total + second_ref[...].astype(jnp.float32)).astype(jnp.bfloat16)


def total_chains(chains, *others):
    keeps = jnp.stack([has(chain.order[-1]) for chain in chains]).astype(jnp.int32)
    rows, hidden = chains[0].kept.shape
    count = 4
    part = rows // 2 // count
    block = pl.BlockSpec((part, hidden), lambda i, k: (i, 0))
    operands, specs = [], []
    for c, chain in enumerate(chains):
        stay = pl.BlockSpec((part, hidden), lambda i, k, c=c: (k[c] * count + i, 0))
        operands += [chain.kept, chain.came, after(chain.flying, *others)]
        specs += [stay, stay, block]
    outs = pl.pallas_call(
        total_kernel,
        out_shape=[jax.ShapeDtypeStruct((rows // 2, hidden), jnp.bfloat16)] * 2,
        grid_spec=pltpu.PrefetchScalarGridSpec(
            num_scalar_prefetch=1, grid=(count,), in_specs=specs, out_specs=[block] * 2
        ),
        compiler_params=pltpu.CompilerParams(vmem_limit_bytes=58 << 20),
        cost_estimate=pl.CostEstimate(flops=0, bytes_accessed=rows, transcendentals=0),
    )(keeps, *operands)
    for chain, out in zip(chains, outs):
        chain.send(out)
    return list(outs)


class Cube:
    def __init__(self, kept, sent, order, share):
        shape = [2] * len(order)
        shape[len(order) - order[0].bit_length()] = 1
        self.value, sent = [array.reshape(*shape, share, -1) for array in (kept, sent)]
        self.order = order
        self.flying = swap(sent, order[0])
        self.stage = 1

    def axis(self, bit):
        return len(self.order) - bit.bit_length()

    def halve(self, *others):
        bit = self.order[self.stage]
        keep = has(bit).astype(jnp.int32)
        part = lambda index: lax.dynamic_slice_in_dim(self.value, index, 1, self.axis(bit))
        self.value, sent = part(keep), part(1 - keep).astype(jnp.bfloat16)
        self.flying = swap(after(sent, *others), bit)
        self.stage += 1
        return sent

    def add(self, *others):
        self.value = self.value + after(self.flying, *others).astype(jnp.float32)

    def back(self, *others):
        self.stage -= 1
        self.flying = swap(after(self.value, *others), self.order[self.stage])
        return self.value

    def join(self, *others):
        bit = self.order[self.stage]
        self.value = join(self.value, after(self.flying, *others), bit, self.axis(bit))


def scalar_call(kernel, outs, scalars, *operands, scratch=(), flops=0):
    whole = lambda array: pl.BlockSpec(array.shape, lambda i, p: (0,) * len(array.shape))
    return pl.pallas_call(
        kernel,
        out_shape=outs,
        grid_spec=pltpu.PrefetchScalarGridSpec(
            num_scalar_prefetch=1,
            grid=(1,),
            in_specs=[whole(array) for array in operands],
            out_specs=[whole(out) for out in outs],
            scratch_shapes=scratch,
        ),
        name="scalar_call",
        compiler_params=pltpu.CompilerParams(vmem_limit_bytes=58 << 20),
        cost_estimate=pl.CostEstimate(flops=flops, bytes_accessed=1024, transcendentals=0),
    )(scalars, *operands)


def pack_kernel(size, side, place_ref, *refs):
    chips = size // 2
    values = refs[:4]
    out_ref = refs[4 + chips]
    all_ref = refs[5 + chips]
    for h in range(2):
        total = values[2 * h][...] + values[2 * h + 1][...].astype(jnp.float32)
        total = total.astype(jnp.bfloat16)
        for c in range(chips):
            all_ref[h * chips + c] = total[:, c * side : (c + 1) * side]
        out_ref[h] = total[:, chips * side :]
    for k in range(chips):
        chip = lax.rem(place_ref[0] - k + chips, chips)
        for core in range(2):
            refs[4 + k][core] = all_ref[2 * chip + core]


def pack_heads(place, cubes, size, side):
    chips = size // 2
    share, line = cubes[0].value.shape[-2:]
    low = jnp.bfloat16
    outs = [jax.ShapeDtypeStruct((2, share, side), low)] * chips
    outs.append(jax.ShapeDtypeStruct((2, share, line - chips * side), low))
    operands = []
    for cube in cubes:
        operands += [cube.value.reshape(share, line), cube.flying.reshape(share, line)]
    *parcels, out_sums = scalar_call(
        lambda *refs: pack_kernel(size, side, *refs),
        outs,
        place,
        *operands,
        scratch=[pltpu.VMEM((size, share, side), low)],
        flops=200000000000,
    )
    return parcels, out_sums


def split_kernel(place_ref, *refs):
    chips = len(refs) - 2
    core = lax.rem(place_ref[1], 2)
    for k in range(chips):
        refs[chips][k] = refs[k][core]
        refs[chips + 1][k] = refs[k][1 - core]


def split_cores(place, got):
    out = jax.ShapeDtypeStruct((len(got),) + got[0].shape[1:], got[0].dtype)
    return scalar_call(split_kernel, [out, out], place, *got)


def unpack_kernel(place_ref, stay_ref, came_ref, out_ref, low_ref, high_ref, all_ref):
    chips, _, side = stay_ref.shape
    core = lax.rem(place_ref[1], 2)
    for k in range(chips):
        chip = lax.rem(place_ref[0] + k, chips)
        all_ref[2 * chip + core] = stay_ref[k]
        all_ref[2 * chip + 1 - core] = came_ref[k]
    for h, rows_ref in enumerate((low_ref, high_ref)):
        for c in range(chips):
            rows_ref[:, c * side : (c + 1) * side] = all_ref[h * chips + c]
        rows_ref[:, chips * side :] = out_ref[h]


def unpack_heads(place, stay, came, out_sums):
    chips, share, side = stay.shape
    line = chips * side + out_sums.shape[2]
    out = jax.ShapeDtypeStruct((share, line), stay.dtype)
    return scalar_call(
        unpack_kernel,
        [out, out],
        place,
        stay,
        came,
        out_sums,
        scratch=[pltpu.VMEM((2 * chips, share, side), stay.dtype)],
        flops=2000000000,
    )


class Exchange:
    def __init__(self, fetched, bits):
        size = fetched.shape[0]
        fetched = fetched.reshape((size,) + (1,) * len(bits) + fetched.shape[1:])
        self.values = [fetched[: size // 2], fetched[size // 2 :]]
        self.orders = (bits, bits[::-1])
        self.stage = 0
        self.fly()

    def fly(self):
        self.flying = [
            swap(value, order[self.stage]) for value, order in zip(self.values, self.orders)
        ]

    def step(self, *others):
        bits = len(self.orders[0])
        for h, order in enumerate(self.orders):
            bit = order[self.stage]
            came = after(self.flying[h], *others)
            self.values[h] = join(self.values[h], came, bit, bits - (bit.bit_length() - 1))
        self.stage += 1
        if self.stage < bits:
            self.fly()
        return list(self.values)

    def finish(self, *others):
        while self.stage < len(self.orders[0]):
            self.step(*others)
        return [value.reshape(-1, value.shape[-1]) for value in self.values]


def per_device(
    inputs,
    segments,
    positions,
    expert_ids,
    attn_gain,
    w_query,
    key_weight,
    value_weight,
    w_out,
    ffn_gain,
    router,
    w_gate,
    w_up,
    w_down,
    grad_out,
):
    size = lax.axis_size("ctx")
    me = lax.axis_index("ctx")
    reps = lax.axis_size("rep")
    bits = [1 << i for i in range(reps.bit_length() - 1)]
    own = inputs.shape[1]
    tokens = size * own
    groups = KEY_VALUE_HEADS
    copies = size // groups
    query_width = HEAD_GROUP * HEAD_SIZE
    width = query_width + 2 * HEAD_SIZE
    copy_index = me % copies
    rows_own = w_out.shape[0]
    experts_own = w_gate.shape[0]
    experts_all = size * experts_own
    block = 2 * own
    chips = size // 2
    chip = me // 2
    odd = me % 2 == 1
    share = rows_own // reps
    share_start = lax.axis_index("rep") * share

    columns = jnp.concatenate(
        [
            segments[0][:, None],
            positions[0][:, None] // 64,
            positions[0][:, None] % 64,
            expert_ids[0],
        ],
        1,
    ).astype(jnp.bfloat16)
    columns = jnp.pad(columns, ((0, 0), (0, 128 - columns.shape[1])))
    shared = lambda array: lax.dynamic_slice_in_dim(array, share_start, share, 0)

    rows = jnp.concatenate(
        [
            jnp.concatenate([inputs[0], columns], 1),
            jnp.pad(shared(w_out), ((0, 0), (0, 128))),
        ],
        0,
    )
    gathered = lax.all_gather(rows, "ctx", axis=0)
    cotangent = lax.all_gather(after(grad_out[0], rows), "ctx", axis=0, tiled=True)

    def from_chip(value, k):
        return lax.ppermute(value, "ctx", [(i, (i - 2 * k) % size) for i in range(size)])

    def from_core(value):
        return lax.ppermute(value, "ctx", [(i, i ^ 1) for i in range(size)])

    def cores(mine, others, axis):
        return jnp.concatenate(
            [jnp.where(odd, others, mine), jnp.where(odd, mine, others)], axis
        )

    side_width = -(-(width + 2 + router.shape[1]) // 128) * 128
    head_columns = jnp.concatenate(
        [
            shared(w_query).reshape(share, groups, query_width),
            shared(key_weight).reshape(share, groups, HEAD_SIZE),
            shared(value_weight).reshape(share, groups, HEAD_SIZE),
            jnp.broadcast_to(shared(attn_gain)[:, None, None], (share, groups, 1)),
            jnp.broadcast_to(shared(ffn_gain)[:, None, None], (share, groups, 1)),
            jnp.broadcast_to(shared(router)[:, None, :], (share, groups, router.shape[1])),
        ],
        -1,
    )
    used = head_columns.shape[-1]
    head_columns = jnp.pad(head_columns, ((0, 0), (0, 0), (0, side_width - used)))
    head_columns = jnp.repeat(jnp.transpose(head_columns, (1, 0, 2)), copies, 0)
    head_columns = lax.all_to_all(head_columns, "ctx", split_axis=0, concat_axis=0, tiled=True)
    head_halves = Exchange(head_columns, bits).finish()
    head_all = jnp.concatenate(head_halves, 0)
    gain_one = head_all[:, width].astype(jnp.float32)
    gain_two = head_all[:, width + 1].astype(jnp.float32)
    router_all = head_all[:, width + 2 : used]

    (
        normed_one,
        query,
        key,
        value,
        mixed,
        packed,
        log_total,
        cosine_table,
        sine_table,
        segment_rows,
    ) = attend(gathered, gain_one, head_halves, own, block)
    out_exchange = Exchange(gathered[:, own:, :MODEL_WIDTH], bits)

    part = tokens // copies
    mixed_all = lax.all_gather(
        after(
            lax.dynamic_slice_in_dim(packed, copy_index * part // 2, part // 2, 0),
            cotangent,
            out_exchange.step(),
        ),
        "ctx",
        axis=0,
    ).reshape(groups, tokens // 2, 2 * query_width)
    w_out_halves = out_exchange.finish()

    flag = lambda bit: has(bit).astype(jnp.int32)
    place = jnp.stack([chip, me, flag(bits[0]), flag(bits[-1])]).astype(jnp.int32)
    (
        normed_two,
        scaled_one,
        scaled_two,
        grad_gate_pre,
        grad_up_pre,
        grad_live,
        grad_rows,
        middle_own,
        normed_own,
        gates_own,
    ) = layer_rows(
        place,
        mixed_all,
        w_out_halves,
        gathered,
        gain_two,
        router_all,
        cotangent,
        (w_gate, w_up, w_down),
        own,
        block,
    )

    products = lambda e, dtype: expert_products(
        normed_two, grad_gate_pre, grad_up_pre, scaled_one, scaled_two, grad_live, e, dtype
    )
    grad_two_sum = lax.psum_scatter(grad_rows, "ctx", scatter_dimension=0, tiled=True)
    normed_two, grad_live = after((normed_two, grad_live), grad_rows)
    chains = [Chain(bits), Chain(bits[::-1])]
    for chain, sent in zip(chains, products(0, jnp.bfloat16)):
        chain.send(sent)
    normed_two, grad_live = after((normed_two, grad_live), *[chain.sent for chain in chains])
    for chain, kept in zip(chains, products(1, jnp.float32)):
        chain.kept = kept
    out_rows = output_rows(place, after(scaled_one, *[c.kept for c in chains]), w_down, block)

    grad_middle, grad_branch, grad_mixed, grad_logits, gain_two_grad = turn_rows(
        place,
        after(grad_two_sum, out_rows),
        gates_own,
        router_all,
        gain_two,
        middle_own,
        grad_live,
        w_out_halves,
    )
    grad_branch_all = lax.all_gather(grad_branch, "ctx", axis=0, tiled=True)

    def deal_chips(blocks):
        blocks = blocks.reshape((chips, 2) + blocks.shape[1:])
        got = [blocks[(chip - k) % chips] for k in range(chips)]
        return jnp.stack([got[0]] + [from_chip(got[k], k) for k in range(1, chips)])

    def deal_cores(got):
        stay = jnp.where(odd, got[:, 1], got[:, 0])
        go = from_core(jnp.where(odd, got[:, 0], got[:, 1]))
        both = cores(stay[:, None], go[:, None], 1)
        both = jnp.concatenate([both, both], 0)
        both = lax.dynamic_slice_in_dim(both, (chips - chip) % chips, chips, 0)
        return both.reshape((size,) + both.shape[2:])

    got = deal_chips(jnp.repeat(grad_mixed, copies, 0))
    sent = [got]
    while chains[0].stage < len(bits):
        sent = halve_chains(chains, *sent)
    grad_mixed_all = deal_cores(after(got, *sent)).reshape(tokens, query_width)
    grad_query, grad_pair = attend_back(
        query,
        grad_mixed_all,
        log_total,
        cosine_table,
        sine_table,
        gathered,
        segment_rows,
        key,
        value,
        own,
    )
    if copies > 1:
        places = jnp.arange(tokens, dtype=jnp.int32)
        counted = (places // part == copy_index)[:, None]
        grad_query = jnp.where(counted, grad_query, jnp.zeros((), jnp.bfloat16))
        grad_pair = jnp.where(counted, grad_pair, jnp.zeros((), jnp.bfloat16))
    sent = total_chains(chains, grad_pair)
    both_rows, *halves = close_rows(
        place,
        after(grad_query, *sent),
        grad_pair,
        head_all,
        gathered,
        normed_one,
        gain_two_grad,
        normed_own,
        grad_logits,
        out_rows,
        lax.dynamic_slice_in_dim(mixed, copy_index * rows_own, rows_own, 1),
        grad_branch_all,
        reps,
        side_width,
        block,
    )
    both_sums = lax.psum_scatter(both_rows, "ctx", scatter_dimension=0, tiled=True)

    line = size // 2 * side_width
    cubes = [
        Cube(halves[h], halves[2 + h], order, share)
        for h, order in enumerate((bits, bits[::-1]))
    ]
    while chains[0].stage < chains[0].steps - 1:
        sent = [chain.step(*halves) for chain in chains]
    pieces = [chain.ends(*halves) for chain in chains]
    sent = [part[0] for part in pieces]
    while cubes[0].stage < len(bits):
        flying = after([cube.flying for cube in cubes], *sent)
        for cube, arrived in zip(cubes, flying):
            cube.flying = arrived
            cube.add()
        sent = [cube.halve() for cube in cubes]
    first = [chain.last(part[0]) for chain, part in zip(chains, pieces)]
    second = [chain.last(after(part[1], *sent)) for chain, part in zip(chains, pieces)]
    flags = jnp.stack([flag(chain.order[n]) for n in range(2) for chain in chains])
    for chain in chains:
        chain.own, chain.came = after((chain.own, chain.came), *sent)
    grad_gate, grad_up, grad_down = own_outputs(flags, chains)
    for cube in cubes:
        cube.flying = after(cube.flying, grad_gate, grad_up, grad_down)
    parcels, out_sums = pack_heads(place, cubes, size, side_width)
    parcels = after(parcels, *first)
    got = [parcels[0]] + [from_chip(parcels[k], k) for k in range(1, chips)]
    stay, go = split_cores(place, got)
    came = from_core(after(go, *second))
    third = [chain.last(after(part[2], *second)) for chain, part in zip(chains, pieces)]
    for cube, value in zip(cubes, unpack_heads(place, stay, came, out_sums)):
        cube.value = value.reshape((1,) * len(bits) + value.shape)
    sent = [cube.back() for cube in cubes]
    fourth = [chain.last(after(part[3], *third)) for chain, part in zip(chains, pieces)]
    while cubes[0].stage > 0:
        for cube in cubes:
            cube.join(*third)
        sent = [cube.back() for cube in cubes]
    arrived = []
    for side in range(2):
        arrived += [first[side], second[side], third[side]]
    grad_gate, grad_up = into_outputs(flags, grad_gate, grad_up, after(arrived, *sent))
    output, grad_in = finish_rows(
        both_sums, middle_own, segments[0][:, None], grad_middle, gain_one, inputs[0]
    )
    for cube in cubes:
        cube.join(grad_gate, grad_up, output, grad_in)
    head_outs = head_outputs(
        *[cube.value.reshape(rows_own, -1) for cube in cubes], copies, side_width, experts_all
    )
    arrived = []
    for side in range(2):
        arrived += [third[side], fourth[side]]
    grad_down = down_outputs(flags, grad_down, after(arrived, head_outs))

    return (
        output[None],
        grad_in[None],
        head_outs[4][0],
        *head_outs[:4],
        head_outs[4][1],
        head_outs[5],
        grad_gate,
        grad_up,
        grad_down,
    )


def solution(mesh):
    return jax.shard_map(
        per_device,
        mesh=mesh,
        in_specs=(
            P("rep", "ctx", None),
            P("rep", "ctx"),
            P("rep", "ctx"),
            P("rep", "ctx", None),
            P("ctx"),
            P("ctx", None),
            P("ctx", None),
            P("ctx", None),
            P("ctx", None),
            P("ctx"),
            P("ctx", None),
            P("ctx", None, None),
            P("ctx", None, None),
            P("ctx", None, None),
            P("rep", "ctx", None),
        ),
        out_specs=(
            P("rep", "ctx", None),
            P("rep", "ctx", None),
            P("ctx"),
            P("ctx", None),
            P("ctx", None),
            P("ctx", None),
            P("ctx", None),
            P("ctx"),
            P("ctx", None),
            P("ctx", None, None),
            P("ctx", None, None),
            P("ctx", None, None),
        ),
        check_vma=False,
    )
```

```python
import jax
import jax.numpy as jnp
from jax import lax
from jax.experimental import pallas as pl
from jax.experimental.pallas import tpu as pltpu
from jax.sharding import PartitionSpec as P

MODEL_WIDTH = 1536
QUERY_HEADS = 24
KEY_VALUE_HEADS = 8
HEAD_GROUP = QUERY_HEADS // KEY_VALUE_HEADS
HEAD_SIZE = 64
TOPK = 8

EPS = 1e-06
THETA = 10000.0
MASK_FLOOR = -1e30

ROWS = (((0,), (0,)), ((), ()))
COLUMNS = (((1,), (1,)), ((), ()))


def dot(left, right, contract=(((1,), (0,)), ((), ()))):
    return lax.dot_general(left, right, contract, preferred_element_type=jnp.float32)


def norm_back(grad_base, base, scale):
    return scale * (grad_base - base * jnp.mean(grad_base * base, -1, keepdims=True))


def turn(rows):
    half = HEAD_SIZE // 2
    return jnp.concatenate([-rows[:, half:], rows[:, :half]], 1)


def turn_back(rows):
    half = HEAD_SIZE // 2
    return jnp.concatenate([rows[:, half:], -rows[:, :half]], 1)


def stack_heads(rows):
    return jnp.concatenate(
        [rows[:, h * HEAD_SIZE : (h + 1) * HEAD_SIZE] for h in range(HEAD_GROUP)], 0
    )


def side_heads(rows):
    block = rows.shape[0] // HEAD_GROUP
    return jnp.concatenate([rows[h * block : (h + 1) * block] for h in range(HEAD_GROUP)], 1)


def lanes(values, combine):
    total = values[:, :128]
    for start in range(128, values.shape[1], 128):
        total = combine(total, values[:, start : start + 128])
    return total


def masked_scores(stacked, keys, row_segments, key_segments, row_start, key_start):
    block = row_segments.shape[0]
    scores = dot(stacked, keys, COLUMNS) * HEAD_SIZE ** (-0.5)
    row_place = row_start + lax.broadcasted_iota(jnp.int32, (block, block), 0)
    key_place = key_start + lax.broadcasted_iota(jnp.int32, (block, block), 1)
    allowed = (row_segments == key_segments) & (key_place <= row_place)
    scores = scores.reshape(HEAD_GROUP, block, block)
    return jnp.where(allowed[None], scores, MASK_FLOOR).reshape(HEAD_GROUP * block, block)


def first_block(row_segments, segment_ref, step):
    here = jnp.max(row_segments[:1, :1])
    segments = segment_ref[...]
    number = lax.broadcasted_iota(jnp.int32, segments.shape, 0)
    return jnp.min(jnp.where((segments == here) & (number <= step), number, step))


def token_rows(block, own, features):
    count = block // own
    return (
        pl.BlockSpec((count, own, features), lambda i, *_: (i, 0, 0)),
        pl.BlockSpec((count, own, 128), lambda i, *_: (i, 0, features // 128)),
    )


def flat(ref):
    return ref[...].reshape(-1, ref.shape[-1])


def whole_block(*shape):
    return pl.BlockSpec(shape, lambda *i: (0,) * len(shape), pipeline_mode=pl.Buffered(1))


def attend_kernel(
    hidden_ref,
    column_ref,
    gain_ref,
    low_ref,
    high_ref,
    rate_ref,
    normed_ref,
    query_ref,
    key_ref,
    value_ref,
    mixed_ref,
    packed_ref,
    log_ref,
    cosine_ref,
    sine_ref,
    segment_ref,
    score_ref,
):
    step = pl.program_id(0)
    block = query_ref.shape[0]
    query_width = query_ref.shape[1]
    width = query_width + 2 * HEAD_SIZE
    here = pl.ds(pl.multiple_of(step * block, block), block)
    columns = flat(column_ref).astype(jnp.float32)
    row_segments = columns[:, :1]
    segment_ref[step] = jnp.transpose(columns)[:1, :]
    angles = (columns[:, 1:2] * 64.0 + columns[:, 2:3]) * rate_ref[...]
    cosine = jnp.cos(angles)
    sine = jnp.sin(angles)
    cosine_ref[...] = cosine
    sine_ref[...] = sine
    hidden = flat(hidden_ref).astype(jnp.float32)
    scale = lax.rsqrt(jnp.mean(hidden * hidden, -1, keepdims=True) + EPS)
    normed = (hidden * scale * gain_ref[...]).astype(jnp.bfloat16)
    normed_ref[...] = normed
    middle = low_ref.shape[0]
    raw = dot(normed[:, :middle], low_ref[:, :width]) + dot(
        normed[:, middle:], high_ref[:, :width]
    )
    key_raw = raw[:, query_width : query_width + HEAD_SIZE]
    key_ref[here, :] = (key_raw * cosine + turn(key_raw) * sine).astype(jnp.bfloat16)
    value_ref[here, :] = raw[:, query_width + HEAD_SIZE :].astype(jnp.bfloat16)
    query_raw = stack_heads(raw[:, :query_width])
    cosine = jnp.concatenate([cosine] * HEAD_GROUP, 0)
    sine = jnp.concatenate([sine] * HEAD_GROUP, 0)
    query = (query_raw * cosine + turn(query_raw) * sine).astype(jnp.bfloat16)
    query_ref[...] = side_heads(query)
    rows = HEAD_GROUP * block
    first = first_block(row_segments, segment_ref, step)

    def first_pass(index, top):
        there = pl.ds(pl.multiple_of(index * block, block), block)
        scores = masked_scores(
            query,
            key_ref[there, :],
            row_segments,
            segment_ref[index],
            step * block,
            index * block,
        )
        score_ref[index] = scores
        return jnp.maximum(top, lanes(scores, jnp.maximum))

    top = lax.fori_loop(
        first, step + 1, first_pass, jnp.full((rows, 128), MASK_FLOOR, jnp.float32)
    )
    top = jnp.max(top, -1, keepdims=True)

    def second_pass(index, carry):
        total, mixed = carry
        there = pl.ds(pl.multiple_of(index * block, block), block)
        weights = jnp.exp(score_ref[index] - top)
        mixed = mixed + dot(weights.astype(jnp.bfloat16), value_ref[there, :])
        return total + lanes(weights, jnp.add), mixed

    total, mixed = lax.fori_loop(
        first,
        step + 1,
        second_pass,
        (
            jnp.zeros((rows, 128), jnp.float32),
            jnp.zeros((rows, HEAD_SIZE), jnp.float32),
        ),
    )
    total = jnp.sum(total, -1, keepdims=True)
    mixed = side_heads((mixed / total).astype(jnp.bfloat16))
    mixed_ref[...] = mixed
    packed_ref[...] = jnp.concatenate([mixed[: block // 2], mixed[block // 2 :]], 1)
    log_ref[...] = (top + jnp.log(total)).reshape(HEAD_GROUP, block, 1)


def attend(gathered, gain, weights, own, block):
    tokens, features = gathered.shape[0] * own, gain.shape[0]
    query_width = HEAD_GROUP * HEAD_SIZE
    steps = tokens // block
    half = jnp.arange(HEAD_SIZE // 2, dtype=jnp.float32)
    rate = THETA ** (-(2.0 * half) / HEAD_SIZE)
    rate = jnp.concatenate([rate, rate])[None, :]
    rows = lambda width: pl.BlockSpec((block, width), lambda i: (i, 0))
    resident = lambda *shape: pl.BlockSpec(shape, lambda i: (0,) * len(shape))
    shaped = jax.ShapeDtypeStruct
    return pl.pallas_call(
        attend_kernel,
        out_shape=(
            shaped((tokens, features), jnp.bfloat16),
            shaped((tokens, query_width), jnp.bfloat16),
            shaped((tokens, HEAD_SIZE), jnp.bfloat16),
            shaped((tokens, HEAD_SIZE), jnp.bfloat16),
            shaped((tokens, query_width), jnp.bfloat16),
            shaped((tokens // 2, 2 * query_width), jnp.bfloat16),
            shaped((HEAD_GROUP, tokens, 1), jnp.float32),
            shaped((tokens, HEAD_SIZE), jnp.float32),
            shaped((tokens, HEAD_SIZE), jnp.float32),
            shaped((steps, 1, block), jnp.float32),
        ),
        grid=(steps,),
        in_specs=[
            *token_rows(block, own, features),
            whole_block(1, features),
            whole_block(*weights[0].shape),
            whole_block(*weights[1].shape),
            whole_block(1, HEAD_SIZE),
        ],
        out_specs=[
            rows(features),
            rows(query_width),
            resident(tokens, HEAD_SIZE),
            resident(tokens, HEAD_SIZE),
            rows(query_width),
            pl.BlockSpec((block // 2, 2 * query_width), lambda i: (i, 0)),
            pl.BlockSpec((HEAD_GROUP, block, 1), lambda i: (0, i, 0)),
            rows(HEAD_SIZE),
            rows(HEAD_SIZE),
            resident(steps, 1, block),
        ],
        scratch_shapes=[pltpu.VMEM((steps, HEAD_GROUP * block, block), jnp.float32)],
        compiler_params=pltpu.CompilerParams(vmem_limit_bytes=48 << 20),
        cost_estimate=pl.CostEstimate(flops=0, bytes_accessed=tokens, transcendentals=0),
    )(gathered, gathered, gain[None, :], *weights, rate)


def attend_back_kernel(
    query_ref,
    grad_ref,
    log_ref,
    cosine_ref,
    sine_ref,
    column_ref,
    segment_ref,
    key_ref,
    value_ref,
    key_cosine_ref,
    key_sine_ref,
    grad_query_ref,
    grad_pair_ref,
    probs_ref,
    grad_probs_ref,
    grad_key_ref,
    grad_value_ref,
):
    step = pl.program_id(0)
    block = query_ref.shape[0]
    rows = HEAD_GROUP * block

    @pl.when(step == 0)
    def _():
        grad_key_ref[...] = jnp.zeros_like(grad_key_ref)
        grad_value_ref[...] = jnp.zeros_like(grad_value_ref)

    query = stack_heads(query_ref[...])
    grad = stack_heads(grad_ref[...])
    log_total = log_ref[...].reshape(rows, 1)
    row_segments = flat(column_ref).astype(jnp.float32)[:, :1]
    first = first_block(row_segments, segment_ref, step)

    def first_pass(index, delta):
        there = pl.ds(pl.multiple_of(index * block, block), block)
        scores = masked_scores(
            query,
            key_ref[there, :],
            row_segments,
            segment_ref[index],
            step * block,
            index * block,
        )
        probs = jnp.exp(scores - log_total)
        grad_probs = dot(grad, value_ref[there, :], COLUMNS)
        probs_ref[index] = probs
        grad_probs_ref[index] = grad_probs
        grad_value_ref[there, :] += dot(probs.astype(jnp.bfloat16), grad, ROWS)
        return delta + lanes(probs * grad_probs, jnp.add)

    delta = lax.fori_loop(first, step + 1, first_pass, jnp.zeros((rows, 128), jnp.float32))
    delta = jnp.sum(delta, -1, keepdims=True)

    def second_pass(index, grad_query):
        there = pl.ds(pl.multiple_of(index * block, block), block)
        grad_scores = (probs_ref[index] * (grad_probs_ref[index] - delta)).astype(jnp.bfloat16)
        grad_key_ref[there, :] += dot(grad_scores, query, ROWS)
        return grad_query + dot(grad_scores, key_ref[there, :])

    grad_query = lax.fori_loop(
        first, step + 1, second_pass, jnp.zeros((rows, HEAD_SIZE), jnp.float32)
    )
    score_scale = HEAD_SIZE ** (-0.5)
    cosine = jnp.concatenate([cosine_ref[...]] * HEAD_GROUP, 0)
    sine = jnp.concatenate([sine_ref[...]] * HEAD_GROUP, 0)
    grad_query = grad_query * score_scale
    grad_query = grad_query * cosine + turn_back(grad_query * sine)
    grad_query_ref[...] = side_heads(grad_query.astype(jnp.bfloat16))

    @pl.when(step == pl.num_programs(0) - 1)
    def _():
        @pl.loop(0, pl.num_programs(0))
        def _(index):
            there = pl.ds(pl.multiple_of(index * block, block), block)
            grad_key = grad_key_ref[there, :] * score_scale
            turned = turn_back(grad_key * key_sine_ref[there, :])
            grad_key = grad_key * key_cosine_ref[there, :] + turned
            grad_pair_ref[there, :] = jnp.concatenate(
                [grad_key, grad_value_ref[there, :]], 1
            ).astype(jnp.bfloat16)


def attend_back(query, grad, log_total, cosine, sine, gathered, segments, key, value, own):
    tokens, query_width = query.shape
    steps, _, block = segments.shape
    features = gathered.shape[2] - 128
    rows = lambda width: pl.BlockSpec((block, width), lambda i: (i, 0))
    resident = lambda *shape: pl.BlockSpec(shape, lambda i: (0,) * len(shape))
    return pl.pallas_call(
        attend_back_kernel,
        out_shape=(
            jax.ShapeDtypeStruct((tokens, query_width), jnp.bfloat16),
            jax.ShapeDtypeStruct((tokens, 2 * HEAD_SIZE), jnp.bfloat16),
        ),
        grid=(steps,),
        in_specs=[
            rows(query_width),
            rows(query_width),
            pl.BlockSpec((HEAD_GROUP, block, 1), lambda i: (0, i, 0)),
            rows(HEAD_SIZE),
            rows(HEAD_SIZE),
            token_rows(block, own, features)[1],
            whole_block(steps, 1, block),
            whole_block(tokens, HEAD_SIZE),
            whole_block(tokens, HEAD_SIZE),
            whole_block(tokens, HEAD_SIZE),
            whole_block(tokens, HEAD_SIZE),
        ],
        out_specs=[rows(query_width), resident(tokens, 2 * HEAD_SIZE)],
        scratch_shapes=[
            pltpu.VMEM((steps, HEAD_GROUP * block, block), jnp.float32),
            pltpu.VMEM((steps, HEAD_GROUP * block, block), jnp.float32),
            pltpu.VMEM((tokens, HEAD_SIZE), jnp.float32),
            pltpu.VMEM((tokens, HEAD_SIZE), jnp.float32),
        ],
        compiler_params=pltpu.CompilerParams(vmem_limit_bytes=48 << 20),
        cost_estimate=pl.CostEstimate(flops=0, bytes_accessed=tokens, transcendentals=0),
    )(query, grad, log_total, cosine, sine, gathered, segments, key, value, cosine, sine)


def slot_of(e, keeps, experts_own):
    pick = experts_own // 2
    high, low = e // pick, e % pick
    return (1 - (high ^ keeps)) * pick + low


def layer_kernel(
    place_ref,
    mixed_ref,
    low_ref,
    high_ref,
    hidden_ref,
    column_ref,
    gain_ref,
    router_ref,
    cotangent_ref,
    gate_any,
    up_any,
    down_any,
    normed_ref,
    scaled_one_ref,
    scaled_two_ref,
    grad_gate_ref,
    grad_up_ref,
    grad_live_ref,
    grad_rows_ref,
    middle_own_ref,
    normed_own_ref,
    gates_own_ref,
    gate_weight_ref,
    up_weight_ref,
    down_weight_ref,
    middle_ref,
    gates_ref,
    semaphores,
):
    step = pl.program_id(0)
    block, features = cotangent_ref.shape
    own = middle_own_ref.shape[0]
    groups = mixed_ref.shape[0]
    experts_own = gate_weight_ref.shape[0]
    experts_all = router_ref.shape[1]
    copies = [
        pltpu.make_async_copy(source, target, semaphores.at[n])
        for n, (source, target) in enumerate(
            (
                (gate_any, gate_weight_ref),
                (up_any, up_weight_ref),
                (down_any, down_weight_ref),
            )
        )
    ]

    @pl.when(step == 0)
    def _():
        for copy in copies:
            copy.start()

    width = mixed_ref.shape[2] // 2
    mixed = jnp.concatenate(
        [
            jnp.concatenate([mixed_ref[g, :, side : side + width] for g in range(groups)], 1)
            for side in (0, width)
        ],
        0,
    )
    half = low_ref.shape[0]
    middle = dot(mixed[:, :half], low_ref[...]) + dot(mixed[:, half:], high_ref[...])
    middle = flat(hidden_ref).astype(jnp.float32) + middle
    middle_ref[...] = middle
    scale = lax.rsqrt(jnp.mean(middle * middle, -1, keepdims=True) + EPS)
    normed = (middle * scale * gain_ref[...]).astype(jnp.bfloat16)
    normed_ref[...] = normed
    logits = dot(normed, router_ref[...])
    columns = flat(column_ref).astype(jnp.float32)
    number = lax.broadcasted_iota(jnp.int32, logits.shape, 1)
    named = columns[:, 3:4] == number.astype(jnp.float32)
    for slot in range(1, TOPK):
        named = named | (columns[:, 3 + slot : 4 + slot] == number.astype(jnp.float32))
    logits = jnp.where(named, logits, MASK_FLOOR)
    shifted = jnp.exp(logits - jnp.max(logits, -1, keepdims=True))
    shifted = jnp.where(named, shifted, 0.0)
    gates = shifted / jnp.sum(shifted, -1, keepdims=True)
    gates_ref[...] = gates
    grad_live_ref[...] = jnp.where(
        columns[:, :1] > 0, cotangent_ref[...], jnp.zeros((), jnp.bfloat16)
    )

    @pl.when(place_ref[0] == step)
    def _():
        there = pl.ds(pl.multiple_of(lax.rem(place_ref[1], 2) * own, own), own)
        middle_own_ref[...] = middle_ref[there, :]
        normed_own_ref[...] = normed_ref[there, :]
        gates_own_ref[...] = gates_ref[there, :]

    @pl.when(step == 0)
    def _():
        for copy in copies:
            copy.wait()

    first = place_ref[1] * experts_own

    def one_expert(e, grad_gates):
        one = slot_of(e, place_ref[2], experts_own)
        two = slot_of(e, place_ref[3], experts_own)
        gates = gates_ref[...]
        gate = jnp.sum(jnp.where(number == first + e, gates, 0.0), -1, keepdims=True)
        gate_pre = dot(normed_ref[...], gate_weight_ref[e])
        up_pre = dot(normed_ref[...], up_weight_ref[e])
        grad_plain = dot(grad_live_ref[...], down_weight_ref[e], COLUMNS)
        sigma = jax.nn.sigmoid(gate_pre)
        silu = gate_pre * sigma
        acted = silu * up_pre
        grad_acted = gate * grad_plain
        scaled = (gate * acted).astype(jnp.bfloat16)
        scaled_one_ref[one] = scaled
        scaled_two_ref[two] = scaled
        grad_gate_ref[one] = (
            grad_acted * up_pre * (sigma * (1.0 + gate_pre * (1.0 - sigma)))
        ).astype(jnp.bfloat16)
        grad_up_ref[two] = (grad_acted * silu).astype(jnp.bfloat16)
        return grad_gates + jnp.where(
            number == first + e, jnp.sum(acted * grad_plain, -1, keepdims=True), 0.0
        )

    grad_gates = lax.fori_loop(
        0, experts_own, one_expert, jnp.zeros(gates.shape, jnp.float32)
    )
    one = [slot_of(e, place_ref[2], experts_own) for e in range(experts_own)]
    two = [slot_of(e, place_ref[3], experts_own) for e in range(experts_own)]
    size = 512

    @pl.loop(0, features // size)
    def _(index):
        part = pl.ds(pl.multiple_of(index * size, size), size)
        grad = 0.0
        for e in range(experts_own):
            grad = grad + dot(grad_gate_ref[one[e]], gate_weight_ref[e, part, :], COLUMNS)
            grad = grad + dot(grad_up_ref[two[e]], up_weight_ref[e, part, :], COLUMNS)
        grad_rows_ref[:, part] = grad.astype(jnp.bfloat16)

    rough = grad_gates.astype(jnp.bfloat16)
    fine = (grad_gates - rough.astype(jnp.float32)).astype(jnp.bfloat16)
    rest = jnp.zeros((block, 128 - 2 * experts_all), jnp.bfloat16)
    grad_rows_ref[:, features:] = jnp.concatenate([rough, fine, rest], 1)


def layer_rows(place, mixed, weights, gathered, gain, router, cotangent, experts, own, block):
    groups, _, width = mixed.shape
    tokens, features = cotangent.shape
    experts_all = router.shape[1]
    experts_own, _, hidden = experts[0].shape
    rows = lambda columns: pl.BlockSpec((block, columns), lambda i, p: (i, 0))
    resident = lambda *shape: pl.BlockSpec(shape, lambda i, p: (0,) * len(shape))
    spread = pl.BlockSpec((experts_own, block, hidden), lambda i, p: (0, i, 0))
    low = jnp.bfloat16
    shaped = jax.ShapeDtypeStruct
    wide = shaped((experts_own, tokens, hidden), low)
    return pl.pallas_call(
        layer_kernel,
        out_shape=(
            shaped((tokens, features), low),
            wide,
            wide,
            wide,
            wide,
            shaped((tokens, features), low),
            shaped((tokens, features + 128), low),
            shaped((own, features), jnp.float32),
            shaped((own, features), low),
            shaped((own, experts_all), jnp.float32),
        ),
        grid_spec=pltpu.PrefetchScalarGridSpec(
            num_scalar_prefetch=1,
            grid=(tokens // block,),
            in_specs=[
                pl.BlockSpec((groups, block // 2, width), lambda i, p: (0, i, 0)),
                whole_block(*weights[0].shape),
                whole_block(*weights[1].shape),
                *token_rows(block, own, features),
                whole_block(1, features),
                whole_block(features, experts_all),
                rows(features),
                *[pl.BlockSpec(memory_space=pl.ANY)] * 3,
            ],
            out_specs=[
                rows(features),
                spread,
                spread,
                spread,
                spread,
                rows(features),
                rows(features + 128),
                resident(own, features),
                resident(own, features),
                resident(own, experts_all),
            ],
            scratch_shapes=[
                *[pltpu.VMEM(array.shape, low) for array in experts],
                pltpu.VMEM((block, features), jnp.float32),
                pltpu.VMEM((block, experts_all), jnp.float32),
                pltpu.SemaphoreType.DMA((3,)),
            ],
        ),
        compiler_params=pltpu.CompilerParams(vmem_limit_bytes=58 << 20),
        cost_estimate=pl.CostEstimate(
            flops=12 * tokens * features * hidden * experts_own,
            bytes_accessed=6 * features * hidden * experts_own + 20 * tokens * features,
            transcendentals=tokens * hidden * experts_own,
        ),
    )(
        place,
        mixed,
        *weights,
        gathered,
        gathered,
        gain[None, :],
        router,
        cotangent,
        *experts,
    )


def product_kernel(
    e,
    left_any,
    gate_any,
    up_any,
    scaled_one_any,
    scaled_two_any,
    live_any,
    out_one_any,
    out_two_any,
    left_ref,
    right_ref,
    scaled_ref,
    live_ref,
    out_ref,
    came,
    gone,
):
    tiles, _, tile = left_ref.shape
    hidden = scaled_ref.shape[2]
    half = live_ref.shape[2]
    narrow = half - hidden
    top = tiles * tile
    copy = pltpu.make_async_copy
    rights = [
        copy(source.at[e], right_ref.at[:, n * hidden : (n + 1) * hidden], came.at[n])
        for n, source in enumerate((gate_any, up_any))
    ]
    lefts = [
        copy(left_any.at[:, i * tile : (i + 1) * tile], left_ref.at[i], came.at[2 + i])
        for i in range(tiles)
    ]

    def result(n, rows, place):
        target = (out_one_any, out_two_any)[n]
        return copy(out_ref.at[n, rows, :], target.at[rows, :], gone.at[place])

    def tile_rows(i):
        return pl.ds(pl.multiple_of(i * tile, tile), tile)

    downs = []
    for n, source in enumerate((scaled_one_any, scaled_two_any)):
        place = 2 + tiles + 2 * n
        downs.append(copy(source.at[e], scaled_ref.at[n], came.at[place]))
        downs.append(
            copy(
                live_any.at[:, n * half : (n + 1) * half], live_ref.at[n], came.at[place + 1]
            )
        )
    for each in rights + lefts + downs:
        each.start()
    for each in rights:
        each.wait()

    @pl.loop(0, tiles)
    def _(i):
        copy(left_any.at[:, tile_rows(i)], left_ref.at[i], came.at[2 + i]).wait()
        both = dot(left_ref[i], right_ref[...], ROWS).astype(out_ref.dtype)
        for n in range(2):
            out_ref[n, tile_rows(i), :] = both[:, n * hidden : (n + 1) * hidden]
            result(n, tile_rows(i), 2 * i + n).start()

    rest = slice(top, top + half)
    for n in range(2):
        downs[2 * n].wait()
        downs[2 * n + 1].wait()
        product = dot(scaled_ref[n], live_ref[n], ROWS).astype(out_ref.dtype)
        out_ref[n, top : top + hidden, :] = product[:, :hidden]
        out_ref[n, top + hidden : top + half, :narrow] = product[:narrow, hidden:]
        out_ref[n, top + hidden : top + half, narrow:] = product[narrow:, hidden:]
        result(n, rest, 2 * tiles + n).start()

    @pl.loop(0, tiles)
    def _(i):
        for n in range(2):
            result(n, tile_rows(i), 2 * i + n).wait()

    for n in range(2):
        result(n, rest, 2 * tiles + n).wait()


def expert_products(left, gate, up, scaled_one, scaled_two, live, e, dtype):
    tokens, features = left.shape
    hidden = gate.shape[2]
    half = features // 2
    tile = 512
    tiles = features // tile
    rows = features + half
    low = jnp.bfloat16
    anywhere = pl.BlockSpec(memory_space=pl.ANY)
    return pl.pallas_call(
        lambda *refs: product_kernel(e, *refs),
        name="expert_products",
        out_shape=(jax.ShapeDtypeStruct((rows, hidden), dtype),) * 2,
        in_specs=[anywhere] * 6,
        out_specs=[anywhere] * 2,
        scratch_shapes=[
            pltpu.VMEM((tiles, tokens, tile), low),
            pltpu.VMEM((tokens, 2 * hidden), low),
            pltpu.VMEM((2, tokens, hidden), low),
            pltpu.VMEM((2, tokens, half), low),
            pltpu.VMEM((2, rows, hidden), dtype),
            pltpu.SemaphoreType.DMA((6 + tiles,)),
            pltpu.SemaphoreType.DMA((2 * tiles + 2,)),
        ],
        compiler_params=pltpu.CompilerParams(vmem_limit_bytes=58 << 20),
        cost_estimate=pl.CostEstimate(flops=0, bytes_accessed=tokens, transcendentals=0),
    )(left, gate, up, scaled_one, scaled_two, live)


def output_kernel(place_ref, scaled_ref, down_weight_ref, out_ref):
    experts_own, _, features = down_weight_ref.shape
    size = 512

    @pl.loop(0, features // size)
    def _(index):
        part = pl.ds(pl.multiple_of(index * size, size), size)
        out = 0.0
        for e in range(experts_own):
            slot = slot_of(e, place_ref[2], experts_own)
            out = out + dot(scaled_ref[slot], down_weight_ref[e, :, part])
        out_ref[:, part] = out.astype(jnp.bfloat16)


def output_rows(place, scaled, w_down, block):
    experts_own, tokens, hidden = scaled.shape
    features = w_down.shape[2]
    return pl.pallas_call(
        output_kernel,
        out_shape=jax.ShapeDtypeStruct((tokens, features), jnp.bfloat16),
        grid_spec=pltpu.PrefetchScalarGridSpec(
            num_scalar_prefetch=1,
            grid=(tokens // block,),
            in_specs=[
                pl.BlockSpec((experts_own, block, hidden), lambda i, p: (0, i, 0)),
                whole_block(*w_down.shape),
            ],
            out_specs=pl.BlockSpec((block, features), lambda i, p: (i, 0)),
        ),
        compiler_params=pltpu.CompilerParams(vmem_limit_bytes=52 << 20),
        cost_estimate=pl.CostEstimate(flops=0, bytes_accessed=tokens, transcendentals=0),
    )(place, scaled, w_down)


def turn_kernel(
    place_ref,
    sum_ref,
    gates_ref,
    router_ref,
    gain_ref,
    middle_ref,
    live_ref,
    low_ref,
    high_ref,
    grad_middle_ref,
    branch_ref,
    mixed_ref,
    logits_ref,
    gain_grad_ref,
):
    features = middle_ref.shape[1]
    experts = gates_ref.shape[1]
    groups, _, width = mixed_ref.shape
    extra = sum_ref[:, features:].astype(jnp.float32)
    grad_gates = extra[:, :experts] + extra[:, experts : 2 * experts]
    gates = gates_ref[...]
    grad_logits = gates * (grad_gates - jnp.sum(gates * grad_gates, -1, keepdims=True))
    grad_logits = grad_logits.astype(jnp.bfloat16)
    logits_ref[...] = grad_logits
    grad = sum_ref[:, :features].astype(jnp.float32) + dot(grad_logits, router_ref[...], COLUMNS)
    middle = middle_ref[...]
    scale = lax.rsqrt(jnp.mean(middle * middle, -1, keepdims=True) + EPS)
    base = middle * scale
    gain_grad_ref[...] = jnp.sum(grad * base, 0, keepdims=True)
    grad_middle = live_ref[...].astype(jnp.float32) + norm_back(grad * gain_ref[...], base, scale)
    grad_middle_ref[...] = grad_middle
    branch = grad_middle.astype(jnp.bfloat16)
    branch_ref[...] = branch
    for half, weight_ref in enumerate((low_ref, high_ref)):
        mixed = dot(branch, weight_ref[...], COLUMNS).astype(jnp.bfloat16)
        for g in range(groups // 2):
            mixed_ref[half * (groups // 2) + g] = mixed[:, g * width : (g + 1) * width]


def turn_rows(place, sums, gates, router, gain, middle, live, weights):
    own, features = sums.shape[0], middle.shape[1]
    experts = gates.shape[1]
    groups = KEY_VALUE_HEADS
    shaped = jax.ShapeDtypeStruct
    rows = lambda width: pl.BlockSpec((own, width), lambda i, p: (p[1], 0))
    resident = lambda *shape: pl.BlockSpec(shape, lambda i, p: (0,) * len(shape))
    outs = (
        shaped((own, features), jnp.float32),
        shaped((own, features), jnp.bfloat16),
        shaped((groups, own, features // groups), jnp.bfloat16),
        shaped((own, experts), jnp.bfloat16),
        shaped((1, features), jnp.float32),
    )
    return pl.pallas_call(
        turn_kernel,
        out_shape=outs,
        grid_spec=pltpu.PrefetchScalarGridSpec(
            num_scalar_prefetch=1,
            grid=(1,),
            in_specs=[
                whole_block(*sums.shape),
                whole_block(*gates.shape),
                whole_block(*router.shape),
                whole_block(1, features),
                whole_block(*middle.shape),
                rows(features),
                whole_block(*weights[0].shape),
                whole_block(*weights[1].shape),
            ],
            out_specs=[resident(*out.shape) for out in outs],
        ),
        compiler_params=pltpu.CompilerParams(vmem_limit_bytes=58 << 20),
        cost_estimate=pl.CostEstimate(flops=0, bytes_accessed=own, transcendentals=0),
    )(place, sums, gates, router, gain[None, :], middle, live, *weights)


def close_kernel(
    reps,
    place_ref,
    query_ref,
    pair_ref,
    weight_ref,
    hidden_ref,
    normed_ref,
    gain_two_ref,
    normed_own_ref,
    logits_ref,
    rows_ref,
    mixed_ref,
    branch_ref,
    grad_ref,
    kept_one_ref,
    kept_two_ref,
    sent_one_ref,
    sent_two_ref,
    product_ref,
    gain_ref,
    out_ref,
    head_ref,
):
    step = pl.program_id(0)
    both = query_ref.shape[1] + pair_ref.shape[1]
    heads = jnp.concatenate([query_ref[...], pair_ref[...]], 1)
    grad = dot(heads, weight_ref[:, :both], COLUMNS)
    grad_ref[:, : grad.shape[1]] = grad.astype(jnp.bfloat16)
    grad_ref[:, grad.shape[1] :] = rows_ref[...]
    hidden = flat(hidden_ref).astype(jnp.float32)
    scale = lax.rsqrt(jnp.mean(hidden * hidden, -1, keepdims=True) + EPS)
    normed = normed_ref[...]

    @pl.when(step == 0)
    def _():
        gain_ref[...] = jnp.zeros_like(gain_ref)
        product_ref[...] = jnp.zeros_like(product_ref)
        out_ref[...] = jnp.zeros_like(out_ref)

    gain_ref[...] += jnp.sum(grad * (hidden * scale), 0, keepdims=True)
    product_ref[...] += dot(normed, heads, ROWS)
    out_ref[...] += dot(mixed_ref[...], branch_ref[...], ROWS)

    @pl.when(step == pl.num_programs(0) - 1)
    def _():
        features = product_ref.shape[0]
        rows = out_ref.shape[0]
        share = rows // reps
        experts = logits_ref.shape[1]
        line = kept_one_ref.shape[1]
        count = features // rows
        side = (line - features // 2) // (count // 2)
        gains = jnp.concatenate(
            [gain_ref[...], gain_two_ref[...], jnp.zeros((6, features), jnp.float32)], 0
        )
        gains = jnp.transpose(gains)
        router = dot(normed_own_ref[...], logits_ref[...], ROWS)
        rest = jnp.zeros((rows, side - both - 8 - experts), jnp.float32)
        for h in range(2):
            for c in range(count // 2):
                place = h * (count // 2) + c
                part = slice(place * rows, (place + 1) * rows)
                head_ref[h, :, c * side : (c + 1) * side] = jnp.concatenate(
                    [product_ref[part, :], gains[part], router[part], rest], 1
                )
            half = features // 2
            head_ref[h, :, count // 2 * side :] = out_ref[:, h * half : (h + 1) * half]
        sides = ((0, kept_one_ref, sent_one_ref), (1, kept_two_ref, sent_two_ref))
        for h, kept_ref, sent_ref in sides:
            bit = 1 if h == 0 else reps // 2
            for index in range(reps // 2):
                base = index // bit * 2 * bit + index % bit
                here = slice(index * share, (index + 1) * share)
                lower = head_ref[h, base * share : (base + 1) * share, :]
                upper = head_ref[h, (base + bit) * share : (base + bit + 1) * share, :]
                kept_ref[here, :] = jnp.where(place_ref[2 + h] > 0, upper, lower)
                sent_ref[here, :] = jnp.where(place_ref[2 + h] > 0, lower, upper).astype(jnp.bfloat16)


def close_rows(
    place,
    query,
    pair,
    weight,
    gathered,
    normed,
    gain_two_grad,
    normed_two,
    logits,
    out_rows,
    mixed,
    branch,
    reps,
    side,
    block,
):
    tokens, features = normed.shape
    own = logits.shape[0]
    both = query.shape[1] + pair.shape[1]
    rows_own = mixed.shape[1]
    rows = lambda width: pl.BlockSpec((block, width), lambda i, k: (i, 0))
    resident = lambda *shape: pl.BlockSpec(shape, lambda i, k: (0,) * len(shape))
    shaped = jax.ShapeDtypeStruct
    line = features // rows_own // 2 * side + features // 2
    half = (rows_own // 2, line)
    return pl.pallas_call(
        lambda *refs: close_kernel(reps, *refs),
        name="close",
        out_shape=(
            shaped((tokens, 2 * features), jnp.bfloat16),
            shaped(half, jnp.float32),
            shaped(half, jnp.float32),
            shaped(half, jnp.bfloat16),
            shaped(half, jnp.bfloat16),
        ),
        grid_spec=pltpu.PrefetchScalarGridSpec(
            num_scalar_prefetch=1,
            grid=(tokens // block,),
            in_specs=[
                rows(query.shape[1]),
                rows(pair.shape[1]),
                whole_block(*weight.shape),
                token_rows(block, own, features)[0],
                rows(features),
                whole_block(1, features),
                whole_block(own, features),
                whole_block(*logits.shape),
                rows(features),
                rows(rows_own),
                rows(features),
            ],
            out_specs=[rows(2 * features), *[resident(*half)] * 4],
            scratch_shapes=[
                pltpu.VMEM((features, both), jnp.float32),
                pltpu.VMEM((1, features), jnp.float32),
                pltpu.VMEM((rows_own, features), jnp.float32),
                pltpu.VMEM((2, rows_own, line), jnp.float32),
            ],
        ),
        compiler_params=pltpu.CompilerParams(vmem_limit_bytes=56 << 20),
        cost_estimate=pl.CostEstimate(flops=0, bytes_accessed=tokens, transcendentals=0),
    )(
        place,
        query,
        pair,
        weight,
        gathered,
        normed,
        gain_two_grad,
        normed_two,
        logits,
        out_rows,
        mixed,
        branch,
    )


def head_kernel(
    copies,
    side,
    low_ref,
    high_ref,
    query_ref,
    key_ref,
    value_ref,
    out_ref,
    gains_ref,
    router_ref,
):
    groups = KEY_VALUE_HEADS
    count = groups * copies
    halves = [low_ref[...].astype(jnp.float32), high_ref[...].astype(jnp.float32)]
    width = query_ref.shape[1] // groups
    parts = []
    for c in range(count):
        place = c % (count // 2) * side
        parts.append(halves[c // (count // 2)][:, place : place + side])
    heads = []
    small = 0.0
    for g in range(groups):
        total = parts[g * copies]
        for p in range(1, copies):
            total = total + parts[g * copies + p]
        heads.append(total)
        small = small + total[:, width + 2 * HEAD_SIZE :]
    gains_ref[...] = jnp.transpose(small[:, :8])
    router_ref[...] = small[:, 8 : 8 + router_ref.shape[1]]
    query_ref[...] = jnp.concatenate([head[:, :width] for head in heads], 1)
    key_ref[...] = jnp.concatenate([head[:, width : width + HEAD_SIZE] for head in heads], 1)
    value_ref[...] = jnp.concatenate(
        [head[:, width + HEAD_SIZE : width + 2 * HEAD_SIZE] for head in heads], 1
    )
    out_ref[...] = jnp.concatenate([half[:, count // 2 * side :] for half in halves], 1)


def head_outputs(low, high, copies, side, experts):
    rows = low.shape[0]
    groups = KEY_VALUE_HEADS
    query_width = QUERY_HEADS * HEAD_SIZE
    shaped = lambda width: jax.ShapeDtypeStruct((rows, width), jnp.float32)
    return pl.pallas_call(
        lambda *refs: head_kernel(copies, side, *refs),
        name="head_outputs",
        out_shape=(
            shaped(query_width),
            shaped(groups * HEAD_SIZE),
            shaped(groups * HEAD_SIZE),
            shaped(MODEL_WIDTH),
            jax.ShapeDtypeStruct((8, rows), jnp.float32),
            shaped(experts),
        ),
        compiler_params=pltpu.CompilerParams(vmem_limit_bytes=58 << 20),
        cost_estimate=pl.CostEstimate(flops=0, bytes_accessed=rows, transcendentals=0),
    )(low, high)


def fold_down(out_ref, value):
    hidden = out_ref.shape[0]
    narrow = hidden // 2
    out_ref[:, :hidden] = value[:hidden]
    out_ref[:narrow, hidden:] = value[hidden:, :narrow]
    out_ref[narrow:, hidden:] = value[hidden:, narrow:]


def own_kernel(flags_ref, *refs):
    down_ref = refs[6]
    for side in range(2):

        @pl.when(pl.program_id(0) == side)
        def _():
            own, came = refs[2 * side][...], refs[2 * side + 1][...]
            out_ref = refs[4 + side]
            rows = own.shape[0]
            rest = out_ref.shape[0] - rows
            late = flags_ref[2 + side] > 0
            high = jnp.where(late, own, came).astype(jnp.float32)
            out_ref[:rows, :] = jnp.where(late, came, own).astype(jnp.float32)
            out_ref[rows:, :] = high[:rest]
            fold_down(down_ref, high[rest:])


def own_outputs(flags, chains):
    rows, hidden = chains[0].own.shape
    features = 2 * rows * 2 // 3
    operands = []
    for chain in chains:
        operands += [chain.own, chain.came]
    into = lambda side: pl.BlockSpec((None, features, hidden), lambda s, k: (k[side], 0, 0))
    shaped = lambda *shape: jax.ShapeDtypeStruct((2,) + shape, jnp.float32)
    return pl.pallas_call(
        own_kernel,
        name="own_outputs",
        out_shape=(
            shaped(features, hidden),
            shaped(features, hidden),
            shaped(hidden, features),
        ),
        grid_spec=pltpu.PrefetchScalarGridSpec(
            num_scalar_prefetch=1,
            grid=(2,),
            in_specs=[whole_block(rows, hidden)] * 4,
            out_specs=[
                into(0),
                into(1),
                pl.BlockSpec((None, hidden, features // 2), lambda s, k: (k[s], 0, s)),
            ],
        ),
        compiler_params=pltpu.CompilerParams(vmem_limit_bytes=58 << 20),
        cost_estimate=pl.CostEstimate(flops=0, bytes_accessed=rows, transcendentals=0),
    )(flags, *operands)


def into_kernel(flags_ref, gate_any, up_any, *refs):
    for side in range(2):

        @pl.when(pl.program_id(0) == side)
        def _():
            first_ref, second_ref, third_ref = refs[3 * side : 3 * side + 3]
            out_ref = refs[6 + side]
            half = first_ref.shape[0]
            rest = out_ref.shape[0] - 2 * half
            out_ref[:half, :] = first_ref[...].astype(jnp.float32)
            out_ref[half : 2 * half, :] = second_ref[...].astype(jnp.float32)
            out_ref[2 * half :, :] = third_ref[:rest, :].astype(jnp.float32)


def into_outputs(flags, gate, up, pieces):
    _, features, hidden = gate.shape
    into = lambda side: pl.BlockSpec((None, features, hidden), lambda s, k: (1 - k[side], 0, 0))
    anywhere = pl.BlockSpec(memory_space=pl.ANY)
    return pl.pallas_call(
        into_kernel,
        name="into_outputs",
        out_shape=(jax.ShapeDtypeStruct(gate.shape, gate.dtype),) * 2,
        grid_spec=pltpu.PrefetchScalarGridSpec(
            num_scalar_prefetch=1,
            grid=(2,),
            in_specs=[anywhere] * 2 + [whole_block(*piece.shape) for piece in pieces],
            out_specs=[into(0), into(1)],
        ),
        input_output_aliases={1: 0, 2: 1},
        compiler_params=pltpu.CompilerParams(vmem_limit_bytes=58 << 20),
        cost_estimate=pl.CostEstimate(flops=0, bytes_accessed=features, transcendentals=0),
    )(flags, gate, up, *pieces)


def down_kernel(flags_ref, down_any, *refs):
    for side in range(2):

        @pl.when(pl.program_id(0) == side)
        def _():
            third_ref, last_ref = refs[2 * side : 2 * side + 2]
            out_ref = refs[4]
            rest = third_ref.shape[0] + last_ref.shape[0] - out_ref.shape[1]
            value = jnp.concatenate([third_ref[rest:, :], last_ref[...]], 0)
            fold_down(out_ref, value.astype(jnp.float32))


def down_outputs(flags, down, pieces):
    _, hidden, features = down.shape
    return pl.pallas_call(
        down_kernel,
        name="down_outputs",
        out_shape=jax.ShapeDtypeStruct(down.shape, down.dtype),
        grid_spec=pltpu.PrefetchScalarGridSpec(
            num_scalar_prefetch=1,
            grid=(2,),
            in_specs=[pl.BlockSpec(memory_space=pl.ANY)]
            + [whole_block(*piece.shape) for piece in pieces],
            out_specs=pl.BlockSpec(
                (None, hidden, features // 2), lambda s, k: (1 - k[s], 0, s)
            ),
        ),
        input_output_aliases={1: 0},
        compiler_params=pltpu.CompilerParams(vmem_limit_bytes=58 << 20),
        cost_estimate=pl.CostEstimate(flops=0, bytes_accessed=features, transcendentals=0),
    )(flags, down, *pieces)


def after(values, *others):
    values, _ = lax.optimization_barrier((values, others))
    return values


def swap(value, bit):
    size = lax.axis_size("rep")
    return lax.ppermute(value, "rep", [(i, i ^ bit) for i in range(size)])


def has(bit):
    return (lax.axis_index("rep") & bit) != 0


def join(value, came, bit, axis):
    upper = has(bit)
    return jnp.concatenate(
        [jnp.where(upper, came, value), jnp.where(upper, value, came)], axis
    )


class Chain:
    def __init__(self, order):
        self.order = order
        self.stage = 0
        self.steps = 2 * len(order)

    def send(self, sent):
        bit = self.order[min(self.stage, self.steps - 1 - self.stage)]
        self.sent = sent
        self.stage += 1
        if self.stage < self.steps:
            self.flying = swap(sent, bit)

    def step(self, *others):
        came = after(self.flying, *others)
        self.send(join(self.sent, came, self.order[self.steps - self.stage], 0))
        return self.sent

    def ends(self, *others):
        self.own = self.sent
        self.came = after(self.flying, *others)
        upper = has(self.order[1])
        half = self.own.shape[0] // 2
        begin, end = slice(0, half), slice(half, 2 * half)
        low = lambda rows: jnp.where(upper, self.came[rows], self.own[rows])
        high = lambda rows: jnp.where(upper, self.own[rows], self.came[rows])
        return [low(begin), low(end), high(begin), high(end)]

    def last(self, piece):
        return swap(piece, self.order[0])


def halve_kernel(keeps_ref, *refs):
    count = len(refs) // 3
    for chain in range(2):
        for place in range(0, count, 2):
            value_ref, came_ref = refs[count * chain + place : count * chain + place + 2]
            out_ref = refs[2 * count + chain * (count // 2) + place // 2]
            out_ref[...] = (value_ref[...] + came_ref[...].astype(jnp.float32)).astype(
                out_ref.dtype
            )


def halve_chains(chains, *others):
    order = [chain.order[chain.stage] for chain in chains]
    last = chains[0].stage == len(chains[0].order) - 1
    keeps = jnp.stack([has(bit) for bit in order]).astype(jnp.int32)
    rows, hidden = chains[0].kept.shape
    count = 2
    part = rows // 2 // count
    operands, specs = [], []
    for c, chain in enumerate(chains):
        chain.came = after(chain.flying, *others)
        for flip in (1,) if last else (1, 0):
            index = lambda i, k, c=c, flip=flip: ((k[c] ^ flip) * count + i, 0)
            operands += [chain.kept, chain.came]
            specs += [pl.BlockSpec((part, hidden), index)] * 2
    block = pl.BlockSpec((part, hidden), lambda i, k: (i, 0))
    shaped = lambda dtype: jax.ShapeDtypeStruct((rows // 2, hidden), dtype)
    each = [shaped(jnp.bfloat16)] if last else [shaped(jnp.bfloat16), shaped(jnp.float32)]
    outs = pl.pallas_call(
        halve_kernel,
        out_shape=each * 2,
        grid_spec=pltpu.PrefetchScalarGridSpec(
            num_scalar_prefetch=1,
            grid=(count,),
            in_specs=specs,
            out_specs=[block] * (2 * len(each)),
        ),
        compiler_params=pltpu.CompilerParams(vmem_limit_bytes=58 << 20),
        cost_estimate=pl.CostEstimate(
            flops=60000 * rows * hidden, bytes_accessed=12 * rows * hidden, transcendentals=0
        ),
    )(keeps, *operands)
    for c, chain in enumerate(chains):
        if not last:
            chain.kept = outs[2 * c + 1]
        chain.send(outs[len(each) * c])
    return [chain.sent for chain in chains]


def total_kernel(keeps_ref, *refs):
    for chain in range(2):
        kept_ref, first_ref, second_ref = refs[3 * chain : 3 * chain + 3]
        total = kept_ref[...] + first_ref[...].astype(jnp.float32)
        refs[6 + chain][...] = (total + second_ref[...].astype(jnp.float32)).astype(jnp.bfloat16)


def total_chains(chains, *others):
    keeps = jnp.stack([has(chain.order[-1]) for chain in chains]).astype(jnp.int32)
    rows, hidden = chains[0].kept.shape
    count = 2
    part = rows // 2 // count
    block = pl.BlockSpec((part, hidden), lambda i, k: (i, 0))
    operands, specs = [], []
    for c, chain in enumerate(chains):
        stay = pl.BlockSpec((part, hidden), lambda i, k, c=c: (k[c] * count + i, 0))
        operands += [chain.kept, chain.came, after(chain.flying, *others)]
        specs += [stay, stay, block]
    outs = pl.pallas_call(
        total_kernel,
        out_shape=[jax.ShapeDtypeStruct((rows // 2, hidden), jnp.bfloat16)] * 2,
        grid_spec=pltpu.PrefetchScalarGridSpec(
            num_scalar_prefetch=1, grid=(count,), in_specs=specs, out_specs=[block] * 2
        ),
        compiler_params=pltpu.CompilerParams(vmem_limit_bytes=58 << 20),
        cost_estimate=pl.CostEstimate(flops=0, bytes_accessed=rows, transcendentals=0),
    )(keeps, *operands)
    for chain, out in zip(chains, outs):
        chain.send(out)
    return list(outs)


class Cube:
    def __init__(self, kept, sent, order, share):
        shape = [2] * len(order)
        shape[len(order) - order[0].bit_length()] = 1
        self.value, sent = [array.reshape(*shape, share, -1) for array in (kept, sent)]
        self.order = order
        self.flying = swap(sent, order[0])
        self.stage = 1

    def axis(self, bit):
        return len(self.order) - bit.bit_length()

    def halve(self, *others):
        bit = self.order[self.stage]
        keep = has(bit).astype(jnp.int32)
        part = lambda index: lax.dynamic_slice_in_dim(self.value, index, 1, self.axis(bit))
        self.value, sent = part(keep), part(1 - keep).astype(jnp.bfloat16)
        self.flying = swap(after(sent, *others), bit)
        self.stage += 1
        return sent

    def add(self, *others):
        self.value = self.value + after(self.flying, *others).astype(jnp.float32)

    def back(self, *others):
        self.stage -= 1
        self.flying = swap(after(self.value, *others), self.order[self.stage])
        return self.value

    def join(self, *others):
        bit = self.order[self.stage]
        self.value = join(self.value, after(self.flying, *others), bit, self.axis(bit))


def scalar_call(kernel, outs, scalars, *operands, scratch=(), flops=0):
    whole = lambda array: pl.BlockSpec(array.shape, lambda i, p: (0,) * len(array.shape))
    return pl.pallas_call(
        kernel,
        out_shape=outs,
        grid_spec=pltpu.PrefetchScalarGridSpec(
            num_scalar_prefetch=1,
            grid=(1,),
            in_specs=[whole(array) for array in operands],
            out_specs=[whole(out) for out in outs],
            scratch_shapes=scratch,
        ),
        name="scalar_call",
        compiler_params=pltpu.CompilerParams(vmem_limit_bytes=58 << 20),
        cost_estimate=pl.CostEstimate(flops=flops, bytes_accessed=1024, transcendentals=0),
    )(scalars, *operands)


def pack_kernel(size, side, place_ref, *refs):
    chips = size // 2
    values = refs[:4]
    out_ref = refs[4 + chips]
    all_ref = refs[5 + chips]
    for h in range(2):
        total = values[2 * h][...] + values[2 * h + 1][...].astype(jnp.float32)
        total = total.astype(jnp.bfloat16)
        for c in range(chips):
            all_ref[h * chips + c] = total[:, c * side : (c + 1) * side]
        out_ref[h] = total[:, chips * side :]
    for k in range(chips):
        chip = lax.rem(place_ref[0] - k + chips, chips)
        for core in range(2):
            refs[4 + k][core] = all_ref[2 * chip + core]


def pack_heads(place, cubes, size, side):
    chips = size // 2
    share, line = cubes[0].value.shape[-2:]
    low = jnp.bfloat16
    outs = [jax.ShapeDtypeStruct((2, share, side), low)] * chips
    outs.append(jax.ShapeDtypeStruct((2, share, line - chips * side), low))
    operands = []
    for cube in cubes:
        operands += [cube.value.reshape(share, line), cube.flying.reshape(share, line)]
    *parcels, out_sums = scalar_call(
        lambda *refs: pack_kernel(size, side, *refs),
        outs,
        place,
        *operands,
        scratch=[pltpu.VMEM((size, share, side), low)],
        flops=200000000000,
    )
    return parcels, out_sums


def split_kernel(place_ref, *refs):
    chips = len(refs) - 2
    core = lax.rem(place_ref[1], 2)
    for k in range(chips):
        refs[chips][k] = refs[k][core]
        refs[chips + 1][k] = refs[k][1 - core]


def split_cores(place, got):
    out = jax.ShapeDtypeStruct((len(got),) + got[0].shape[1:], got[0].dtype)
    return scalar_call(split_kernel, [out, out], place, *got)


def unpack_kernel(place_ref, stay_ref, came_ref, out_ref, low_ref, high_ref, all_ref):
    chips, _, side = stay_ref.shape
    core = lax.rem(place_ref[1], 2)
    for k in range(chips):
        chip = lax.rem(place_ref[0] + k, chips)
        all_ref[2 * chip + core] = stay_ref[k]
        all_ref[2 * chip + 1 - core] = came_ref[k]
    for h, rows_ref in enumerate((low_ref, high_ref)):
        for c in range(chips):
            rows_ref[:, c * side : (c + 1) * side] = all_ref[h * chips + c]
        rows_ref[:, chips * side :] = out_ref[h]


def unpack_heads(place, stay, came, out_sums):
    chips, share, side = stay.shape
    line = chips * side + out_sums.shape[2]
    out = jax.ShapeDtypeStruct((share, line), stay.dtype)
    return scalar_call(
        unpack_kernel,
        [out, out],
        place,
        stay,
        came,
        out_sums,
        scratch=[pltpu.VMEM((2 * chips, share, side), stay.dtype)],
    )


class Exchange:
    def __init__(self, fetched, bits):
        size = fetched.shape[0]
        fetched = fetched.reshape((size,) + (1,) * len(bits) + fetched.shape[1:])
        self.values = [fetched[: size // 2], fetched[size // 2 :]]
        self.orders = (bits, bits[::-1])
        self.stage = 0
        self.fly()

    def fly(self):
        self.flying = [
            swap(value, order[self.stage]) for value, order in zip(self.values, self.orders)
        ]

    def step(self, *others):
        bits = len(self.orders[0])
        for h, order in enumerate(self.orders):
            bit = order[self.stage]
            came = after(self.flying[h], *others)
            self.values[h] = join(self.values[h], came, bit, bits - (bit.bit_length() - 1))
        self.stage += 1
        if self.stage < bits:
            self.fly()
        return list(self.values)

    def finish(self, *others):
        while self.stage < len(self.orders[0]):
            self.step(*others)
        return [value.reshape(-1, value.shape[-1]) for value in self.values]


def per_device(
    inputs,
    segments,
    positions,
    expert_ids,
    attn_gain,
    w_query,
    key_weight,
    value_weight,
    w_out,
    ffn_gain,
    router,
    w_gate,
    w_up,
    w_down,
    grad_out,
):
    size = lax.axis_size("ctx")
    me = lax.axis_index("ctx")
    reps = lax.axis_size("rep")
    bits = [1 << i for i in range(reps.bit_length() - 1)]
    own = inputs.shape[1]
    tokens = size * own
    groups = KEY_VALUE_HEADS
    copies = size // groups
    query_width = HEAD_GROUP * HEAD_SIZE
    width = query_width + 2 * HEAD_SIZE
    copy_index = me % copies
    rows_own = w_out.shape[0]
    experts_own = w_gate.shape[0]
    experts_all = size * experts_own
    block = 2 * own
    chips = size // 2
    chip = me // 2
    odd = me % 2 == 1
    share = rows_own // reps
    share_start = lax.axis_index("rep") * share

    columns = jnp.concatenate(
        [
            segments[0][:, None],
            positions[0][:, None] // 64,
            positions[0][:, None] % 64,
            expert_ids[0],
        ],
        1,
    ).astype(jnp.bfloat16)
    columns = jnp.pad(columns, ((0, 0), (0, 128 - columns.shape[1])))
    shared = lambda array: lax.dynamic_slice_in_dim(array, share_start, share, 0)

    rows = jnp.concatenate(
        [
            jnp.concatenate([inputs[0], columns], 1),
            jnp.pad(shared(w_out), ((0, 0), (0, 128))),
        ],
        0,
    )
    gathered = lax.all_gather(rows, "ctx", axis=0)
    cotangent = lax.all_gather(after(grad_out[0], rows), "ctx", axis=0, tiled=True)

    def from_chip(value, k):
        return lax.ppermute(value, "ctx", [(i, (i - 2 * k) % size) for i in range(size)])

    def from_core(value):
        return lax.ppermute(value, "ctx", [(i, i ^ 1) for i in range(size)])

    def cores(mine, others, axis):
        return jnp.concatenate(
            [jnp.where(odd, others, mine), jnp.where(odd, mine, others)], axis
        )

    side_width = -(-(width + 2 + router.shape[1]) // 128) * 128
    head_columns = jnp.concatenate(
        [
            shared(w_query).reshape(share, groups, query_width),
            shared(key_weight).reshape(share, groups, HEAD_SIZE),
            shared(value_weight).reshape(share, groups, HEAD_SIZE),
            jnp.broadcast_to(shared(attn_gain)[:, None, None], (share, groups, 1)),
            jnp.broadcast_to(shared(ffn_gain)[:, None, None], (share, groups, 1)),
            jnp.broadcast_to(shared(router)[:, None, :], (share, groups, router.shape[1])),
        ],
        -1,
    )
    used = head_columns.shape[-1]
    head_columns = jnp.pad(head_columns, ((0, 0), (0, 0), (0, side_width - used)))
    head_columns = jnp.repeat(jnp.transpose(head_columns, (1, 0, 2)), copies, 0)
    head_columns = lax.all_to_all(head_columns, "ctx", split_axis=0, concat_axis=0, tiled=True)
    head_halves = Exchange(head_columns, bits).finish()
    head_all = jnp.concatenate(head_halves, 0)
    gain_one = head_all[:, width].astype(jnp.float32)
    gain_two = head_all[:, width + 1].astype(jnp.float32)
    router_all = head_all[:, width + 2 : used]

    (
        normed_one,
        query,
        key,
        value,
        mixed,
        packed,
        log_total,
        cosine_table,
        sine_table,
        segment_rows,
    ) = attend(gathered, gain_one, head_halves, own, block)
    out_exchange = Exchange(gathered[:, own:, :MODEL_WIDTH], bits)

    part = tokens // copies
    mixed_all = lax.all_gather(
        after(
            lax.dynamic_slice_in_dim(packed, copy_index * part // 2, part // 2, 0),
            cotangent,
            out_exchange.step(),
        ),
        "ctx",
        axis=0,
    ).reshape(groups, tokens // 2, 2 * query_width)
    w_out_halves = out_exchange.finish()

    flag = lambda bit: has(bit).astype(jnp.int32)
    place = jnp.stack([chip, me, flag(bits[0]), flag(bits[-1])]).astype(jnp.int32)
    (
        normed_two,
        scaled_one,
        scaled_two,
        grad_gate_pre,
        grad_up_pre,
        grad_live,
        grad_rows,
        middle_own,
        normed_own,
        gates_own,
    ) = layer_rows(
        place,
        mixed_all,
        w_out_halves,
        gathered,
        gain_two,
        router_all,
        cotangent,
        (w_gate, w_up, w_down),
        own,
        block,
    )

    products = lambda e, dtype: expert_products(
        normed_two, grad_gate_pre, grad_up_pre, scaled_one, scaled_two, grad_live, e, dtype
    )
    grad_two_sum = lax.psum_scatter(grad_rows, "ctx", scatter_dimension=0, tiled=True)
    normed_two, grad_live = after((normed_two, grad_live), grad_rows)
    chains = [Chain(bits), Chain(bits[::-1])]
    for chain, sent in zip(chains, products(0, jnp.bfloat16)):
        chain.send(sent)
    normed_two, grad_live = after((normed_two, grad_live), *[chain.sent for chain in chains])
    for chain, kept in zip(chains, products(1, jnp.float32)):
        chain.kept = kept
    out_rows = output_rows(place, after(scaled_one, *[c.kept for c in chains]), w_down, block)

    grad_middle, grad_branch, grad_mixed, grad_logits, gain_two_grad = turn_rows(
        place,
        after(grad_two_sum, out_rows),
        gates_own,
        router_all,
        gain_two,
        middle_own,
        grad_live,
        w_out_halves,
    )
    grad_branch_all = lax.all_gather(grad_branch, "ctx", axis=0, tiled=True)

    def deal_chips(blocks):
        blocks = blocks.reshape((chips, 2) + blocks.shape[1:])
        got = [blocks[(chip - k) % chips] for k in range(chips)]
        return jnp.stack([got[0]] + [from_chip(got[k], k) for k in range(1, chips)])

    def deal_cores(got):
        stay = jnp.where(odd, got[:, 1], got[:, 0])
        go = from_core(jnp.where(odd, got[:, 0], got[:, 1]))
        both = cores(stay[:, None], go[:, None], 1)
        both = jnp.concatenate([both, both], 0)
        both = lax.dynamic_slice_in_dim(both, (chips - chip) % chips, chips, 0)
        return both.reshape((size,) + both.shape[2:])

    got = deal_chips(jnp.repeat(grad_mixed, copies, 0))
    sent = [got]
    while chains[0].stage < len(bits):
        sent = halve_chains(chains, *sent)
    grad_mixed_all = deal_cores(after(got, *sent)).reshape(tokens, query_width)
    grad_query, grad_pair = attend_back(
        query,
        grad_mixed_all,
        log_total,
        cosine_table,
        sine_table,
        gathered,
        segment_rows,
        key,
        value,
        own,
    )
    if copies > 1:
        places = jnp.arange(tokens, dtype=jnp.int32)
        counted = (places // part == copy_index)[:, None]
        grad_query = jnp.where(counted, grad_query, jnp.zeros((), jnp.bfloat16))
        grad_pair = jnp.where(counted, grad_pair, jnp.zeros((), jnp.bfloat16))
    sent = total_chains(chains, grad_pair)
    both_rows, *halves = close_rows(
        place,
        after(grad_query, *sent),
        grad_pair,
        head_all,
        gathered,
        normed_one,
        gain_two_grad,
        normed_own,
        grad_logits,
        out_rows,
        lax.dynamic_slice_in_dim(mixed, copy_index * rows_own, rows_own, 1),
        grad_branch_all,
        reps,
        side_width,
        block,
    )
    both_sums = lax.psum_scatter(
        both_rows, "ctx", scatter_dimension=0, tiled=True
    ).astype(jnp.float32)
    grad_one, out_sum = both_sums[:, :MODEL_WIDTH], both_sums[:, MODEL_WIDTH:]

    line = size // 2 * side_width
    cubes = [
        Cube(halves[h], halves[2 + h], order, share)
        for h, order in enumerate((bits, bits[::-1]))
    ]
    while chains[0].stage < chains[0].steps - 1:
        sent = [chain.step(*halves) for chain in chains]
    pieces = [chain.ends(*halves) for chain in chains]
    sent = [part[0] for part in pieces]
    while cubes[0].stage < len(bits):
        flying = after([cube.flying for cube in cubes], *sent)
        for cube, arrived in zip(cubes, flying):
            cube.flying = arrived
            cube.add()
        sent = [cube.halve() for cube in cubes]
    first = [chain.last(part[0]) for chain, part in zip(chains, pieces)]
    second = [chain.last(after(part[1], *sent)) for chain, part in zip(chains, pieces)]
    flags = jnp.stack([flag(chain.order[n]) for n in range(2) for chain in chains])
    for chain in chains:
        chain.own, chain.came = after((chain.own, chain.came), *sent)
    grad_gate, grad_up, grad_down = own_outputs(flags, chains)
    for cube in cubes:
        cube.flying = after(cube.flying, grad_gate, grad_up, grad_down)
    parcels, out_sums = pack_heads(place, cubes, size, side_width)
    parcels = after(parcels, *first)
    got = [parcels[0]] + [from_chip(parcels[k], k) for k in range(1, chips)]
    stay, go = split_cores(place, got)
    came = from_core(after(go, *second))
    third = [chain.last(after(part[2], *second)) for chain, part in zip(chains, pieces)]
    for cube, value in zip(cubes, unpack_heads(place, stay, came, out_sums)):
        cube.value = value.reshape((1,) * len(bits) + value.shape)
    sent = [cube.back() for cube in cubes]
    fourth = [chain.last(after(part[3], *third)) for chain, part in zip(chains, pieces)]
    while cubes[0].stage > 0:
        for cube in cubes:
            cube.join(*third)
        sent = [cube.back() for cube in cubes]
    arrived = []
    for side in range(2):
        arrived += [first[side], second[side], third[side]]
    grad_gate, grad_up = into_outputs(flags, grad_gate, grad_up, after(arrived, *sent))
    output = jnp.where((segments[0] != 0)[:, None], middle_own + out_sum, 0.0)
    own_hidden = inputs[0].astype(jnp.float32)
    own_scale = lax.rsqrt(jnp.mean(own_hidden * own_hidden, -1, keepdims=True) + EPS)
    grad_in = grad_middle + norm_back(grad_one * gain_one, own_hidden * own_scale, own_scale)
    for cube in cubes:
        cube.join(grad_gate, grad_up, output, grad_in)
    head_outs = head_outputs(
        *[cube.value.reshape(rows_own, -1) for cube in cubes], copies, side_width, experts_all
    )
    arrived = []
    for side in range(2):
        arrived += [third[side], fourth[side]]
    grad_down = down_outputs(flags, grad_down, after(arrived, head_outs))

    return (
        output.astype(jnp.bfloat16)[None],
        grad_in[None],
        head_outs[4][0],
        *head_outs[:4],
        head_outs[4][1],
        head_outs[5],
        grad_gate,
        grad_up,
        grad_down,
    )


def solution(mesh):
    return jax.shard_map(
        per_device,
        mesh=mesh,
        in_specs=(
            P("rep", "ctx", None),
            P("rep", "ctx"),
            P("rep", "ctx"),
            P("rep", "ctx", None),
            P("ctx"),
            P("ctx", None),
            P("ctx", None),
            P("ctx", None),
            P("ctx", None),
            P("ctx"),
            P("ctx", None),
            P("ctx", None, None),
            P("ctx", None, None),
            P("ctx", None, None),
            P("rep", "ctx", None),
        ),
        out_specs=(
            P("rep", "ctx", None),
            P("rep", "ctx", None),
            P("ctx"),
            P("ctx", None),
            P("ctx", None),
            P("ctx", None),
            P("ctx", None),
            P("ctx"),
            P("ctx", None),
            P("ctx", None, None),
            P("ctx", None, None),
            P("ctx", None, None),
        ),
        check_vma=False,
    )
```
